128 devices in a mesh: axial: 4 (over x), azim: 32 (over z, y, core).
Axes of the slice: x: 4, y: 4, z: 4, core: 2. Of those that a mesh axis runs over, the one named last changes fastest.
Arguments:
- density: float32 [64, 256, 512], P(None, 'azim', 'axial'), may hold values from 0.5 to 2
- velocity: float32 [3, 64, 256, 512], P(None, None, 'azim', 'axial'), may hold values from -3 to 3
- pressure: float32 [64, 256, 512], P(None, 'azim', 'axial'), may hold values from 0.4 to 1.5
- axial_metric: float32 [3, 64, 256, 512], P(None, None, 'azim', 'axial'), may hold values from -4 to 4
- azim_metric: float32 [3, 64, 256, 512], P(None, None, 'azim', 'axial'), may hold values from -4 to 4
- volume: float32 [64, 256, 512], P(None, 'azim', 'axial'), may hold values from 0.5 to 2
- radial_term: float32 [5, 64, 256, 512], P(None, None, 'azim', 'axial'), may hold values from -6 to 6
- panel_area: float32 [256, 512], P('azim', 'axial'), may hold values from 0.5 to 2
- observer_ids: int32 [4, 256, 512], P(None, 'azim', 'axial'), may hold values from 0 to 511
- bin_ids: int32 [4, 256, 512], P(None, 'azim', 'axial'), may hold values from 0 to 127
- weight_ids: int32 [4, 256, 512], P(None, 'azim', 'axial'), may hold values from 0 to 255
- bin_weights: float32 [256], replicated, may hold values from 0.2 to 1
Outputs:
- new_state: float32 [5, 64, 256, 512], P(None, None, 'azim', 'axial')
- signals: float32 [512, 128], P(('axial', 'azim'))
The draws below stay inside these ranges and needn't reach their ends.
All inputs are finite; a program needn't handle non-finite values.
Results may differ from the reference program's by a relative error of at most 0.0003.
Values sent between devices are 32-bit elements; how exact they have to be, the bound alone decides.
A program may use at most 128 MiB of HBM per device.

```python
import math
import jax
import jax.numpy as jnp
from jax import lax

PLANES = 64
OBSERVERS = 512
TIME_BINS = 128
ENTRIES = 4
TABLE = 256
NA = 512
NAZ = 256


def place_ends(array, stream_key, least, largest):
    shape = array.shape
    place = [jax.random.randint(jax.random.fold_in(stream_key, axis), (), 0, shape[axis]) for axis in range(len(shape))]
    array = array.at[tuple(place)].set(least)
    longest = shape.index(max(shape))
    place[longest] = (place[longest] + 1) % shape[longest]
    return array.at[tuple(place)].set(largest)


def levels(rng, shape, cuts, smallest, high):
    factor_of, own = 1.0, jax.random.fold_in(rng, 6)
    for dim, parts in cuts:
        steps = jnp.exp(jax.random.uniform(jax.random.fold_in(own, dim), (parts,), jnp.float32, smallest / len(cuts), high / len(cuts)))
        factor_of = factor_of * jnp.repeat(steps, shape[dim] // parts).reshape([-1 if axis == dim else 1 for axis in range(len(shape))])
    return factor_of


def noise(key, shape, spread, reach, shards=(), kind=jnp.bfloat16):
    values = jax.random.normal(key, shape, jnp.float32) * spread
    if len(shards) > 0:
        values = levels(key, shape, shards, -0.22, 0.18) * values
    return jnp.clip(values, min=-reach, max=reach).astype(kind)


def setup_inputs(seed: int = 0) -> dict:
    key_list = jax.random.split(jax.random.key(seed), 13)
    density = jnp.clip(jnp.exp(math.log(2.0) - 1.3862944 * jax.random.uniform(key_list[0], (PLANES, NAZ, NA), jnp.float32) ** levels(key_list[0], (PLANES, NAZ, NA), ((1, 32), (2, 4)), -0.2, 0.2)), 0.5, 2.0)
    velocity = noise(key_list[1], (3, PLANES, NAZ, NA), 0.5, 3.0, ((2, 32), (3, 4)), jnp.float32)
    pressure = jnp.clip(jnp.exp(math.log(1.5) - 1.3217558 * jax.random.uniform(key_list[2], (PLANES, NAZ, NA), jnp.float32) ** levels(key_list[2], (PLANES, NAZ, NA), ((1, 32), (2, 4)), -0.2, 0.2)), 0.4, 1.5)
    axial_metric = noise(key_list[3], (3, PLANES, NAZ, NA), 1.0, 4.0, ((2, 32), (3, 4)), jnp.float32)
    azim_metric = noise(key_list[4], (3, PLANES, NAZ, NA), 1.0, 4.0, ((2, 32), (3, 4)), jnp.float32)
    volume = jnp.clip(jnp.exp(math.log(2.0) - 1.3862944 * jax.random.uniform(key_list[5], (PLANES, NAZ, NA), jnp.float32) ** levels(key_list[5], (PLANES, NAZ, NA), ((1, 32), (2, 4)), -0.2, 0.2)), 0.5, 2.0)
    radial_term = noise(key_list[6], (5, PLANES, NAZ, NA), 1.0, 6.0, ((2, 32), (3, 4)), jnp.float32)
    panel_area = jnp.clip(jnp.exp(math.log(2.0) - 1.3862944 * jax.random.uniform(key_list[7], (NAZ, NA), jnp.float32) ** levels(key_list[7], (NAZ, NA), ((0, 32), (1, 4)), -0.2, 0.2)), 0.5, 2.0)
    observer_ids = place_ends(jax.random.randint(key_list[8], (ENTRIES, NAZ, NA), 0, OBSERVERS), jax.random.fold_in(key_list[8], 1), 0, OBSERVERS - 1).astype(jnp.int32)
    bin_ids = place_ends(jax.random.randint(key_list[9], (ENTRIES, NAZ, NA), 0, TIME_BINS), jax.random.fold_in(key_list[9], 1), 0, TIME_BINS - 1).astype(jnp.int32)
    weight_ids = place_ends(jax.random.randint(key_list[10], (ENTRIES, NAZ, NA), 0, TABLE), jax.random.fold_in(key_list[10], 1), 0, TABLE - 1).astype(jnp.int32)
    bin_weights = jnp.clip(jax.random.uniform(key_list[11], (TABLE,), jnp.float32, 0.2, 1.0), 0.2, 1.0)
    return dict(density=density, velocity=velocity, pressure=pressure, axial_metric=axial_metric, azim_metric=azim_metric, volume=volume, radial_term=radial_term, panel_area=panel_area, observer_ids=observer_ids, bin_ids=bin_ids, weight_ids=weight_ids, bin_weights=bin_weights)


GAMMA = 1.4
SECTION = 0.25
DERIV_ALPHA = 1.0 / 3.0
FILTER_ALPHA = 0.499
DERIV_A = 14.0 / 9.0
DERIV_B = 1.0 / 9.0

def decay_root(alpha):
    return (-1.0 + math.sqrt(1.0 - 4.0 * alpha * alpha)) / (2.0 * alpha)

def signed_power(base, exponent):
    exponent = jnp.asarray(exponent).astype(jnp.int32)
    parity = jnp.where(exponent % 2 == 0, 1.0, -1.0)
    return parity * jnp.exp(exponent.astype(jnp.float32) * math.log(-base))

def deriv_side(extended, dim):
    length = extended.shape[dim] - 6

    def cells(offset):
        return lax.slice_in_dim(extended, 3 + offset, 3 + offset + length, axis=dim)
    return 0.5 * DERIV_A * (cells(1) - cells(-1)) + 0.25 * DERIV_B * (cells(2) - cells(-2))

def filter_side(extended, dim):
    length = extended.shape[dim] - 6

    def cells(offset):
        return lax.slice_in_dim(extended, 3 + offset, 3 + offset + length, axis=dim)
    beta = FILTER_ALPHA
    coeffs = [(11.0 + 10.0 * beta) / 16.0, (15.0 + 34.0 * beta) / 32.0, (-3.0 + 6.0 * beta) / 16.0, (1.0 - 2.0 * beta) / 32.0]
    total = coeffs[0] * cells(0)
    for shift in range(1, 4):
        total = total + 0.5 * coeffs[shift] * (cells(shift) + cells(-shift))
    return total

def fluxes(density, velocity, pressure, energy, metric, volume):
    contra = metric[0] * velocity[0] + metric[1] * velocity[1] + metric[2] * velocity[2]
    mass_flow = density * contra
    pieces = [volume * mass_flow]
    for comp in range(3):
        pieces.append(volume * (mass_flow * velocity[comp] + metric[comp] * pressure))
    pieces.append(volume * (energy + pressure) * contra)
    return jnp.stack(pieces)

def pad_open(field):
    return jnp.pad(field, ((0, 0), (0, 0), (0, 0), (3, 3)))

def pad_cycle(field):
    return jnp.concatenate([field[:, :, -3:], field, field[:, :, :3]], axis=2)

def open_line(rhs, alpha):
    base = decay_root(alpha)
    factor_g = -alpha / base
    lines = jnp.moveaxis(rhs, 3, 0)

    def forward(carry, row):
        fresh = row + base * carry
        return (fresh, fresh)

    def backward(carry, row):
        fresh = row / factor_g + base * carry
        return (fresh, fresh)
    ignored, upward = lax.scan(forward, jnp.zeros_like(lines[0]), lines)
    ignored, result = lax.scan(backward, jnp.zeros_like(lines[0]), upward, reverse=True)
    return jnp.moveaxis(result, 0, 3)

def cycle_line(rhs, alpha):
    base = decay_root(alpha)
    factor_g = -alpha / base
    lines = jnp.moveaxis(rhs, 2, 0)
    length = lines.shape[0]
    wrap = 1.0 / (1.0 - base ** length)

    def forward(carry, row):
        fresh = row + base * carry
        return (fresh, fresh)
    ignored, upward_zero = lax.scan(forward, jnp.zeros_like(lines[0]), lines)
    steps_ahead = jnp.arange(length, dtype=jnp.int32)
    upward = upward_zero + signed_power(base, steps_ahead + 1)[:, None, None, None] * (upward_zero[-1] * wrap)[None]
    ignored, down_zero = lax.scan(forward, jnp.zeros_like(lines[0]), upward, reverse=True)
    downward = down_zero + signed_power(base, length - steps_ahead)[:, None, None, None] * (down_zero[0] * wrap)[None]
    return jnp.moveaxis(downward / factor_g, 0, 2)

def reference(density, velocity, pressure, axial_metric, azim_metric, volume, radial_term, panel_area, observer_ids, bin_ids, weight_ids, bin_weights):
    energy = pressure / (GAMMA - 1.0) + 0.5 * density * (velocity[0] ** 2 + velocity[1] ** 2 + velocity[2] ** 2)
    state = jnp.concatenate([density[None], density[None] * velocity, energy[None]], axis=0)
    axial_flux = fluxes(density, velocity, pressure, energy, axial_metric, volume)
    azim_flux = fluxes(density, velocity, pressure, energy, azim_metric, volume)
    axial_deriv = open_line(deriv_side(pad_open(axial_flux), 3), DERIV_ALPHA)
    azim_deriv = cycle_line(deriv_side(pad_cycle(azim_flux), 2), DERIV_ALPHA)
    sectioned = state + SECTION * (radial_term - (axial_deriv + azim_deriv) / volume)
    smoothed = open_line(filter_side(pad_open(sectioned), 3), FILTER_ALPHA)
    new_state = cycle_line(filter_side(pad_cycle(smoothed), 2), FILTER_ALPHA)
    surface = new_state[:, 0]
    source = panel_area * (surface[2] + surface[0] - 1.0)
    values = bin_weights[weight_ids] * source[None]
    bucket = observer_ids * TIME_BINS + bin_ids
    signals = jax.ops.segment_sum(values.reshape(-1), bucket.reshape(-1), num_segments=OBSERVERS * TIME_BINS)
    return (new_state, signals.reshape(OBSERVERS, TIME_BINS))
```

```python
import functools
import math

import jax
import jax.numpy as jnp
import ml_dtypes
import numpy as np
from jax import lax
from jax.experimental import pallas as pl
from jax.experimental.pallas import tpu as pltpu
from jax.sharding import PartitionSpec as P

F32 = jnp.float32
BF16 = jnp.bfloat16
MESH = pl.DeviceIdType.MESH

PLANES = 64
FIELDS = 5
ROWS = 8
LANES = 128
AXIAL = 4
AZIM = 32
NA = AXIAL * LANES
NAZ = AZIM * ROWS
SLAB = FIELDS * PLANES
LINES = ROWS * SLAB
BLOCKS = PLANES // 8
SLOTS = 2 * BLOCKS
TILE_ROWS = 8 * FIELDS
HALF = LINES // 2
ENTRY_ROWS = 32
OBSERVERS = 512
TIME_BINS = 128
PEERS = (AZIM - 1) + 2 * (AXIAL - 1)

SECTION = 0.25
DERIV_ALPHA = 1.0 / 3.0
BETA = 0.499


def decay_root(alpha):
    return (-1.0 + math.sqrt(1.0 - 4.0 * alpha * alpha)) / (2.0 * alpha)


DL = decay_root(DERIV_ALPHA)
FL = decay_root(BETA)
C1 = (1.0 / 36.0) / DERIV_ALPHA
DS = 1.0 / math.sqrt(1.0 - 4.0 * DERIV_ALPHA**2)
DK = (7.0 / 9.0 - C1) * DS * (1.0 / DL - DL)
FC = [
    (11.0 + 10.0 * BETA) / 16.0,
    (15.0 + 34.0 * BETA) / 32.0,
    (-3.0 + 6.0 * BETA) / 16.0,
    (1.0 - 2.0 * BETA) / 32.0,
]
FS = 1.0 / math.sqrt(1.0 - 4.0 * BETA**2)
E2 = FC[3] / (2.0 * BETA)
E1 = (FC[2] / 2.0 - E2) / BETA
E0 = (FC[1] / 2.0 - E1 - BETA * E2) / BETA
FK = (FC[0] - E0 - 2.0 * BETA * E1) * FS


def split(values):
    high = values.astype(ml_dtypes.bfloat16)
    low = (values - high.astype(np.float64)).astype(ml_dtypes.bfloat16)
    return high, low


def axial_tables(root, scale, band):
    n, w = NA, LANES
    index = np.arange(n)
    green = scale * (
        np.power(root, np.abs(index[:, None] - index[None, :]))
        - np.power(root, 2 * n - index[:, None] - index[None, :])
    )
    side = np.zeros((n, n))
    for shift, value in band.items():
        side += value * np.eye(n, k=shift)
    whole = green @ side
    left = np.zeros((AXIAL, w))
    right = np.zeros((AXIAL, w))
    for k in range(AXIAL):
        cols = slice(k * w, (k + 1) * w)
        lo, hi = max(0, k * w - 3), min(n, (k + 1) * w + 3)
        m = np.arange(lo, hi)
        left[k] = np.power(root, ((k + 1) * w - m).astype(np.float64)) @ side[lo:hi, cols]
        right[k] = (
            np.power(root, (m - k * w + 1).astype(np.float64))
            - np.power(root, (2 * n - m - k * w + 1).astype(np.float64))
        ) @ side[lo:hi, cols]
    t = np.arange(w)
    own = np.zeros((AXIAL, w, 2 * w), ml_dtypes.bfloat16)
    sent = np.zeros((AXIAL, 2, 32, 2 * w), ml_dtypes.bfloat16)
    taken = np.zeros((AXIAL, 2, 64, 2 * w), ml_dtypes.bfloat16)
    for d in range(AXIAL):
        high, low = split(whole[d * w : (d + 1) * w, d * w : (d + 1) * w].T)
        own[d] = np.concatenate([high, low], axis=1)
        for half in range(2):
            rows = np.zeros((16, w))
            base = half * 4
            rows[base] = left[d]
            rows[base + 1, w - 1] = 1.0
            rows[base + 2, w - 2] = 1.0
            rows[8 + base] = right[d]
            rows[8 + base + 1, 0] = 1.0
            rows[8 + base + 2, 1] = 1.0
            high, low = split(rows)
            sent[d, half] = np.concatenate(
                [np.concatenate([high, high], axis=1), np.concatenate([low, low], axis=1)], axis=0
            )
            rows = np.zeros((32, w))
            for k in range(AXIAL):
                row = k * 8 + half * 4
                i = d * w + t
                if k < d:
                    rows[row] = scale * (
                        np.power(root, (i - (k + 1) * w).astype(np.float64))
                        - np.power(root, (2 * n - i - (k + 1) * w).astype(np.float64))
                    )
                    if k == d - 1:
                        for edge in range(2):
                            col = d * w - 1 - edge
                            for near in range(2 - edge):
                                rows[row + 1 + edge, near] = (
                                    whole[d * w + near, col] - rows[row, near] * left[k, col - k * w]
                                )
                if k > d:
                    rows[row] = scale * np.power(root, (k * w - 1 - i).astype(np.float64))
                    if k == d + 1:
                        for edge in range(2):
                            col = k * w + edge
                            for near in range(2 - edge):
                                rows[row + 1 + edge, w - 1 - near] = (
                                    whole[k * w - 1 - near, col] - rows[row, w - 1 - near] * right[k, edge]
                                )
            high, low = split(rows)
            pair = np.concatenate([high, low], axis=1)
            taken[d, half] = np.concatenate([pair, pair], axis=0)
    return own, sent, taken


def both_tables():
    deriv = axial_tables(DL, DS, {1: 7.0 / 9.0, -1: -7.0 / 9.0, 2: 1.0 / 36.0, -2: -1.0 / 36.0})
    band = {0: FC[0]}
    for shift in range(1, 4):
        band[shift] = band[-shift] = FC[shift] / 2.0
    smooth = axial_tables(FL, FS, band)
    return [np.stack(pair, axis=1) for pair in zip(deriv, smooth)]


def two_terms(value):
    high = value.astype(BF16)
    low = (value - high.astype(F32)).astype(BF16)
    return high, low


def dot_last(left, right):
    return lax.dot_general(left, right, (((1,), (1,)), ((), ())), preferred_element_type=F32)


def dot_first(left, right):
    return lax.dot_general(left, right, (((0,), (0,)), ((), ())), preferred_element_type=F32)


def kernel(
    own_hbm,
    sent_hbm,
    taken_hbm,
    density_hbm,
    velocity_hbm,
    pressure_hbm,
    axial_hbm,
    azim_hbm,
    volume_hbm,
    radial_hbm,
    area_ref,
    observer_ref,
    bin_ref,
    weight_ref,
    table_ref,
    state_hbm,
    signal_ref,
    own,
    sent,
    taken,
    density,
    velocity,
    pressure,
    axial_metric,
    azim_metric,
    volume,
    radial,
    azim_flux,
    base,
    ratio,
    cells,
    lined,
    final,
    edge_send,
    edge_recv,
    moment_send,
    moment_recv,
    start_send,
    start_recv,
    deriv_halo,
    filter_halo,
    observer_hot,
    bin_hot,
    partial,
    part_recv,
    owner_send,
    owner_recv,
    load_sem,
    store_sem,
    edge_send_sem,
    edge_recv_sem,
    moment_send_sem,
    moment_recv_sem,
    start_send_sem,
    start_recv_sem,
    halo_send_sem,
    halo_recv_sem,
    part_send_sem,
    part_recv_sem,
    owner_send_sem,
    owner_recv_sem,
):
    me_a = lax.axis_index("axial")
    me_z = lax.axis_index("azim")
    core = lax.rem(me_z, 2)
    chip = me_z // 2
    twin = me_z + 1 - 2 * core
    reducer = core == 0
    after = lax.rem(me_z + 1, AZIM)
    before = lax.rem(me_z + AZIM - 1, AZIM)

    loads = [
        pltpu.make_async_copy(density_hbm, density, load_sem.at[0]),
        pltpu.make_async_copy(velocity_hbm, velocity, load_sem.at[1]),
        pltpu.make_async_copy(pressure_hbm, pressure, load_sem.at[2]),
        pltpu.make_async_copy(axial_hbm, axial_metric, load_sem.at[3]),
        pltpu.make_async_copy(azim_hbm, azim_metric, load_sem.at[4]),
        pltpu.make_async_copy(volume_hbm, volume, load_sem.at[5]),
        pltpu.make_async_copy(radial_hbm, radial, load_sem.at[6]),
    ]
    for which in range(2):
        loads.append(
            pltpu.make_async_copy(
                own_hbm.at[me_a, which], own.at[which, pl.ds(0, LANES)], load_sem.at[7 + 4 * which]
            )
        )
        loads.append(
            pltpu.make_async_copy(
                own_hbm.at[me_a, which], own.at[which, pl.ds(LANES, LANES)], load_sem.at[8 + 4 * which]
            )
        )
        loads.append(pltpu.make_async_copy(sent_hbm.at[me_a, which], sent.at[which], load_sem.at[9 + 4 * which]))
        loads.append(pltpu.make_async_copy(taken_hbm.at[me_a, which], taken.at[which], load_sem.at[10 + 4 * which]))
    for load in loads:
        load.start()

    barrier = pltpu.get_barrier_semaphore()

    def greet_azim(step, carry):
        other = lax.rem(me_z + step, AZIM)
        pl.semaphore_signal(barrier, inc=1, device_id=(me_a, other), device_id_type=MESH)
        return carry

    lax.fori_loop(1, AZIM, greet_azim, 0)

    def greet_axial(step, carry):
        other = lax.rem(me_a + step, AXIAL)
        pl.semaphore_signal(barrier, inc=1, device_id=(other, me_z), device_id_type=MESH)
        pl.semaphore_signal(barrier, inc=1, device_id=(other, twin), device_id_type=MESH)
        return carry

    lax.fori_loop(1, AXIAL, greet_axial, 0)

    edge_recv[0, pl.ds(me_a, 1)] = jnp.zeros((1, 8, HALF), F32)
    edge_recv[1, pl.ds(me_a, 1)] = jnp.zeros((1, 8, HALF), F32)

    for load in loads:
        load.wait()
    pl.semaphore_wait(barrier, PEERS)

    def send_moments(which, slot):
        target = 2 * slot

        @pl.when(target != me_z)
        def _():
            pltpu.make_async_remote_copy(
                src_ref=moment_send.at[which, slot],
                dst_ref=moment_recv.at[which, me_z],
                send_sem=moment_send_sem.at[which],
                recv_sem=moment_recv_sem.at[which],
                device_id=(me_a, target),
                device_id_type=MESH,
            ).start()

        @pl.when(target == me_z)
        def _():
            pltpu.make_async_copy(
                moment_send.at[which, slot], moment_recv.at[which, me_z], moment_recv_sem.at[which]
            ).start()

    def wait_moment_sends(which):
        @pl.when(reducer)
        def _():
            part = moment_send.at[which, pl.ds(0, SLOTS - 1)]
            pltpu.make_async_copy(part, part, moment_send_sem.at[which]).wait()

        @pl.when(jnp.logical_not(reducer))
        def _():
            part = moment_send.at[which]
            pltpu.make_async_copy(part, part, moment_send_sem.at[which]).wait()

    def reduce_moments(which, root):
        factor = root**ROWS
        wrap = 1.0 / (1.0 - root**NAZ)

        @pl.when(reducer)
        def _():
            part = moment_recv.at[which]
            pltpu.make_async_copy(part, part, moment_recv_sem.at[which]).wait()
            side = lax.rem(chip, 2)

            def place(step):
                return step + side * (AZIM - 1 - 2 * step)

            def gather(step, total):
                return factor * total + moment_recv[which, place(step)]

            first = lax.fori_loop(0, AZIM, gather, jnp.zeros((TILE_ROWS, LANES), F32)) * wrap

            def hand_out(step, now):
                other = place(step)
                start_send[which, other] = now

                @pl.when(other != me_z)
                def _():
                    pltpu.make_async_remote_copy(
                        src_ref=start_send.at[which, other],
                        dst_ref=start_recv.at[which, chip],
                        send_sem=start_send_sem.at[which],
                        recv_sem=start_recv_sem.at[which],
                        device_id=(me_a, other),
                        device_id_type=MESH,
                    ).start()

                @pl.when(other == me_z)
                def _():
                    pltpu.make_async_copy(
                        start_send.at[which, other], start_recv.at[which, chip], start_recv_sem.at[which]
                    ).start()

                return factor * now + moment_recv[which, other]

            lax.fori_loop(0, AZIM, hand_out, first)

    def wait_starts(which):
        part = start_recv.at[which]
        pltpu.make_async_copy(part, part, start_recv_sem.at[which]).wait()

    def wait_start_sends(which):
        @pl.when(reducer)
        def _():
            part = start_send.at[which, pl.ds(0, AZIM - 1)]
            pltpu.make_async_copy(part, part, start_send_sem.at[which]).wait()

    def moments_of(values, root):
        up = root * values[0]
        for row in range(1, ROWS):
            up = root * (up + values[row])
        down = root * values[ROWS - 1]
        for row in range(ROWS - 2, -1, -1):
            down = root * (down + values[row])
        return up, down

    def keep_moments(which, group, field, values, root):
        up, down = moments_of(values, root)
        for half in range(2):
            for side, value in ((0, up), (1, down)):
                moment_send[which, 4 * group + 2 * half + side, pl.ds(8 * field, 8)] = value[8 * half : 8 * half + 8]

    def start_of(which, group, field, side):
        return jnp.concatenate(
            [start_recv[which, 4 * group + 2 * half + side, pl.ds(8 * field, 8)] for half in range(2)], axis=0
        )

    def halo_copies(which, halo, source, depth):
        return (
            pltpu.make_async_remote_copy(
                src_ref=source.at[pl.ds(ROWS - depth, depth)],
                dst_ref=halo.at[0],
                send_sem=halo_send_sem.at[which, 0],
                recv_sem=halo_recv_sem.at[which, 0],
                device_id=(me_a, after),
                device_id_type=MESH,
            ),
            pltpu.make_async_remote_copy(
                src_ref=source.at[pl.ds(0, depth)],
                dst_ref=halo.at[1],
                send_sem=halo_send_sem.at[which, 1],
                recv_sem=halo_recv_sem.at[which, 1],
                device_id=(me_a, before),
                device_id_type=MESH,
            ),
        )

    def edge_copy(which, step):
        other = lax.rem(me_a + step, AXIAL)
        down = jnp.where(other < me_a, 1, 0)
        return pltpu.make_async_remote_copy(
            src_ref=edge_send.at[which, down],
            dst_ref=edge_recv.at[which, me_a],
            send_sem=edge_send_sem.at[which, step - 1],
            recv_sem=edge_recv_sem.at[which, step - 1],
            device_id=(other, me_z),
            device_id_type=MESH,
        )

    def send_edges(which):
        def piece(step, carry):
            at = pl.multiple_of(step * 640, 640)
            total = dot_last(sent[which, 0], cells[which, pl.ds(at, 640)]) + dot_last(
                sent[which, 1], cells[which, pl.ds(HALF + at, 640)]
            )
            total = total[:16] + total[16:]
            edge_send[which, 0, :, pl.ds(at, 640)] = total[:8]
            edge_send[which, 1, :, pl.ds(at, 640)] = total[8:]
            return carry

        lax.fori_loop(0, 2, piece, 0)
        for step in range(1, AXIAL):
            edge_copy(which, step).start()

    def own_part(which):
        def piece(row, carry):
            at = pl.multiple_of(row * SLAB, SLAB)
            total = jnp.dot(cells[which, pl.ds(at, SLAB)], own[which], preferred_element_type=F32)
            lined[row] = total[:, :LANES] + total[:, LANES:]
            return carry

        lax.fori_loop(0, ROWS, piece, 0)

    def add_edges(which):
        for step in range(1, AXIAL):
            edge_copy(which, step).wait_recv()

        def piece(step, carry):
            at = pl.multiple_of(lax.rem(step, 2) * 640, 640)
            received = edge_recv[which, :, :, pl.ds(at, 640)].reshape(32, 640)
            high, low = two_terms(received)
            total = dot_first(jnp.concatenate([high, low], axis=0), taken[which, step // 2])
            total = (total[:, :LANES] + total[:, LANES:]).reshape(2, SLAB, LANES)
            lined[pl.ds(2 * step, 2)] = lined[pl.ds(2 * step, 2)] + total
            return carry

        lax.fori_loop(0, 4, piece, 0)

    def wait_edge_sends(which):
        for step in range(1, AXIAL):
            edge_copy(which, step).wait_send()

    def keep_cells(which, row, field, group, value):
        high, low = two_terms(value)
        at = pl.multiple_of(row * SLAB + field * PLANES + group * 16, 16)
        cells[which, pl.ds(at, 16), pl.ds(0, LANES)] = high
        cells[which, pl.ds(at, 16), pl.ds(LANES, LANES)] = low

    def flux_group(group, carry):
        flux = [[None] * ROWS for _ in range(FIELDS)]
        for row in range(ROWS):
            at = pl.ds(group * 128 + row, 16, stride=ROWS)
            rho, prs, vol = density[at], pressure[at], volume[at]
            vel = [velocity[comp, at] for comp in range(3)]
            energy = 2.5 * prs + 0.5 * rho * (vel[0] * vel[0] + vel[1] * vel[1] + vel[2] * vel[2])
            state = [rho, rho * vel[0], rho * vel[1], rho * vel[2], energy]
            here = pl.ds(pl.multiple_of(group * 16, 16), 16)
            ratio[row, here] = SECTION / vol
            for field in range(FIELDS):
                base[row, pl.ds(pl.multiple_of(field * PLANES + group * 16, 16), 16)] = (
                    state[field] + SECTION * radial[field, at]
                )
            heat = energy + prs
            for metric, azimuthal in ((axial_metric, False), (azim_metric, True)):
                grad = [metric[comp, at] for comp in range(3)]
                contra = vol * (grad[0] * vel[0] + grad[1] * vel[1] + grad[2] * vel[2])
                flow = rho * contra
                push = vol * prs
                parts = [flow] + [flow * vel[comp] + grad[comp] * push for comp in range(3)] + [heat * contra]
                for field in range(FIELDS):
                    if azimuthal:
                        flux[field][row] = parts[field]
                        azim_flux[row, pl.ds(pl.multiple_of(field * PLANES + group * 16, 16), 16)] = parts[field]
                    else:
                        keep_cells(0, row, field, group, parts[field])
        for field in range(FIELDS):
            keep_moments(0, group, field, flux[field], DL)
        for quarter in range(4):
            send_moments(0, 4 * group + quarter)
        return carry

    lax.fori_loop(0, BLOCKS // 2, flux_group, 0)
    for copy in halo_copies(0, deriv_halo, azim_flux, 1):
        copy.start()
    send_edges(0)

    ids = observer_ref[...]
    order = (
        lax.shift_right_logical(ids, 7) * 128
        + (lax.shift_right_logical(ids, 2) & 1) * 64
        + (lax.shift_right_logical(ids, 3) & 15) * 4
        + (ids & 3)
    )
    partial[pl.ds(0, ENTRY_ROWS)] = order.astype(F32)

    def hot_row(row, carry):
        wanted = partial[pl.ds(row, 1)].astype(jnp.int32)
        rows = lax.broadcasted_iota(jnp.int32, (OBSERVERS, LANES), 0)
        at = pl.multiple_of(row * LANES, LANES)
        observer_hot[:, pl.ds(at, LANES)] = jnp.where(rows == wanted, 1.0, 0.0).astype(BF16)
        return carry

    lax.fori_loop(0, ENTRY_ROWS, hot_row, 0)

    own_part(0)
    reduce_moments(0, DL)
    add_edges(0)
    wait_starts(0)
    for copy in halo_copies(0, deriv_halo, azim_flux, 1):
        copy.wait_recv()

    def section_group(group, carry):
        for field in range(FIELDS):
            at = pl.ds(pl.multiple_of(field * PLANES + group * 16, 16), 16)
            here = pl.ds(pl.multiple_of(group * 16, 16), 16)
            flux = [deriv_halo[0, 0, at]] + [azim_flux[row, at] for row in range(ROWS)] + [deriv_halo[1, 0, at]]
            up = [start_of(0, group, field, 0)]
            for row in range(ROWS - 1):
                up.append(DL * (flux[row + 1] + up[-1]))
            down = [start_of(0, group, field, 1)]
            for row in range(ROWS - 1, 0, -1):
                down.append(DL * (flux[row + 1] + down[-1]))
            down = down[::-1]
            for row in range(ROWS):
                deriv = DK * (down[row] - up[row]) + C1 * (flux[row + 2] - flux[row])
                value = base[row, at] - ratio[row, here] * (lined[row, at] + deriv)
                keep_cells(1, row, field, group, value)
        return carry

    lax.fori_loop(0, BLOCKS // 2, section_group, 0)
    send_edges(1)
    own_part(1)
    add_edges(1)
    for copy in halo_copies(1, filter_halo, lined, 2):
        copy.start()

    def moment_group(group, carry):
        for field in range(FIELDS):
            at = pl.ds(pl.multiple_of(field * PLANES + group * 16, 16), 16)
            keep_moments(1, group, field, [lined[row, at] for row in range(ROWS)], FL)
        for quarter in range(4):
            send_moments(1, 4 * group + quarter)
        return carry

    lax.fori_loop(0, BLOCKS // 2, moment_group, 0)
    reduce_moments(1, FL)
    wait_starts(1)
    for copy in halo_copies(1, filter_halo, lined, 2):
        copy.wait_recv()

    def store_copy(group):
        planes = pl.ds(pl.multiple_of(group * 128, 128), 128)
        return pltpu.make_async_copy(final.at[:, planes], state_hbm.at[:, planes], store_sem.at[group])

    def final_group(group, carry):
        for field in range(FIELDS):
            at = pl.ds(pl.multiple_of(field * PLANES + group * 16, 16), 16)
            value = [filter_halo[0, 0, at], filter_halo[0, 1, at]]
            value += [lined[row, at] for row in range(ROWS)]
            value += [filter_halo[1, 0, at], filter_halo[1, 1, at]]
            up = [start_of(1, group, field, 0)]
            for row in range(ROWS - 1):
                up.append(FL * (value[row + 2] + up[-1]))
            down = [start_of(1, group, field, 1)]
            for row in range(ROWS - 1, 0, -1):
                down.append(FL * (value[row + 2] + down[-1]))
            down = down[::-1]
            for row in range(ROWS):
                near = E1 * (value[row + 1] + value[row + 3]) + E2 * (value[row] + value[row + 4])
                result = FK * (up[row] + down[row]) + (FK + E0) * value[row + 2] + near
                final[field, pl.ds(group * 128 + row, 16, stride=ROWS)] = result
        return carry

    def final_step(group, carry):
        final_group(group, carry)
        store_copy(group).start()
        return carry

    lax.fori_loop(0, BLOCKS // 2, final_step, 0)

    source = area_ref[...] * (final[2, pl.ds(0, ROWS)] + final[0, pl.ds(0, ROWS)] - 1.0)
    picks = weight_ref[...]
    low_half = jnp.take_along_axis(
        jnp.broadcast_to(table_ref[pl.ds(0, 1)], (ENTRY_ROWS, LANES)), picks & 127, axis=1
    )
    high_half = jnp.take_along_axis(
        jnp.broadcast_to(table_ref[pl.ds(1, 1)], (ENTRY_ROWS, LANES)), picks & 127, axis=1
    )
    weights = jnp.where(picks < LANES, low_half, high_half)
    values = weights * jnp.concatenate([source] * 4, axis=0)
    high, low = two_terms(values)
    partial[pl.ds(0, ENTRY_ROWS)] = high.astype(F32)
    partial[pl.ds(ENTRY_ROWS, ENTRY_ROWS)] = low.astype(F32)

    def bin_row(row, carry):
        same = lax.broadcasted_iota(jnp.int32, (TIME_BINS, LANES), 0) == bin_ref[pl.ds(row, 1)]
        at = pl.multiple_of(row * LANES, LANES)
        bin_hot[pl.ds(0, TIME_BINS), pl.ds(at, LANES)] = jnp.where(same, partial[pl.ds(row, 1)], 0.0).astype(BF16)
        bin_hot[pl.ds(TIME_BINS, TIME_BINS), pl.ds(at, LANES)] = jnp.where(
            same, partial[pl.ds(ENTRY_ROWS + row, 1)], 0.0
        ).astype(BF16)
        return carry

    lax.fori_loop(0, ENTRY_ROWS, bin_row, 0)

    def sum_rows(step, carry):
        at = pl.ds(pl.multiple_of(step * 128, 128), 128)
        total = dot_last(observer_hot[at], bin_hot[...])
        partial[at] = total[:, :TIME_BINS] + total[:, TIME_BINS:]
        return carry

    lax.fori_loop(0, OBSERVERS // 128, sum_rows, 0)

    mine = me_a * 2 + core

    def part_copy(step):
        other = lax.rem(mine + step, 8)
        other_z = me_z - core + lax.rem(other, 2)
        return pltpu.make_async_remote_copy(
            src_ref=partial.at[pl.ds(pl.multiple_of(other * 64, 64), 64)],
            dst_ref=part_recv.at[step - 1],
            send_sem=part_send_sem.at[step - 1],
            recv_sem=part_recv_sem.at[step - 1],
            device_id=(other // 2, other_z),
            device_id_type=MESH,
        )

    for step in range(1, 8):
        part_copy(step).start()
    total = partial[pl.ds(pl.multiple_of(mine * 64, 64), 64)]
    for step in range(1, 8):
        part_copy(step).wait_recv()
        total = total + part_recv[step - 1]
    for owner in range(16):
        owner_send[owner, pl.ds(0, 4)] = total[4 * owner : 4 * owner + 4]
        owner_send[owner, pl.ds(4, 4)] = jnp.zeros((4, LANES), F32)

    def owner_copy(step):
        other = lax.rem(chip + step, 16)
        return pltpu.make_async_remote_copy(
            src_ref=owner_send.at[other],
            dst_ref=owner_recv.at[step - 1],
            send_sem=owner_send_sem.at[step - 1],
            recv_sem=owner_recv_sem.at[step - 1],
            device_id=(me_a, 2 * other + core),
            device_id_type=MESH,
        )

    for step in range(1, 16):
        owner_copy(step).start()
    result = owner_send[chip]
    for step in range(1, 16):
        owner_copy(step).wait_recv()
        result = result + owner_recv[step - 1]
    signal_ref[...] = result[:4]

    for group in range(BLOCKS // 2):
        store_copy(group).wait()
    for which, halo, source_ref, depth in ((0, deriv_halo, azim_flux, 1), (1, filter_halo, lined, 2)):
        wait_moment_sends(which)
        wait_start_sends(which)
        wait_edge_sends(which)
        for copy in halo_copies(which, halo, source_ref, depth):
            copy.wait_send()
    for step in range(1, 8):
        part_copy(step).wait_send()
    for step in range(1, 16):
        owner_copy(step).wait_send()


def per_device(
    density,
    velocity,
    pressure,
    axial_metric,
    azim_metric,
    volume,
    radial_term,
    panel_area,
    observer_ids,
    bin_ids,
    weight_ids,
    bin_weights,
):
    own, sent, taken = both_tables()
    rows = PLANES * ROWS
    hbm = pl.BlockSpec(memory_space=pl.ANY)
    vmem = pl.BlockSpec(memory_space=pltpu.VMEM)
    dma = pltpu.SemaphoreType.DMA
    state, signals = pl.pallas_call(
        kernel,
        out_shape=(
            jax.ShapeDtypeStruct((FIELDS, rows, LANES), F32),
            jax.ShapeDtypeStruct((4, TIME_BINS), F32),
        ),
        in_specs=[hbm] * 10 + [vmem] * 5,
        out_specs=(hbm, vmem),
        scratch_shapes=[
            pltpu.VMEM((2, 2 * LANES, 2 * LANES), BF16),
            pltpu.VMEM((2, 2, 32, 2 * LANES), BF16),
            pltpu.VMEM((2, 2, 64, 2 * LANES), BF16),
            pltpu.VMEM((rows, LANES), F32),
            pltpu.VMEM((3, rows, LANES), F32),
            pltpu.VMEM((rows, LANES), F32),
            pltpu.VMEM((3, rows, LANES), F32),
            pltpu.VMEM((3, rows, LANES), F32),
            pltpu.VMEM((rows, LANES), F32),
            pltpu.VMEM((FIELDS, rows, LANES), F32),
            pltpu.VMEM((ROWS, SLAB, LANES), F32),
            pltpu.VMEM((ROWS, SLAB, LANES), F32),
            pltpu.VMEM((ROWS, PLANES, LANES), F32),
            pltpu.VMEM((2, LINES, 2 * LANES), BF16),
            pltpu.VMEM((ROWS, SLAB, LANES), F32),
            pltpu.VMEM((FIELDS, rows, LANES), F32),
            pltpu.VMEM((2, 2, 8, HALF), F32),
            pltpu.VMEM((2, AXIAL, 8, HALF), F32),
            pltpu.VMEM((2, SLOTS, TILE_ROWS, LANES), F32),
            pltpu.VMEM((2, AZIM, TILE_ROWS, LANES), F32),
            pltpu.VMEM((2, AZIM, TILE_ROWS, LANES), F32),
            pltpu.VMEM((2, SLOTS, TILE_ROWS, LANES), F32),
            pltpu.VMEM((2, 1, SLAB, LANES), F32),
            pltpu.VMEM((2, 2, SLAB, LANES), F32),
            pltpu.VMEM((OBSERVERS, ENTRY_ROWS * LANES), BF16),
            pltpu.VMEM((2 * TIME_BINS, ENTRY_ROWS * LANES), BF16),
            pltpu.VMEM((OBSERVERS, TIME_BINS), F32),
            pltpu.VMEM((7, 64, TIME_BINS), F32),
            pltpu.VMEM((16, 8, TIME_BINS), F32),
            pltpu.VMEM((15, 8, TIME_BINS), F32),
            dma((15,)),
            dma((BLOCKS // 2,)),
            dma((2, 3)),
            dma((2, 3)),
            dma((2,)),
            dma((2,)),
            dma((2,)),
            dma((2,)),
            dma((2, 2)),
            dma((2, 2)),
            dma((7,)),
            dma((7,)),
            dma((15,)),
            dma((15,)),
        ],
        compiler_params=pltpu.CompilerParams(
            collective_id=0, has_side_effects=True, vmem_limit_bytes=48 * 1024 * 1024
        ),
    )(
        jnp.asarray(own),
        jnp.asarray(sent),
        jnp.asarray(taken),
        density.reshape(rows, LANES),
        velocity.reshape(3, rows, LANES),
        pressure.reshape(rows, LANES),
        axial_metric.reshape(3, rows, LANES),
        azim_metric.reshape(3, rows, LANES),
        volume.reshape(rows, LANES),
        radial_term.reshape(FIELDS, rows, LANES),
        panel_area,
        observer_ids.reshape(ENTRY_ROWS, LANES),
        bin_ids.reshape(ENTRY_ROWS, LANES),
        weight_ids.reshape(ENTRY_ROWS, LANES),
        bin_weights.reshape(2, LANES),
    )
    return state.reshape(FIELDS, PLANES, ROWS, LANES), signals


def solution(mesh):
    placed = (
        P(None, "azim", "axial"),
        P(None, None, "azim", "axial"),
        P(None, "azim", "axial"),
        P(None, None, "azim", "axial"),
        P(None, None, "azim", "axial"),
        P(None, "azim", "axial"),
        P(None, None, "azim", "axial"),
        P("azim", "axial"),
        P(None, "azim", "axial"),
        P(None, "azim", "axial"),
        P(None, "azim", "axial"),
        P(),
    )
    return jax.shard_map(
        per_device,
        mesh=mesh,
        in_specs=placed,
        out_specs=(P(None, None, "azim", "axial"), P(("axial", "azim"), None)),
        check_vma=False,
    )
```

```python
import functools
import math

import jax
import jax.numpy as jnp
import ml_dtypes
import numpy as np
from jax import lax
from jax.experimental import pallas as pl
from jax.experimental.pallas import tpu as pltpu
from jax.sharding import PartitionSpec as P

F32 = jnp.float32
BF16 = jnp.bfloat16
MESH = pl.DeviceIdType.MESH

PLANES = 64
FIELDS = 5
ROWS = 8
LANES = 128
AXIAL = 4
AZIM = 32
NA = AXIAL * LANES
NAZ = AZIM * ROWS
SLAB = FIELDS * PLANES
LINES = ROWS * SLAB
BLOCKS = PLANES // 8
SLOTS = 2 * BLOCKS
TILE_ROWS = 8 * FIELDS
SHARE = (24, 16)
HALF = LINES // 2
ENTRY_ROWS = 32
OBSERVERS = 512
TIME_BINS = 128
PEERS = (AZIM - 1) + 2 * (AXIAL - 1)

SECTION = 0.25
DERIV_ALPHA = 1.0 / 3.0
BETA = 0.499


def decay_root(alpha):
    return (-1.0 + math.sqrt(1.0 - 4.0 * alpha * alpha)) / (2.0 * alpha)


DL = decay_root(DERIV_ALPHA)
FL = decay_root(BETA)
C1 = (1.0 / 36.0) / DERIV_ALPHA
DS = 1.0 / math.sqrt(1.0 - 4.0 * DERIV_ALPHA**2)
DK = (7.0 / 9.0 - C1) * DS * (1.0 / DL - DL)
FC = [
    (11.0 + 10.0 * BETA) / 16.0,
    (15.0 + 34.0 * BETA) / 32.0,
    (-3.0 + 6.0 * BETA) / 16.0,
    (1.0 - 2.0 * BETA) / 32.0,
]
FS = 1.0 / math.sqrt(1.0 - 4.0 * BETA**2)
E2 = FC[3] / (2.0 * BETA)
E1 = (FC[2] / 2.0 - E2) / BETA
E0 = (FC[1] / 2.0 - E1 - BETA * E2) / BETA
FK = (FC[0] - E0 - 2.0 * BETA * E1) * FS


def split(values):
    high = values.astype(ml_dtypes.bfloat16)
    low = (values - high.astype(np.float64)).astype(ml_dtypes.bfloat16)
    return high, low


def axial_tables(root, scale, band):
    n, w = NA, LANES
    index = np.arange(n)
    green = scale * (
        np.power(root, np.abs(index[:, None] - index[None, :]))
        - np.power(root, 2 * n - index[:, None] - index[None, :])
    )
    side = np.zeros((n, n))
    for shift, value in band.items():
        side += value * np.eye(n, k=shift)
    whole = green @ side
    left = np.zeros((AXIAL, w))
    right = np.zeros((AXIAL, w))
    for k in range(AXIAL):
        cols = slice(k * w, (k + 1) * w)
        lo, hi = max(0, k * w - 3), min(n, (k + 1) * w + 3)
        m = np.arange(lo, hi)
        left[k] = np.power(root, ((k + 1) * w - m).astype(np.float64)) @ side[lo:hi, cols]
        right[k] = (
            np.power(root, (m - k * w + 1).astype(np.float64))
            - np.power(root, (2 * n - m - k * w + 1).astype(np.float64))
        ) @ side[lo:hi, cols]
    t = np.arange(w)
    own = np.zeros((AXIAL, w, 2 * w), ml_dtypes.bfloat16)
    sent = np.zeros((AXIAL, 2, 32, 2 * w), ml_dtypes.bfloat16)
    taken = np.zeros((AXIAL, 2, 64, 2 * w), ml_dtypes.bfloat16)
    for d in range(AXIAL):
        high, low = split(whole[d * w : (d + 1) * w, d * w : (d + 1) * w].T)
        own[d] = np.concatenate([high, low], axis=1)
        for half in range(2):
            rows = np.zeros((16, w))
            base = half * 4
            rows[base] = left[d]
            rows[base + 1, w - 1] = 1.0
            rows[base + 2, w - 2] = 1.0
            rows[8 + base] = right[d]
            rows[8 + base + 1, 0] = 1.0
            rows[8 + base + 2, 1] = 1.0
            high, low = split(rows)
            sent[d, half] = np.concatenate(
                [np.concatenate([high, high], axis=1), np.concatenate([low, low], axis=1)], axis=0
            )
            rows = np.zeros((32, w))
            for k in range(AXIAL):
                row = k * 8 + half * 4
                i = d * w + t
                if k < d:
                    rows[row] = scale * (
                        np.power(root, (i - (k + 1) * w).astype(np.float64))
                        - np.power(root, (2 * n - i - (k + 1) * w).astype(np.float64))
                    )
                    if k == d - 1:
                        for edge in range(2):
                            col = d * w - 1 - edge
                            for near in range(2 - edge):
                                rows[row + 1 + edge, near] = (
                                    whole[d * w + near, col] - rows[row, near] * left[k, col - k * w]
                                )
                if k > d:
                    rows[row] = scale * np.power(root, (k * w - 1 - i).astype(np.float64))
                    if k == d + 1:
                        for edge in range(2):
                            col = k * w + edge
                            for near in range(2 - edge):
                                rows[row + 1 + edge, w - 1 - near] = (
                                    whole[k * w - 1 - near, col] - rows[row, w - 1 - near] * right[k, edge]
                                )
            high, low = split(rows)
            pair = np.concatenate([high, low], axis=1)
            taken[d, half] = np.concatenate([pair, pair], axis=0)
    return own, sent, taken


def both_tables():
    deriv = axial_tables(DL, DS, {1: 7.0 / 9.0, -1: -7.0 / 9.0, 2: 1.0 / 36.0, -2: -1.0 / 36.0})
    band = {0: FC[0]}
    for shift in range(1, 4):
        band[shift] = band[-shift] = FC[shift] / 2.0
    smooth = axial_tables(FL, FS, band)
    return [np.stack(pair, axis=1) for pair in zip(deriv, smooth)]


def azimuth_rows():
    gap = np.arange(NAZ)
    line = FK * (np.power(FL, gap) + np.power(FL, NAZ - gap)) / (1.0 - FL**NAZ)
    line[0] = FK * (1.0 + 2.0 * FL**NAZ / (1.0 - FL**NAZ)) + E0
    for shift, value in ((1, E1), (2, E2)):
        line[shift] += value
        line[-shift] += value
    rows = np.arange(ROWS)
    return line[(gap[None, :] - rows[:, None]) % NAZ].astype(np.float32)


def two_terms(value):
    high = value.astype(BF16)
    low = (value - high.astype(F32)).astype(BF16)
    return high, low


def dot_last(left, right):
    return lax.dot_general(left, right, (((1,), (1,)), ((), ())), preferred_element_type=F32)


def dot_first(left, right):
    return lax.dot_general(left, right, (((0,), (0,)), ((), ())), preferred_element_type=F32)


def kernel(
    own_hbm,
    sent_hbm,
    taken_hbm,
    density_hbm,
    velocity_hbm,
    pressure_hbm,
    axial_hbm,
    azim_hbm,
    volume_hbm,
    radial_hbm,
    area_hbm,
    observer_hbm,
    bin_hbm,
    weight_hbm,
    table_hbm,
    azimuth_hbm,
    final,
    signal_ref,
    own,
    sent,
    taken,
    density,
    velocity,
    pressure,
    axial_metric,
    azim_metric,
    volume,
    radial,
    area_ref,
    observer_ref,
    bin_ref,
    weight_ref,
    table_ref,
    azimuth_ref,
    azim_flux,
    base,
    ratio,
    cells,
    lined,
    edge_send,
    edge_recv,
    moment_send,
    moment_recv,
    start_send,
    start_recv,
    deriv_halo,
    filter_halo,
    observer_hot,
    bin_hot,
    partial,
    part_recv,
    owner_send,
    owner_recv,
    plane_send,
    plane_recv,
    load_sem,
    edge_send_sem,
    edge_recv_sem,
    moment_send_sem,
    moment_recv_sem,
    start_send_sem,
    start_recv_sem,
    halo_send_sem,
    halo_recv_sem,
    part_send_sem,
    part_recv_sem,
    owner_send_sem,
    owner_recv_sem,
    plane_send_sem,
    plane_recv_sem,
):
    me_a = lax.axis_index("axial")
    me_z = lax.axis_index("azim")
    core = lax.rem(me_z, 2)
    chip = me_z // 2
    twin = me_z + 1 - 2 * core
    after = lax.rem(me_z + 1, AZIM)
    before = lax.rem(me_z + AZIM - 1, AZIM)

    loads = [
        pltpu.make_async_copy(density_hbm, density, load_sem.at[0]),
        pltpu.make_async_copy(velocity_hbm, velocity, load_sem.at[1]),
        pltpu.make_async_copy(pressure_hbm, pressure, load_sem.at[2]),
        pltpu.make_async_copy(axial_hbm, axial_metric, load_sem.at[3]),
        pltpu.make_async_copy(azim_hbm, azim_metric, load_sem.at[4]),
        pltpu.make_async_copy(volume_hbm, volume, load_sem.at[5]),
        pltpu.make_async_copy(radial_hbm, radial, load_sem.at[6]),
        pltpu.make_async_copy(area_hbm, area_ref, load_sem.at[15]),
        pltpu.make_async_copy(observer_hbm, observer_ref, load_sem.at[16]),
        pltpu.make_async_copy(bin_hbm, bin_ref, load_sem.at[17]),
        pltpu.make_async_copy(weight_hbm, weight_ref, load_sem.at[18]),
        pltpu.make_async_copy(table_hbm, table_ref, load_sem.at[19]),
        pltpu.make_async_copy(azimuth_hbm, azimuth_ref, load_sem.at[20]),
    ]
    for which in range(2):
        loads.append(
            pltpu.make_async_copy(
                own_hbm.at[me_a, which], own.at[which, pl.ds(0, LANES)], load_sem.at[7 + 4 * which]
            )
        )
        loads.append(
            pltpu.make_async_copy(
                own_hbm.at[me_a, which], own.at[which, pl.ds(LANES, LANES)], load_sem.at[8 + 4 * which]
            )
        )
        loads.append(pltpu.make_async_copy(sent_hbm.at[me_a, which], sent.at[which], load_sem.at[9 + 4 * which]))
        loads.append(pltpu.make_async_copy(taken_hbm.at[me_a, which], taken.at[which], load_sem.at[10 + 4 * which]))
    for load in loads:
        load.start()

    barrier = pltpu.get_barrier_semaphore()

    def greet_azim(step, carry):
        other = lax.rem(me_z + step, AZIM)
        pl.semaphore_signal(barrier, inc=1, device_id=(me_a, other), device_id_type=MESH)
        return carry

    lax.fori_loop(1, AZIM, greet_azim, 0)

    def greet_axial(step, carry):
        other = lax.rem(me_a + step, AXIAL)
        pl.semaphore_signal(barrier, inc=1, device_id=(other, me_z), device_id_type=MESH)
        pl.semaphore_signal(barrier, inc=1, device_id=(other, twin), device_id_type=MESH)
        return carry

    lax.fori_loop(1, AXIAL, greet_axial, 0)

    edge_recv[0, pl.ds(me_a, 1)] = jnp.zeros((1, 8, HALF), F32)
    edge_recv[1, pl.ds(me_a, 1)] = jnp.zeros((1, 8, HALF), F32)

    for load in loads:
        load.wait()

    def send_moments(which):
        def piece(step, carry):
            target = lax.rem(me_z + step, AZIM)
            slot, part = target // 2, lax.rem(target, 2)
            for share in range(2):
                rows = pl.ds(share * SHARE[0], SHARE[share])
                source = moment_send.at[which, slot, rows]
                dest = moment_recv.at[which, me_z, pl.ds(0, SHARE[share])]

                @pl.when(jnp.logical_and(part == share, step > 0))
                def _():
                    pltpu.make_async_remote_copy(
                        src_ref=source,
                        dst_ref=dest,
                        send_sem=moment_send_sem.at[which],
                        recv_sem=moment_recv_sem.at[which],
                        device_id=(me_a, target),
                        device_id_type=MESH,
                    ).start()

                @pl.when(jnp.logical_and(part == share, step == 0))
                def _():
                    pltpu.make_async_copy(source, dest, moment_recv_sem.at[which]).start()

            return carry

        lax.fori_loop(0, AZIM, piece, 0)

    def wait_moment_sends(which):
        for share in range(2):

            @pl.when(core == share)
            def _():
                part = moment_send.at[which, pl.ds(0, SLOTS - 1)]
                pltpu.make_async_copy(part, part, moment_send_sem.at[which]).wait()
                part = moment_send.at[which, SLOTS - 1, pl.ds(0, SHARE[1 - share])]
                pltpu.make_async_copy(part, part, moment_send_sem.at[which]).wait()

    def reduce_moments(which, root):
        factor = root**ROWS
        wrap = 1.0 / (1.0 - root**NAZ)
        side = lax.rem(chip, 2)

        def place(step):
            return step + side * (AZIM - 1 - 2 * step)

        for share in range(2):
            rows = pl.ds(0, SHARE[share])
            there = pl.ds(share * SHARE[0], SHARE[share])

            @pl.when(core == share)
            def _():
                part = moment_recv.at[which, :, rows]
                pltpu.make_async_copy(part, part, moment_recv_sem.at[which]).wait()

                def gather(step, total):
                    return factor * total + moment_recv[which, place(step), rows]

                first = lax.fori_loop(0, AZIM, gather, jnp.zeros((SHARE[share], LANES), F32), unroll=8) * wrap

                def follow(step, now):
                    other = place(step)
                    start_send[which, other, rows] = now
                    return factor * now + moment_recv[which, other, rows]

                lax.fori_loop(0, AZIM, follow, first, unroll=8)

                pltpu.make_async_copy(
                    start_send.at[which, me_z, rows], start_recv.at[which, chip, there], start_recv_sem.at[which]
                ).start()

                def hand_out(step, carry):
                    other = lax.rem(me_z + step, AZIM)
                    pltpu.make_async_remote_copy(
                        src_ref=start_send.at[which, other, rows],
                        dst_ref=start_recv.at[which, chip, there],
                        send_sem=start_send_sem.at[which],
                        recv_sem=start_recv_sem.at[which],
                        device_id=(me_a, other),
                        device_id_type=MESH,
                    ).start()
                    return carry

                lax.fori_loop(1, AZIM, hand_out, 0)

    def wait_starts(which):
        part = start_recv.at[which]
        pltpu.make_async_copy(part, part, start_recv_sem.at[which]).wait()

    def wait_start_sends(which):
        for share in range(2):

            @pl.when(core == share)
            def _():
                part = start_send.at[which, pl.ds(0, AZIM - 1), pl.ds(0, SHARE[share])]
                pltpu.make_async_copy(part, part, start_send_sem.at[which]).wait()

    def moments_of(values, root):
        up = root * values[0]
        for row in range(1, ROWS):
            up = root * (up + values[row])
        down = root * values[ROWS - 1]
        for row in range(ROWS - 2, -1, -1):
            down = root * (down + values[row])
        return up, down

    def keep_moments(which, group, field, values, root):
        up, down = moments_of(values, root)
        for half in range(2):
            for side, value in ((0, up), (1, down)):
                moment_send[which, 4 * group + 2 * half + side, pl.ds(8 * field, 8)] = value[8 * half : 8 * half + 8]

    def start_of(which, group, field, side):
        return jnp.concatenate(
            [start_recv[which, 4 * group + 2 * half + side, pl.ds(8 * field, 8)] for half in range(2)], axis=0
        )

    def halo_copies(which, halo, source, depth):
        return (
            pltpu.make_async_remote_copy(
                src_ref=source.at[pl.ds(ROWS - depth, depth)],
                dst_ref=halo.at[0],
                send_sem=halo_send_sem.at[which, 0],
                recv_sem=halo_recv_sem.at[which, 0],
                device_id=(me_a, after),
                device_id_type=MESH,
            ),
            pltpu.make_async_remote_copy(
                src_ref=source.at[pl.ds(0, depth)],
                dst_ref=halo.at[1],
                send_sem=halo_send_sem.at[which, 1],
                recv_sem=halo_recv_sem.at[which, 1],
                device_id=(me_a, before),
                device_id_type=MESH,
            ),
        )

    def edge_copy(which, step):
        other = lax.rem(me_a + step, AXIAL)
        down = jnp.where(other < me_a, 1, 0)
        return pltpu.make_async_remote_copy(
            src_ref=edge_send.at[which, down],
            dst_ref=edge_recv.at[which, me_a],
            send_sem=edge_send_sem.at[which, step - 1],
            recv_sem=edge_recv_sem.at[which, step - 1],
            device_id=(other, me_z),
            device_id_type=MESH,
        )

    def send_edges(which):
        def piece(step, carry):
            at = pl.multiple_of(step * 640, 640)
            total = dot_last(sent[which, 0], cells[which, pl.ds(at, 640)]) + dot_last(
                sent[which, 1], cells[which, pl.ds(HALF + at, 640)]
            )
            total = total[:16] + total[16:]
            edge_send[which, 0, :, pl.ds(at, 640)] = total[:8]
            edge_send[which, 1, :, pl.ds(at, 640)] = total[8:]
            return carry

        lax.fori_loop(0, 2, piece, 0)
        for step in range(1, AXIAL):
            edge_copy(which, step).start()

    def own_part(which):
        def piece(row, carry):
            at = pl.multiple_of(row * SLAB, SLAB)
            total = jnp.dot(cells[which, pl.ds(at, SLAB)], own[which], preferred_element_type=F32)
            lined[row] = total[:, :LANES] + total[:, LANES:]
            return carry

        lax.fori_loop(0, ROWS, piece, 0)

    def add_edges(which):
        for step in range(1, AXIAL):
            edge_copy(which, step).wait_recv()

        def piece(step, carry):
            at = pl.multiple_of(lax.rem(step, 2) * 640, 640)
            received = edge_recv[which, :, :, pl.ds(at, 640)].reshape(32, 640)
            high, low = two_terms(received)
            total = dot_first(jnp.concatenate([high, low], axis=0), taken[which, step // 2])
            total = (total[:, :LANES] + total[:, LANES:]).reshape(2, SLAB, LANES)
            lined[pl.ds(2 * step, 2)] = lined[pl.ds(2 * step, 2)] + total
            return carry

        lax.fori_loop(0, 4, piece, 0)

    def wait_edge_sends(which):
        for step in range(1, AXIAL):
            edge_copy(which, step).wait_send()

    def keep_cells(which, row, field, group, value):
        high, low = two_terms(value)
        at = pl.multiple_of(row * SLAB + field * PLANES + group * 16, 16)
        cells[which, pl.ds(at, 16), pl.ds(0, LANES)] = high
        cells[which, pl.ds(at, 16), pl.ds(LANES, LANES)] = low

    def flux_group(group, carry):
        flux = [[None] * ROWS for _ in range(FIELDS)]
        for row in range(ROWS):
            at = pl.ds(group * 128 + row, 16, stride=ROWS)
            rho, prs, vol = density[at], pressure[at], volume[at]
            vel = [velocity[comp, at] for comp in range(3)]
            energy = 2.5 * prs + 0.5 * rho * (vel[0] * vel[0] + vel[1] * vel[1] + vel[2] * vel[2])
            state = [rho, rho * vel[0], rho * vel[1], rho * vel[2], energy]
            here = pl.ds(pl.multiple_of(group * 16, 16), 16)
            ratio[row, here] = SECTION / vol
            for field in range(FIELDS):
                base[row, pl.ds(pl.multiple_of(field * PLANES + group * 16, 16), 16)] = (
                    state[field] + SECTION * radial[field, at]
                )
            heat = energy + prs
            for metric, azimuthal in ((axial_metric, False), (azim_metric, True)):
                grad = [metric[comp, at] for comp in range(3)]
                contra = vol * (grad[0] * vel[0] + grad[1] * vel[1] + grad[2] * vel[2])
                flow = rho * contra
                push = vol * prs
                parts = [flow] + [flow * vel[comp] + grad[comp] * push for comp in range(3)] + [heat * contra]
                for field in range(FIELDS):
                    if azimuthal:
                        flux[field][row] = parts[field]
                        azim_flux[row, pl.ds(pl.multiple_of(field * PLANES + group * 16, 16), 16)] = parts[field]
                    else:
                        keep_cells(0, row, field, group, parts[field])
        for field in range(FIELDS):
            keep_moments(0, group, field, flux[field], DL)
        return carry

    lax.fori_loop(0, BLOCKS // 2, flux_group, 0)
    pl.semaphore_wait(barrier, PEERS)
    send_moments(0)
    for copy in halo_copies(0, deriv_halo, azim_flux, 1):
        copy.start()
    send_edges(0)

    ids = observer_ref[...]
    order = (
        lax.shift_right_logical(ids, 7) * 128
        + (lax.shift_right_logical(ids, 2) & 1) * 64
        + (lax.shift_right_logical(ids, 3) & 15) * 4
        + (ids & 3)
    )
    partial[pl.ds(0, ENTRY_ROWS)] = order.astype(F32)

    def hot_row(row, carry):
        wanted = partial[pl.ds(row, 1)].astype(jnp.int32)
        rows = lax.broadcasted_iota(jnp.int32, (OBSERVERS, LANES), 0)
        at = pl.multiple_of(row * LANES, LANES)
        observer_hot[:, pl.ds(at, LANES)] = jnp.where(rows == wanted, 1.0, 0.0).astype(BF16)
        return carry

    lax.fori_loop(0, ENTRY_ROWS, hot_row, 0)

    own_part(0)
    reduce_moments(0, DL)
    add_edges(0)
    wait_starts(0)
    for copy in halo_copies(0, deriv_halo, azim_flux, 1):
        copy.wait_recv()

    def section_group(group, carry):
        for field in range(FIELDS):
            at = pl.ds(pl.multiple_of(field * PLANES + group * 16, 16), 16)
            here = pl.ds(pl.multiple_of(group * 16, 16), 16)
            flux = [deriv_halo[0, 0, at]] + [azim_flux[row, at] for row in range(ROWS)] + [deriv_halo[1, 0, at]]
            up = [start_of(0, group, field, 0)]
            for row in range(ROWS - 1):
                up.append(DL * (flux[row + 1] + up[-1]))
            down = [start_of(0, group, field, 1)]
            for row in range(ROWS - 1, 0, -1):
                down.append(DL * (flux[row + 1] + down[-1]))
            down = down[::-1]
            for row in range(ROWS):
                deriv = DK * (down[row] - up[row]) + C1 * (flux[row + 2] - flux[row])
                value = base[row, at] - ratio[row, here] * (lined[row, at] + deriv)
                keep_cells(1, row, field, group, value)
        return carry

    lax.fori_loop(0, BLOCKS // 2, section_group, 0)
    send_edges(1)
    own_part(1)
    add_edges(1)

    plane_send[...] = lined[:, 0] + lined[:, 2 * PLANES]

    def plane_copy(step):
        other = lax.rem(me_z + step, AZIM)
        return pltpu.make_async_remote_copy(
            src_ref=plane_send,
            dst_ref=plane_recv.at[AZIM - step],
            send_sem=plane_send_sem,
            recv_sem=plane_recv_sem,
            device_id=(me_a, other),
            device_id_type=MESH,
        )

    def send_plane(step, carry):
        plane_copy(step).start()
        return carry

    lax.fori_loop(1, AZIM, send_plane, 0)
    plane_recv[0] = plane_send[...]

    def moment_group(group, carry):
        for field in range(FIELDS):
            at = pl.ds(pl.multiple_of(field * PLANES + group * 16, 16), 16)
            keep_moments(1, group, field, [lined[row, at] for row in range(ROWS)], FL)
        return carry

    lax.fori_loop(0, BLOCKS // 2, moment_group, 0)
    send_moments(1)
    for copy in halo_copies(1, filter_halo, lined, 2):
        copy.start()
    pltpu.make_async_copy(
        plane_recv.at[pl.ds(1, AZIM - 1)], plane_recv.at[pl.ds(1, AZIM - 1)], plane_recv_sem
    ).wait()
    filtered = jnp.dot(
        azimuth_ref[...],
        plane_recv[...].reshape(NAZ, LANES),
        preferred_element_type=F32,
        precision=lax.Precision.HIGHEST,
    )
    source = area_ref[...] * (filtered - 1.0)
    picks = weight_ref[...]
    low_half = jnp.take_along_axis(
        jnp.broadcast_to(table_ref[pl.ds(0, 1)], (ENTRY_ROWS, LANES)), picks & 127, axis=1
    )
    high_half = jnp.take_along_axis(
        jnp.broadcast_to(table_ref[pl.ds(1, 1)], (ENTRY_ROWS, LANES)), picks & 127, axis=1
    )
    weights = jnp.where(picks < LANES, low_half, high_half)
    values = weights * jnp.concatenate([source] * 4, axis=0)
    high, low = two_terms(values)
    partial[pl.ds(0, ENTRY_ROWS)] = high.astype(F32)
    partial[pl.ds(ENTRY_ROWS, ENTRY_ROWS)] = low.astype(F32)

    def bin_row(row, carry):
        same = lax.broadcasted_iota(jnp.int32, (TIME_BINS, LANES), 0) == bin_ref[pl.ds(row, 1)]
        at = pl.multiple_of(row * LANES, LANES)
        bin_hot[pl.ds(0, TIME_BINS), pl.ds(at, LANES)] = jnp.where(same, partial[pl.ds(row, 1)], 0.0).astype(BF16)
        bin_hot[pl.ds(TIME_BINS, TIME_BINS), pl.ds(at, LANES)] = jnp.where(
            same, partial[pl.ds(ENTRY_ROWS + row, 1)], 0.0
        ).astype(BF16)
        return carry

    lax.fori_loop(0, ENTRY_ROWS, bin_row, 0)

    total = dot_last(observer_hot[...], bin_hot[...])
    partial[...] = total[:, :TIME_BINS] + total[:, TIME_BINS:]

    mine = me_a * 2 + core

    def part_copy(step):
        other = lax.rem(mine + step, 8)
        other_z = me_z - core + lax.rem(other, 2)
        return pltpu.make_async_remote_copy(
            src_ref=partial.at[pl.ds(pl.multiple_of(other * 64, 64), 64)],
            dst_ref=part_recv.at[step - 1],
            send_sem=part_send_sem.at[step - 1],
            recv_sem=part_recv_sem.at[step - 1],
            device_id=(other // 2, other_z),
            device_id_type=MESH,
        )

    for step in range(1, 8):
        part_copy(step).start()
    reduce_moments(1, FL)
    total = partial[pl.ds(pl.multiple_of(mine * 64, 64), 64)]
    for step in range(1, 8):
        part_copy(step).wait_recv()
        total = total + part_recv[step - 1]
    for owner in range(16):
        owner_send[owner, pl.ds(0, 4)] = total[4 * owner : 4 * owner + 4]
        owner_send[owner, pl.ds(4, 4)] = jnp.zeros((4, LANES), F32)

    def owner_copy(step):
        other = lax.rem(chip + step, 16)
        return pltpu.make_async_remote_copy(
            src_ref=owner_send.at[other],
            dst_ref=owner_recv.at[step - 1],
            send_sem=owner_send_sem.at[step - 1],
            recv_sem=owner_recv_sem.at[step - 1],
            device_id=(me_a, 2 * other + core),
            device_id_type=MESH,
        )

    for step in range(1, 16):
        owner_copy(step).start()
    wait_starts(1)
    for copy in halo_copies(1, filter_halo, lined, 2):
        copy.wait_recv()

    def final_group(group, carry):
        for field in range(FIELDS):
            at = pl.ds(pl.multiple_of(field * PLANES + group * 16, 16), 16)
            value = [filter_halo[0, 0, at], filter_halo[0, 1, at]]
            value += [lined[row, at] for row in range(ROWS)]
            value += [filter_halo[1, 0, at], filter_halo[1, 1, at]]
            up = [start_of(1, group, field, 0)]
            for row in range(ROWS - 1):
                up.append(FL * (value[row + 2] + up[-1]))
            down = [start_of(1, group, field, 1)]
            for row in range(ROWS - 1, 0, -1):
                down.append(FL * (value[row + 2] + down[-1]))
            down = down[::-1]
            for row in range(ROWS):
                near = E1 * (value[row + 1] + value[row + 3]) + E2 * (value[row] + value[row + 4])
                result = FK * (up[row] + down[row]) + (FK + E0) * value[row + 2] + near
                final[field, pl.ds(group * 128 + row, 16, stride=ROWS)] = result
        return carry

    lax.fori_loop(0, BLOCKS // 2, final_group, 0)

    result = owner_send[chip]
    for step in range(1, 16):
        owner_copy(step).wait_recv()
        result = result + owner_recv[step - 1]
    signal_ref[...] = result[:4]

    for which, halo, source_ref, depth in ((0, deriv_halo, azim_flux, 1), (1, filter_halo, lined, 2)):
        wait_moment_sends(which)
        wait_start_sends(which)
        wait_edge_sends(which)
        for copy in halo_copies(which, halo, source_ref, depth):
            copy.wait_send()
    for step in range(1, 8):
        part_copy(step).wait_send()
    for step in range(1, 16):
        owner_copy(step).wait_send()
    pltpu.make_async_copy(
        plane_recv.at[pl.ds(1, AZIM - 1)], plane_recv.at[pl.ds(1, AZIM - 1)], plane_send_sem
    ).wait()


def per_device(
    density,
    velocity,
    pressure,
    axial_metric,
    azim_metric,
    volume,
    radial_term,
    panel_area,
    observer_ids,
    bin_ids,
    weight_ids,
    bin_weights,
):
    own, sent, taken = both_tables()
    rows = PLANES * ROWS
    hbm = pl.BlockSpec(memory_space=pltpu.HBM)
    vmem = pl.BlockSpec(memory_space=pltpu.VMEM)
    dma = pltpu.SemaphoreType.DMA
    state, signals = pl.pallas_call(
        kernel,
        out_shape=(
            jax.ShapeDtypeStruct((FIELDS, rows, LANES), F32),
            jax.ShapeDtypeStruct((4, TIME_BINS), F32),
        ),
        in_specs=[hbm] * 16,
        out_specs=(vmem, vmem),
        scratch_shapes=[
            pltpu.VMEM((2, 2 * LANES, 2 * LANES), BF16),
            pltpu.VMEM((2, 2, 32, 2 * LANES), BF16),
            pltpu.VMEM((2, 2, 64, 2 * LANES), BF16),
            pltpu.VMEM((rows, LANES), F32),
            pltpu.VMEM((3, rows, LANES), F32),
            pltpu.VMEM((rows, LANES), F32),
            pltpu.VMEM((3, rows, LANES), F32),
            pltpu.VMEM((3, rows, LANES), F32),
            pltpu.VMEM((rows, LANES), F32),
            pltpu.VMEM((FIELDS, rows, LANES), F32),
            pltpu.VMEM((ROWS, LANES), F32),
            pltpu.VMEM((ENTRY_ROWS, LANES), jnp.int32),
            pltpu.VMEM((ENTRY_ROWS, LANES), jnp.int32),
            pltpu.VMEM((ENTRY_ROWS, LANES), jnp.int32),
            pltpu.VMEM((2, LANES), F32),
            pltpu.VMEM((ROWS, NAZ), F32),
            pltpu.VMEM((ROWS, SLAB, LANES), F32),
            pltpu.VMEM((ROWS, SLAB, LANES), F32),
            pltpu.VMEM((ROWS, PLANES, LANES), F32),
            pltpu.VMEM((2, LINES, 2 * LANES), BF16),
            pltpu.VMEM((ROWS, SLAB, LANES), F32),
            pltpu.VMEM((2, 2, 8, HALF), F32),
            pltpu.VMEM((2, AXIAL, 8, HALF), F32),
            pltpu.VMEM((2, SLOTS, TILE_ROWS, LANES), F32),
            pltpu.VMEM((2, AZIM, SHARE[0], LANES), F32),
            pltpu.VMEM((2, AZIM, SHARE[0], LANES), F32),
            pltpu.VMEM((2, SLOTS, TILE_ROWS, LANES), F32),
            pltpu.VMEM((2, 1, SLAB, LANES), F32),
            pltpu.VMEM((2, 2, SLAB, LANES), F32),
            pltpu.VMEM((OBSERVERS, ENTRY_ROWS * LANES), BF16),
            pltpu.VMEM((2 * TIME_BINS, ENTRY_ROWS * LANES), BF16),
            pltpu.VMEM((OBSERVERS, TIME_BINS), F32),
            pltpu.VMEM((7, 64, TIME_BINS), F32),
            pltpu.VMEM((16, 8, TIME_BINS), F32),
            pltpu.VMEM((15, 8, TIME_BINS), F32),
            pltpu.VMEM((ROWS, LANES), F32),
            pltpu.VMEM((AZIM, ROWS, LANES), F32),
            dma((21,)),
            dma((2, 3)),
            dma((2, 3)),
            dma((2,)),
            dma((2,)),
            dma((2,)),
            dma((2,)),
            dma((2, 2)),
            dma((2, 2)),
            dma((7,)),
            dma((7,)),
            dma((15,)),
            dma((15,)),
            dma(()),
            dma(()),
        ],
        compiler_params=pltpu.CompilerParams(
            collective_id=0, has_side_effects=True
        ),
    )(
        jnp.asarray(own),
        jnp.asarray(sent),
        jnp.asarray(taken),
        density.reshape(rows, LANES),
        velocity.reshape(3, rows, LANES),
        pressure.reshape(rows, LANES),
        axial_metric.reshape(3, rows, LANES),
        azim_metric.reshape(3, rows, LANES),
        volume.reshape(rows, LANES),
        radial_term.reshape(FIELDS, rows, LANES),
        panel_area,
        observer_ids.reshape(ENTRY_ROWS, LANES),
        bin_ids.reshape(ENTRY_ROWS, LANES),
        weight_ids.reshape(ENTRY_ROWS, LANES),
        bin_weights.reshape(2, LANES),
        jnp.asarray(azimuth_rows()),
    )
    return state.reshape(FIELDS, PLANES, ROWS, LANES), signals


def solution(mesh):
    placed = (
        P(None, "azim", "axial"),
        P(None, None, "azim", "axial"),
        P(None, "azim", "axial"),
        P(None, None, "azim", "axial"),
        P(None, None, "azim", "axial"),
        P(None, "azim", "axial"),
        P(None, None, "azim", "axial"),
        P("azim", "axial"),
        P(None, "azim", "axial"),
        P(None, "azim", "axial"),
        P(None, "azim", "axial"),
        P(),
    )
    return jax.shard_map(
        per_device,
        mesh=mesh,
        in_specs=placed,
        out_specs=(P(None, None, "azim", "axial"), P(("axial", "azim"), None)),
        check_vma=False,
    )
```

```python
import functools
import math

import jax
import jax.numpy as jnp
import ml_dtypes
import numpy as np
from jax import lax
from jax.experimental import pallas as pl
from jax.experimental.pallas import tpu as pltpu
from jax.sharding import PartitionSpec as P

F32 = jnp.float32
BF16 = jnp.bfloat16
MESH = pl.DeviceIdType.MESH

PLANES = 64
FIELDS = 5
ROWS = 8
LANES = 128
AXIAL = 4
AZIM = 32
NA = AXIAL * LANES
NAZ = AZIM * ROWS
SLAB = FIELDS * PLANES
LINES = ROWS * SLAB
BLOCKS = PLANES // 8
SLOTS = 2 * BLOCKS
TILE_ROWS = 8 * FIELDS
SHARE = (24, 16)
HALF = LINES // 2
ENTRY_ROWS = 32
OBSERVERS = 512
TIME_BINS = 128
PEERS = (AZIM - 1) + 2 * (AXIAL - 1)

SECTION = 0.25
DERIV_ALPHA = 1.0 / 3.0
BETA = 0.499


def decay_root(alpha):
    return (-1.0 + math.sqrt(1.0 - 4.0 * alpha * alpha)) / (2.0 * alpha)


DL = decay_root(DERIV_ALPHA)
FL = decay_root(BETA)
C1 = (1.0 / 36.0) / DERIV_ALPHA
DS = 1.0 / math.sqrt(1.0 - 4.0 * DERIV_ALPHA**2)
DK = (7.0 / 9.0 - C1) * DS * (1.0 / DL - DL)
FC = [
    (11.0 + 10.0 * BETA) / 16.0,
    (15.0 + 34.0 * BETA) / 32.0,
    (-3.0 + 6.0 * BETA) / 16.0,
    (1.0 - 2.0 * BETA) / 32.0,
]
FS = 1.0 / math.sqrt(1.0 - 4.0 * BETA**2)
E2 = FC[3] / (2.0 * BETA)
E1 = (FC[2] / 2.0 - E2) / BETA
E0 = (FC[1] / 2.0 - E1 - BETA * E2) / BETA
FK = (FC[0] - E0 - 2.0 * BETA * E1) * FS


def split(values):
    high = values.astype(ml_dtypes.bfloat16)
    low = (values - high.astype(np.float64)).astype(ml_dtypes.bfloat16)
    return high, low


def axial_tables(root, scale, band):
    n, w = NA, LANES
    index = np.arange(n)
    green = scale * (
        np.power(root, np.abs(index[:, None] - index[None, :]))
        - np.power(root, 2 * n - index[:, None] - index[None, :])
    )
    side = np.zeros((n, n))
    for shift, value in band.items():
        side += value * np.eye(n, k=shift)
    whole = green @ side
    left = np.zeros((AXIAL, w))
    right = np.zeros((AXIAL, w))
    for k in range(AXIAL):
        cols = slice(k * w, (k + 1) * w)
        lo, hi = max(0, k * w - 3), min(n, (k + 1) * w + 3)
        m = np.arange(lo, hi)
        left[k] = np.power(root, ((k + 1) * w - m).astype(np.float64)) @ side[lo:hi, cols]
        right[k] = (
            np.power(root, (m - k * w + 1).astype(np.float64))
            - np.power(root, (2 * n - m - k * w + 1).astype(np.float64))
        ) @ side[lo:hi, cols]
    t = np.arange(w)
    full = np.stack([whole[d * w : (d + 1) * w].T for d in range(AXIAL)]).astype(np.float32)
    own = np.zeros((AXIAL, w, 2 * w), ml_dtypes.bfloat16)
    sent = np.zeros((AXIAL, 2, 32, 2 * w), ml_dtypes.bfloat16)
    taken = np.zeros((AXIAL, 2, 64, 2 * w), ml_dtypes.bfloat16)
    for d in range(AXIAL):
        high, low = split(whole[d * w : (d + 1) * w, d * w : (d + 1) * w].T)
        own[d] = np.concatenate([high, low], axis=1)
        for half in range(2):
            rows = np.zeros((16, w))
            base = half * 4
            rows[base] = left[d]
            rows[base + 1, w - 1] = 1.0
            rows[base + 2, w - 2] = 1.0
            rows[8 + base] = right[d]
            rows[8 + base + 1, 0] = 1.0
            rows[8 + base + 2, 1] = 1.0
            high, low = split(rows)
            sent[d, half] = np.concatenate(
                [np.concatenate([high, high], axis=1), np.concatenate([low, low], axis=1)], axis=0
            )
            rows = np.zeros((32, w))
            for k in range(AXIAL):
                row = k * 8 + half * 4
                i = d * w + t
                if k < d:
                    rows[row] = scale * (
                        np.power(root, (i - (k + 1) * w).astype(np.float64))
                        - np.power(root, (2 * n - i - (k + 1) * w).astype(np.float64))
                    )
                    if k == d - 1:
                        for edge in range(2):
                            col = d * w - 1 - edge
                            for near in range(2 - edge):
                                rows[row + 1 + edge, near] = (
                                    whole[d * w + near, col] - rows[row, near] * left[k, col - k * w]
                                )
                if k > d:
                    rows[row] = scale * np.power(root, (k * w - 1 - i).astype(np.float64))
                    if k == d + 1:
                        for edge in range(2):
                            col = k * w + edge
                            for near in range(2 - edge):
                                rows[row + 1 + edge, w - 1 - near] = (
                                    whole[k * w - 1 - near, col] - rows[row, w - 1 - near] * right[k, edge]
                                )
            high, low = split(rows)
            pair = np.concatenate([high, low], axis=1)
            taken[d, half] = np.concatenate([pair, pair], axis=0)
    return own, sent, taken, full


def both_tables():
    deriv = axial_tables(DL, DS, {1: 7.0 / 9.0, -1: -7.0 / 9.0, 2: 1.0 / 36.0, -2: -1.0 / 36.0})
    band = {0: FC[0]}
    for shift in range(1, 4):
        band[shift] = band[-shift] = FC[shift] / 2.0
    smooth = axial_tables(FL, FS, band)
    return [np.stack(pair, axis=1) for pair in zip(deriv, smooth)]


def azimuth_rows():
    gap = np.arange(NAZ)
    slope = DK * (np.power(DL, gap) - np.power(DL, NAZ - gap)) / (1.0 - DL**NAZ)
    slope[0] = 0.0
    slope[1] += C1
    slope[-1] -= C1
    line = FK * (np.power(FL, gap) + np.power(FL, NAZ - gap)) / (1.0 - FL**NAZ)
    line[0] = FK * (1.0 + 2.0 * FL**NAZ / (1.0 - FL**NAZ)) + E0
    for shift, value in ((1, E1), (2, E2)):
        line[shift] += value
        line[-shift] += value
    rows = np.arange(ROWS)
    at = (gap[None, :] - rows[:, None]) % NAZ
    return np.stack([slope[at], line[at]]).astype(np.float32)


def two_terms(value):
    high = value.astype(BF16)
    low = (value - high.astype(F32)).astype(BF16)
    return high, low


def dot_last(left, right):
    return lax.dot_general(left, right, (((1,), (1,)), ((), ())), preferred_element_type=F32)


def dot_first(left, right):
    return lax.dot_general(left, right, (((0,), (0,)), ((), ())), preferred_element_type=F32)


def kernel(
    own_hbm,
    sent_hbm,
    taken_hbm,
    density_hbm,
    velocity_hbm,
    pressure_hbm,
    axial_hbm,
    azim_hbm,
    volume_hbm,
    radial_hbm,
    area_hbm,
    observer_hbm,
    bin_hbm,
    weight_hbm,
    table_hbm,
    azimuth_hbm,
    full_hbm,
    final,
    signal_ref,
    own,
    sent,
    taken,
    density,
    velocity,
    pressure,
    axial_metric,
    azim_metric,
    volume,
    radial,
    area_ref,
    observer_ref,
    bin_ref,
    weight_ref,
    table_ref,
    azimuth_ref,
    full,
    azim_flux,
    base,
    ratio,
    cells,
    lined,
    edge_send,
    edge_recv,
    moment_send,
    moment_recv,
    start_send,
    start_recv,
    deriv_halo,
    filter_halo,
    observer_hot,
    bin_hot,
    partial,
    part_recv,
    owner_send,
    owner_recv,
    plane_send,
    plane_recv,
    axial_send,
    axial_recv,
    panel_axial,
    load_sem,
    early_sem,
    late_sem,
    edge_send_sem,
    edge_recv_sem,
    moment_send_sem,
    moment_recv_sem,
    start_send_sem,
    start_recv_sem,
    halo_send_sem,
    halo_recv_sem,
    part_send_sem,
    part_recv_sem,
    owner_send_sem,
    owner_recv_sem,
    plane_send_sem,
    plane_recv_sem,
    axial_send_sem,
    axial_recv_sem,
):
    me_a = lax.axis_index("axial")
    me_z = lax.axis_index("azim")
    core = lax.rem(me_z, 2)
    chip = me_z // 2
    twin = me_z + 1 - 2 * core
    after = lax.rem(me_z + 1, AZIM)
    before = lax.rem(me_z + AZIM - 1, AZIM)

    def early_loads(group):
        part = pl.ds(pl.multiple_of(group * 128, 128), 128)
        whole = slice(None)
        return [
            pltpu.make_async_copy(source.at[where], dest.at[where], early_sem.at[number, group])
            for number, (source, dest, where) in enumerate(
                (
                    (density_hbm, density, (part,)),
                    (velocity_hbm, velocity, (whole, part)),
                    (pressure_hbm, pressure, (part,)),
                    (volume_hbm, volume, (part,)),
                    (azim_hbm, azim_metric, (whole, part)),
                )
            )
        ]

    def late_loads(group):
        part = pl.ds(pl.multiple_of(group * 128, 128), 128)
        return [
            pltpu.make_async_copy(axial_hbm.at[:, part], axial_metric.at[:, part], late_sem.at[0, group]),
            pltpu.make_async_copy(radial_hbm.at[:, part], radial.at[:, part], late_sem.at[1, group]),
        ]

    loads = [
        pltpu.make_async_copy(area_hbm, area_ref, load_sem.at[0]),
        pltpu.make_async_copy(observer_hbm, observer_ref, load_sem.at[1]),
        pltpu.make_async_copy(bin_hbm, bin_ref, load_sem.at[2]),
        pltpu.make_async_copy(weight_hbm, weight_ref, load_sem.at[3]),
        pltpu.make_async_copy(table_hbm, table_ref, load_sem.at[4]),
        pltpu.make_async_copy(azimuth_hbm, azimuth_ref, load_sem.at[5]),
        pltpu.make_async_copy(full_hbm.at[me_a], full, load_sem.at[6]),
    ]
    for which in range(2):
        loads.append(
            pltpu.make_async_copy(
                own_hbm.at[me_a, which], own.at[which, pl.ds(0, LANES)], load_sem.at[7 + 4 * which]
            )
        )
        loads.append(
            pltpu.make_async_copy(
                own_hbm.at[me_a, which], own.at[which, pl.ds(LANES, LANES)], load_sem.at[8 + 4 * which]
            )
        )
        loads.append(pltpu.make_async_copy(sent_hbm.at[me_a, which], sent.at[which], load_sem.at[9 + 4 * which]))
        loads.append(pltpu.make_async_copy(taken_hbm.at[me_a, which], taken.at[which], load_sem.at[10 + 4 * which]))
    for group in range(BLOCKS // 2):
        for load in early_loads(group):
            load.start()
    for group in range(BLOCKS // 2):
        for load in late_loads(group):
            load.start()
    for load in loads:
        load.start()

    barrier = pltpu.get_barrier_semaphore()

    def greet_azim(step, carry):
        other = lax.rem(me_z + step, AZIM)
        pl.semaphore_signal(barrier, inc=1, device_id=(me_a, other), device_id_type=MESH)
        return carry

    lax.fori_loop(1, AZIM, greet_azim, 0)

    def greet_axial(step, carry):
        other = lax.rem(me_a + step, AXIAL)
        pl.semaphore_signal(barrier, inc=1, device_id=(other, me_z), device_id_type=MESH)
        pl.semaphore_signal(barrier, inc=1, device_id=(other, twin), device_id_type=MESH)
        return carry

    lax.fori_loop(1, AXIAL, greet_axial, 0)

    edge_recv[0, pl.ds(me_a, 1)] = jnp.zeros((1, 8, HALF), F32)
    edge_recv[1, pl.ds(me_a, 1)] = jnp.zeros((1, 8, HALF), F32)


    def moment_copy(which, slot, share):
        return pltpu.make_async_remote_copy(
            src_ref=moment_send.at[which, slot, pl.ds(share * SHARE[0], SHARE[share])],
            dst_ref=moment_recv.at[which, me_z, pl.ds(0, SHARE[share])],
            send_sem=moment_send_sem.at[which],
            recv_sem=moment_recv_sem.at[which],
            device_id=(me_a, 2 * slot + share),
            device_id_type=MESH,
        )

    def send_moments(which):
        def to_chip(step, carry):
            slot = lax.rem(chip + step, SLOTS)
            for share in range(2):
                moment_copy(which, slot, share).start()
            return carry

        lax.fori_loop(1, SLOTS, to_chip, 0)
        for share in range(2):

            @pl.when(core == share)
            def _():
                moment_copy(which, chip, 1 - share).start()
                pltpu.make_async_copy(
                    moment_send.at[which, chip, pl.ds(share * SHARE[0], SHARE[share])],
                    moment_recv.at[which, me_z, pl.ds(0, SHARE[share])],
                    moment_recv_sem.at[which],
                ).start()

    def wait_moment_sends(which):
        for share in range(2):

            @pl.when(core == share)
            def _():
                part = moment_send.at[which, pl.ds(0, SLOTS - 1)]
                pltpu.make_async_copy(part, part, moment_send_sem.at[which]).wait()
                part = moment_send.at[which, SLOTS - 1, pl.ds(0, SHARE[1 - share])]
                pltpu.make_async_copy(part, part, moment_send_sem.at[which]).wait()

    def reduce_moments(which, root):
        factor = root**ROWS
        wrap = 1.0 / (1.0 - root**NAZ)
        side = lax.rem(chip, 2)

        def place(step):
            return step + side * (AZIM - 1 - 2 * step)

        for share in range(2):
            rows = pl.ds(0, SHARE[share])
            there = pl.ds(share * SHARE[0], SHARE[share])

            @pl.when(core == share)
            def _():
                part = moment_recv.at[which, :, rows]
                pltpu.make_async_copy(part, part, moment_recv_sem.at[which]).wait()

                def gather(step, total):
                    return factor * total + moment_recv[which, place(step), rows]

                first = lax.fori_loop(0, AZIM, gather, jnp.zeros((SHARE[share], LANES), F32), unroll=8) * wrap

                def follow(step, now):
                    other = place(step)
                    start_send[which, other, rows] = now
                    return factor * now + moment_recv[which, other, rows]

                lax.fori_loop(0, AZIM, follow, first, unroll=8)

                pltpu.make_async_copy(
                    start_send.at[which, me_z, rows], start_recv.at[which, chip, there], start_recv_sem.at[which]
                ).start()

                def hand_out(step, carry):
                    other = lax.rem(me_z + step, AZIM)
                    pltpu.make_async_remote_copy(
                        src_ref=start_send.at[which, other, rows],
                        dst_ref=start_recv.at[which, chip, there],
                        send_sem=start_send_sem.at[which],
                        recv_sem=start_recv_sem.at[which],
                        device_id=(me_a, other),
                        device_id_type=MESH,
                    ).start()
                    return carry

                lax.fori_loop(1, AZIM, hand_out, 0)

    def wait_starts(which):
        part = start_recv.at[which]
        pltpu.make_async_copy(part, part, start_recv_sem.at[which]).wait()

    def wait_start_sends(which):
        for share in range(2):

            @pl.when(core == share)
            def _():
                part = start_send.at[which, pl.ds(0, AZIM - 1), pl.ds(0, SHARE[share])]
                pltpu.make_async_copy(part, part, start_send_sem.at[which]).wait()

    def moments_of(values, root):
        up = root * values[0]
        for row in range(1, ROWS):
            up = root * (up + values[row])
        down = root * values[ROWS - 1]
        for row in range(ROWS - 2, -1, -1):
            down = root * (down + values[row])
        return up, down

    def keep_moments(which, group, field, values, root):
        up, down = moments_of(values, root)
        for half in range(2):
            for side, value in ((0, up), (1, down)):
                moment_send[which, 4 * group + 2 * half + side, pl.ds(8 * field, 8)] = value[8 * half : 8 * half + 8]

    def start_of(which, group, field, side):
        return jnp.concatenate(
            [start_recv[which, 4 * group + 2 * half + side, pl.ds(8 * field, 8)] for half in range(2)], axis=0
        )

    def halo_copies(which, halo, source, depth):
        return (
            pltpu.make_async_remote_copy(
                src_ref=source.at[pl.ds(ROWS - depth, depth)],
                dst_ref=halo.at[0],
                send_sem=halo_send_sem.at[which, 0],
                recv_sem=halo_recv_sem.at[which, 0],
                device_id=(me_a, after),
                device_id_type=MESH,
            ),
            pltpu.make_async_remote_copy(
                src_ref=source.at[pl.ds(0, depth)],
                dst_ref=halo.at[1],
                send_sem=halo_send_sem.at[which, 1],
                recv_sem=halo_recv_sem.at[which, 1],
                device_id=(me_a, before),
                device_id_type=MESH,
            ),
        )

    def edge_copy(which, step):
        other = lax.rem(me_a + step, AXIAL)
        down = jnp.where(other < me_a, 1, 0)
        return pltpu.make_async_remote_copy(
            src_ref=edge_send.at[which, down],
            dst_ref=edge_recv.at[which, me_a],
            send_sem=edge_send_sem.at[which, step - 1],
            recv_sem=edge_recv_sem.at[which, step - 1],
            device_id=(other, me_z),
            device_id_type=MESH,
        )

    def send_edges(which):
        def piece(step, carry):
            at = pl.multiple_of(step * 640, 640)
            total = dot_last(sent[which, 0], cells[which, pl.ds(at, 640)]) + dot_last(
                sent[which, 1], cells[which, pl.ds(HALF + at, 640)]
            )
            total = total[:16] + total[16:]
            edge_send[which, 0, :, pl.ds(at, 640)] = total[:8]
            edge_send[which, 1, :, pl.ds(at, 640)] = total[8:]
            return carry

        lax.fori_loop(0, 2, piece, 0)
        for step in range(1, AXIAL):
            edge_copy(which, step).start()

    def own_part(which):
        def piece(row, carry):
            at = pl.multiple_of(row * SLAB, SLAB)
            total = jnp.dot(cells[which, pl.ds(at, SLAB)], own[which], preferred_element_type=F32)
            lined[row] = total[:, :LANES] + total[:, LANES:]
            return carry

        lax.fori_loop(0, ROWS, piece, 0)

    def add_edges(which):
        for step in range(1, AXIAL):
            edge_copy(which, step).wait_recv()

        def piece(step, carry):
            at = pl.multiple_of(lax.rem(step, 2) * 640, 640)
            received = edge_recv[which, :, :, pl.ds(at, 640)].reshape(32, 640)
            high, low = two_terms(received)
            total = dot_first(jnp.concatenate([high, low], axis=0), taken[which, step // 2])
            total = (total[:, :LANES] + total[:, LANES:]).reshape(2, SLAB, LANES)
            lined[pl.ds(2 * step, 2)] = lined[pl.ds(2 * step, 2)] + total
            return carry

        lax.fori_loop(0, 4, piece, 0)

    def wait_edge_sends(which):
        for step in range(1, AXIAL):
            edge_copy(which, step).wait_send()

    def keep_cells(which, row, field, group, value):
        high, low = two_terms(value)
        at = pl.multiple_of(row * SLAB + field * PLANES + group * 16, 16)
        cells[which, pl.ds(at, 16), pl.ds(0, LANES)] = high
        cells[which, pl.ds(at, 16), pl.ds(LANES, LANES)] = low

    def axial_copy(which, step):
        return pltpu.make_async_remote_copy(
            src_ref=axial_send.at[which],
            dst_ref=axial_recv.at[which, me_a],
            send_sem=axial_send_sem.at[which, step - 1],
            recv_sem=axial_recv_sem.at[which, step - 1],
            device_id=(lax.rem(me_a + step, AXIAL), me_z),
            device_id_type=MESH,
        )

    def send_axial(which, value):
        axial_send[which] = value
        axial_recv[which, pl.ds(me_a, 1)] = value[None]
        for step in range(1, AXIAL):
            axial_copy(which, step).start()

    def take_axial(which):
        for step in range(1, AXIAL):
            axial_copy(which, step).wait_recv()
        line = jnp.concatenate([axial_recv[which, k] for k in range(AXIAL)], axis=1)
        return jnp.dot(line, full[which], preferred_element_type=F32, precision=lax.Precision.HIGHEST)

    def send_plane(which, value):
        plane_send[which] = value
        plane_recv[which, 0] = value

        def piece(step, carry):
            pltpu.make_async_remote_copy(
                src_ref=plane_send.at[which],
                dst_ref=plane_recv.at[which, AZIM - step],
                send_sem=plane_send_sem.at[which],
                recv_sem=plane_recv_sem.at[which],
                device_id=(me_a, lax.rem(me_z + step, AZIM)),
                device_id_type=MESH,
            ).start()
            return carry

        lax.fori_loop(1, AZIM, piece, 0)

    def plane_wait(which, sem):
        part = plane_recv.at[which, pl.ds(1, AZIM - 1)]
        pltpu.make_async_copy(part, part, sem.at[which]).wait()

    def take_plane(which):
        plane_wait(which, plane_recv_sem)
        return jnp.dot(
            azimuth_ref[which],
            plane_recv[which].reshape(NAZ, LANES),
            preferred_element_type=F32,
            precision=lax.Precision.HIGHEST,
        )

    def flux_of(metric, at, rho, vel, prs, vol, heat):
        grad = [metric[comp, at] for comp in range(3)]
        contra = vol * (grad[0] * vel[0] + grad[1] * vel[1] + grad[2] * vel[2])
        flow = rho * contra
        push = vol * prs
        return [flow] + [flow * vel[comp] + grad[comp] * push for comp in range(3)] + [heat * contra]

    def cells_at(group, row):
        at = pl.ds(group * 128 + row, 16, stride=ROWS)
        rho, prs, vol = density[at], pressure[at], volume[at]
        vel = [velocity[comp, at] for comp in range(3)]
        energy = 2.5 * prs + 0.5 * rho * (vel[0] * vel[0] + vel[1] * vel[1] + vel[2] * vel[2])
        return at, rho, vel, prs, vol, energy

    def azim_group(group, carry):
        for load in early_loads(group):
            load.wait()
        flux = [[None] * ROWS for _ in range(FIELDS)]
        for row in range(ROWS):
            at, rho, vel, prs, vol, energy = cells_at(group, row)
            parts = flux_of(azim_metric, at, rho, vel, prs, vol, energy + prs)
            for field in range(FIELDS):
                flux[field][row] = parts[field]
                azim_flux[row, pl.ds(pl.multiple_of(field * PLANES + group * 16, 16), 16)] = parts[field]
        for field in range(FIELDS):
            keep_moments(0, group, field, flux[field], DL)
        return carry

    lax.fori_loop(0, BLOCKS // 2, azim_group, 0)
    pl.semaphore_wait(barrier, PEERS)
    send_moments(0)
    send_plane(0, azim_flux[:, 0] + azim_flux[:, 2 * PLANES])
    for copy in halo_copies(0, deriv_halo, azim_flux, 1):
        copy.start()

    def axial_group(group, carry):
        for load in late_loads(group):
            load.wait()
        for row in range(ROWS):
            at, rho, vel, prs, vol, energy = cells_at(group, row)
            state = [rho, rho * vel[0], rho * vel[1], rho * vel[2], energy]
            ratio[row, pl.ds(pl.multiple_of(group * 16, 16), 16)] = SECTION / vol
            for field in range(FIELDS):
                base[row, pl.ds(pl.multiple_of(field * PLANES + group * 16, 16), 16)] = (
                    state[field] + SECTION * radial[field, at]
                )
            parts = flux_of(axial_metric, at, rho, vel, prs, vol, energy + prs)
            for field in range(FIELDS):
                keep_cells(0, row, field, group, parts[field])
            panel_axial[group, pl.ds(row, 1)] = parts[0][:1] + parts[2][:1]
        return carry

    lax.fori_loop(0, BLOCKS // 2, axial_group, 0)
    send_axial(0, panel_axial[0])
    for load in loads:
        load.wait()
    send_edges(0)

    ids = observer_ref[...]
    order = (
        lax.shift_right_logical(ids, 7) * 128
        + (lax.shift_right_logical(ids, 2) & 1) * 64
        + (lax.shift_right_logical(ids, 3) & 15) * 4
        + (ids & 3)
    )
    partial[pl.ds(0, ENTRY_ROWS)] = order.astype(F32)

    def hot_row(row, carry):
        wanted = partial[pl.ds(row, 1)].astype(jnp.int32)
        rows = lax.broadcasted_iota(jnp.int32, (OBSERVERS, LANES), 0)
        at = pl.multiple_of(row * LANES, LANES)
        observer_hot[:, pl.ds(at, LANES)] = jnp.where(rows == wanted, 1.0, 0.0).astype(BF16)
        return carry

    lax.fori_loop(0, ENTRY_ROWS, hot_row, 0)

    own_part(0)
    reduce_moments(0, DL)
    change = take_axial(0) + take_plane(0)
    send_axial(1, base[:, 0] + base[:, 2 * PLANES] - ratio[:, 0] * change)
    add_edges(0)
    send_plane(1, take_axial(1))
    wait_starts(0)
    for copy in halo_copies(0, deriv_halo, azim_flux, 1):
        copy.wait_recv()

    def section_group(group, carry):
        for field in range(FIELDS):
            at = pl.ds(pl.multiple_of(field * PLANES + group * 16, 16), 16)
            here = pl.ds(pl.multiple_of(group * 16, 16), 16)
            flux = [deriv_halo[0, 0, at]] + [azim_flux[row, at] for row in range(ROWS)] + [deriv_halo[1, 0, at]]
            up = [start_of(0, group, field, 0)]
            for row in range(ROWS - 1):
                up.append(DL * (flux[row + 1] + up[-1]))
            down = [start_of(0, group, field, 1)]
            for row in range(ROWS - 1, 0, -1):
                down.append(DL * (flux[row + 1] + down[-1]))
            down = down[::-1]
            for row in range(ROWS):
                deriv = DK * (down[row] - up[row]) + C1 * (flux[row + 2] - flux[row])
                value = base[row, at] - ratio[row, here] * (lined[row, at] + deriv)
                keep_cells(1, row, field, group, value)
        return carry

    lax.fori_loop(0, BLOCKS // 2, section_group, 0)
    send_edges(1)
    own_part(1)
    add_edges(1)

    def moment_group(group, carry):
        for field in range(FIELDS):
            at = pl.ds(pl.multiple_of(field * PLANES + group * 16, 16), 16)
            keep_moments(1, group, field, [lined[row, at] for row in range(ROWS)], FL)
        return carry

    lax.fori_loop(0, BLOCKS // 2, moment_group, 0)
    send_moments(1)
    for copy in halo_copies(1, filter_halo, lined, 2):
        copy.start()
    source = area_ref[...] * (take_plane(1) - 1.0)
    picks = weight_ref[...]
    low_half = jnp.take_along_axis(
        jnp.broadcast_to(table_ref[pl.ds(0, 1)], (ENTRY_ROWS, LANES)), picks & 127, axis=1
    )
    high_half = jnp.take_along_axis(
        jnp.broadcast_to(table_ref[pl.ds(1, 1)], (ENTRY_ROWS, LANES)), picks & 127, axis=1
    )
    weights = jnp.where(picks < LANES, low_half, high_half)
    values = weights * jnp.concatenate([source] * 4, axis=0)
    high, low = two_terms(values)
    partial[pl.ds(0, ENTRY_ROWS)] = high.astype(F32)
    partial[pl.ds(ENTRY_ROWS, ENTRY_ROWS)] = low.astype(F32)

    def bin_row(row, carry):
        same = lax.broadcasted_iota(jnp.int32, (TIME_BINS, LANES), 0) == bin_ref[pl.ds(row, 1)]
        at = pl.multiple_of(row * LANES, LANES)
        bin_hot[pl.ds(0, TIME_BINS), pl.ds(at, LANES)] = jnp.where(same, partial[pl.ds(row, 1)], 0.0).astype(BF16)
        bin_hot[pl.ds(TIME_BINS, TIME_BINS), pl.ds(at, LANES)] = jnp.where(
            same, partial[pl.ds(ENTRY_ROWS + row, 1)], 0.0
        ).astype(BF16)
        return carry

    lax.fori_loop(0, ENTRY_ROWS, bin_row, 0)

    total = dot_last(observer_hot[...], bin_hot[...])
    partial[...] = total[:, :TIME_BINS] + total[:, TIME_BINS:]

    mine = me_a * 2 + core

    def part_copy(step):
        other = lax.rem(mine + step, 8)
        other_z = me_z - core + lax.rem(other, 2)
        return pltpu.make_async_remote_copy(
            src_ref=partial.at[pl.ds(pl.multiple_of(other * 64, 64), 64)],
            dst_ref=part_recv.at[step - 1],
            send_sem=part_send_sem.at[step - 1],
            recv_sem=part_recv_sem.at[step - 1],
            device_id=(other // 2, other_z),
            device_id_type=MESH,
        )

    for step in range(1, 8):
        part_copy(step).start()
    reduce_moments(1, FL)
    total = partial[pl.ds(pl.multiple_of(mine * 64, 64), 64)]
    for step in range(1, 8):
        part_copy(step).wait_recv()
        total = total + part_recv[step - 1]
    for owner in range(16):
        owner_send[owner, pl.ds(0, 4)] = total[4 * owner : 4 * owner + 4]
        owner_send[owner, pl.ds(4, 4)] = jnp.zeros((4, LANES), F32)

    def owner_copy(step):
        other = lax.rem(chip + step, 16)
        return pltpu.make_async_remote_copy(
            src_ref=owner_send.at[other],
            dst_ref=owner_recv.at[step - 1],
            send_sem=owner_send_sem.at[step - 1],
            recv_sem=owner_recv_sem.at[step - 1],
            device_id=(me_a, 2 * other + core),
            device_id_type=MESH,
        )

    for step in range(1, 16):
        owner_copy(step).start()
    wait_starts(1)
    for copy in halo_copies(1, filter_halo, lined, 2):
        copy.wait_recv()

    def final_group(group, carry):
        for field in range(FIELDS):
            at = pl.ds(pl.multiple_of(field * PLANES + group * 16, 16), 16)
            value = [filter_halo[0, 0, at], filter_halo[0, 1, at]]
            value += [lined[row, at] for row in range(ROWS)]
            value += [filter_halo[1, 0, at], filter_halo[1, 1, at]]
            up = [start_of(1, group, field, 0)]
            for row in range(ROWS - 1):
                up.append(FL * (value[row + 2] + up[-1]))
            down = [start_of(1, group, field, 1)]
            for row in range(ROWS - 1, 0, -1):
                down.append(FL * (value[row + 2] + down[-1]))
            down = down[::-1]
            for row in range(ROWS):
                near = E1 * (value[row + 1] + value[row + 3]) + E2 * (value[row] + value[row + 4])
                result = FK * (up[row] + down[row]) + (FK + E0) * value[row + 2] + near
                final[field, pl.ds(group * 128 + row, 16, stride=ROWS)] = result
        return carry

    lax.fori_loop(0, BLOCKS // 2, final_group, 0)

    result = owner_send[chip]
    for step in range(1, 16):
        owner_copy(step).wait_recv()
        result = result + owner_recv[step - 1]
    signal_ref[...] = result[:4]

    for which, halo, source_ref, depth in ((0, deriv_halo, azim_flux, 1), (1, filter_halo, lined, 2)):
        wait_moment_sends(which)
        wait_start_sends(which)
        wait_edge_sends(which)
        for copy in halo_copies(which, halo, source_ref, depth):
            copy.wait_send()
    for step in range(1, 8):
        part_copy(step).wait_send()
    for step in range(1, 16):
        owner_copy(step).wait_send()
    for which in range(2):
        plane_wait(which, plane_send_sem)
        for step in range(1, AXIAL):
            axial_copy(which, step).wait_send()


def per_device(
    density,
    velocity,
    pressure,
    axial_metric,
    azim_metric,
    volume,
    radial_term,
    panel_area,
    observer_ids,
    bin_ids,
    weight_ids,
    bin_weights,
):
    own, sent, taken, full = both_tables()
    rows = PLANES * ROWS
    hbm = pl.BlockSpec(memory_space=pltpu.HBM)
    vmem = pl.BlockSpec(memory_space=pltpu.VMEM)
    dma = pltpu.SemaphoreType.DMA
    state, signals = pl.pallas_call(
        kernel,
        out_shape=(
            jax.ShapeDtypeStruct((FIELDS, rows, LANES), F32),
            jax.ShapeDtypeStruct((4, TIME_BINS), F32),
        ),
        in_specs=[hbm] * 17,
        out_specs=(vmem, vmem),
        scratch_shapes=[
            pltpu.VMEM((2, 2 * LANES, 2 * LANES), BF16),
            pltpu.VMEM((2, 2, 32, 2 * LANES), BF16),
            pltpu.VMEM((2, 2, 64, 2 * LANES), BF16),
            pltpu.VMEM((rows, LANES), F32),
            pltpu.VMEM((3, rows, LANES), F32),
            pltpu.VMEM((rows, LANES), F32),
            pltpu.VMEM((3, rows, LANES), F32),
            pltpu.VMEM((3, rows, LANES), F32),
            pltpu.VMEM((rows, LANES), F32),
            pltpu.VMEM((FIELDS, rows, LANES), F32),
            pltpu.VMEM((ROWS, LANES), F32),
            pltpu.VMEM((ENTRY_ROWS, LANES), jnp.int32),
            pltpu.VMEM((ENTRY_ROWS, LANES), jnp.int32),
            pltpu.VMEM((ENTRY_ROWS, LANES), jnp.int32),
            pltpu.VMEM((2, LANES), F32),
            pltpu.VMEM((2, ROWS, NAZ), F32),
            pltpu.VMEM((2, NA, LANES), F32),
            pltpu.VMEM((ROWS, SLAB, LANES), F32),
            pltpu.VMEM((ROWS, SLAB, LANES), F32),
            pltpu.VMEM((ROWS, PLANES, LANES), F32),
            pltpu.VMEM((2, LINES, 2 * LANES), BF16),
            pltpu.VMEM((ROWS, SLAB, LANES), F32),
            pltpu.VMEM((2, 2, 8, HALF), F32),
            pltpu.VMEM((2, AXIAL, 8, HALF), F32),
            pltpu.VMEM((2, SLOTS, TILE_ROWS, LANES), F32),
            pltpu.VMEM((2, AZIM, SHARE[0], LANES), F32),
            pltpu.VMEM((2, AZIM, SHARE[0], LANES), F32),
            pltpu.VMEM((2, SLOTS, TILE_ROWS, LANES), F32),
            pltpu.VMEM((2, 1, SLAB, LANES), F32),
            pltpu.VMEM((2, 2, SLAB, LANES), F32),
            pltpu.VMEM((OBSERVERS, ENTRY_ROWS * LANES), BF16),
            pltpu.VMEM((2 * TIME_BINS, ENTRY_ROWS * LANES), BF16),
            pltpu.VMEM((OBSERVERS, TIME_BINS), F32),
            pltpu.VMEM((7, 64, TIME_BINS), F32),
            pltpu.VMEM((16, 8, TIME_BINS), F32),
            pltpu.VMEM((15, 8, TIME_BINS), F32),
            pltpu.VMEM((2, ROWS, LANES), F32),
            pltpu.VMEM((2, AZIM, ROWS, LANES), F32),
            pltpu.VMEM((2, ROWS, LANES), F32),
            pltpu.VMEM((2, AXIAL, ROWS, LANES), F32),
            pltpu.VMEM((BLOCKS // 2, ROWS, LANES), F32),
            dma((15,)),
            dma((5, BLOCKS // 2)),
            dma((2, BLOCKS // 2)),
            dma((2, 3)),
            dma((2, 3)),
            dma((2,)),
            dma((2,)),
            dma((2,)),
            dma((2,)),
            dma((2, 2)),
            dma((2, 2)),
            dma((7,)),
            dma((7,)),
            dma((15,)),
            dma((15,)),
            dma((2,)),
            dma((2,)),
            dma((2, 3)),
            dma((2, 3)),
        ],
        compiler_params=pltpu.CompilerParams(
            collective_id=0, has_side_effects=True
        ),
    )(
        jnp.asarray(own),
        jnp.asarray(sent),
        jnp.asarray(taken),
        density.reshape(rows, LANES),
        velocity.reshape(3, rows, LANES),
        pressure.reshape(rows, LANES),
        axial_metric.reshape(3, rows, LANES),
        azim_metric.reshape(3, rows, LANES),
        volume.reshape(rows, LANES),
        radial_term.reshape(FIELDS, rows, LANES),
        panel_area,
        observer_ids.reshape(ENTRY_ROWS, LANES),
        bin_ids.reshape(ENTRY_ROWS, LANES),
        weight_ids.reshape(ENTRY_ROWS, LANES),
        bin_weights.reshape(2, LANES),
        jnp.asarray(azimuth_rows()),
        jnp.asarray(full),
    )
    return state.reshape(FIELDS, PLANES, ROWS, LANES), signals


def solution(mesh):
    placed = (
        P(None, "azim", "axial"),
        P(None, None, "azim", "axial"),
        P(None, "azim", "axial"),
        P(None, None, "azim", "axial"),
        P(None, None, "azim", "axial"),
        P(None, "azim", "axial"),
        P(None, None, "azim", "axial"),
        P("azim", "axial"),
        P(None, "azim", "axial"),
        P(None, "azim", "axial"),
        P(None, "azim", "axial"),
        P(),
    )
    return jax.shard_map(
        per_device,
        mesh=mesh,
        in_specs=placed,
        out_specs=(P(None, None, "azim", "axial"), P(("axial", "azim"), None)),
        check_vma=False,
    )
```

```python
import functools
import math

import jax
import jax.numpy as jnp
import ml_dtypes
import numpy as np
from jax import lax
from jax.experimental import pallas as pl
from jax.experimental.pallas import tpu as pltpu
from jax.sharding import PartitionSpec as P

F32 = jnp.float32
BF16 = jnp.bfloat16
MESH = pl.DeviceIdType.MESH

PLANES = 64
FIELDS = 5
ROWS = 8
LANES = 128
AXIAL = 4
AZIM = 32
NA = AXIAL * LANES
NAZ = AZIM * ROWS
SLAB = FIELDS * PLANES
LINES = ROWS * SLAB
BLOCKS = PLANES // 8
SLOTS = 2 * BLOCKS
TILE_ROWS = 8 * FIELDS
SHARE = (24, 16)
HALF = LINES // 2
ENTRY_ROWS = 32
OBSERVERS = 512
TIME_BINS = 128
PEERS = (AZIM - 1) + 2 * (AXIAL - 1)

SECTION = 0.25
DERIV_ALPHA = 1.0 / 3.0
BETA = 0.499


def decay_root(alpha):
    return (-1.0 + math.sqrt(1.0 - 4.0 * alpha * alpha)) / (2.0 * alpha)


DL = decay_root(DERIV_ALPHA)
FL = decay_root(BETA)
C1 = (1.0 / 36.0) / DERIV_ALPHA
DS = 1.0 / math.sqrt(1.0 - 4.0 * DERIV_ALPHA**2)
DK = (7.0 / 9.0 - C1) * DS * (1.0 / DL - DL)
FC = [
    (11.0 + 10.0 * BETA) / 16.0,
    (15.0 + 34.0 * BETA) / 32.0,
    (-3.0 + 6.0 * BETA) / 16.0,
    (1.0 - 2.0 * BETA) / 32.0,
]
FS = 1.0 / math.sqrt(1.0 - 4.0 * BETA**2)
E2 = FC[3] / (2.0 * BETA)
E1 = (FC[2] / 2.0 - E2) / BETA
E0 = (FC[1] / 2.0 - E1 - BETA * E2) / BETA
FK = (FC[0] - E0 - 2.0 * BETA * E1) * FS


def split(values):
    high = values.astype(ml_dtypes.bfloat16)
    low = (values - high.astype(np.float64)).astype(ml_dtypes.bfloat16)
    return high, low


def axial_tables(root, scale, band):
    n, w = NA, LANES
    index = np.arange(n)
    green = scale * (
        np.power(root, np.abs(index[:, None] - index[None, :]))
        - np.power(root, 2 * n - index[:, None] - index[None, :])
    )
    side = np.zeros((n, n))
    for shift, value in band.items():
        side += value * np.eye(n, k=shift)
    whole = green @ side
    left = np.zeros((AXIAL, w))
    right = np.zeros((AXIAL, w))
    for k in range(AXIAL):
        cols = slice(k * w, (k + 1) * w)
        lo, hi = max(0, k * w - 3), min(n, (k + 1) * w + 3)
        m = np.arange(lo, hi)
        left[k] = np.power(root, ((k + 1) * w - m).astype(np.float64)) @ side[lo:hi, cols]
        right[k] = (
            np.power(root, (m - k * w + 1).astype(np.float64))
            - np.power(root, (2 * n - m - k * w + 1).astype(np.float64))
        ) @ side[lo:hi, cols]
    t = np.arange(w)
    full = np.stack([whole[d * w : (d + 1) * w].T for d in range(AXIAL)]).astype(np.float32)
    own = np.zeros((AXIAL, w, 2 * w), ml_dtypes.bfloat16)
    sent = np.zeros((AXIAL, 2, 32, 2 * w), ml_dtypes.bfloat16)
    taken = np.zeros((AXIAL, 2, 64, 2 * w), ml_dtypes.bfloat16)
    for d in range(AXIAL):
        high, low = split(whole[d * w : (d + 1) * w, d * w : (d + 1) * w].T)
        own[d] = np.concatenate([high, low], axis=1)
        for half in range(2):
            rows = np.zeros((16, w))
            base = half * 4
            rows[base] = left[d]
            rows[base + 1, w - 1] = 1.0
            rows[base + 2, w - 2] = 1.0
            rows[8 + base] = right[d]
            rows[8 + base + 1, 0] = 1.0
            rows[8 + base + 2, 1] = 1.0
            high, low = split(rows)
            sent[d, half] = np.concatenate(
                [np.concatenate([high, high], axis=1), np.concatenate([low, low], axis=1)], axis=0
            )
            rows = np.zeros((32, w))
            for k in range(AXIAL):
                row = k * 8 + half * 4
                i = d * w + t
                if k < d:
                    rows[row] = scale * (
                        np.power(root, (i - (k + 1) * w).astype(np.float64))
                        - np.power(root, (2 * n - i - (k + 1) * w).astype(np.float64))
                    )
                    if k == d - 1:
                        for edge in range(2):
                            col = d * w - 1 - edge
                            for near in range(2 - edge):
                                rows[row + 1 + edge, near] = (
                                    whole[d * w + near, col] - rows[row, near] * left[k, col - k * w]
                                )
                if k > d:
                    rows[row] = scale * np.power(root, (k * w - 1 - i).astype(np.float64))
                    if k == d + 1:
                        for edge in range(2):
                            col = k * w + edge
                            for near in range(2 - edge):
                                rows[row + 1 + edge, w - 1 - near] = (
                                    whole[k * w - 1 - near, col] - rows[row, w - 1 - near] * right[k, edge]
                                )
            high, low = split(rows)
            pair = np.concatenate([high, low], axis=1)
            taken[d, half] = np.concatenate([pair, pair], axis=0)
    return own, sent, taken, full


def both_tables():
    deriv = axial_tables(DL, DS, {1: 7.0 / 9.0, -1: -7.0 / 9.0, 2: 1.0 / 36.0, -2: -1.0 / 36.0})
    band = {0: FC[0]}
    for shift in range(1, 4):
        band[shift] = band[-shift] = FC[shift] / 2.0
    smooth = axial_tables(FL, FS, band)
    return [np.stack(pair, axis=1) for pair in zip(deriv, smooth)]


def azimuth_rows():
    gap = np.arange(NAZ)
    slope = DK * (np.power(DL, gap) - np.power(DL, NAZ - gap)) / (1.0 - DL**NAZ)
    slope[0] = 0.0
    slope[1] += C1
    slope[-1] -= C1
    line = FK * (np.power(FL, gap) + np.power(FL, NAZ - gap)) / (1.0 - FL**NAZ)
    line[0] = FK * (1.0 + 2.0 * FL**NAZ / (1.0 - FL**NAZ)) + E0
    for shift, value in ((1, E1), (2, E2)):
        line[shift] += value
        line[-shift] += value
    rows = np.arange(ROWS)
    at = (gap[None, :] - rows[:, None]) % NAZ
    return np.stack([slope[at], line[at]]).astype(np.float32)


def two_terms(value):
    high = value.astype(BF16)
    low = (value - high.astype(F32)).astype(BF16)
    return high, low


def dot_last(left, right):
    return lax.dot_general(left, right, (((1,), (1,)), ((), ())), preferred_element_type=F32)


def dot_first(left, right):
    return lax.dot_general(left, right, (((0,), (0,)), ((), ())), preferred_element_type=F32)


def start_of(starts, group, field, side):
    return jnp.concatenate(
        [starts[4 * group + 2 * half + side, pl.ds(8 * field, 8)] for half in range(2)], axis=0
    )


def finish_kernel(
    lined_hbm, halo_hbm, start_hbm, signal_hbm, state_hbm, result_hbm, lined, halo, starts, final, load_sem, store_sem
):
    signal_copy = pltpu.make_async_copy(signal_hbm, result_hbm, store_sem.at[BLOCKS // 2])
    signal_copy.start()

    def loads(group):
        slots = pl.ds(pl.multiple_of(4 * group, 4), 4)
        planes = pl.ds(pl.multiple_of(16 * group, 16), 16)
        return [
            pltpu.make_async_copy(start_hbm.at[slots], starts.at[slots], load_sem.at[group, 0]),
            pltpu.make_async_copy(lined_hbm.at[:, :, planes], lined.at[:, :, planes], load_sem.at[group, 1]),
            pltpu.make_async_copy(halo_hbm.at[:, :, planes], halo.at[:, :, planes], load_sem.at[group, 2]),
        ]

    def store(group):
        planes = pl.ds(pl.multiple_of(group * 128, 128), 128)
        return pltpu.make_async_copy(final.at[:, planes], state_hbm.at[:, planes], store_sem.at[group])

    for group in range(BLOCKS // 2):
        for load in loads(group):
            load.start()

    def final_group(group, carry):
        for load in loads(group):
            load.wait()
        planes = pl.ds(pl.multiple_of(group * 16, 16), 16)
        for field in range(FIELDS):
            value = [halo[row, field, planes] for row in range(2)]
            value += [lined[row, field, planes] for row in range(ROWS)]
            value += [halo[2 + row, field, planes] for row in range(2)]
            up = [start_of(starts, group, field, 0)]
            for row in range(ROWS - 1):
                up.append(FL * (value[row + 2] + up[-1]))
            down = [start_of(starts, group, field, 1)]
            for row in range(ROWS - 1, 0, -1):
                down.append(FL * (value[row + 2] + down[-1]))
            down = down[::-1]
            for row in range(ROWS):
                near = E1 * (value[row + 1] + value[row + 3]) + E2 * (value[row] + value[row + 4])
                result = FK * (up[row] + down[row]) + (FK + E0) * value[row + 2] + near
                final[field, pl.ds(group * 128 + row, 16, stride=ROWS)] = result
        store(group).start()
        return carry

    lax.fori_loop(0, BLOCKS // 2, final_group, 0)
    for group in range(BLOCKS // 2):
        store(group).wait()
    signal_copy.wait()


def kernel(
    own_hbm,
    sent_hbm,
    taken_hbm,
    density_hbm,
    velocity_hbm,
    pressure_hbm,
    axial_hbm,
    azim_hbm,
    volume_hbm,
    radial_hbm,
    area_hbm,
    observer_hbm,
    bin_hbm,
    weight_hbm,
    table_hbm,
    azimuth_hbm,
    full_hbm,
    lined_hbm,
    filter_halo,
    start_hbm,
    signal_ref,
    own,
    sent,
    taken,
    density,
    velocity,
    pressure,
    axial_metric,
    azim_metric,
    volume,
    radial,
    area_ref,
    observer_ref,
    bin_ref,
    weight_ref,
    table_ref,
    azimuth_ref,
    full,
    azim_flux,
    base,
    ratio,
    cells,
    lined,
    edge_send,
    edge_recv,
    moment_send,
    moment_recv,
    start_send,
    start_recv,
    deriv_halo,
    observer_hot,
    bin_hot,
    partial,
    part_recv,
    owner_send,
    owner_recv,
    plane_send,
    plane_recv,
    axial_send,
    axial_recv,
    panel_axial,
    keep_sem,
    load_sem,
    early_sem,
    late_sem,
    edge_send_sem,
    edge_recv_sem,
    moment_send_sem,
    moment_recv_sem,
    start_send_sem,
    start_recv_sem,
    halo_send_sem,
    halo_recv_sem,
    part_send_sem,
    part_recv_sem,
    owner_send_sem,
    owner_recv_sem,
    plane_send_sem,
    plane_recv_sem,
    axial_send_sem,
    axial_recv_sem,
):
    me_a = lax.axis_index("axial")
    me_z = lax.axis_index("azim")
    core = lax.rem(me_z, 2)
    chip = me_z // 2
    twin = me_z + 1 - 2 * core
    after = lax.rem(me_z + 1, AZIM)
    before = lax.rem(me_z + AZIM - 1, AZIM)

    def early_loads(group):
        part = pl.ds(pl.multiple_of(group * 128, 128), 128)
        whole = slice(None)
        return [
            pltpu.make_async_copy(source.at[where], dest.at[where], early_sem.at[number, group])
            for number, (source, dest, where) in enumerate(
                (
                    (density_hbm, density, (part,)),
                    (velocity_hbm, velocity, (whole, part)),
                    (pressure_hbm, pressure, (part,)),
                    (volume_hbm, volume, (part,)),
                    (azim_hbm, azim_metric, (whole, part)),
                )
            )
        ]

    def late_loads(group):
        part = pl.ds(pl.multiple_of(group * 128, 128), 128)
        return [
            pltpu.make_async_copy(axial_hbm.at[:, part], axial_metric.at[:, part], late_sem.at[0, group]),
            pltpu.make_async_copy(radial_hbm.at[:, part], radial.at[:, part], late_sem.at[1, group]),
        ]

    loads = [
        pltpu.make_async_copy(area_hbm, area_ref, load_sem.at[0]),
        pltpu.make_async_copy(observer_hbm, observer_ref, load_sem.at[1]),
        pltpu.make_async_copy(bin_hbm, bin_ref, load_sem.at[2]),
        pltpu.make_async_copy(weight_hbm, weight_ref, load_sem.at[3]),
        pltpu.make_async_copy(table_hbm, table_ref, load_sem.at[4]),
        pltpu.make_async_copy(azimuth_hbm, azimuth_ref, load_sem.at[5]),
        pltpu.make_async_copy(full_hbm.at[me_a], full, load_sem.at[6]),
    ]
    for which in range(2):
        loads.append(
            pltpu.make_async_copy(
                own_hbm.at[me_a, which], own.at[which, pl.ds(0, LANES)], load_sem.at[7 + 4 * which]
            )
        )
        loads.append(
            pltpu.make_async_copy(
                own_hbm.at[me_a, which], own.at[which, pl.ds(LANES, LANES)], load_sem.at[8 + 4 * which]
            )
        )
        loads.append(pltpu.make_async_copy(sent_hbm.at[me_a, which], sent.at[which], load_sem.at[9 + 4 * which]))
        loads.append(pltpu.make_async_copy(taken_hbm.at[me_a, which], taken.at[which], load_sem.at[10 + 4 * which]))
    for group in range(BLOCKS // 2):
        for load in early_loads(group):
            load.start()
    for group in range(BLOCKS // 2):
        for load in late_loads(group):
            load.start()
    for load in loads:
        load.start()

    starts = (start_recv, start_hbm)
    barrier = pltpu.get_barrier_semaphore()

    def greet_azim(step, carry):
        other = lax.rem(me_z + step, AZIM)
        pl.semaphore_signal(barrier, inc=1, device_id=(me_a, other), device_id_type=MESH)
        return carry

    lax.fori_loop(1, AZIM, greet_azim, 0)

    def greet_axial(step, carry):
        other = lax.rem(me_a + step, AXIAL)
        pl.semaphore_signal(barrier, inc=1, device_id=(other, me_z), device_id_type=MESH)
        pl.semaphore_signal(barrier, inc=1, device_id=(other, twin), device_id_type=MESH)
        return carry

    lax.fori_loop(1, AXIAL, greet_axial, 0)

    edge_recv[0, pl.ds(me_a, 1)] = jnp.zeros((1, 8, HALF), F32)
    edge_recv[1, pl.ds(me_a, 1)] = jnp.zeros((1, 8, HALF), F32)


    def moment_copy(which, slot, share):
        return pltpu.make_async_remote_copy(
            src_ref=moment_send.at[which, slot, pl.ds(share * SHARE[0], SHARE[share])],
            dst_ref=moment_recv.at[which, me_z, pl.ds(0, SHARE[share])],
            send_sem=moment_send_sem.at[which],
            recv_sem=moment_recv_sem.at[which],
            device_id=(me_a, 2 * slot + share),
            device_id_type=MESH,
        )

    def send_moments(which):
        def to_chip(step, carry):
            slot = lax.rem(chip + step, SLOTS)
            for share in range(2):
                moment_copy(which, slot, share).start()
            return carry

        lax.fori_loop(1, SLOTS, to_chip, 0)
        for share in range(2):

            @pl.when(core == share)
            def _():
                moment_copy(which, chip, 1 - share).start()
                pltpu.make_async_copy(
                    moment_send.at[which, chip, pl.ds(share * SHARE[0], SHARE[share])],
                    moment_recv.at[which, me_z, pl.ds(0, SHARE[share])],
                    moment_recv_sem.at[which],
                ).start()

    def wait_moment_sends(which):
        for share in range(2):

            @pl.when(core == share)
            def _():
                part = moment_send.at[which, pl.ds(0, SLOTS - 1)]
                pltpu.make_async_copy(part, part, moment_send_sem.at[which]).wait()
                part = moment_send.at[which, SLOTS - 1, pl.ds(0, SHARE[1 - share])]
                pltpu.make_async_copy(part, part, moment_send_sem.at[which]).wait()

    def reduce_moments(which, root):
        factor = root**ROWS
        wrap = 1.0 / (1.0 - root**NAZ)
        side = lax.rem(chip, 2)

        def place(step):
            return step + side * (AZIM - 1 - 2 * step)

        for share in range(2):
            rows = pl.ds(0, SHARE[share])
            there = pl.ds(share * SHARE[0], SHARE[share])

            @pl.when(core == share)
            def _():
                part = moment_recv.at[which, :, rows]
                pltpu.make_async_copy(part, part, moment_recv_sem.at[which]).wait()

                def gather(step, total):
                    return factor * total + moment_recv[which, place(step), rows]

                first = lax.fori_loop(0, AZIM, gather, jnp.zeros((SHARE[share], LANES), F32), unroll=8) * wrap

                def follow(step, now):
                    other = place(step)
                    start_send[which, other, rows] = now
                    return factor * now + moment_recv[which, other, rows]

                lax.fori_loop(0, AZIM, follow, first, unroll=8)

                pltpu.make_async_copy(
                    start_send.at[which, me_z, rows], starts[which].at[chip, there], start_recv_sem.at[which]
                ).start()

                def hand_out(step, carry):
                    other = lax.rem(me_z + step, AZIM)
                    pltpu.make_async_remote_copy(
                        src_ref=start_send.at[which, other, rows],
                        dst_ref=starts[which].at[chip, there],
                        send_sem=start_send_sem.at[which],
                        recv_sem=start_recv_sem.at[which],
                        device_id=(me_a, other),
                        device_id_type=MESH,
                    ).start()
                    return carry

                lax.fori_loop(1, AZIM, hand_out, 0)

    def wait_starts(which):
        part = starts[which]
        pltpu.make_async_copy(part, part, start_recv_sem.at[which]).wait()

    def wait_start_sends(which):
        for share in range(2):

            @pl.when(core == share)
            def _():
                part = start_send.at[which, pl.ds(0, AZIM - 1), pl.ds(0, SHARE[share])]
                pltpu.make_async_copy(part, part, start_send_sem.at[which]).wait()

    def moments_of(values, root):
        up = root * values[0]
        for row in range(1, ROWS):
            up = root * (up + values[row])
        down = root * values[ROWS - 1]
        for row in range(ROWS - 2, -1, -1):
            down = root * (down + values[row])
        return up, down

    def keep_moments(which, group, field, values, root):
        up, down = moments_of(values, root)
        for half in range(2):
            for side, value in ((0, up), (1, down)):
                moment_send[which, 4 * group + 2 * half + side, pl.ds(8 * field, 8)] = value[8 * half : 8 * half + 8]

    def halo_copies(which, halo, source, depth):
        return (
            pltpu.make_async_remote_copy(
                src_ref=source.at[pl.ds(ROWS - depth, depth)],
                dst_ref=halo.at[0],
                send_sem=halo_send_sem.at[which, 0],
                recv_sem=halo_recv_sem.at[which, 0],
                device_id=(me_a, after),
                device_id_type=MESH,
            ),
            pltpu.make_async_remote_copy(
                src_ref=source.at[pl.ds(0, depth)],
                dst_ref=halo.at[1],
                send_sem=halo_send_sem.at[which, 1],
                recv_sem=halo_recv_sem.at[which, 1],
                device_id=(me_a, before),
                device_id_type=MESH,
            ),
        )

    def edge_copy(which, step):
        other = lax.rem(me_a + step, AXIAL)
        down = jnp.where(other < me_a, 1, 0)
        return pltpu.make_async_remote_copy(
            src_ref=edge_send.at[which, down],
            dst_ref=edge_recv.at[which, me_a],
            send_sem=edge_send_sem.at[which, step - 1],
            recv_sem=edge_recv_sem.at[which, step - 1],
            device_id=(other, me_z),
            device_id_type=MESH,
        )

    def send_edges(which):
        def piece(step, carry):
            at = pl.multiple_of(step * 640, 640)
            total = dot_last(sent[which, 0], cells[which, pl.ds(at, 640)]) + dot_last(
                sent[which, 1], cells[which, pl.ds(HALF + at, 640)]
            )
            total = total[:16] + total[16:]
            edge_send[which, 0, :, pl.ds(at, 640)] = total[:8]
            edge_send[which, 1, :, pl.ds(at, 640)] = total[8:]
            return carry

        lax.fori_loop(0, 2, piece, 0)
        for step in range(1, AXIAL):
            edge_copy(which, step).start()

    def own_part(which):
        def piece(row, carry):
            at = pl.multiple_of(row * SLAB, SLAB)
            total = jnp.dot(cells[which, pl.ds(at, SLAB)], own[which], preferred_element_type=F32)
            lined[row] = total[:, :LANES] + total[:, LANES:]
            return carry

        lax.fori_loop(0, ROWS, piece, 0)

    def add_edges(which):
        for step in range(1, AXIAL):
            edge_copy(which, step).wait_recv()

        def piece(step, carry):
            at = pl.multiple_of(lax.rem(step, 2) * 640, 640)
            received = edge_recv[which, :, :, pl.ds(at, 640)].reshape(32, 640)
            high, low = two_terms(received)
            total = dot_first(jnp.concatenate([high, low], axis=0), taken[which, step // 2])
            total = (total[:, :LANES] + total[:, LANES:]).reshape(2, SLAB, LANES)
            lined[pl.ds(2 * step, 2)] = lined[pl.ds(2 * step, 2)] + total
            return carry

        lax.fori_loop(0, 4, piece, 0)

    def wait_edge_sends(which):
        for step in range(1, AXIAL):
            edge_copy(which, step).wait_send()

    def keep_cells(which, row, field, group, value):
        high, low = two_terms(value)
        at = pl.multiple_of(row * SLAB + field * PLANES + group * 16, 16)
        cells[which, pl.ds(at, 16), pl.ds(0, LANES)] = high
        cells[which, pl.ds(at, 16), pl.ds(LANES, LANES)] = low

    def axial_copy(which, step):
        return pltpu.make_async_remote_copy(
            src_ref=axial_send.at[which],
            dst_ref=axial_recv.at[which, me_a],
            send_sem=axial_send_sem.at[which, step - 1],
            recv_sem=axial_recv_sem.at[which, step - 1],
            device_id=(lax.rem(me_a + step, AXIAL), me_z),
            device_id_type=MESH,
        )

    def send_axial(which, value):
        axial_send[which] = value
        axial_recv[which, pl.ds(me_a, 1)] = value[None]
        for step in range(1, AXIAL):
            axial_copy(which, step).start()

    def take_axial(which):
        for step in range(1, AXIAL):
            axial_copy(which, step).wait_recv()
        line = jnp.concatenate([axial_recv[which, k] for k in range(AXIAL)], axis=1)
        return jnp.dot(line, full[which], preferred_element_type=F32, precision=lax.Precision.HIGHEST)

    def send_plane(which, value):
        plane_send[which] = value
        plane_recv[which, 0] = value

        def piece(step, carry):
            pltpu.make_async_remote_copy(
                src_ref=plane_send.at[which],
                dst_ref=plane_recv.at[which, AZIM - step],
                send_sem=plane_send_sem.at[which],
                recv_sem=plane_recv_sem.at[which],
                device_id=(me_a, lax.rem(me_z + step, AZIM)),
                device_id_type=MESH,
            ).start()
            return carry

        lax.fori_loop(1, AZIM, piece, 0)

    def plane_wait(which, sem):
        part = plane_recv.at[which, pl.ds(1, AZIM - 1)]
        pltpu.make_async_copy(part, part, sem.at[which]).wait()

    def take_plane(which):
        plane_wait(which, plane_recv_sem)
        return jnp.dot(
            azimuth_ref[which],
            plane_recv[which].reshape(NAZ, LANES),
            preferred_element_type=F32,
            precision=lax.Precision.HIGHEST,
        )

    def flux_of(metric, at, rho, vel, prs, vol, heat):
        grad = [metric[comp, at] for comp in range(3)]
        contra = vol * (grad[0] * vel[0] + grad[1] * vel[1] + grad[2] * vel[2])
        flow = rho * contra
        push = vol * prs
        return [flow] + [flow * vel[comp] + grad[comp] * push for comp in range(3)] + [heat * contra]

    def cells_at(group, row):
        at = pl.ds(group * 128 + row, 16, stride=ROWS)
        rho, prs, vol = density[at], pressure[at], volume[at]
        vel = [velocity[comp, at] for comp in range(3)]
        energy = 2.5 * prs + 0.5 * rho * (vel[0] * vel[0] + vel[1] * vel[1] + vel[2] * vel[2])
        return at, rho, vel, prs, vol, energy

    def azim_group(group, carry):
        for load in early_loads(group):
            load.wait()
        flux = [[None] * ROWS for _ in range(FIELDS)]
        for row in range(ROWS):
            at, rho, vel, prs, vol, energy = cells_at(group, row)
            parts = flux_of(azim_metric, at, rho, vel, prs, vol, energy + prs)
            for field in range(FIELDS):
                flux[field][row] = parts[field]
                azim_flux[row, pl.ds(pl.multiple_of(field * PLANES + group * 16, 16), 16)] = parts[field]
        for field in range(FIELDS):
            keep_moments(0, group, field, flux[field], DL)
        return carry

    lax.fori_loop(0, BLOCKS // 2, azim_group, 0)
    pl.semaphore_wait(barrier, PEERS)
    send_moments(0)
    send_plane(0, azim_flux[:, 0] + azim_flux[:, 2 * PLANES])
    for copy in halo_copies(0, deriv_halo, azim_flux, 1):
        copy.start()

    def axial_group(group, carry):
        for load in late_loads(group):
            load.wait()
        for row in range(ROWS):
            at, rho, vel, prs, vol, energy = cells_at(group, row)
            state = [rho, rho * vel[0], rho * vel[1], rho * vel[2], energy]
            ratio[row, pl.ds(pl.multiple_of(group * 16, 16), 16)] = SECTION / vol
            for field in range(FIELDS):
                base[row, pl.ds(pl.multiple_of(field * PLANES + group * 16, 16), 16)] = (
                    state[field] + SECTION * radial[field, at]
                )
            parts = flux_of(axial_metric, at, rho, vel, prs, vol, energy + prs)
            for field in range(FIELDS):
                keep_cells(0, row, field, group, parts[field])
            panel_axial[group, pl.ds(row, 1)] = parts[0][:1] + parts[2][:1]
        return carry

    lax.fori_loop(0, BLOCKS // 2, axial_group, 0)
    send_axial(0, panel_axial[0])
    for load in loads:
        load.wait()
    send_edges(0)

    ids = observer_ref[...]
    order = (
        lax.shift_right_logical(ids, 7) * 128
        + (lax.shift_right_logical(ids, 2) & 1) * 64
        + (lax.shift_right_logical(ids, 3) & 15) * 4
        + (ids & 3)
    )
    partial[pl.ds(0, ENTRY_ROWS)] = order.astype(F32)

    def hot_row(row, carry):
        wanted = partial[pl.ds(row, 1)].astype(jnp.int32)
        rows = lax.broadcasted_iota(jnp.int32, (OBSERVERS, LANES), 0)
        at = pl.multiple_of(row * LANES, LANES)
        observer_hot[:, pl.ds(at, LANES)] = jnp.where(rows == wanted, 1.0, 0.0).astype(BF16)
        return carry

    lax.fori_loop(0, ENTRY_ROWS, hot_row, 0)

    own_part(0)
    reduce_moments(0, DL)
    change = take_axial(0) + take_plane(0)
    send_axial(1, base[:, 0] + base[:, 2 * PLANES] - ratio[:, 0] * change)
    add_edges(0)
    send_plane(1, take_axial(1))
    wait_starts(0)
    for copy in halo_copies(0, deriv_halo, azim_flux, 1):
        copy.wait_recv()

    def section_group(group, carry):
        for field in range(FIELDS):
            at = pl.ds(pl.multiple_of(field * PLANES + group * 16, 16), 16)
            here = pl.ds(pl.multiple_of(group * 16, 16), 16)
            flux = [deriv_halo[0, 0, at]] + [azim_flux[row, at] for row in range(ROWS)] + [deriv_halo[1, 0, at]]
            up = [start_of(start_recv, group, field, 0)]
            for row in range(ROWS - 1):
                up.append(DL * (flux[row + 1] + up[-1]))
            down = [start_of(start_recv, group, field, 1)]
            for row in range(ROWS - 1, 0, -1):
                down.append(DL * (flux[row + 1] + down[-1]))
            down = down[::-1]
            for row in range(ROWS):
                deriv = DK * (down[row] - up[row]) + C1 * (flux[row + 2] - flux[row])
                value = base[row, at] - ratio[row, here] * (lined[row, at] + deriv)
                keep_cells(1, row, field, group, value)
        return carry

    lax.fori_loop(0, BLOCKS // 2, section_group, 0)
    send_edges(1)
    own_part(1)
    add_edges(1)

    keep = pltpu.make_async_copy(lined, lined_hbm, keep_sem)
    keep.start()

    def moment_group(group, carry):
        for field in range(FIELDS):
            at = pl.ds(pl.multiple_of(field * PLANES + group * 16, 16), 16)
            keep_moments(1, group, field, [lined[row, at] for row in range(ROWS)], FL)
        return carry

    lax.fori_loop(0, BLOCKS // 2, moment_group, 0)
    send_moments(1)
    for copy in halo_copies(1, filter_halo, lined, 2):
        copy.start()
    source = area_ref[...] * (take_plane(1) - 1.0)
    picks = weight_ref[...]
    low_half = jnp.take_along_axis(
        jnp.broadcast_to(table_ref[pl.ds(0, 1)], (ENTRY_ROWS, LANES)), picks & 127, axis=1
    )
    high_half = jnp.take_along_axis(
        jnp.broadcast_to(table_ref[pl.ds(1, 1)], (ENTRY_ROWS, LANES)), picks & 127, axis=1
    )
    weights = jnp.where(picks < LANES, low_half, high_half)
    values = weights * jnp.concatenate([source] * 4, axis=0)
    high, low = two_terms(values)
    partial[pl.ds(0, ENTRY_ROWS)] = high.astype(F32)
    partial[pl.ds(ENTRY_ROWS, ENTRY_ROWS)] = low.astype(F32)

    def bin_row(row, carry):
        same = lax.broadcasted_iota(jnp.int32, (TIME_BINS, LANES), 0) == bin_ref[pl.ds(row, 1)]
        at = pl.multiple_of(row * LANES, LANES)
        bin_hot[pl.ds(0, TIME_BINS), pl.ds(at, LANES)] = jnp.where(same, partial[pl.ds(row, 1)], 0.0).astype(BF16)
        bin_hot[pl.ds(TIME_BINS, TIME_BINS), pl.ds(at, LANES)] = jnp.where(
            same, partial[pl.ds(ENTRY_ROWS + row, 1)], 0.0
        ).astype(BF16)
        return carry

    lax.fori_loop(0, ENTRY_ROWS, bin_row, 0)

    total = dot_last(observer_hot[...], bin_hot[...])
    partial[...] = total[:, :TIME_BINS] + total[:, TIME_BINS:]

    mine = me_a * 2 + core

    def part_copy(step):
        other = lax.rem(mine + step, 8)
        other_z = me_z - core + lax.rem(other, 2)
        return pltpu.make_async_remote_copy(
            src_ref=partial.at[pl.ds(pl.multiple_of(other * 64, 64), 64)],
            dst_ref=part_recv.at[step - 1],
            send_sem=part_send_sem.at[step - 1],
            recv_sem=part_recv_sem.at[step - 1],
            device_id=(other // 2, other_z),
            device_id_type=MESH,
        )

    for step in range(1, 8):
        part_copy(step).start()
    reduce_moments(1, FL)
    total = partial[pl.ds(pl.multiple_of(mine * 64, 64), 64)]
    for step in range(1, 8):
        part_copy(step).wait_recv()
        total = total + part_recv[step - 1]
    for owner in range(16):
        owner_send[owner, pl.ds(0, 4)] = total[4 * owner : 4 * owner + 4]
        owner_send[owner, pl.ds(4, 4)] = jnp.zeros((4, LANES), F32)

    def owner_copy(step):
        other = lax.rem(chip + step, 16)
        return pltpu.make_async_remote_copy(
            src_ref=owner_send.at[other],
            dst_ref=owner_recv.at[step - 1],
            send_sem=owner_send_sem.at[step - 1],
            recv_sem=owner_recv_sem.at[step - 1],
            device_id=(me_a, 2 * other + core),
            device_id_type=MESH,
        )

    for step in range(1, 16):
        owner_copy(step).start()
    wait_starts(1)
    for copy in halo_copies(1, filter_halo, lined, 2):
        copy.wait_recv()

    result = owner_send[chip]
    for step in range(1, 16):
        owner_copy(step).wait_recv()
        result = result + owner_recv[step - 1]
    signal_ref[...] = result[:4]
    keep.wait()

    for which, halo, source_ref, depth in ((0, deriv_halo, azim_flux, 1), (1, filter_halo, lined, 2)):
        wait_moment_sends(which)
        wait_start_sends(which)
        wait_edge_sends(which)
        for copy in halo_copies(which, halo, source_ref, depth):
            copy.wait_send()
    for step in range(1, 8):
        part_copy(step).wait_send()
    for step in range(1, 16):
        owner_copy(step).wait_send()
    for which in range(2):
        plane_wait(which, plane_send_sem)
        for step in range(1, AXIAL):
            axial_copy(which, step).wait_send()


def per_device(
    density,
    velocity,
    pressure,
    axial_metric,
    azim_metric,
    volume,
    radial_term,
    panel_area,
    observer_ids,
    bin_ids,
    weight_ids,
    bin_weights,
):
    own, sent, taken, full = both_tables()
    rows = PLANES * ROWS
    hbm = pl.BlockSpec(memory_space=pltpu.HBM)
    vmem = pl.BlockSpec(memory_space=pltpu.VMEM)
    dma = pltpu.SemaphoreType.DMA
    lined, halo, starts, partial_signals = pl.pallas_call(
        kernel,
        out_shape=(
            jax.ShapeDtypeStruct((ROWS, SLAB, LANES), F32),
            jax.ShapeDtypeStruct((2, 2, SLAB, LANES), F32),
            jax.ShapeDtypeStruct((SLOTS, TILE_ROWS, LANES), F32),
            jax.ShapeDtypeStruct((4, TIME_BINS), F32),
        ),
        in_specs=[hbm] * 17,
        out_specs=(hbm, hbm, hbm, vmem),
        scratch_shapes=[
            pltpu.VMEM((2, 2 * LANES, 2 * LANES), BF16),
            pltpu.VMEM((2, 2, 32, 2 * LANES), BF16),
            pltpu.VMEM((2, 2, 64, 2 * LANES), BF16),
            pltpu.VMEM((rows, LANES), F32),
            pltpu.VMEM((3, rows, LANES), F32),
            pltpu.VMEM((rows, LANES), F32),
            pltpu.VMEM((3, rows, LANES), F32),
            pltpu.VMEM((3, rows, LANES), F32),
            pltpu.VMEM((rows, LANES), F32),
            pltpu.VMEM((FIELDS, rows, LANES), F32),
            pltpu.VMEM((ROWS, LANES), F32),
            pltpu.VMEM((ENTRY_ROWS, LANES), jnp.int32),
            pltpu.VMEM((ENTRY_ROWS, LANES), jnp.int32),
            pltpu.VMEM((ENTRY_ROWS, LANES), jnp.int32),
            pltpu.VMEM((2, LANES), F32),
            pltpu.VMEM((2, ROWS, NAZ), F32),
            pltpu.VMEM((2, NA, LANES), F32),
            pltpu.VMEM((ROWS, SLAB, LANES), F32),
            pltpu.VMEM((ROWS, SLAB, LANES), F32),
            pltpu.VMEM((ROWS, PLANES, LANES), F32),
            pltpu.VMEM((2, LINES, 2 * LANES), BF16),
            pltpu.VMEM((ROWS, SLAB, LANES), F32),
            pltpu.VMEM((2, 2, 8, HALF), F32),
            pltpu.VMEM((2, AXIAL, 8, HALF), F32),
            pltpu.VMEM((2, SLOTS, TILE_ROWS, LANES), F32),
            pltpu.VMEM((2, AZIM, SHARE[0], LANES), F32),
            pltpu.VMEM((2, AZIM, SHARE[0], LANES), F32),
            pltpu.VMEM((SLOTS, TILE_ROWS, LANES), F32),
            pltpu.VMEM((2, 1, SLAB, LANES), F32),
            pltpu.VMEM((OBSERVERS, ENTRY_ROWS * LANES), BF16),
            pltpu.VMEM((2 * TIME_BINS, ENTRY_ROWS * LANES), BF16),
            pltpu.VMEM((OBSERVERS, TIME_BINS), F32),
            pltpu.VMEM((7, 64, TIME_BINS), F32),
            pltpu.VMEM((16, 8, TIME_BINS), F32),
            pltpu.VMEM((15, 8, TIME_BINS), F32),
            pltpu.VMEM((2, ROWS, LANES), F32),
            pltpu.VMEM((2, AZIM, ROWS, LANES), F32),
            pltpu.VMEM((2, ROWS, LANES), F32),
            pltpu.VMEM((2, AXIAL, ROWS, LANES), F32),
            pltpu.VMEM((BLOCKS // 2, ROWS, LANES), F32),
            dma(()),
            dma((15,)),
            dma((5, BLOCKS // 2)),
            dma((2, BLOCKS // 2)),
            dma((2, 3)),
            dma((2, 3)),
            dma((2,)),
            dma((2,)),
            dma((2,)),
            dma((2,)),
            dma((2, 2)),
            dma((2, 2)),
            dma((7,)),
            dma((7,)),
            dma((15,)),
            dma((15,)),
            dma((2,)),
            dma((2,)),
            dma((2, 3)),
            dma((2, 3)),
        ],
        compiler_params=pltpu.CompilerParams(
            collective_id=0, has_side_effects=True
        ),
    )(
        jnp.asarray(own),
        jnp.asarray(sent),
        jnp.asarray(taken),
        density.reshape(rows, LANES),
        velocity.reshape(3, rows, LANES),
        pressure.reshape(rows, LANES),
        axial_metric.reshape(3, rows, LANES),
        azim_metric.reshape(3, rows, LANES),
        volume.reshape(rows, LANES),
        radial_term.reshape(FIELDS, rows, LANES),
        panel_area,
        observer_ids.reshape(ENTRY_ROWS, LANES),
        bin_ids.reshape(ENTRY_ROWS, LANES),
        weight_ids.reshape(ENTRY_ROWS, LANES),
        bin_weights.reshape(2, LANES),
        jnp.asarray(azimuth_rows()),
        jnp.asarray(full),
    )
    state, signals = pl.pallas_call(
        finish_kernel,
        out_shape=(
            jax.ShapeDtypeStruct((FIELDS, rows, LANES), F32),
            jax.ShapeDtypeStruct((4, TIME_BINS), F32),
        ),
        in_specs=[hbm] * 4,
        out_specs=(hbm, hbm),
        scratch_shapes=[
            pltpu.VMEM((ROWS, FIELDS, PLANES, LANES), F32),
            pltpu.VMEM((4, FIELDS, PLANES, LANES), F32),
            pltpu.VMEM((SLOTS, TILE_ROWS, LANES), F32),
            pltpu.VMEM((FIELDS, rows, LANES), F32),
            dma((BLOCKS // 2, 3)),
            dma((BLOCKS // 2 + 1,)),
        ],
    )(
        lined.reshape(ROWS, FIELDS, PLANES, LANES),
        halo.reshape(4, FIELDS, PLANES, LANES),
        starts,
        partial_signals,
    )
    return state.reshape(FIELDS, PLANES, ROWS, LANES), signals


def solution(mesh):
    placed = (
        P(None, "azim", "axial"),
        P(None, None, "azim", "axial"),
        P(None, "azim", "axial"),
        P(None, None, "azim", "axial"),
        P(None, None, "azim", "axial"),
        P(None, "azim", "axial"),
        P(None, None, "azim", "axial"),
        P("azim", "axial"),
        P(None, "azim", "axial"),
        P(None, "azim", "axial"),
        P(None, "azim", "axial"),
        P(),
    )
    return jax.shard_map(
        per_device,
        mesh=mesh,
        in_specs=placed,
        out_specs=(P(None, None, "azim", "axial"), P(("axial", "azim"), None)),
        check_vma=False,
    )
```

```python
import functools
import math

import jax
import jax.numpy as jnp
import ml_dtypes
import numpy as np
from jax import lax
from jax.experimental import pallas as pl
from jax.experimental.pallas import tpu as pltpu
from jax.sharding import PartitionSpec as P

F32 = jnp.float32
BF16 = jnp.bfloat16
MESH = pl.DeviceIdType.MESH

PLANES = 64
FIELDS = 5
ROWS = 8
LANES = 128
AXIAL = 4
AZIM = 32
NA = AXIAL * LANES
NAZ = AZIM * ROWS
SLAB = FIELDS * PLANES
LINES = ROWS * SLAB
BLOCKS = PLANES // 8
SLOTS = 2 * BLOCKS
TILE_ROWS = 8 * FIELDS
SHARE = (24, 16)
STEPS = (2, 1, 3, 0)
AWAY = tuple((dz, dy) for dz in STEPS[:3] for dy in STEPS[:3]) + ((2, 0), (0, 2), (1, 0), (3, 0), (0, 1), (0, 3))
HALF = LINES // 2
ENTRY_ROWS = 32
OBSERVERS = 512
TIME_BINS = 128
PEERS = (AZIM - 1) + 2 * (AXIAL - 1)

SECTION = 0.25
DERIV_ALPHA = 1.0 / 3.0
BETA = 0.499


def decay_root(alpha):
    return (-1.0 + math.sqrt(1.0 - 4.0 * alpha * alpha)) / (2.0 * alpha)


DL = decay_root(DERIV_ALPHA)
FL = decay_root(BETA)
C1 = (1.0 / 36.0) / DERIV_ALPHA
DS = 1.0 / math.sqrt(1.0 - 4.0 * DERIV_ALPHA**2)
DK = (7.0 / 9.0 - C1) * DS * (1.0 / DL - DL)
FC = [
    (11.0 + 10.0 * BETA) / 16.0,
    (15.0 + 34.0 * BETA) / 32.0,
    (-3.0 + 6.0 * BETA) / 16.0,
    (1.0 - 2.0 * BETA) / 32.0,
]
FS = 1.0 / math.sqrt(1.0 - 4.0 * BETA**2)
E2 = FC[3] / (2.0 * BETA)
E1 = (FC[2] / 2.0 - E2) / BETA
E0 = (FC[1] / 2.0 - E1 - BETA * E2) / BETA
FK = (FC[0] - E0 - 2.0 * BETA * E1) * FS


def split(values):
    high = values.astype(ml_dtypes.bfloat16)
    low = (values - high.astype(np.float64)).astype(ml_dtypes.bfloat16)
    return high, low


def axial_tables(root, scale, band):
    n, w = NA, LANES
    index = np.arange(n)
    green = scale * (
        np.power(root, np.abs(index[:, None] - index[None, :]))
        - np.power(root, 2 * n - index[:, None] - index[None, :])
    )
    side = np.zeros((n, n))
    for shift, value in band.items():
        side += value * np.eye(n, k=shift)
    whole = green @ side
    left = np.zeros((AXIAL, w))
    right = np.zeros((AXIAL, w))
    for k in range(AXIAL):
        cols = slice(k * w, (k + 1) * w)
        lo, hi = max(0, k * w - 3), min(n, (k + 1) * w + 3)
        m = np.arange(lo, hi)
        left[k] = np.power(root, ((k + 1) * w - m).astype(np.float64)) @ side[lo:hi, cols]
        right[k] = (
            np.power(root, (m - k * w + 1).astype(np.float64))
            - np.power(root, (2 * n - m - k * w + 1).astype(np.float64))
        ) @ side[lo:hi, cols]
    t = np.arange(w)
    full = np.stack([whole[d * w : (d + 1) * w].T for d in range(AXIAL)]).astype(np.float32)
    own = np.zeros((AXIAL, w, 2 * w), ml_dtypes.bfloat16)
    sent = np.zeros((AXIAL, 2, 32, 2 * w), ml_dtypes.bfloat16)
    taken = np.zeros((AXIAL, 2, 64, 2 * w), ml_dtypes.bfloat16)
    for d in range(AXIAL):
        high, low = split(whole[d * w : (d + 1) * w, d * w : (d + 1) * w].T)
        own[d] = np.concatenate([high, low], axis=1)
        for half in range(2):
            rows = np.zeros((16, w))
            base = half * 4
            rows[base] = left[d]
            rows[base + 1, w - 1] = 1.0
            rows[base + 2, w - 2] = 1.0
            rows[8 + base] = right[d]
            rows[8 + base + 1, 0] = 1.0
            rows[8 + base + 2, 1] = 1.0
            high, low = split(rows)
            sent[d, half] = np.concatenate(
                [np.concatenate([high, high], axis=1), np.concatenate([low, low], axis=1)], axis=0
            )
            rows = np.zeros((32, w))
            for k in range(AXIAL):
                row = k * 8 + half * 4
                i = d * w + t
                if k < d:
                    rows[row] = scale * (
                        np.power(root, (i - (k + 1) * w).astype(np.float64))
                        - np.power(root, (2 * n - i - (k + 1) * w).astype(np.float64))
                    )
                    if k == d - 1:
                        for edge in range(2):
                            col = d * w - 1 - edge
                            for near in range(2 - edge):
                                rows[row + 1 + edge, near] = (
                                    whole[d * w + near, col] - rows[row, near] * left[k, col - k * w]
                                )
                if k > d:
                    rows[row] = scale * np.power(root, (k * w - 1 - i).astype(np.float64))
                    if k == d + 1:
                        for edge in range(2):
                            col = k * w + edge
                            for near in range(2 - edge):
                                rows[row + 1 + edge, w - 1 - near] = (
                                    whole[k * w - 1 - near, col] - rows[row, w - 1 - near] * right[k, edge]
                                )
            high, low = split(rows)
            pair = np.concatenate([high, low], axis=1)
            taken[d, half] = np.concatenate([pair, pair], axis=0)
    return own, sent, taken, full


def both_tables():
    deriv = axial_tables(DL, DS, {1: 7.0 / 9.0, -1: -7.0 / 9.0, 2: 1.0 / 36.0, -2: -1.0 / 36.0})
    band = {0: FC[0]}
    for shift in range(1, 4):
        band[shift] = band[-shift] = FC[shift] / 2.0
    smooth = axial_tables(FL, FS, band)
    return [np.stack(pair, axis=1) for pair in zip(deriv, smooth)]


def azimuth_rows():
    gap = np.arange(NAZ)
    slope = DK * (np.power(DL, gap) - np.power(DL, NAZ - gap)) / (1.0 - DL**NAZ)
    slope[0] = 0.0
    slope[1] += C1
    slope[-1] -= C1
    line = FK * (np.power(FL, gap) + np.power(FL, NAZ - gap)) / (1.0 - FL**NAZ)
    line[0] = FK * (1.0 + 2.0 * FL**NAZ / (1.0 - FL**NAZ)) + E0
    for shift, value in ((1, E1), (2, E2)):
        line[shift] += value
        line[-shift] += value
    rows = np.arange(ROWS)
    at = (gap[None, :] - rows[:, None]) % NAZ
    return np.stack([slope[at], line[at]]).astype(np.float32)


def two_terms(value):
    high = value.astype(BF16)
    low = (value - high.astype(F32)).astype(BF16)
    return high, low


def dot_last(left, right):
    return lax.dot_general(left, right, (((1,), (1,)), ((), ())), preferred_element_type=F32)


def dot_first(left, right):
    return lax.dot_general(left, right, (((0,), (0,)), ((), ())), preferred_element_type=F32)


def start_of(starts, group, field, side):
    return jnp.concatenate(
        [starts[4 * group + 2 * half + side, pl.ds(8 * field, 8)] for half in range(2)], axis=0
    )


def finish_kernel(
    lined_hbm,
    halo_hbm,
    start_hbm,
    part_hbm,
    state_hbm,
    signal_hbm,
    lined,
    halo,
    starts,
    final,
    parts,
    signals,
    load_sem,
    store_sem,
    part_sem,
):
    part_copy = pltpu.make_async_copy(part_hbm, parts, part_sem.at[0])
    signal_copy = pltpu.make_async_copy(signals, signal_hbm, part_sem.at[1])

    def loads(group):
        slots = pl.ds(pl.multiple_of(4 * group, 4), 4)
        planes = pl.ds(pl.multiple_of(16 * group, 16), 16)
        return [
            pltpu.make_async_copy(start_hbm.at[slots], starts.at[slots], load_sem.at[group, 0]),
            pltpu.make_async_copy(lined_hbm.at[:, :, planes], lined.at[:, :, planes], load_sem.at[group, 1]),
            pltpu.make_async_copy(halo_hbm.at[:, :, planes], halo.at[:, :, planes], load_sem.at[group, 2]),
        ]

    def store(group):
        planes = pl.ds(pl.multiple_of(group * 128, 128), 128)
        return pltpu.make_async_copy(final.at[:, planes], state_hbm.at[:, planes], store_sem.at[group])

    for group in range(BLOCKS // 2):
        for load in loads(group):
            load.start()
        if group == 0:
            part_copy.start()

    def final_group(group, carry):
        for load in loads(group):
            load.wait()
        planes = pl.ds(pl.multiple_of(group * 16, 16), 16)
        for field in range(FIELDS):
            value = [halo[row, field, planes] for row in range(2)]
            value += [lined[row, field, planes] for row in range(ROWS)]
            value += [halo[2 + row, field, planes] for row in range(2)]
            up = [start_of(starts, group, field, 0)]
            for row in range(ROWS - 1):
                up.append(FL * (value[row + 2] + up[-1]))
            down = [start_of(starts, group, field, 1)]
            for row in range(ROWS - 1, 0, -1):
                down.append(FL * (value[row + 2] + down[-1]))
            down = down[::-1]
            for row in range(ROWS):
                near = E1 * (value[row + 1] + value[row + 3]) + E2 * (value[row] + value[row + 4])
                result = FK * (up[row] + down[row]) + (FK + E0) * value[row + 2] + near
                final[field, pl.ds(group * 128 + row, 16, stride=ROWS)] = result
        store(group).start()
        return carry

    final_group(0, 0)
    part_copy.wait()
    signals[...] = jnp.sum(parts[...], axis=0)[:4]
    signal_copy.start()
    lax.fori_loop(1, BLOCKS // 2, final_group, 0)
    for group in range(BLOCKS // 2):
        store(group).wait()
    signal_copy.wait()


def kernel(
    own_hbm,
    sent_hbm,
    taken_hbm,
    density_hbm,
    velocity_hbm,
    pressure_hbm,
    axial_hbm,
    azim_hbm,
    volume_hbm,
    radial_hbm,
    area_hbm,
    observer_hbm,
    bin_hbm,
    weight_hbm,
    table_hbm,
    azimuth_hbm,
    full_hbm,
    lined_hbm,
    filter_halo,
    start_hbm,
    owner_hbm,
    own,
    sent,
    taken,
    density,
    velocity,
    pressure,
    axial_metric,
    azim_metric,
    volume,
    radial,
    area_ref,
    observer_ref,
    bin_ref,
    weight_ref,
    table_ref,
    azimuth_ref,
    full,
    azim_flux,
    base,
    ratio,
    cells,
    lined,
    edge_send,
    edge_recv,
    moment_send,
    moment_recv,
    start_send,
    start_recv,
    deriv_halo,
    observer_hot,
    bin_hot,
    partial,
    part_recv,
    owner_send,
    plane_send,
    plane_recv,
    axial_send,
    axial_recv,
    panel_axial,
    keep_sem,
    owner_sem,
    load_sem,
    early_sem,
    late_sem,
    edge_send_sem,
    edge_recv_sem,
    moment_send_sem,
    moment_recv_sem,
    start_send_sem,
    start_recv_sem,
    halo_send_sem,
    halo_recv_sem,
    part_send_sem,
    part_recv_sem,
    owner_send_sem,
    owner_recv_sem,
    plane_send_sem,
    plane_recv_sem,
    axial_send_sem,
    axial_recv_sem,
):
    me_a = lax.axis_index("axial")
    me_z = lax.axis_index("azim")
    core = lax.rem(me_z, 2)
    chip = me_z // 2
    twin = me_z + 1 - 2 * core
    after = lax.rem(me_z + 1, AZIM)
    before = lax.rem(me_z + AZIM - 1, AZIM)

    def chip_at(step):
        return 4 * lax.rem(chip // 4 + step[0], 4) + lax.rem(chip + step[1], 4)

    def group_at(step):
        away = jnp.where(step == 0, STEPS[0], jnp.where(step == 1, STEPS[1], jnp.where(step == 2, STEPS[2], 0)))
        return lax.rem(chip // 4 + away, 4)

    def early_loads(group):
        part = pl.ds(pl.multiple_of(group * 128, 128), 128)
        whole = slice(None)
        return [
            pltpu.make_async_copy(source.at[where], dest.at[where], early_sem.at[number, group])
            for number, (source, dest, where) in enumerate(
                (
                    (density_hbm, density, (part,)),
                    (velocity_hbm, velocity, (whole, part)),
                    (pressure_hbm, pressure, (part,)),
                    (volume_hbm, volume, (part,)),
                    (azim_hbm, azim_metric, (whole, part)),
                )
            )
        ]

    def late_loads(group):
        part = pl.ds(pl.multiple_of(group * 128, 128), 128)
        return [
            pltpu.make_async_copy(axial_hbm.at[:, part], axial_metric.at[:, part], late_sem.at[0, group]),
            pltpu.make_async_copy(radial_hbm.at[:, part], radial.at[:, part], late_sem.at[1, group]),
        ]

    loads = [
        pltpu.make_async_copy(area_hbm, area_ref, load_sem.at[0]),
        pltpu.make_async_copy(observer_hbm, observer_ref, load_sem.at[1]),
        pltpu.make_async_copy(bin_hbm, bin_ref, load_sem.at[2]),
        pltpu.make_async_copy(weight_hbm, weight_ref, load_sem.at[3]),
        pltpu.make_async_copy(table_hbm, table_ref, load_sem.at[4]),
        pltpu.make_async_copy(azimuth_hbm, azimuth_ref, load_sem.at[5]),
        pltpu.make_async_copy(full_hbm.at[me_a], full, load_sem.at[6]),
    ]
    for which in range(2):
        loads.append(
            pltpu.make_async_copy(
                own_hbm.at[me_a, which], own.at[which, pl.ds(0, LANES)], load_sem.at[7 + 4 * which]
            )
        )
        loads.append(
            pltpu.make_async_copy(
                own_hbm.at[me_a, which], own.at[which, pl.ds(LANES, LANES)], load_sem.at[8 + 4 * which]
            )
        )
        loads.append(pltpu.make_async_copy(sent_hbm.at[me_a, which], sent.at[which], load_sem.at[9 + 4 * which]))
        loads.append(pltpu.make_async_copy(taken_hbm.at[me_a, which], taken.at[which], load_sem.at[10 + 4 * which]))
    for step in range(BLOCKS // 2):
        for load in early_loads(group_at(step)):
            load.start()
    for group in range(BLOCKS // 2):
        for load in late_loads(group):
            load.start()
    for load in loads:
        load.start()

    starts = (start_recv, start_hbm)

    barrier = pltpu.get_barrier_semaphore()

    def greet_azim(step, carry):
        other = lax.rem(me_z + step, AZIM)
        pl.semaphore_signal(barrier, inc=1, device_id=(me_a, other), device_id_type=MESH)
        return carry

    lax.fori_loop(1, AZIM, greet_azim, 0)

    def greet_axial(step, carry):
        other = lax.rem(me_a + step, AXIAL)
        pl.semaphore_signal(barrier, inc=1, device_id=(other, me_z), device_id_type=MESH)
        pl.semaphore_signal(barrier, inc=1, device_id=(other, twin), device_id_type=MESH)
        return carry

    lax.fori_loop(1, AXIAL, greet_axial, 0)

    edge_recv[0, pl.ds(me_a, 1)] = jnp.zeros((1, 8, HALF), F32)
    edge_recv[1, pl.ds(me_a, 1)] = jnp.zeros((1, 8, HALF), F32)


    def moment_copy(which, slot, share):
        return pltpu.make_async_remote_copy(
            src_ref=moment_send.at[which, slot, pl.ds(share * SHARE[0], SHARE[share])],
            dst_ref=moment_recv.at[which, me_z, pl.ds(0, SHARE[share])],
            send_sem=moment_send_sem.at[which],
            recv_sem=moment_recv_sem.at[which],
            device_id=(me_a, 2 * slot + share),
            device_id_type=MESH,
        )

    def send_moments(which, step):
        row = 4 * group_at(step)
        for turn in STEPS[:3]:
            for share in range(2):
                moment_copy(which, row + lax.rem(chip + turn, 4), share).start()

        @pl.when(step < 3)
        def _():
            for share in range(2):
                moment_copy(which, row + lax.rem(chip, 4), share).start()

        for share in range(2):

            @pl.when(jnp.logical_and(step == 3, core == share))
            def _():
                moment_copy(which, chip, 1 - share).start()
                pltpu.make_async_copy(
                    moment_send.at[which, chip, pl.ds(share * SHARE[0], SHARE[share])],
                    moment_recv.at[which, me_z, pl.ds(0, SHARE[share])],
                    moment_recv_sem.at[which],
                ).start()

    def wait_moment_sends(which):
        for share in range(2):

            @pl.when(core == share)
            def _():
                part = moment_send.at[which, pl.ds(0, SLOTS - 1)]
                pltpu.make_async_copy(part, part, moment_send_sem.at[which]).wait()
                part = moment_send.at[which, SLOTS - 1, pl.ds(0, SHARE[1 - share])]
                pltpu.make_async_copy(part, part, moment_send_sem.at[which]).wait()

    def reduce_moments(which, root):
        factor = root**ROWS
        wrap = 1.0 / (1.0 - root**NAZ)
        side = lax.rem(chip, 2)

        def place(step):
            return step + side * (AZIM - 1 - 2 * step)

        for share in range(2):
            rows = pl.ds(0, SHARE[share])
            there = pl.ds(share * SHARE[0], SHARE[share])

            @pl.when(core == share)
            def _():
                part = moment_recv.at[which, :, rows]
                pltpu.make_async_copy(part, part, moment_recv_sem.at[which]).wait()

                def gather(step, total):
                    return factor * total + moment_recv[which, place(step), rows]

                first = lax.fori_loop(0, AZIM, gather, jnp.zeros((SHARE[share], LANES), F32), unroll=8) * wrap

                def follow(step, now):
                    other = place(step)
                    start_send[which, other, rows] = now
                    return factor * now + moment_recv[which, other, rows]

                lax.fori_loop(0, AZIM, follow, first, unroll=8)

                pltpu.make_async_copy(
                    start_send.at[which, me_z, rows], starts[which].at[chip, there], start_recv_sem.at[which]
                ).start()

                def hand_out(other):
                    pltpu.make_async_remote_copy(
                        src_ref=start_send.at[which, other, rows],
                        dst_ref=starts[which].at[chip, there],
                        send_sem=start_send_sem.at[which],
                        recv_sem=start_recv_sem.at[which],
                        device_id=(me_a, other),
                        device_id_type=MESH,
                    ).start()

                for step in AWAY:
                    for half in range(2):
                        hand_out(2 * chip_at(step) + half)
                hand_out(twin)

    def wait_starts(which):
        part = starts[which]
        pltpu.make_async_copy(part, part, start_recv_sem.at[which]).wait()

    def wait_start_sends(which):
        for share in range(2):

            @pl.when(core == share)
            def _():
                part = start_send.at[which, pl.ds(0, AZIM - 1), pl.ds(0, SHARE[share])]
                pltpu.make_async_copy(part, part, start_send_sem.at[which]).wait()

    def moments_of(values, root):
        up = root * values[0]
        for row in range(1, ROWS):
            up = root * (up + values[row])
        down = root * values[ROWS - 1]
        for row in range(ROWS - 2, -1, -1):
            down = root * (down + values[row])
        return up, down

    def keep_moments(which, group, field, values, root):
        up, down = moments_of(values, root)
        for half in range(2):
            for side, value in ((0, up), (1, down)):
                moment_send[which, 4 * group + 2 * half + side, pl.ds(8 * field, 8)] = value[8 * half : 8 * half + 8]

    def halo_copies(which, halo, source, depth):
        return (
            pltpu.make_async_remote_copy(
                src_ref=source.at[pl.ds(ROWS - depth, depth)],
                dst_ref=halo.at[0],
                send_sem=halo_send_sem.at[which, 0],
                recv_sem=halo_recv_sem.at[which, 0],
                device_id=(me_a, after),
                device_id_type=MESH,
            ),
            pltpu.make_async_remote_copy(
                src_ref=source.at[pl.ds(0, depth)],
                dst_ref=halo.at[1],
                send_sem=halo_send_sem.at[which, 1],
                recv_sem=halo_recv_sem.at[which, 1],
                device_id=(me_a, before),
                device_id_type=MESH,
            ),
        )

    def edge_copy(which, step):
        other = lax.rem(me_a + step, AXIAL)
        down = jnp.where(other < me_a, 1, 0)
        return pltpu.make_async_remote_copy(
            src_ref=edge_send.at[which, down],
            dst_ref=edge_recv.at[which, me_a],
            send_sem=edge_send_sem.at[which, step - 1],
            recv_sem=edge_recv_sem.at[which, step - 1],
            device_id=(other, me_z),
            device_id_type=MESH,
        )

    def send_edges(which):
        def piece(step, carry):
            at = pl.multiple_of(step * 640, 640)
            total = dot_last(sent[which, 0], cells[which, pl.ds(at, 640)]) + dot_last(
                sent[which, 1], cells[which, pl.ds(HALF + at, 640)]
            )
            total = total[:16] + total[16:]
            edge_send[which, 0, :, pl.ds(at, 640)] = total[:8]
            edge_send[which, 1, :, pl.ds(at, 640)] = total[8:]
            return carry

        lax.fori_loop(0, 2, piece, 0)
        for step in STEPS[:3]:
            edge_copy(which, step).start()

    def own_part(which):
        def piece(row, carry):
            at = pl.multiple_of(row * SLAB, SLAB)
            total = jnp.dot(cells[which, pl.ds(at, SLAB)], own[which], preferred_element_type=F32)
            lined[row] = total[:, :LANES] + total[:, LANES:]
            return carry

        lax.fori_loop(0, ROWS, piece, 0)

    def add_edges(which):
        for step in range(1, AXIAL):
            edge_copy(which, step).wait_recv()

        def piece(step, carry):
            at = pl.multiple_of(lax.rem(step, 2) * 640, 640)
            received = edge_recv[which, :, :, pl.ds(at, 640)].reshape(32, 640)
            high, low = two_terms(received)
            total = dot_first(jnp.concatenate([high, low], axis=0), taken[which, step // 2])
            total = (total[:, :LANES] + total[:, LANES:]).reshape(2, SLAB, LANES)
            lined[pl.ds(2 * step, 2)] = lined[pl.ds(2 * step, 2)] + total
            return carry

        lax.fori_loop(0, 4, piece, 0)

    def wait_edge_sends(which):
        for step in range(1, AXIAL):
            edge_copy(which, step).wait_send()

    def keep_cells(which, row, field, group, value):
        high, low = two_terms(value)
        at = pl.multiple_of(row * SLAB + field * PLANES + group * 16, 16)
        cells[which, pl.ds(at, 16), pl.ds(0, LANES)] = high
        cells[which, pl.ds(at, 16), pl.ds(LANES, LANES)] = low

    def axial_copy(which, step):
        return pltpu.make_async_remote_copy(
            src_ref=axial_send.at[which],
            dst_ref=axial_recv.at[which, me_a],
            send_sem=axial_send_sem.at[which, step - 1],
            recv_sem=axial_recv_sem.at[which, step - 1],
            device_id=(lax.rem(me_a + step, AXIAL), me_z),
            device_id_type=MESH,
        )

    def send_axial(which, value):
        axial_send[which] = value
        axial_recv[which, pl.ds(me_a, 1)] = value[None]
        for step in STEPS[:3]:
            axial_copy(which, step).start()

    def take_axial(which):
        for step in range(1, AXIAL):
            axial_copy(which, step).wait_recv()
        line = jnp.concatenate([axial_recv[which, k] for k in range(AXIAL)], axis=1)
        return jnp.dot(line, full[which], preferred_element_type=F32, precision=lax.Precision.HIGHEST)

    def send_plane(which, value):
        plane_send[which] = value
        plane_recv[which, 0] = value

        def piece(other):
            pltpu.make_async_remote_copy(
                src_ref=plane_send.at[which],
                dst_ref=plane_recv.at[which, lax.rem(me_z - other + AZIM, AZIM)],
                send_sem=plane_send_sem.at[which],
                recv_sem=plane_recv_sem.at[which],
                device_id=(me_a, other),
                device_id_type=MESH,
            ).start()

        for step in AWAY:
            for half in range(2):
                piece(2 * chip_at(step) + half)
        piece(twin)

    def plane_wait(which, sem):
        part = plane_recv.at[which, pl.ds(1, AZIM - 1)]
        pltpu.make_async_copy(part, part, sem.at[which]).wait()

    def take_plane(which):
        plane_wait(which, plane_recv_sem)
        return jnp.dot(
            azimuth_ref[which],
            plane_recv[which].reshape(NAZ, LANES),
            preferred_element_type=F32,
            precision=lax.Precision.HIGHEST,
        )

    def flux_of(metric, at, rho, vel, prs, vol, heat):
        grad = [metric[comp, at] for comp in range(3)]
        contra = vol * (grad[0] * vel[0] + grad[1] * vel[1] + grad[2] * vel[2])
        flow = rho * contra
        push = vol * prs
        return [flow] + [flow * vel[comp] + grad[comp] * push for comp in range(3)] + [heat * contra]

    def cells_at(group, row):
        at = pl.ds(group * 128 + row, 16, stride=ROWS)
        rho, prs, vol = density[at], pressure[at], volume[at]
        vel = [velocity[comp, at] for comp in range(3)]
        energy = 2.5 * prs + 0.5 * rho * (vel[0] * vel[0] + vel[1] * vel[1] + vel[2] * vel[2])
        return at, rho, vel, prs, vol, energy

    def azim_group(step, carry):
        group = group_at(step)
        for load in early_loads(group):
            load.wait()
        flux = [[None] * ROWS for _ in range(FIELDS)]
        for row in range(ROWS):
            at, rho, vel, prs, vol, energy = cells_at(group, row)
            parts = flux_of(azim_metric, at, rho, vel, prs, vol, energy + prs)
            for field in range(FIELDS):
                flux[field][row] = parts[field]
                azim_flux[row, pl.ds(pl.multiple_of(field * PLANES + group * 16, 16), 16)] = parts[field]
        for field in range(FIELDS):
            keep_moments(0, group, field, flux[field], DL)

        @pl.when(step == 0)
        def _():
            pl.semaphore_wait(barrier, PEERS)

        send_moments(0, step)
        return carry

    lax.fori_loop(0, BLOCKS // 2, azim_group, 0)
    send_plane(0, azim_flux[:, 0] + azim_flux[:, 2 * PLANES])
    for copy in halo_copies(0, deriv_halo, azim_flux, 1):
        copy.start()

    def axial_group(group, carry):
        for load in late_loads(group):
            load.wait()
        for row in range(ROWS):
            at, rho, vel, prs, vol, energy = cells_at(group, row)
            state = [rho, rho * vel[0], rho * vel[1], rho * vel[2], energy]
            ratio[row, pl.ds(pl.multiple_of(group * 16, 16), 16)] = SECTION / vol
            for field in range(FIELDS):
                base[row, pl.ds(pl.multiple_of(field * PLANES + group * 16, 16), 16)] = (
                    state[field] + SECTION * radial[field, at]
                )
            parts = flux_of(axial_metric, at, rho, vel, prs, vol, energy + prs)
            for field in range(FIELDS):
                keep_cells(0, row, field, group, parts[field])
            panel_axial[group, pl.ds(row, 1)] = parts[0][:1] + parts[2][:1]
        return carry

    lax.fori_loop(0, BLOCKS // 2, axial_group, 0)
    send_axial(0, panel_axial[0])
    for load in loads:
        load.wait()
    send_edges(0)

    ids = observer_ref[...]
    order = (
        lax.shift_right_logical(ids, 7) * 128
        + (lax.shift_right_logical(ids, 2) & 1) * 64
        + (lax.shift_right_logical(ids, 3) & 15) * 4
        + (ids & 3)
    )
    partial[pl.ds(0, ENTRY_ROWS)] = order.astype(F32)

    def hot_row(row, carry):
        wanted = partial[pl.ds(row, 1)].astype(jnp.int32)
        rows = lax.broadcasted_iota(jnp.int32, (OBSERVERS, LANES), 0)
        at = pl.multiple_of(row * LANES, LANES)
        observer_hot[:, pl.ds(at, LANES)] = jnp.where(rows == wanted, 1.0, 0.0).astype(BF16)
        return carry

    lax.fori_loop(0, ENTRY_ROWS, hot_row, 0)

    own_part(0)
    reduce_moments(0, DL)
    change = take_axial(0) + take_plane(0)
    send_axial(1, base[:, 0] + base[:, 2 * PLANES] - ratio[:, 0] * change)
    add_edges(0)
    send_plane(1, take_axial(1))
    wait_starts(0)
    for copy in halo_copies(0, deriv_halo, azim_flux, 1):
        copy.wait_recv()

    def section_group(group, carry):
        for field in range(FIELDS):
            at = pl.ds(pl.multiple_of(field * PLANES + group * 16, 16), 16)
            here = pl.ds(pl.multiple_of(group * 16, 16), 16)
            flux = [deriv_halo[0, 0, at]] + [azim_flux[row, at] for row in range(ROWS)] + [deriv_halo[1, 0, at]]
            up = [start_of(start_recv, group, field, 0)]
            for row in range(ROWS - 1):
                up.append(DL * (flux[row + 1] + up[-1]))
            down = [start_of(start_recv, group, field, 1)]
            for row in range(ROWS - 1, 0, -1):
                down.append(DL * (flux[row + 1] + down[-1]))
            down = down[::-1]
            for row in range(ROWS):
                deriv = DK * (down[row] - up[row]) + C1 * (flux[row + 2] - flux[row])
                value = base[row, at] - ratio[row, here] * (lined[row, at] + deriv)
                keep_cells(1, row, field, group, value)
        return carry

    lax.fori_loop(0, BLOCKS // 2, section_group, 0)
    send_edges(1)
    own_part(1)
    add_edges(1)

    keep = pltpu.make_async_copy(lined, lined_hbm, keep_sem)
    keep.start()

    def moment_group(step, carry):
        group = group_at(step)
        for field in range(FIELDS):
            at = pl.ds(pl.multiple_of(field * PLANES + group * 16, 16), 16)
            keep_moments(1, group, field, [lined[row, at] for row in range(ROWS)], FL)
        send_moments(1, step)
        return carry

    lax.fori_loop(0, BLOCKS // 2, moment_group, 0)
    source = area_ref[...] * (take_plane(1) - 1.0)
    picks = weight_ref[...]
    low_half = jnp.take_along_axis(
        jnp.broadcast_to(table_ref[pl.ds(0, 1)], (ENTRY_ROWS, LANES)), picks & 127, axis=1
    )
    high_half = jnp.take_along_axis(
        jnp.broadcast_to(table_ref[pl.ds(1, 1)], (ENTRY_ROWS, LANES)), picks & 127, axis=1
    )
    weights = jnp.where(picks < LANES, low_half, high_half)
    values = weights * jnp.concatenate([source] * 4, axis=0)
    high, low = two_terms(values)
    partial[pl.ds(0, ENTRY_ROWS)] = high.astype(F32)
    partial[pl.ds(ENTRY_ROWS, ENTRY_ROWS)] = low.astype(F32)

    def bin_row(row, carry):
        same = lax.broadcasted_iota(jnp.int32, (TIME_BINS, LANES), 0) == bin_ref[pl.ds(row, 1)]
        at = pl.multiple_of(row * LANES, LANES)
        bin_hot[pl.ds(0, TIME_BINS), pl.ds(at, LANES)] = jnp.where(same, partial[pl.ds(row, 1)], 0.0).astype(BF16)
        bin_hot[pl.ds(TIME_BINS, TIME_BINS), pl.ds(at, LANES)] = jnp.where(
            same, partial[pl.ds(ENTRY_ROWS + row, 1)], 0.0
        ).astype(BF16)
        return carry

    lax.fori_loop(0, ENTRY_ROWS, bin_row, 0)

    total = dot_last(observer_hot[...], bin_hot[...])
    partial[...] = total[:, :TIME_BINS] + total[:, TIME_BINS:]

    mine = me_a * 2 + core

    def part_copy(step):
        other = lax.rem(mine + step, 8)
        other_z = me_z - core + lax.rem(other, 2)
        return pltpu.make_async_remote_copy(
            src_ref=partial.at[pl.ds(pl.multiple_of(other * 64, 64), 64)],
            dst_ref=part_recv.at[step - 1],
            send_sem=part_send_sem.at[step - 1],
            recv_sem=part_recv_sem.at[step - 1],
            device_id=(other // 2, other_z),
            device_id_type=MESH,
        )

    for step in range(1, 8):
        part_copy(step).start()
    for copy in halo_copies(1, filter_halo, lined, 2):
        copy.start()
    reduce_moments(1, FL)
    total = partial[pl.ds(pl.multiple_of(mine * 64, 64), 64)]
    for step in range(1, 8):
        part_copy(step).wait_recv()
        total = total + part_recv[step - 1]
    for owner in range(16):
        owner_send[owner, pl.ds(0, 4)] = total[4 * owner : 4 * owner + 4]
        owner_send[owner, pl.ds(4, 4)] = jnp.zeros((4, LANES), F32)

    def owner_copy(step):
        other = lax.rem(chip + step, 16)
        return pltpu.make_async_remote_copy(
            src_ref=owner_send.at[other],
            dst_ref=owner_hbm.at[step],
            send_sem=owner_send_sem.at[step - 1],
            recv_sem=owner_recv_sem.at[step - 1],
            device_id=(me_a, 2 * other + core),
            device_id_type=MESH,
        )

    for step in range(1, 16):
        owner_copy(step).start()
    own_copy = pltpu.make_async_copy(owner_send.at[chip], owner_hbm.at[0], owner_sem)
    own_copy.start()
    wait_starts(1)
    for copy in halo_copies(1, filter_halo, lined, 2):
        copy.wait_recv()

    own_copy.wait()
    for step in range(1, 16):
        owner_copy(step).wait_recv()
    keep.wait()

    for which, halo, source_ref, depth in ((0, deriv_halo, azim_flux, 1), (1, filter_halo, lined, 2)):
        wait_moment_sends(which)
        wait_start_sends(which)
        wait_edge_sends(which)
        for copy in halo_copies(which, halo, source_ref, depth):
            copy.wait_send()
    for step in range(1, 8):
        part_copy(step).wait_send()
    for step in range(1, 16):
        owner_copy(step).wait_send()
    for which in range(2):
        plane_wait(which, plane_send_sem)
        for step in range(1, AXIAL):
            axial_copy(which, step).wait_send()


def per_device(
    density,
    velocity,
    pressure,
    axial_metric,
    azim_metric,
    volume,
    radial_term,
    panel_area,
    observer_ids,
    bin_ids,
    weight_ids,
    bin_weights,
):
    own, sent, taken, full = both_tables()
    rows = PLANES * ROWS
    hbm = pl.BlockSpec(memory_space=pltpu.HBM)
    dma = pltpu.SemaphoreType.DMA
    lined, halo, starts, parts = pl.pallas_call(
        kernel,
        out_shape=(
            jax.ShapeDtypeStruct((ROWS, SLAB, LANES), F32),
            jax.ShapeDtypeStruct((2, 2, SLAB, LANES), F32),
            jax.ShapeDtypeStruct((SLOTS, TILE_ROWS, LANES), F32),
            jax.ShapeDtypeStruct((16, 8, TIME_BINS), F32),
        ),
        in_specs=[hbm] * 17,
        out_specs=(hbm, hbm, hbm, hbm),
        scratch_shapes=[
            pltpu.VMEM((2, 2 * LANES, 2 * LANES), BF16),
            pltpu.VMEM((2, 2, 32, 2 * LANES), BF16),
            pltpu.VMEM((2, 2, 64, 2 * LANES), BF16),
            pltpu.VMEM((rows, LANES), F32),
            pltpu.VMEM((3, rows, LANES), F32),
            pltpu.VMEM((rows, LANES), F32),
            pltpu.VMEM((3, rows, LANES), F32),
            pltpu.VMEM((3, rows, LANES), F32),
            pltpu.VMEM((rows, LANES), F32),
            pltpu.VMEM((FIELDS, rows, LANES), F32),
            pltpu.VMEM((ROWS, LANES), F32),
            pltpu.VMEM((ENTRY_ROWS, LANES), jnp.int32),
            pltpu.VMEM((ENTRY_ROWS, LANES), jnp.int32),
            pltpu.VMEM((ENTRY_ROWS, LANES), jnp.int32),
            pltpu.VMEM((2, LANES), F32),
            pltpu.VMEM((2, ROWS, NAZ), F32),
            pltpu.VMEM((2, NA, LANES), F32),
            pltpu.VMEM((ROWS, SLAB, LANES), F32),
            pltpu.VMEM((ROWS, SLAB, LANES), F32),
            pltpu.VMEM((ROWS, PLANES, LANES), F32),
            pltpu.VMEM((2, LINES, 2 * LANES), BF16),
            pltpu.VMEM((ROWS, SLAB, LANES), F32),
            pltpu.VMEM((2, 2, 8, HALF), F32),
            pltpu.VMEM((2, AXIAL, 8, HALF), F32),
            pltpu.VMEM((2, SLOTS, TILE_ROWS, LANES), F32),
            pltpu.VMEM((2, AZIM, SHARE[0], LANES), F32),
            pltpu.VMEM((2, AZIM, SHARE[0], LANES), F32),
            pltpu.VMEM((SLOTS, TILE_ROWS, LANES), F32),
            pltpu.VMEM((2, 1, SLAB, LANES), F32),
            pltpu.VMEM((OBSERVERS, ENTRY_ROWS * LANES), BF16),
            pltpu.VMEM((2 * TIME_BINS, ENTRY_ROWS * LANES), BF16),
            pltpu.VMEM((OBSERVERS, TIME_BINS), F32),
            pltpu.VMEM((7, 64, TIME_BINS), F32),
            pltpu.VMEM((16, 8, TIME_BINS), F32),
            pltpu.VMEM((2, ROWS, LANES), F32),
            pltpu.VMEM((2, AZIM, ROWS, LANES), F32),
            pltpu.VMEM((2, ROWS, LANES), F32),
            pltpu.VMEM((2, AXIAL, ROWS, LANES), F32),
            pltpu.VMEM((BLOCKS // 2, ROWS, LANES), F32),
            dma(()),
            dma(()),
            dma((15,)),
            dma((5, BLOCKS // 2)),
            dma((2, BLOCKS // 2)),
            dma((2, 3)),
            dma((2, 3)),
            dma((2,)),
            dma((2,)),
            dma((2,)),
            dma((2,)),
            dma((2, 2)),
            dma((2, 2)),
            dma((7,)),
            dma((7,)),
            dma((15,)),
            dma((15,)),
            dma((2,)),
            dma((2,)),
            dma((2, 3)),
            dma((2, 3)),
        ],
        compiler_params=pltpu.CompilerParams(
            collective_id=0, has_side_effects=True
        ),
    )(
        jnp.asarray(own),
        jnp.asarray(sent),
        jnp.asarray(taken),
        density.reshape(rows, LANES),
        velocity.reshape(3, rows, LANES),
        pressure.reshape(rows, LANES),
        axial_metric.reshape(3, rows, LANES),
        azim_metric.reshape(3, rows, LANES),
        volume.reshape(rows, LANES),
        radial_term.reshape(FIELDS, rows, LANES),
        panel_area,
        observer_ids.reshape(ENTRY_ROWS, LANES),
        bin_ids.reshape(ENTRY_ROWS, LANES),
        weight_ids.reshape(ENTRY_ROWS, LANES),
        bin_weights.reshape(2, LANES),
        jnp.asarray(azimuth_rows()),
        jnp.asarray(full),
    )
    state, signals = pl.pallas_call(
        finish_kernel,
        out_shape=(
            jax.ShapeDtypeStruct((FIELDS, rows, LANES), F32),
            jax.ShapeDtypeStruct((4, TIME_BINS), F32),
        ),
        in_specs=[hbm] * 4,
        out_specs=(hbm, hbm),
        scratch_shapes=[
            pltpu.VMEM((ROWS, FIELDS, PLANES, LANES), F32),
            pltpu.VMEM((4, FIELDS, PLANES, LANES), F32),
            pltpu.VMEM((SLOTS, TILE_ROWS, LANES), F32),
            pltpu.VMEM((FIELDS, rows, LANES), F32),
            pltpu.VMEM((16, 8, TIME_BINS), F32),
            pltpu.VMEM((4, TIME_BINS), F32),
            dma((BLOCKS // 2, 3)),
            dma((BLOCKS // 2,)),
            dma((2,)),
        ],
    )(
        lined.reshape(ROWS, FIELDS, PLANES, LANES),
        halo.reshape(4, FIELDS, PLANES, LANES),
        starts,
        parts,
    )
    return state.reshape(FIELDS, PLANES, ROWS, LANES), signals


def solution(mesh):
    placed = (
        P(None, "azim", "axial"),
        P(None, None, "azim", "axial"),
        P(None, "azim", "axial"),
        P(None, None, "azim", "axial"),
        P(None, None, "azim", "axial"),
        P(None, "azim", "axial"),
        P(None, None, "azim", "axial"),
        P("azim", "axial"),
        P(None, "azim", "axial"),
        P(None, "azim", "axial"),
        P(None, "azim", "axial"),
        P(),
    )
    return jax.shard_map(
        per_device,
        mesh=mesh,
        in_specs=placed,
        out_specs=(P(None, None, "azim", "axial"), P(("axial", "azim"), None)),
        check_vma=False,
    )
```

```python
import functools
import math

import jax
import jax.numpy as jnp
import ml_dtypes
import numpy as np
from jax import lax
from jax.experimental import pallas as pl
from jax.experimental.pallas import tpu as pltpu
from jax.sharding import PartitionSpec as P

F32 = jnp.float32
BF16 = jnp.bfloat16
MESH = pl.DeviceIdType.MESH

PLANES = 64
FIELDS = 5
ROWS = 8
LANES = 128
AXIAL = 4
AZIM = 32
NA = AXIAL * LANES
NAZ = AZIM * ROWS
SLAB = FIELDS * PLANES
BLOCKS = PLANES // 8
SLOTS = 2 * BLOCKS
TILE_ROWS = 8 * FIELDS
PARTS = ((0, 3), (3, 2))
PART_OF = (0, 0, 0, 1, 1)
SHARE = (((0, 16), (16, 8)), ((24, 8), (32, 8)))
STEPS = (2, 1, 3, 0)
AWAY = tuple((dz, dy) for dz in STEPS[:3] for dy in STEPS[:3]) + ((2, 0), (0, 2), (1, 0), (3, 0), (0, 1), (0, 3))
ENTRY_ROWS = 32
OBSERVERS = 512
TIME_BINS = 128
PEERS = (AZIM - 1) + 2 * (AXIAL - 1)

SECTION = 0.25
DERIV_ALPHA = 1.0 / 3.0
BETA = 0.499


def decay_root(alpha):
    return (-1.0 + math.sqrt(1.0 - 4.0 * alpha * alpha)) / (2.0 * alpha)


DL = decay_root(DERIV_ALPHA)
FL = decay_root(BETA)
C1 = (1.0 / 36.0) / DERIV_ALPHA
DS = 1.0 / math.sqrt(1.0 - 4.0 * DERIV_ALPHA**2)
DK = (7.0 / 9.0 - C1) * DS * (1.0 / DL - DL)
FC = [
    (11.0 + 10.0 * BETA) / 16.0,
    (15.0 + 34.0 * BETA) / 32.0,
    (-3.0 + 6.0 * BETA) / 16.0,
    (1.0 - 2.0 * BETA) / 32.0,
]
FS = 1.0 / math.sqrt(1.0 - 4.0 * BETA**2)
E2 = FC[3] / (2.0 * BETA)
E1 = (FC[2] / 2.0 - E2) / BETA
E0 = (FC[1] / 2.0 - E1 - BETA * E2) / BETA
FK = (FC[0] - E0 - 2.0 * BETA * E1) * FS


def split(values):
    high = values.astype(ml_dtypes.bfloat16)
    low = (values - high.astype(np.float64)).astype(ml_dtypes.bfloat16)
    return high, low


def axial_tables(root, scale, band):
    n, w = NA, LANES
    index = np.arange(n)
    green = scale * (
        np.power(root, np.abs(index[:, None] - index[None, :]))
        - np.power(root, 2 * n - index[:, None] - index[None, :])
    )
    side = np.zeros((n, n))
    for shift, value in band.items():
        side += value * np.eye(n, k=shift)
    whole = green @ side
    left = np.zeros((AXIAL, w))
    right = np.zeros((AXIAL, w))
    for k in range(AXIAL):
        cols = slice(k * w, (k + 1) * w)
        lo, hi = max(0, k * w - 3), min(n, (k + 1) * w + 3)
        m = np.arange(lo, hi)
        left[k] = np.power(root, ((k + 1) * w - m).astype(np.float64)) @ side[lo:hi, cols]
        right[k] = (
            np.power(root, (m - k * w + 1).astype(np.float64))
            - np.power(root, (2 * n - m - k * w + 1).astype(np.float64))
        ) @ side[lo:hi, cols]
    t = np.arange(w)
    full = np.stack([whole[d * w : (d + 1) * w].T for d in range(AXIAL)]).astype(np.float32)
    sent = np.zeros((AXIAL, 2, 32, 2 * w), ml_dtypes.bfloat16)
    taken = np.zeros((AXIAL, 2, 64, 2 * w), ml_dtypes.bfloat16)
    for d in range(AXIAL):
        for half in range(2):
            rows = np.zeros((16, w))
            base = half * 4
            rows[base] = left[d]
            rows[base + 1, w - 1] = 1.0
            rows[base + 2, w - 2] = 1.0
            rows[8 + base] = right[d]
            rows[8 + base + 1, 0] = 1.0
            rows[8 + base + 2, 1] = 1.0
            high, low = split(rows)
            sent[d, half] = np.concatenate(
                [np.concatenate([high, high], axis=1), np.concatenate([low, low], axis=1)], axis=0
            )
            rows = np.zeros((32, w))
            for k in range(AXIAL):
                row = k * 8 + half * 4
                i = d * w + t
                if k < d:
                    rows[row] = scale * (
                        np.power(root, (i - (k + 1) * w).astype(np.float64))
                        - np.power(root, (2 * n - i - (k + 1) * w).astype(np.float64))
                    )
                    if k == d - 1:
                        for edge in range(2):
                            col = d * w - 1 - edge
                            for near in range(2 - edge):
                                rows[row + 1 + edge, near] = (
                                    whole[d * w + near, col] - rows[row, near] * left[k, col - k * w]
                                )
                if k > d:
                    rows[row] = scale * np.power(root, (k * w - 1 - i).astype(np.float64))
                    if k == d + 1:
                        for edge in range(2):
                            col = k * w + edge
                            for near in range(2 - edge):
                                rows[row + 1 + edge, w - 1 - near] = (
                                    whole[k * w - 1 - near, col] - rows[row, w - 1 - near] * right[k, edge]
                                )
            high, low = split(rows)
            pair = np.concatenate([high, low], axis=1)
            taken[d, half] = np.concatenate([pair, pair], axis=0)
    return sent, taken, full


def both_tables():
    deriv = axial_tables(DL, DS, {1: 7.0 / 9.0, -1: -7.0 / 9.0, 2: 1.0 / 36.0, -2: -1.0 / 36.0})
    band = {0: FC[0]}
    for shift in range(1, 4):
        band[shift] = band[-shift] = FC[shift] / 2.0
    smooth = axial_tables(FL, FS, band)
    return [np.stack(pair, axis=1) for pair in zip(deriv, smooth)]


def azimuth_rows():
    gap = np.arange(NAZ)
    slope = DK * (np.power(DL, gap) - np.power(DL, NAZ - gap)) / (1.0 - DL**NAZ)
    slope[0] = 0.0
    slope[1] += C1
    slope[-1] -= C1
    line = FK * (np.power(FL, gap) + np.power(FL, NAZ - gap)) / (1.0 - FL**NAZ)
    line[0] = FK * (1.0 + 2.0 * FL**NAZ / (1.0 - FL**NAZ)) + E0
    for shift, value in ((1, E1), (2, E2)):
        line[shift] += value
        line[-shift] += value
    rows = np.arange(ROWS)
    at = (gap[None, :] - rows[:, None]) % NAZ
    return np.stack([slope[at], line[at]]).astype(np.float32)


def two_terms(value):
    high = value.astype(BF16)
    low = (value - high.astype(F32)).astype(BF16)
    return high, low


def dot_last(left, right):
    return lax.dot_general(left, right, (((1,), (1,)), ((), ())), preferred_element_type=F32)


def dot_first(left, right):
    return lax.dot_general(left, right, (((0,), (0,)), ((), ())), preferred_element_type=F32)


def start_of(starts, group, field, side):
    return jnp.concatenate(
        [starts[4 * group + 2 * half + side, pl.ds(8 * field, 8)] for half in range(2)], axis=0
    )


def finish_kernel(
    lined_hbm,
    halo_hbm,
    start_hbm,
    part_hbm,
    state_hbm,
    signal_hbm,
    lined,
    halo,
    starts,
    final,
    parts,
    signals,
    load_sem,
    store_sem,
    part_sem,
):
    part_copy = pltpu.make_async_copy(part_hbm, parts, part_sem.at[0])
    signal_copy = pltpu.make_async_copy(signals, signal_hbm, part_sem.at[1])

    def loads(group):
        slots = pl.ds(pl.multiple_of(4 * group, 4), 4)
        planes = pl.ds(pl.multiple_of(16 * group, 16), 16)
        return [
            pltpu.make_async_copy(start_hbm.at[slots], starts.at[slots], load_sem.at[group, 0]),
            pltpu.make_async_copy(lined_hbm.at[:, :, planes], lined.at[:, :, planes], load_sem.at[group, 1]),
            pltpu.make_async_copy(halo_hbm.at[:, :, planes], halo.at[:, :, planes], load_sem.at[group, 2]),
        ]

    def store(group):
        planes = pl.ds(pl.multiple_of(group * 128, 128), 128)
        return pltpu.make_async_copy(final.at[:, planes], state_hbm.at[:, planes], store_sem.at[group])

    for group in range(BLOCKS // 2):
        for load in loads(group):
            load.start()
        if group == 0:
            part_copy.start()

    def final_group(group, carry):
        for load in loads(group):
            load.wait()
        planes = pl.ds(pl.multiple_of(group * 16, 16), 16)
        for field in range(FIELDS):
            value = [halo[row, field, planes] for row in range(2)]
            value += [lined[row, field, planes] for row in range(ROWS)]
            value += [halo[2 + row, field, planes] for row in range(2)]
            up = [start_of(starts, group, field, 0)]
            for row in range(ROWS - 1):
                up.append(FL * (value[row + 2] + up[-1]))
            down = [start_of(starts, group, field, 1)]
            for row in range(ROWS - 1, 0, -1):
                down.append(FL * (value[row + 2] + down[-1]))
            down = down[::-1]
            for row in range(ROWS):
                near = E1 * (value[row + 1] + value[row + 3]) + E2 * (value[row] + value[row + 4])
                result = FK * (up[row] + down[row]) + (FK + E0) * value[row + 2] + near
                final[field, pl.ds(group * 128 + row, 16, stride=ROWS)] = result
        store(group).start()
        return carry

    final_group(0, 0)
    part_copy.wait()
    signals[...] = jnp.sum(parts[...], axis=0)[:4]
    signal_copy.start()
    lax.fori_loop(1, BLOCKS // 2, final_group, 0)
    for group in range(BLOCKS // 2):
        store(group).wait()
    signal_copy.wait()


def kernel(
    sent_hbm,
    taken_hbm,
    density_hbm,
    velocity_hbm,
    pressure_hbm,
    axial_hbm,
    azim_hbm,
    volume_hbm,
    radial_hbm,
    area_hbm,
    observer_hbm,
    bin_hbm,
    weight_hbm,
    table_hbm,
    azimuth_hbm,
    full_hbm,
    lined_hbm,
    filter_halo,
    start_hbm,
    owner_hbm,
    own,
    sent,
    taken,
    density,
    velocity,
    pressure,
    axial_metric,
    azim_metric,
    volume,
    radial,
    area_ref,
    observer_ref,
    bin_ref,
    weight_ref,
    table_ref,
    azimuth_ref,
    full,
    azim_flux,
    base,
    ratio,
    cells_a,
    cells_b,
    lined_a,
    lined_b,
    edge_send_a,
    edge_send_b,
    edge_recv_a,
    edge_recv_b,
    moment_send,
    moment_recv,
    start_send,
    start_recv,
    deriv_halo,
    observer_hot,
    bin_hot,
    partial,
    part_recv,
    owner_send,
    plane_send,
    plane_recv,
    axial_send,
    axial_recv,
    panel_axial,
    keep_sem,
    owner_sem,
    load_sem,
    early_sem,
    late_sem,
    edge_send_sem,
    edge_recv_sem,
    moment_send_sem,
    moment_recv_sem,
    start_send_sem,
    start_recv_sem,
    halo_send_sem,
    halo_recv_sem,
    part_send_sem,
    part_recv_sem,
    owner_send_sem,
    owner_recv_sem,
    plane_send_sem,
    plane_recv_sem,
    axial_send_sem,
    axial_recv_sem,
):
    me_a = lax.axis_index("axial")
    me_z = lax.axis_index("azim")
    core = lax.rem(me_z, 2)
    chip = me_z // 2
    twin = me_z + 1 - 2 * core
    after = lax.rem(me_z + 1, AZIM)
    before = lax.rem(me_z + AZIM - 1, AZIM)

    def chip_at(step):
        return 4 * lax.rem(chip // 4 + step[0], 4) + lax.rem(chip + step[1], 4)

    def group_at(step):
        away = jnp.where(step == 0, STEPS[0], jnp.where(step == 1, STEPS[1], jnp.where(step == 2, STEPS[2], 0)))
        return lax.rem(chip // 4 + away, 4)

    def early_loads(group):
        part = pl.ds(pl.multiple_of(group * 128, 128), 128)
        whole = slice(None)
        return [
            pltpu.make_async_copy(source.at[where], dest.at[where], early_sem.at[number, group])
            for number, (source, dest, where) in enumerate(
                (
                    (density_hbm, density, (part,)),
                    (velocity_hbm, velocity, (whole, part)),
                    (pressure_hbm, pressure, (part,)),
                    (volume_hbm, volume, (part,)),
                    (azim_hbm, azim_metric, (whole, part)),
                )
            )
        ]

    def late_loads(group):
        part = pl.ds(pl.multiple_of(group * 128, 128), 128)
        return [
            pltpu.make_async_copy(axial_hbm.at[:, part], axial_metric.at[:, part], late_sem.at[0, group]),
            pltpu.make_async_copy(radial_hbm.at[:, part], radial.at[:, part], late_sem.at[1, group]),
        ]

    loads = [
        pltpu.make_async_copy(area_hbm, area_ref, load_sem.at[0]),
        pltpu.make_async_copy(observer_hbm, observer_ref, load_sem.at[1]),
        pltpu.make_async_copy(bin_hbm, bin_ref, load_sem.at[2]),
        pltpu.make_async_copy(weight_hbm, weight_ref, load_sem.at[3]),
        pltpu.make_async_copy(table_hbm, table_ref, load_sem.at[4]),
        pltpu.make_async_copy(azimuth_hbm, azimuth_ref, load_sem.at[5]),
        pltpu.make_async_copy(full_hbm.at[me_a], full, load_sem.at[6]),
    ]
    for which in range(2):
        loads.append(pltpu.make_async_copy(sent_hbm.at[me_a, which], sent.at[which], load_sem.at[7 + 2 * which]))
        loads.append(pltpu.make_async_copy(taken_hbm.at[me_a, which], taken.at[which], load_sem.at[8 + 2 * which]))
    for step in range(BLOCKS // 2):
        for load in early_loads(group_at(step)):
            load.start()
    for group in range(BLOCKS // 2):
        for load in late_loads(group):
            load.start()
    for load in loads:
        load.start()

    starts = (start_recv, start_hbm)
    cells, lined = (cells_a, cells_b), (lined_a, lined_b)
    edge_send, edge_recv = (edge_send_a, edge_send_b), (edge_recv_a, edge_recv_b)

    barrier = pltpu.get_barrier_semaphore()

    def greet_azim(step, carry):
        other = lax.rem(me_z + step, AZIM)
        pl.semaphore_signal(barrier, inc=1, device_id=(me_a, other), device_id_type=MESH)
        return carry

    lax.fori_loop(1, AZIM, greet_azim, 0)

    def greet_axial(step, carry):
        other = lax.rem(me_a + step, AXIAL)
        pl.semaphore_signal(barrier, inc=1, device_id=(other, me_z), device_id_type=MESH)
        pl.semaphore_signal(barrier, inc=1, device_id=(other, twin), device_id_type=MESH)
        return carry

    lax.fori_loop(1, AXIAL, greet_axial, 0)

    for part in range(2):
        for which in range(2):
            edge_recv[part][which, pl.ds(me_a, 1)] = jnp.zeros((1, 8, 4 * PLANES * PARTS[part][1]), F32)

    def moment_source(which, part, slot, share):
        first, rows = SHARE[part][share]
        return moment_send.at[which, slot, pl.ds(first, rows)]

    def moment_copy(which, part, slot, share):
        return pltpu.make_async_remote_copy(
            src_ref=moment_source(which, part, slot, share),
            dst_ref=moment_recv.at[which, part, me_z, pl.ds(0, SHARE[part][share][1])],
            send_sem=moment_send_sem.at[which, part],
            recv_sem=moment_recv_sem.at[which, part],
            device_id=(me_a, 2 * slot + share),
            device_id_type=MESH,
        )

    def send_moments(which, part, step):
        row = 4 * group_at(step)
        for turn in STEPS[:3]:
            for share in range(2):
                moment_copy(which, part, row + lax.rem(chip + turn, 4), share).start()

        @pl.when(step < 3)
        def _():
            for share in range(2):
                moment_copy(which, part, row + lax.rem(chip, 4), share).start()

        for share in range(2):

            @pl.when(jnp.logical_and(step == 3, core == share))
            def _():
                moment_copy(which, part, chip, 1 - share).start()
                pltpu.make_async_copy(
                    moment_source(which, part, chip, share),
                    moment_recv.at[which, part, me_z, pl.ds(0, SHARE[part][share][1])],
                    moment_recv_sem.at[which, part],
                ).start()

    def wait_moment_sends(which, part):
        for share in range(2):

            @pl.when(core == share)
            def _():
                rows = pl.ds(8 * PARTS[part][0], 8 * PARTS[part][1])
                sent_rows = moment_send.at[which, pl.ds(0, SLOTS - 1), rows]
                pltpu.make_async_copy(sent_rows, sent_rows, moment_send_sem.at[which, part]).wait()
                sent_rows = moment_source(which, part, SLOTS - 1, 1 - share)
                pltpu.make_async_copy(sent_rows, sent_rows, moment_send_sem.at[which, part]).wait()

    def reduce_moments(which, part, root):
        factor = root**ROWS
        wrap = 1.0 / (1.0 - root**NAZ)
        side = lax.rem(chip, 2)

        def place(step):
            return step + side * (AZIM - 1 - 2 * step)

        for share in range(2):
            first_row, count = SHARE[part][share]
            rows, there = pl.ds(0, count), pl.ds(first_row, count)

            @pl.when(core == share)
            def _():
                arrived = moment_recv.at[which, part, :, rows]
                pltpu.make_async_copy(arrived, arrived, moment_recv_sem.at[which, part]).wait()

                def gather(step, total):
                    return factor * total + moment_recv[which, part, place(step), rows]

                first = lax.fori_loop(0, AZIM, gather, jnp.zeros((count, LANES), F32), unroll=8) * wrap

                def follow(step, now):
                    other = place(step)
                    start_send[which, part, other, rows] = now
                    return factor * now + moment_recv[which, part, other, rows]

                lax.fori_loop(0, AZIM, follow, first, unroll=8)

                def hand_out(other):
                    pltpu.make_async_remote_copy(
                        src_ref=start_send.at[which, part, other, rows],
                        dst_ref=starts[which].at[chip, there],
                        send_sem=start_send_sem.at[which, part],
                        recv_sem=start_recv_sem.at[which, part],
                        device_id=(me_a, other),
                        device_id_type=MESH,
                    ).start()

                for step in AWAY:
                    for half in range(2):
                        hand_out(2 * chip_at(step) + half)
                hand_out(twin)
                pltpu.make_async_copy(
                    start_send.at[which, part, me_z, rows],
                    starts[which].at[chip, there],
                    start_recv_sem.at[which, part],
                ).start()

    def wait_starts(which, part):
        arrived = starts[which].at[:, pl.ds(8 * PARTS[part][0], 8 * PARTS[part][1])]
        pltpu.make_async_copy(arrived, arrived, start_recv_sem.at[which, part]).wait()

    def wait_start_sends(which, part):
        for share in range(2):

            @pl.when(core == share)
            def _():
                gone = start_send.at[which, part, pl.ds(0, AZIM - 1), pl.ds(0, SHARE[part][share][1])]
                pltpu.make_async_copy(gone, gone, start_send_sem.at[which, part]).wait()

    def moments_of(values, root):
        up = root * values[0]
        for row in range(1, ROWS):
            up = root * (up + values[row])
        down = root * values[ROWS - 1]
        for row in range(ROWS - 2, -1, -1):
            down = root * (down + values[row])
        return up, down

    def keep_moments(which, group, field, values, root):
        up, down = moments_of(values, root)
        for half in range(2):
            for side, value in ((0, up), (1, down)):
                moment_send[which, 4 * group + 2 * half + side, pl.ds(8 * field, 8)] = value[8 * half : 8 * half + 8]

    def halo_copies(which):
        copies = []
        for part in range(2):
            if which == 1:
                source, halo, depth = lined[part], filter_halo, 2
                there = pl.ds(PLANES * PARTS[part][0], PLANES * PARTS[part][1])
            else:
                source, halo, depth = azim_flux, deriv_halo, 1
                there = pl.ds(0, SLAB)
                if part == 1:
                    break
            for side, other, rows in ((0, after, pl.ds(ROWS - depth, depth)), (1, before, pl.ds(0, depth))):
                copies.append(
                    pltpu.make_async_remote_copy(
                        src_ref=source.at[rows],
                        dst_ref=halo.at[side, :, there],
                        send_sem=halo_send_sem.at[which, part, side],
                        recv_sem=halo_recv_sem.at[which, part, side],
                        device_id=(me_a, other),
                        device_id_type=MESH,
                    )
                )
        return copies

    def edge_copy(which, part, step):
        other = lax.rem(me_a + step, AXIAL)
        down = jnp.where(other < me_a, 1, 0)
        return pltpu.make_async_remote_copy(
            src_ref=edge_send[part].at[which, down],
            dst_ref=edge_recv[part].at[which, me_a],
            send_sem=edge_send_sem.at[which, part, step - 1],
            recv_sem=edge_recv_sem.at[which, part, step - 1],
            device_id=(other, me_z),
            device_id_type=MESH,
        )

    def send_edges(which, part):
        slab = PLANES * PARTS[part][1]

        def piece(step, carry):
            at = pl.multiple_of(step * 2 * slab, 2 * slab)
            total = dot_last(sent[which, 0], cells[part][which, pl.ds(at, 2 * slab)]) + dot_last(
                sent[which, 1], cells[part][which, pl.ds(4 * slab + at, 2 * slab)]
            )
            total = total[:16] + total[16:]
            edge_send[part][which, 0, :, pl.ds(at, 2 * slab)] = total[:8]
            edge_send[part][which, 1, :, pl.ds(at, 2 * slab)] = total[8:]
            return carry

        lax.fori_loop(0, 2, piece, 0, unroll=True)
        for step in STEPS[:3]:
            edge_copy(which, part, step).start()

    def own_part(which, part):
        slab = PLANES * PARTS[part][1]

        def piece(step, carry):
            at = pl.multiple_of(step * 2 * slab, 2 * slab)
            total = jnp.dot(cells[part][which, pl.ds(at, 2 * slab)], own[which], preferred_element_type=F32)
            lined[part][pl.ds(2 * step, 2)] = (total[:, :LANES] + total[:, LANES:]).reshape(2, slab, LANES)
            return carry

        lax.fori_loop(0, 4, piece, 0, unroll=True)

    def add_edges(which, part):
        slab = PLANES * PARTS[part][1]
        for step in range(1, AXIAL):
            edge_copy(which, part, step).wait_recv()

        def piece(step, carry):
            at = pl.multiple_of(lax.rem(step, 2) * 2 * slab, 2 * slab)
            received = edge_recv[part][which, :, :, pl.ds(at, 2 * slab)].reshape(32, 2 * slab)
            high, low = two_terms(received)
            total = dot_first(jnp.concatenate([high, low], axis=0), taken[which, step // 2])
            total = (total[:, :LANES] + total[:, LANES:]).reshape(2, slab, LANES)
            lined[part][pl.ds(2 * step, 2)] = lined[part][pl.ds(2 * step, 2)] + total
            return carry

        lax.fori_loop(0, 4, piece, 0, unroll=True)

    def keep_cells(which, row, field, group, value):
        part = PART_OF[field]
        first, count = PARTS[part]
        high, low = two_terms(value)
        at = pl.multiple_of((row * count + field - first) * PLANES + group * 16, 16)
        cells[part][which, pl.ds(at, 16), pl.ds(0, LANES)] = high
        cells[part][which, pl.ds(at, 16), pl.ds(LANES, LANES)] = low

    def axial_copy(which, step):
        return pltpu.make_async_remote_copy(
            src_ref=axial_send.at[which],
            dst_ref=axial_recv.at[which, me_a],
            send_sem=axial_send_sem.at[which, step - 1],
            recv_sem=axial_recv_sem.at[which, step - 1],
            device_id=(lax.rem(me_a + step, AXIAL), me_z),
            device_id_type=MESH,
        )

    def send_axial(which, value):
        axial_send[which] = value
        axial_recv[which, pl.ds(me_a, 1)] = value[None]
        for step in STEPS[:3]:
            axial_copy(which, step).start()

    def take_axial(which):
        for step in range(1, AXIAL):
            axial_copy(which, step).wait_recv()
        line = jnp.concatenate([axial_recv[which, k] for k in range(AXIAL)], axis=1)
        return jnp.dot(line, full[which], preferred_element_type=F32, precision=lax.Precision.HIGHEST)

    def send_plane(which, value):
        plane_send[which] = value
        plane_recv[which, 0] = value

        def piece(other):
            pltpu.make_async_remote_copy(
                src_ref=plane_send.at[which],
                dst_ref=plane_recv.at[which, lax.rem(me_z - other + AZIM, AZIM)],
                send_sem=plane_send_sem.at[which],
                recv_sem=plane_recv_sem.at[which],
                device_id=(me_a, other),
                device_id_type=MESH,
            ).start()

        for step in AWAY:
            for half in range(2):
                piece(2 * chip_at(step) + half)
        piece(twin)

    def plane_wait(which, sem):
        part = plane_recv.at[which, pl.ds(1, AZIM - 1)]
        pltpu.make_async_copy(part, part, sem.at[which]).wait()

    def take_plane(which):
        plane_wait(which, plane_recv_sem)
        return jnp.dot(
            azimuth_ref[which],
            plane_recv[which].reshape(NAZ, LANES),
            preferred_element_type=F32,
            precision=lax.Precision.HIGHEST,
        )

    def flux_of(metric, at, rho, vel, prs, vol, heat):
        grad = [metric[comp, at] for comp in range(3)]
        contra = vol * (grad[0] * vel[0] + grad[1] * vel[1] + grad[2] * vel[2])
        flow = rho * contra
        push = vol * prs
        return [flow] + [flow * vel[comp] + grad[comp] * push for comp in range(3)] + [heat * contra]

    def cells_at(group, row):
        at = pl.ds(group * 128 + row, 16, stride=ROWS)
        rho, prs, vol = density[at], pressure[at], volume[at]
        vel = [velocity[comp, at] for comp in range(3)]
        energy = 2.5 * prs + 0.5 * rho * (vel[0] * vel[0] + vel[1] * vel[1] + vel[2] * vel[2])
        return at, rho, vel, prs, vol, energy

    def azim_group(step, carry):
        group = group_at(step)
        for load in early_loads(group):
            load.wait()
        flux = [[None] * ROWS for _ in range(FIELDS)]
        for row in range(ROWS):
            at, rho, vel, prs, vol, energy = cells_at(group, row)
            parts = flux_of(azim_metric, at, rho, vel, prs, vol, energy + prs)
            for field in range(FIELDS):
                flux[field][row] = parts[field]
                azim_flux[row, pl.ds(pl.multiple_of(field * PLANES + group * 16, 16), 16)] = parts[field]
        for field in range(FIELDS):
            keep_moments(0, group, field, flux[field], DL)

        @pl.when(step == 0)
        def _():
            pl.semaphore_wait(barrier, PEERS)

        send_moments(0, 0, step)
        return carry

    lax.fori_loop(0, BLOCKS // 2, azim_group, 0)

    def send_rest(step, carry):
        send_moments(0, 1, step)
        return carry

    lax.fori_loop(0, BLOCKS // 2, send_rest, 0)
    send_plane(0, azim_flux[:, 0] + azim_flux[:, 2 * PLANES])
    for copy in halo_copies(0):
        copy.start()

    def axial_group(group, carry):
        for load in late_loads(group):
            load.wait()
        for row in range(ROWS):
            at, rho, vel, prs, vol, energy = cells_at(group, row)
            state = [rho, rho * vel[0], rho * vel[1], rho * vel[2], energy]
            ratio[row, pl.ds(pl.multiple_of(group * 16, 16), 16)] = SECTION / vol
            for field in range(FIELDS):
                base[row, pl.ds(pl.multiple_of(field * PLANES + group * 16, 16), 16)] = (
                    state[field] + SECTION * radial[field, at]
                )
            parts = flux_of(axial_metric, at, rho, vel, prs, vol, energy + prs)
            for field in range(FIELDS):
                keep_cells(0, row, field, group, parts[field])
            panel_axial[group, pl.ds(row, 1)] = parts[0][:1] + parts[2][:1]
        return carry

    lax.fori_loop(0, BLOCKS // 2, axial_group, 0)
    send_axial(0, panel_axial[0])
    for load in loads:
        load.wait()
    send_edges(0, 0)
    send_edges(0, 1)

    ids = observer_ref[...]
    order = (
        lax.shift_right_logical(ids, 7) * 128
        + (lax.shift_right_logical(ids, 2) & 1) * 64
        + (lax.shift_right_logical(ids, 3) & 15) * 4
        + (ids & 3)
    )
    partial[pl.ds(0, ENTRY_ROWS)] = order.astype(F32)

    def hot_row(row, carry):
        wanted = partial[pl.ds(row, 1)].astype(jnp.int32)
        rows = lax.broadcasted_iota(jnp.int32, (OBSERVERS, LANES), 0)
        at = pl.multiple_of(row * LANES, LANES)
        observer_hot[:, pl.ds(at, LANES)] = jnp.where(rows == wanted, 1.0, 0.0).astype(BF16)
        return carry

    lax.fori_loop(0, ENTRY_ROWS, hot_row, 0)

    for which in range(2):
        high, low = two_terms(full[which, pl.ds(pl.multiple_of(me_a * LANES, LANES), LANES)])
        for top in range(2):
            own[which, pl.ds(top * LANES, LANES), pl.ds(0, LANES)] = high
            own[which, pl.ds(top * LANES, LANES), pl.ds(LANES, LANES)] = low
    own_part(0, 0)
    own_part(0, 1)
    reduce_moments(0, 0, DL)
    reduce_moments(0, 1, DL)
    change = take_axial(0) + take_plane(0)
    send_axial(1, base[:, 0] + base[:, 2 * PLANES] - ratio[:, 0] * change)
    add_edges(0, 0)
    add_edges(0, 1)

    def section(part):
        first, count = PARTS[part]

        def section_group(group, carry):
            here = pl.ds(pl.multiple_of(group * 16, 16), 16)
            for field in range(first, first + count):
                at = pl.ds(pl.multiple_of(field * PLANES + group * 16, 16), 16)
                inside = pl.ds(pl.multiple_of((field - first) * PLANES + group * 16, 16), 16)
                flux = [deriv_halo[0, 0, at]] + [azim_flux[row, at] for row in range(ROWS)] + [deriv_halo[1, 0, at]]
                up = [start_of(start_recv, group, field, 0)]
                for row in range(ROWS - 1):
                    up.append(DL * (flux[row + 1] + up[-1]))
                down = [start_of(start_recv, group, field, 1)]
                for row in range(ROWS - 1, 0, -1):
                    down.append(DL * (flux[row + 1] + down[-1]))
                down = down[::-1]
                for row in range(ROWS):
                    deriv = DK * (down[row] - up[row]) + C1 * (flux[row + 2] - flux[row])
                    value = base[row, at] - ratio[row, here] * (lined[part][row, inside] + deriv)
                    keep_cells(1, row, field, group, value)
            return carry

        lax.fori_loop(0, BLOCKS // 2, section_group, 0)

    def smoothed_moments(part):
        first, count = PARTS[part]

        def moment_group(step, carry):
            group = group_at(step)
            for field in range(first, first + count):
                inside = pl.ds(pl.multiple_of((field - first) * PLANES + group * 16, 16), 16)
                keep_moments(1, group, field, [lined[part][row, inside] for row in range(ROWS)], FL)
            send_moments(1, part, step)
            return carry

        lax.fori_loop(0, BLOCKS // 2, moment_group, 0)

    wait_starts(0, 0)
    for copy in halo_copies(0):
        copy.wait_recv()
    section(0)
    send_edges(1, 0)
    wait_starts(0, 1)
    section(1)
    send_edges(1, 1)
    send_plane(1, take_axial(1))
    own_part(1, 0)
    own_part(1, 1)
    add_edges(1, 0)
    smoothed_moments(0)
    add_edges(1, 1)
    smoothed_moments(1)
    for copy in halo_copies(1):
        copy.start()
    keeps = [
        pltpu.make_async_copy(
            lined[part],
            lined_hbm.at[:, pl.ds(PLANES * PARTS[part][0], PLANES * PARTS[part][1])],
            keep_sem.at[part],
        )
        for part in range(2)
    ]
    for keep in keeps:
        keep.start()

    source = area_ref[...] * (take_plane(1) - 1.0)
    picks = weight_ref[...]
    low_half = jnp.take_along_axis(
        jnp.broadcast_to(table_ref[pl.ds(0, 1)], (ENTRY_ROWS, LANES)), picks & 127, axis=1
    )
    high_half = jnp.take_along_axis(
        jnp.broadcast_to(table_ref[pl.ds(1, 1)], (ENTRY_ROWS, LANES)), picks & 127, axis=1
    )
    weights = jnp.where(picks < LANES, low_half, high_half)
    values = weights * jnp.concatenate([source] * 4, axis=0)
    high, low = two_terms(values)
    partial[pl.ds(0, ENTRY_ROWS)] = high.astype(F32)
    partial[pl.ds(ENTRY_ROWS, ENTRY_ROWS)] = low.astype(F32)

    def bin_row(row, carry):
        same = lax.broadcasted_iota(jnp.int32, (TIME_BINS, LANES), 0) == bin_ref[pl.ds(row, 1)]
        at = pl.multiple_of(row * LANES, LANES)
        bin_hot[pl.ds(0, TIME_BINS), pl.ds(at, LANES)] = jnp.where(same, partial[pl.ds(row, 1)], 0.0).astype(BF16)
        bin_hot[pl.ds(TIME_BINS, TIME_BINS), pl.ds(at, LANES)] = jnp.where(
            same, partial[pl.ds(ENTRY_ROWS + row, 1)], 0.0
        ).astype(BF16)
        return carry

    lax.fori_loop(0, ENTRY_ROWS, bin_row, 0)

    total = dot_last(observer_hot[...], bin_hot[...])
    partial[...] = total[:, :TIME_BINS] + total[:, TIME_BINS:]

    mine = me_a * 2 + core

    def part_copy(step):
        other = lax.rem(mine + step, 8)
        other_z = me_z - core + lax.rem(other, 2)
        return pltpu.make_async_remote_copy(
            src_ref=partial.at[pl.ds(pl.multiple_of(other * 64, 64), 64)],
            dst_ref=part_recv.at[step - 1],
            send_sem=part_send_sem.at[step - 1],
            recv_sem=part_recv_sem.at[step - 1],
            device_id=(other // 2, other_z),
            device_id_type=MESH,
        )

    for step in range(1, 8):
        part_copy(step).start()
    reduce_moments(1, 0, FL)
    reduce_moments(1, 1, FL)
    total = partial[pl.ds(pl.multiple_of(mine * 64, 64), 64)]
    for step in range(1, 8):
        part_copy(step).wait_recv()
        total = total + part_recv[step - 1]
    for owner in range(16):
        owner_send[owner, pl.ds(0, 4)] = total[4 * owner : 4 * owner + 4]
        owner_send[owner, pl.ds(4, 4)] = jnp.zeros((4, LANES), F32)

    def owner_copy(step):
        other = lax.rem(chip + step, 16)
        return pltpu.make_async_remote_copy(
            src_ref=owner_send.at[other],
            dst_ref=owner_hbm.at[step],
            send_sem=owner_send_sem.at[step - 1],
            recv_sem=owner_recv_sem.at[step - 1],
            device_id=(me_a, 2 * other + core),
            device_id_type=MESH,
        )

    for step in range(1, 16):
        owner_copy(step).start()
    own_copy = pltpu.make_async_copy(owner_send.at[chip], owner_hbm.at[0], owner_sem)
    own_copy.start()
    for part in range(2):
        wait_starts(1, part)
    for copy in halo_copies(1):
        copy.wait_recv()

    own_copy.wait()
    for step in range(1, 16):
        owner_copy(step).wait_recv()
    for keep in keeps:
        keep.wait()

    for which in range(2):
        for part in range(2):
            wait_moment_sends(which, part)
            wait_start_sends(which, part)
            for step in range(1, AXIAL):
                edge_copy(which, part, step).wait_send()
        for copy in halo_copies(which):
            copy.wait_send()
    for step in range(1, 8):
        part_copy(step).wait_send()
    for step in range(1, 16):
        owner_copy(step).wait_send()
    for which in range(2):
        plane_wait(which, plane_send_sem)
        for step in range(1, AXIAL):
            axial_copy(which, step).wait_send()


def per_device(
    density,
    velocity,
    pressure,
    axial_metric,
    azim_metric,
    volume,
    radial_term,
    panel_area,
    observer_ids,
    bin_ids,
    weight_ids,
    bin_weights,
):
    sent, taken, full = both_tables()
    rows = PLANES * ROWS
    slabs = [PLANES * count for _, count in PARTS]
    hbm = pl.BlockSpec(memory_space=pltpu.HBM)
    dma = pltpu.SemaphoreType.DMA
    lined, halo, starts, parts = pl.pallas_call(
        kernel,
        out_shape=(
            jax.ShapeDtypeStruct((ROWS, SLAB, LANES), F32),
            jax.ShapeDtypeStruct((2, 2, SLAB, LANES), F32),
            jax.ShapeDtypeStruct((SLOTS, TILE_ROWS, LANES), F32),
            jax.ShapeDtypeStruct((16, 8, TIME_BINS), F32),
        ),
        in_specs=[hbm] * 16,
        out_specs=(hbm, hbm, hbm, hbm),
        scratch_shapes=[
            pltpu.VMEM((2, 2 * LANES, 2 * LANES), BF16),
            pltpu.VMEM((2, 2, 32, 2 * LANES), BF16),
            pltpu.VMEM((2, 2, 64, 2 * LANES), BF16),
            pltpu.VMEM((rows, LANES), F32),
            pltpu.VMEM((3, rows, LANES), F32),
            pltpu.VMEM((rows, LANES), F32),
            pltpu.VMEM((3, rows, LANES), F32),
            pltpu.VMEM((3, rows, LANES), F32),
            pltpu.VMEM((rows, LANES), F32),
            pltpu.VMEM((FIELDS, rows, LANES), F32),
            pltpu.VMEM((ROWS, LANES), F32),
            pltpu.VMEM((ENTRY_ROWS, LANES), jnp.int32),
            pltpu.VMEM((ENTRY_ROWS, LANES), jnp.int32),
            pltpu.VMEM((ENTRY_ROWS, LANES), jnp.int32),
            pltpu.VMEM((2, LANES), F32),
            pltpu.VMEM((2, ROWS, NAZ), F32),
            pltpu.VMEM((2, NA, LANES), F32),
            pltpu.VMEM((ROWS, SLAB, LANES), F32),
            pltpu.VMEM((ROWS, SLAB, LANES), F32),
            pltpu.VMEM((ROWS, PLANES, LANES), F32),
            *[pltpu.VMEM((2, ROWS * slab, 2 * LANES), BF16) for slab in slabs],
            *[pltpu.VMEM((ROWS, slab, LANES), F32) for slab in slabs],
            *[pltpu.VMEM((2, 2, 8, 4 * slab), F32) for slab in slabs],
            *[pltpu.VMEM((2, AXIAL, 8, 4 * slab), F32) for slab in slabs],
            pltpu.VMEM((2, SLOTS, TILE_ROWS, LANES), F32),
            pltpu.VMEM((2, 2, AZIM, 16, LANES), F32),
            pltpu.VMEM((2, 2, AZIM, 16, LANES), F32),
            pltpu.VMEM((SLOTS, TILE_ROWS, LANES), F32),
            pltpu.VMEM((2, 1, SLAB, LANES), F32),
            pltpu.VMEM((OBSERVERS, ENTRY_ROWS * LANES), BF16),
            pltpu.VMEM((2 * TIME_BINS, ENTRY_ROWS * LANES), BF16),
            pltpu.VMEM((OBSERVERS, TIME_BINS), F32),
            pltpu.VMEM((7, 64, TIME_BINS), F32),
            pltpu.VMEM((16, 8, TIME_BINS), F32),
            pltpu.VMEM((2, ROWS, LANES), F32),
            pltpu.VMEM((2, AZIM, ROWS, LANES), F32),
            pltpu.VMEM((2, ROWS, LANES), F32),
            pltpu.VMEM((2, AXIAL, ROWS, LANES), F32),
            pltpu.VMEM((BLOCKS // 2, ROWS, LANES), F32),
            dma((2,)),
            dma(()),
            dma((11,)),
            dma((5, BLOCKS // 2)),
            dma((2, BLOCKS // 2)),
            dma((2, 2, 3)),
            dma((2, 2, 3)),
            dma((2, 2)),
            dma((2, 2)),
            dma((2, 2)),
            dma((2, 2)),
            dma((2, 2, 2)),
            dma((2, 2, 2)),
            dma((7,)),
            dma((7,)),
            dma((15,)),
            dma((15,)),
            dma((2,)),
            dma((2,)),
            dma((2, 3)),
            dma((2, 3)),
        ],
        compiler_params=pltpu.CompilerParams(
            collective_id=0, has_side_effects=True
        ),
    )(
        jnp.asarray(sent),
        jnp.asarray(taken),
        density.reshape(rows, LANES),
        velocity.reshape(3, rows, LANES),
        pressure.reshape(rows, LANES),
        axial_metric.reshape(3, rows, LANES),
        azim_metric.reshape(3, rows, LANES),
        volume.reshape(rows, LANES),
        radial_term.reshape(FIELDS, rows, LANES),
        panel_area,
        observer_ids.reshape(ENTRY_ROWS, LANES),
        bin_ids.reshape(ENTRY_ROWS, LANES),
        weight_ids.reshape(ENTRY_ROWS, LANES),
        bin_weights.reshape(2, LANES),
        jnp.asarray(azimuth_rows()),
        jnp.asarray(full),
    )
    state, signals = pl.pallas_call(
        finish_kernel,
        out_shape=(
            jax.ShapeDtypeStruct((FIELDS, rows, LANES), F32),
            jax.ShapeDtypeStruct((4, TIME_BINS), F32),
        ),
        in_specs=[hbm] * 4,
        out_specs=(hbm, hbm),
        scratch_shapes=[
            pltpu.VMEM((ROWS, FIELDS, PLANES, LANES), F32),
            pltpu.VMEM((4, FIELDS, PLANES, LANES), F32),
            pltpu.VMEM((SLOTS, TILE_ROWS, LANES), F32),
            pltpu.VMEM((FIELDS, rows, LANES), F32),
            pltpu.VMEM((16, 8, TIME_BINS), F32),
            pltpu.VMEM((4, TIME_BINS), F32),
            dma((BLOCKS // 2, 3)),
            dma((BLOCKS // 2,)),
            dma((2,)),
        ],
    )(
        lined.reshape(ROWS, FIELDS, PLANES, LANES),
        halo.reshape(4, FIELDS, PLANES, LANES),
        starts,
        parts,
    )
    return state.reshape(FIELDS, PLANES, ROWS, LANES), signals


def solution(mesh):
    placed = (
        P(None, "azim", "axial"),
        P(None, None, "azim", "axial"),
        P(None, "azim", "axial"),
        P(None, None, "azim", "axial"),
        P(None, None, "azim", "axial"),
        P(None, "azim", "axial"),
        P(None, None, "azim", "axial"),
        P("azim", "axial"),
        P(None, "azim", "axial"),
        P(None, "azim", "axial"),
        P(None, "azim", "axial"),
        P(),
    )
    return jax.shard_map(
        per_device,
        mesh=mesh,
        in_specs=placed,
        out_specs=(P(None, None, "azim", "axial"), P(("axial", "azim"), None)),
        check_vma=False,
    )
```

```python
import functools
import math

import jax
import jax.numpy as jnp
import ml_dtypes
import numpy as np
from jax import lax
from jax.experimental import pallas as pl
from jax.experimental.pallas import tpu as pltpu
from jax.sharding import PartitionSpec as P

F32 = jnp.float32
BF16 = jnp.bfloat16
MESH = pl.DeviceIdType.MESH

PLANES = 64
FIELDS = 5
ROWS = 8
LANES = 128
AXIAL = 4
AZIM = 32
NA = AXIAL * LANES
NAZ = AZIM * ROWS
SLAB = FIELDS * PLANES
BLOCKS = PLANES // 8
SLOTS = 2 * BLOCKS
TILE_ROWS = 8 * FIELDS
PARTS = ((0, 3), (3, 2))
PART_OF = (0, 0, 0, 1, 1)
SHARE = (((0, 16), (16, 8)), ((24, 8), (32, 8)))
STEPS = (2, 1, 3, 0)
AWAY = tuple((dz, dy) for dz in STEPS[:3] for dy in STEPS[:3]) + ((2, 0), (0, 2), (1, 0), (3, 0), (0, 1), (0, 3))
ENTRY_ROWS = 32
OBSERVERS = 512
TIME_BINS = 128
PEERS = (AZIM - 1) + 2 * (AXIAL - 1)

SECTION = 0.25
DERIV_ALPHA = 1.0 / 3.0
BETA = 0.499


def decay_root(alpha):
    return (-1.0 + math.sqrt(1.0 - 4.0 * alpha * alpha)) / (2.0 * alpha)


DL = decay_root(DERIV_ALPHA)
FL = decay_root(BETA)
C1 = (1.0 / 36.0) / DERIV_ALPHA
DS = 1.0 / math.sqrt(1.0 - 4.0 * DERIV_ALPHA**2)
DK = (7.0 / 9.0 - C1) * DS * (1.0 / DL - DL)
FC = [
    (11.0 + 10.0 * BETA) / 16.0,
    (15.0 + 34.0 * BETA) / 32.0,
    (-3.0 + 6.0 * BETA) / 16.0,
    (1.0 - 2.0 * BETA) / 32.0,
]
FS = 1.0 / math.sqrt(1.0 - 4.0 * BETA**2)
E2 = FC[3] / (2.0 * BETA)
E1 = (FC[2] / 2.0 - E2) / BETA
E0 = (FC[1] / 2.0 - E1 - BETA * E2) / BETA
FK = (FC[0] - E0 - 2.0 * BETA * E1) * FS


def split(values):
    high = values.astype(ml_dtypes.bfloat16)
    low = (values - high.astype(np.float64)).astype(ml_dtypes.bfloat16)
    return high, low


def axial_tables(root, scale, band):
    n, w = NA, LANES
    index = np.arange(n)
    green = scale * (
        np.power(root, np.abs(index[:, None] - index[None, :]))
        - np.power(root, 2 * n - index[:, None] - index[None, :])
    )
    side = np.zeros((n, n))
    for shift, value in band.items():
        side += value * np.eye(n, k=shift)
    whole = green @ side
    left = np.zeros((AXIAL, w))
    right = np.zeros((AXIAL, w))
    for k in range(AXIAL):
        cols = slice(k * w, (k + 1) * w)
        lo, hi = max(0, k * w - 3), min(n, (k + 1) * w + 3)
        m = np.arange(lo, hi)
        left[k] = np.power(root, ((k + 1) * w - m).astype(np.float64)) @ side[lo:hi, cols]
        right[k] = (
            np.power(root, (m - k * w + 1).astype(np.float64))
            - np.power(root, (2 * n - m - k * w + 1).astype(np.float64))
        ) @ side[lo:hi, cols]
    t = np.arange(w)
    full = np.stack([whole[d * w : (d + 1) * w].T for d in range(AXIAL)]).astype(np.float32)
    sent = np.zeros((AXIAL, 2, 32, 2 * w), ml_dtypes.bfloat16)
    taken = np.zeros((AXIAL, 2, 64, 2 * w), ml_dtypes.bfloat16)
    for d in range(AXIAL):
        for half in range(2):
            rows = np.zeros((16, w))
            base = half * 4
            rows[base] = left[d]
            rows[base + 1, w - 1] = 1.0
            rows[base + 2, w - 2] = 1.0
            rows[8 + base] = right[d]
            rows[8 + base + 1, 0] = 1.0
            rows[8 + base + 2, 1] = 1.0
            high, low = split(rows)
            sent[d, half] = np.concatenate(
                [np.concatenate([high, high], axis=1), np.concatenate([low, low], axis=1)], axis=0
            )
            rows = np.zeros((32, w))
            for k in range(AXIAL):
                row = k * 8 + half * 4
                i = d * w + t
                if k < d:
                    rows[row] = scale * (
                        np.power(root, (i - (k + 1) * w).astype(np.float64))
                        - np.power(root, (2 * n - i - (k + 1) * w).astype(np.float64))
                    )
                    if k == d - 1:
                        for edge in range(2):
                            col = d * w - 1 - edge
                            for near in range(2 - edge):
                                rows[row + 1 + edge, near] = (
                                    whole[d * w + near, col] - rows[row, near] * left[k, col - k * w]
                                )
                if k > d:
                    rows[row] = scale * np.power(root, (k * w - 1 - i).astype(np.float64))
                    if k == d + 1:
                        for edge in range(2):
                            col = k * w + edge
                            for near in range(2 - edge):
                                rows[row + 1 + edge, w - 1 - near] = (
                                    whole[k * w - 1 - near, col] - rows[row, w - 1 - near] * right[k, edge]
                                )
            high, low = split(rows)
            pair = np.concatenate([high, low], axis=1)
            taken[d, half] = np.concatenate([pair, pair], axis=0)
    return sent, taken, full


def both_tables():
    deriv = axial_tables(DL, DS, {1: 7.0 / 9.0, -1: -7.0 / 9.0, 2: 1.0 / 36.0, -2: -1.0 / 36.0})
    band = {0: FC[0]}
    for shift in range(1, 4):
        band[shift] = band[-shift] = FC[shift] / 2.0
    smooth = axial_tables(FL, FS, band)
    return [np.stack(pair, axis=1) for pair in zip(deriv, smooth)]


def azimuth_rows():
    gap = np.arange(NAZ)
    slope = DK * (np.power(DL, gap) - np.power(DL, NAZ - gap)) / (1.0 - DL**NAZ)
    slope[0] = 0.0
    slope[1] += C1
    slope[-1] -= C1
    line = FK * (np.power(FL, gap) + np.power(FL, NAZ - gap)) / (1.0 - FL**NAZ)
    line[0] = FK * (1.0 + 2.0 * FL**NAZ / (1.0 - FL**NAZ)) + E0
    for shift, value in ((1, E1), (2, E2)):
        line[shift] += value
        line[-shift] += value
    rows = np.arange(ROWS)
    at = (gap[None, :] - rows[:, None]) % NAZ
    return np.stack([slope[at], line[at]]).astype(np.float32)


def two_terms(value):
    high = value.astype(BF16)
    low = (value - high.astype(F32)).astype(BF16)
    return high, low


def dot_last(left, right):
    return lax.dot_general(left, right, (((1,), (1,)), ((), ())), preferred_element_type=F32)


def dot_first(left, right):
    return lax.dot_general(left, right, (((0,), (0,)), ((), ())), preferred_element_type=F32)


def start_of(starts, group, field, side):
    return jnp.concatenate(
        [starts[4 * group + 2 * half + side, pl.ds(8 * field, 8)] for half in range(2)], axis=0
    )


def finish_kernel(
    near_hbm, start_hbm, part_hbm, state_hbm, signal_hbm, near, starts, final, parts, signals, load_sem, store_sem, part_sem
):
    part_copy = pltpu.make_async_copy(part_hbm, parts, part_sem.at[0])
    signal_copy = pltpu.make_async_copy(signals, signal_hbm, part_sem.at[1])

    def loads(group):
        slots = pl.ds(4 * group, 4)
        planes = pl.ds(16 * group, 16)
        return [
            pltpu.make_async_copy(start_hbm.at[slots], starts.at[slots], load_sem.at[group, 0]),
            pltpu.make_async_copy(near_hbm.at[:, :, planes], near.at[:, :, planes], load_sem.at[group, 1]),
        ]

    def store(group):
        planes = pl.ds(128 * group, 128)
        return pltpu.make_async_copy(final.at[:, planes], state_hbm.at[:, planes], store_sem.at[group])

    for group in range(BLOCKS // 2):
        for load in loads(group):
            load.start()
    part_copy.start()

    for group in range(BLOCKS // 2):
        for load in loads(group):
            load.wait()
        planes = pl.ds(16 * group, 16)
        for field in range(FIELDS):
            up = FK * start_of(starts, group, field, 0)
            down = FK * start_of(starts, group, field, 1)
            for row in range(ROWS):
                result = near[row, field, planes] + (FL**row * up + FL ** (ROWS - 1 - row) * down)
                final[field, pl.ds(128 * group + row, 16, stride=ROWS)] = result
        store(group).start()
        if group == 0:
            part_copy.wait()
            signals[...] = jnp.sum(parts[...], axis=0)[:4]
            signal_copy.start()

    for group in range(BLOCKS // 2):
        store(group).wait()
    signal_copy.wait()


def kernel(
    sent_hbm,
    taken_hbm,
    density_hbm,
    velocity_hbm,
    pressure_hbm,
    axial_hbm,
    azim_hbm,
    volume_hbm,
    radial_hbm,
    area_hbm,
    observer_hbm,
    bin_hbm,
    weight_hbm,
    table_hbm,
    azimuth_hbm,
    full_hbm,
    near_hbm,
    start_hbm,
    owner_hbm,
    own,
    sent,
    taken,
    density,
    velocity,
    pressure,
    axial_metric,
    azim_metric,
    volume,
    radial,
    area_ref,
    observer_ref,
    bin_ref,
    weight_ref,
    table_ref,
    azimuth_ref,
    full,
    azim_flux,
    base,
    ratio,
    cells_a,
    cells_b,
    lined_a,
    lined_b,
    edge_send_a,
    edge_send_b,
    edge_recv_a,
    edge_recv_b,
    moment_send,
    moment_recv,
    start_send,
    start_recv,
    deriv_halo,
    filter_halo,
    near,
    observer_hot,
    bin_hot,
    partial,
    part_recv,
    owner_send,
    plane_send,
    plane_recv,
    axial_send,
    axial_recv,
    panel_axial,
    keep_sem,
    owner_sem,
    load_sem,
    early_sem,
    late_sem,
    edge_send_sem,
    edge_recv_sem,
    moment_send_sem,
    moment_recv_sem,
    start_send_sem,
    start_recv_sem,
    halo_send_sem,
    halo_recv_sem,
    part_send_sem,
    part_recv_sem,
    owner_send_sem,
    owner_recv_sem,
    plane_send_sem,
    plane_recv_sem,
    axial_send_sem,
    axial_recv_sem,
):
    me_a = lax.axis_index("axial")
    me_z = lax.axis_index("azim")
    core = lax.rem(me_z, 2)
    chip = me_z // 2
    twin = me_z + 1 - 2 * core
    after = lax.rem(me_z + 1, AZIM)
    before = lax.rem(me_z + AZIM - 1, AZIM)

    def chip_at(step):
        return 4 * lax.rem(chip // 4 + step[0], 4) + lax.rem(chip + step[1], 4)

    def group_at(step):
        away = jnp.where(step == 0, STEPS[0], jnp.where(step == 1, STEPS[1], jnp.where(step == 2, STEPS[2], 0)))
        return lax.rem(chip // 4 + away, 4)

    def early_loads(group):
        part = pl.ds(pl.multiple_of(group * 128, 128), 128)
        whole = slice(None)
        return [
            pltpu.make_async_copy(source.at[where], dest.at[where], early_sem.at[number, group])
            for number, (source, dest, where) in enumerate(
                (
                    (density_hbm, density, (part,)),
                    (velocity_hbm, velocity, (whole, part)),
                    (pressure_hbm, pressure, (part,)),
                    (volume_hbm, volume, (part,)),
                    (azim_hbm, azim_metric, (whole, part)),
                )
            )
        ]

    def late_loads(group):
        part = pl.ds(pl.multiple_of(group * 128, 128), 128)
        return [
            pltpu.make_async_copy(axial_hbm.at[:, part], axial_metric.at[:, part], late_sem.at[0, group]),
            pltpu.make_async_copy(radial_hbm.at[:, part], radial.at[:, part], late_sem.at[1, group]),
        ]

    loads = [
        pltpu.make_async_copy(area_hbm, area_ref, load_sem.at[0]),
        pltpu.make_async_copy(observer_hbm, observer_ref, load_sem.at[1]),
        pltpu.make_async_copy(bin_hbm, bin_ref, load_sem.at[2]),
        pltpu.make_async_copy(weight_hbm, weight_ref, load_sem.at[3]),
        pltpu.make_async_copy(table_hbm, table_ref, load_sem.at[4]),
        pltpu.make_async_copy(azimuth_hbm, azimuth_ref, load_sem.at[5]),
        pltpu.make_async_copy(full_hbm.at[me_a], full, load_sem.at[6]),
    ]
    for which in range(2):
        loads.append(pltpu.make_async_copy(sent_hbm.at[me_a, which], sent.at[which], load_sem.at[7 + 2 * which]))
        loads.append(pltpu.make_async_copy(taken_hbm.at[me_a, which], taken.at[which], load_sem.at[8 + 2 * which]))
    for step in range(BLOCKS // 2):
        for load in early_loads(group_at(step)):
            load.start()

    starts = (start_recv, start_hbm)
    cells, lined = (cells_a, cells_b), (lined_a, lined_b)
    edge_send, edge_recv = (edge_send_a, edge_send_b), (edge_recv_a, edge_recv_b)

    barrier = pltpu.get_barrier_semaphore()

    def greet_azim(step, carry):
        other = lax.rem(me_z + step, AZIM)
        pl.semaphore_signal(barrier, inc=1, device_id=(me_a, other), device_id_type=MESH)
        return carry

    lax.fori_loop(1, AZIM, greet_azim, 0)

    def greet_axial(step, carry):
        other = lax.rem(me_a + step, AXIAL)
        pl.semaphore_signal(barrier, inc=1, device_id=(other, me_z), device_id_type=MESH)
        pl.semaphore_signal(barrier, inc=1, device_id=(other, twin), device_id_type=MESH)
        return carry

    lax.fori_loop(1, AXIAL, greet_axial, 0)

    for part in range(2):
        for which in range(2):
            edge_recv[part][which, pl.ds(me_a, 1)] = jnp.zeros((1, 8, 4 * PLANES * PARTS[part][1]), F32)

    def moment_source(which, part, slot, share):
        first, rows = SHARE[part][share]
        return moment_send.at[which, slot, pl.ds(first, rows)]

    def moment_copy(which, part, slot, share):
        return pltpu.make_async_remote_copy(
            src_ref=moment_source(which, part, slot, share),
            dst_ref=moment_recv.at[which, part, me_z, pl.ds(0, SHARE[part][share][1])],
            send_sem=moment_send_sem.at[which, part],
            recv_sem=moment_recv_sem.at[which, part],
            device_id=(me_a, 2 * slot + share),
            device_id_type=MESH,
        )

    def send_moments(which, part, step):
        row = 4 * group_at(step)
        for turn in STEPS[:3]:
            for share in range(2):
                moment_copy(which, part, row + lax.rem(chip + turn, 4), share).start()

        @pl.when(step < 3)
        def _():
            for share in range(2):
                moment_copy(which, part, row + lax.rem(chip, 4), share).start()

        for share in range(2):

            @pl.when(jnp.logical_and(step == 3, core == share))
            def _():
                moment_copy(which, part, chip, 1 - share).start()
                pltpu.make_async_copy(
                    moment_source(which, part, chip, share),
                    moment_recv.at[which, part, me_z, pl.ds(0, SHARE[part][share][1])],
                    moment_recv_sem.at[which, part],
                ).start()

    def wait_moment_sends(which, part):
        for share in range(2):

            @pl.when(core == share)
            def _():
                rows = pl.ds(8 * PARTS[part][0], 8 * PARTS[part][1])
                sent_rows = moment_send.at[which, pl.ds(0, SLOTS - 1), rows]
                pltpu.make_async_copy(sent_rows, sent_rows, moment_send_sem.at[which, part]).wait()
                sent_rows = moment_source(which, part, SLOTS - 1, 1 - share)
                pltpu.make_async_copy(sent_rows, sent_rows, moment_send_sem.at[which, part]).wait()

    def reduce_moments(which, part, root):
        factor = root**ROWS
        wrap = 1.0 / (1.0 - root**NAZ)
        side = lax.rem(chip, 2)

        def place(step):
            return step + side * (AZIM - 1 - 2 * step)

        for share in range(2):
            first_row, count = SHARE[part][share]
            rows, there = pl.ds(0, count), pl.ds(first_row, count)

            @pl.when(core == share)
            def _():
                arrived = moment_recv.at[which, part, :, rows]
                pltpu.make_async_copy(arrived, arrived, moment_recv_sem.at[which, part]).wait()

                def gather(step, total):
                    return factor * total + moment_recv[which, part, place(step), rows]

                first = lax.fori_loop(0, AZIM, gather, jnp.zeros((count, LANES), F32), unroll=8) * wrap

                def follow(step, now):
                    other = place(step)
                    start_send[which, part, other, rows] = now
                    return factor * now + moment_recv[which, part, other, rows]

                lax.fori_loop(0, AZIM, follow, first, unroll=8)

                def hand_out(other):
                    pltpu.make_async_remote_copy(
                        src_ref=start_send.at[which, part, other, rows],
                        dst_ref=starts[which].at[chip, there],
                        send_sem=start_send_sem.at[which, part],
                        recv_sem=start_recv_sem.at[which, part],
                        device_id=(me_a, other),
                        device_id_type=MESH,
                    ).start()

                for step in AWAY:
                    for half in range(2):
                        hand_out(2 * chip_at(step) + half)
                hand_out(twin)
                pltpu.make_async_copy(
                    start_send.at[which, part, me_z, rows],
                    starts[which].at[chip, there],
                    start_recv_sem.at[which, part],
                ).start()

    def wait_starts(which, part):
        arrived = starts[which].at[:, pl.ds(8 * PARTS[part][0], 8 * PARTS[part][1])]
        pltpu.make_async_copy(arrived, arrived, start_recv_sem.at[which, part]).wait()

    def wait_start_sends(which, part):
        for share in range(2):

            @pl.when(core == share)
            def _():
                gone = start_send.at[which, part, pl.ds(0, AZIM - 1), pl.ds(0, SHARE[part][share][1])]
                pltpu.make_async_copy(gone, gone, start_send_sem.at[which, part]).wait()

    def moments_of(values, root):
        up = root * values[0]
        for row in range(1, ROWS):
            up = root * (up + values[row])
        down = root * values[ROWS - 1]
        for row in range(ROWS - 2, -1, -1):
            down = root * (down + values[row])
        return up, down

    def keep_moments(which, group, field, values, root):
        up, down = moments_of(values, root)
        for half in range(2):
            for side, value in ((0, up), (1, down)):
                moment_send[which, 4 * group + 2 * half + side, pl.ds(8 * field, 8)] = value[8 * half : 8 * half + 8]

    def halo_copies(which):
        copies = []
        for part in range(2):
            if which == 1:
                source, halo, depth = lined[part], filter_halo, 2
                there = pl.ds(PLANES * PARTS[part][0], PLANES * PARTS[part][1])
            else:
                source, halo, depth = azim_flux, deriv_halo, 1
                there = pl.ds(0, SLAB)
                if part == 1:
                    break
            for side, other, rows in ((0, after, pl.ds(ROWS - depth, depth)), (1, before, pl.ds(0, depth))):
                copies.append(
                    pltpu.make_async_remote_copy(
                        src_ref=source.at[rows],
                        dst_ref=halo.at[side, :, there],
                        send_sem=halo_send_sem.at[which, part, side],
                        recv_sem=halo_recv_sem.at[which, part, side],
                        device_id=(me_a, other),
                        device_id_type=MESH,
                    )
                )
        return copies

    def edge_copy(which, part, step):
        other = lax.rem(me_a + step, AXIAL)
        down = jnp.where(other < me_a, 1, 0)
        return pltpu.make_async_remote_copy(
            src_ref=edge_send[part].at[which, down],
            dst_ref=edge_recv[part].at[which, me_a],
            send_sem=edge_send_sem.at[which, part, step - 1],
            recv_sem=edge_recv_sem.at[which, part, step - 1],
            device_id=(other, me_z),
            device_id_type=MESH,
        )

    def send_edges(which, part):
        slab = PLANES * PARTS[part][1]

        def piece(step, carry):
            at = pl.multiple_of(step * 2 * slab, 2 * slab)
            total = dot_last(sent[which, 0], cells[part][which, pl.ds(at, 2 * slab)]) + dot_last(
                sent[which, 1], cells[part][which, pl.ds(4 * slab + at, 2 * slab)]
            )
            total = total[:16] + total[16:]
            edge_send[part][which, 0, :, pl.ds(at, 2 * slab)] = total[:8]
            edge_send[part][which, 1, :, pl.ds(at, 2 * slab)] = total[8:]
            return carry

        lax.fori_loop(0, 2, piece, 0, unroll=True)
        for step in STEPS[:3]:
            edge_copy(which, part, step).start()

    def own_part(which, part):
        slab = PLANES * PARTS[part][1]

        def piece(step, carry):
            at = pl.multiple_of(step * 2 * slab, 2 * slab)
            total = jnp.dot(cells[part][which, pl.ds(at, 2 * slab)], own[which], preferred_element_type=F32)
            lined[part][pl.ds(2 * step, 2)] = (total[:, :LANES] + total[:, LANES:]).reshape(2, slab, LANES)
            return carry

        lax.fori_loop(0, 4, piece, 0, unroll=True)

    def add_edges(which, part):
        slab = PLANES * PARTS[part][1]
        for step in range(1, AXIAL):
            edge_copy(which, part, step).wait_recv()

        def piece(step, carry):
            at = pl.multiple_of(lax.rem(step, 2) * 2 * slab, 2 * slab)
            received = edge_recv[part][which, :, :, pl.ds(at, 2 * slab)].reshape(32, 2 * slab)
            high, low = two_terms(received)
            total = dot_first(jnp.concatenate([high, low], axis=0), taken[which, step // 2])
            total = (total[:, :LANES] + total[:, LANES:]).reshape(2, slab, LANES)
            lined[part][pl.ds(2 * step, 2)] = lined[part][pl.ds(2 * step, 2)] + total
            return carry

        lax.fori_loop(0, 4, piece, 0, unroll=True)

    def keep_cells(which, row, field, group, value):
        part = PART_OF[field]
        first, count = PARTS[part]
        high, low = two_terms(value)
        at = pl.multiple_of((row * count + field - first) * PLANES + group * 16, 16)
        cells[part][which, pl.ds(at, 16), pl.ds(0, LANES)] = high
        cells[part][which, pl.ds(at, 16), pl.ds(LANES, LANES)] = low

    def axial_copy(which, step):
        return pltpu.make_async_remote_copy(
            src_ref=axial_send.at[which],
            dst_ref=axial_recv.at[which, me_a],
            send_sem=axial_send_sem.at[which, step - 1],
            recv_sem=axial_recv_sem.at[which, step - 1],
            device_id=(lax.rem(me_a + step, AXIAL), me_z),
            device_id_type=MESH,
        )

    def send_axial(which, value):
        axial_send[which] = value
        axial_recv[which, pl.ds(me_a, 1)] = value[None]
        for step in STEPS[:3]:
            axial_copy(which, step).start()

    def take_axial(which):
        for step in range(1, AXIAL):
            axial_copy(which, step).wait_recv()
        line = jnp.concatenate([axial_recv[which, k] for k in range(AXIAL)], axis=1)
        return jnp.dot(line, full[which], preferred_element_type=F32, precision=lax.Precision.HIGHEST)

    def send_plane(which, value):
        plane_send[which] = value
        plane_recv[which, 0] = value

        def piece(other):
            pltpu.make_async_remote_copy(
                src_ref=plane_send.at[which],
                dst_ref=plane_recv.at[which, lax.rem(me_z - other + AZIM, AZIM)],
                send_sem=plane_send_sem.at[which],
                recv_sem=plane_recv_sem.at[which],
                device_id=(me_a, other),
                device_id_type=MESH,
            ).start()

        for step in AWAY:
            for half in range(2):
                piece(2 * chip_at(step) + half)
        piece(twin)

    def plane_wait(which, sem):
        part = plane_recv.at[which, pl.ds(1, AZIM - 1)]
        pltpu.make_async_copy(part, part, sem.at[which]).wait()

    def take_plane(which):
        plane_wait(which, plane_recv_sem)
        return jnp.dot(
            azimuth_ref[which],
            plane_recv[which].reshape(NAZ, LANES),
            preferred_element_type=F32,
            precision=lax.Precision.HIGHEST,
        )

    def flux_of(metric, at, rho, vel, prs, vol, heat):
        grad = [metric[comp, at] for comp in range(3)]
        contra = vol * (grad[0] * vel[0] + grad[1] * vel[1] + grad[2] * vel[2])
        flow = rho * contra
        push = vol * prs
        return [flow] + [flow * vel[comp] + grad[comp] * push for comp in range(3)] + [heat * contra]

    def cells_at(group, row):
        at = pl.ds(group * 128 + row, 16, stride=ROWS)
        rho, prs, vol = density[at], pressure[at], volume[at]
        vel = [velocity[comp, at] for comp in range(3)]
        energy = 2.5 * prs + 0.5 * rho * (vel[0] * vel[0] + vel[1] * vel[1] + vel[2] * vel[2])
        return at, rho, vel, prs, vol, energy

    def azim_group(step, carry):
        group = group_at(step)
        for load in early_loads(group):
            load.wait()
        for load in late_loads(group):
            load.start()
        flux = [[None] * ROWS for _ in range(FIELDS)]
        for row in range(ROWS):
            at, rho, vel, prs, vol, energy = cells_at(group, row)
            parts = flux_of(azim_metric, at, rho, vel, prs, vol, energy + prs)
            for field in range(FIELDS):
                flux[field][row] = parts[field]
                azim_flux[row, pl.ds(pl.multiple_of(field * PLANES + group * 16, 16), 16)] = parts[field]
        for field in range(FIELDS):
            keep_moments(0, group, field, flux[field], DL)

        @pl.when(step == 0)
        def _():
            pl.semaphore_wait(barrier, PEERS)

        send_moments(0, 0, step)
        return carry

    lax.fori_loop(0, BLOCKS // 2, azim_group, 0)

    for load in loads:
        load.start()

    def send_rest(step, carry):
        send_moments(0, 1, step)
        return carry

    lax.fori_loop(0, BLOCKS // 2, send_rest, 0)
    send_plane(0, azim_flux[:, 0] + azim_flux[:, 2 * PLANES])
    for copy in halo_copies(0):
        copy.start()

    def axial_group(group, carry):
        for load in late_loads(group):
            load.wait()
        for row in range(ROWS):
            at, rho, vel, prs, vol, energy = cells_at(group, row)
            state = [rho, rho * vel[0], rho * vel[1], rho * vel[2], energy]
            ratio[row, pl.ds(pl.multiple_of(group * 16, 16), 16)] = SECTION / vol
            for field in range(FIELDS):
                base[row, pl.ds(pl.multiple_of(field * PLANES + group * 16, 16), 16)] = (
                    state[field] + SECTION * radial[field, at]
                )
            parts = flux_of(axial_metric, at, rho, vel, prs, vol, energy + prs)
            for field in range(FIELDS):
                keep_cells(0, row, field, group, parts[field])
            panel_axial[group, pl.ds(row, 1)] = parts[0][:1] + parts[2][:1]
        return carry

    lax.fori_loop(0, BLOCKS // 2, axial_group, 0)
    send_axial(0, panel_axial[0])
    for load in loads:
        load.wait()
    send_edges(0, 0)
    send_edges(0, 1)

    ids = observer_ref[...]
    order = (
        lax.shift_right_logical(ids, 7) * 128
        + (lax.shift_right_logical(ids, 2) & 1) * 64
        + (lax.shift_right_logical(ids, 3) & 15) * 4
        + (ids & 3)
    )
    partial[pl.ds(0, ENTRY_ROWS)] = order.astype(F32)

    def hot_row(row, carry):
        wanted = partial[pl.ds(row, 1)].astype(jnp.int32)
        rows = lax.broadcasted_iota(jnp.int32, (OBSERVERS, LANES), 0)
        at = pl.multiple_of(row * LANES, LANES)
        observer_hot[:, pl.ds(at, LANES)] = jnp.where(rows == wanted, 1.0, 0.0).astype(BF16)
        same = lax.broadcasted_iota(jnp.int32, (TIME_BINS, LANES), 0) == bin_ref[pl.ds(row, 1)]
        bin_hot[pl.ds(0, TIME_BINS), pl.ds(at, LANES)] = jnp.where(same, 1.0, 0.0).astype(BF16)
        return carry

    lax.fori_loop(0, ENTRY_ROWS, hot_row, 0)

    for which in range(2):
        high, low = two_terms(full[which, pl.ds(pl.multiple_of(me_a * LANES, LANES), LANES)])
        for top in range(2):
            own[which, pl.ds(top * LANES, LANES), pl.ds(0, LANES)] = high
            own[which, pl.ds(top * LANES, LANES), pl.ds(LANES, LANES)] = low
    own_part(0, 0)
    own_part(0, 1)
    reduce_moments(0, 0, DL)
    reduce_moments(0, 1, DL)
    change = take_axial(0) + take_plane(0)
    send_axial(1, base[:, 0] + base[:, 2 * PLANES] - ratio[:, 0] * change)
    add_edges(0, 0)
    add_edges(0, 1)

    def section(part):
        first, count = PARTS[part]

        def section_group(group, carry):
            here = pl.ds(pl.multiple_of(group * 16, 16), 16)
            for field in range(first, first + count):
                at = pl.ds(pl.multiple_of(field * PLANES + group * 16, 16), 16)
                inside = pl.ds(pl.multiple_of((field - first) * PLANES + group * 16, 16), 16)
                flux = [deriv_halo[0, 0, at]] + [azim_flux[row, at] for row in range(ROWS)] + [deriv_halo[1, 0, at]]
                up = [start_of(start_recv, group, field, 0)]
                for row in range(ROWS - 1):
                    up.append(DL * (flux[row + 1] + up[-1]))
                down = [start_of(start_recv, group, field, 1)]
                for row in range(ROWS - 1, 0, -1):
                    down.append(DL * (flux[row + 1] + down[-1]))
                down = down[::-1]
                for row in range(ROWS):
                    deriv = DK * (down[row] - up[row]) + C1 * (flux[row + 2] - flux[row])
                    value = base[row, at] - ratio[row, here] * (lined[part][row, inside] + deriv)
                    keep_cells(1, row, field, group, value)
            return carry

        lax.fori_loop(0, BLOCKS // 2, section_group, 0)

    def smoothed_moments(part):
        first, count = PARTS[part]

        def moment_group(step, carry):
            group = group_at(step)
            for field in range(first, first + count):
                inside = pl.ds(pl.multiple_of((field - first) * PLANES + group * 16, 16), 16)
                keep_moments(1, group, field, [lined[part][row, inside] for row in range(ROWS)], FL)
            send_moments(1, part, step)
            return carry

        lax.fori_loop(0, BLOCKS // 2, moment_group, 0)

    wait_starts(0, 0)
    for copy in halo_copies(0):
        copy.wait_recv()
    section(0)
    send_edges(1, 0)
    send_plane(1, take_axial(1))
    wait_starts(0, 1)
    section(1)
    send_edges(1, 1)
    own_part(1, 0)
    own_part(1, 1)
    add_edges(1, 0)
    smoothed_moments(0)
    add_edges(1, 1)
    smoothed_moments(1)
    for copy in halo_copies(1):
        copy.start()

    source = area_ref[...] * (take_plane(1) - 1.0)
    picks = weight_ref[...]
    low_half = jnp.take_along_axis(
        jnp.broadcast_to(table_ref[pl.ds(0, 1)], (ENTRY_ROWS, LANES)), picks & 127, axis=1
    )
    high_half = jnp.take_along_axis(
        jnp.broadcast_to(table_ref[pl.ds(1, 1)], (ENTRY_ROWS, LANES)), picks & 127, axis=1
    )
    weights = jnp.where(picks < LANES, low_half, high_half)
    values = weights * jnp.concatenate([source] * 4, axis=0)
    high, low = two_terms(values)
    partial[pl.ds(0, ENTRY_ROWS)] = high.astype(F32)
    partial[pl.ds(ENTRY_ROWS, ENTRY_ROWS)] = low.astype(F32)

    def bin_row(row, carry):
        at = pl.multiple_of(row * LANES, LANES)
        mask = bin_hot[pl.ds(0, TIME_BINS), pl.ds(at, LANES)]
        for term in range(2):
            value = jnp.broadcast_to(partial[pl.ds(term * ENTRY_ROWS + row, 1)], (TIME_BINS, LANES)).astype(BF16)
            bin_hot[pl.ds(term * TIME_BINS, TIME_BINS), pl.ds(at, LANES)] = mask * value
        return carry

    lax.fori_loop(0, ENTRY_ROWS, bin_row, 0)

    total = dot_last(observer_hot[...], bin_hot[...])
    partial[...] = total[:, :TIME_BINS] + total[:, TIME_BINS:]

    mine = me_a * 2 + core

    def part_copy(step):
        other = lax.rem(mine + step, 8)
        other_z = me_z - core + lax.rem(other, 2)
        return pltpu.make_async_remote_copy(
            src_ref=partial.at[pl.ds(pl.multiple_of(other * 64, 64), 64)],
            dst_ref=part_recv.at[step - 1],
            send_sem=part_send_sem.at[step - 1],
            recv_sem=part_recv_sem.at[step - 1],
            device_id=(other // 2, other_z),
            device_id_type=MESH,
        )

    for step in range(1, 8):
        part_copy(step).start()
    reduce_moments(1, 0, FL)
    reduce_moments(1, 1, FL)
    total = partial[pl.ds(pl.multiple_of(mine * 64, 64), 64)]
    for step in range(1, 8):
        part_copy(step).wait_recv()
        total = total + part_recv[step - 1]
    for owner in range(16):
        owner_send[owner, pl.ds(0, 4)] = total[4 * owner : 4 * owner + 4]
        owner_send[owner, pl.ds(4, 4)] = jnp.zeros((4, LANES), F32)

    def owner_copy(step):
        other = lax.rem(chip + step, 16)
        return pltpu.make_async_remote_copy(
            src_ref=owner_send.at[other],
            dst_ref=owner_hbm.at[step],
            send_sem=owner_send_sem.at[step - 1],
            recv_sem=owner_recv_sem.at[step - 1],
            device_id=(me_a, 2 * other + core),
            device_id_type=MESH,
        )

    for step in range(1, 16):
        owner_copy(step).start()
    own_copy = pltpu.make_async_copy(owner_send.at[chip], owner_hbm.at[0], owner_sem)
    own_copy.start()
    for copy in halo_copies(1):
        copy.wait_recv()

    def near_group(group, carry):
        for field in range(FIELDS):
            part = PART_OF[field]
            at = pl.ds(pl.multiple_of(field * PLANES + group * 16, 16), 16)
            inside = pl.ds(pl.multiple_of((field - PARTS[part][0]) * PLANES + group * 16, 16), 16)
            value = [filter_halo[0, row, at] for row in range(2)]
            value += [lined[part][row, inside] for row in range(ROWS)]
            value += [filter_halo[1, row, at] for row in range(2)]
            up = [None]
            down = [None]
            for row in range(ROWS - 1):
                up.append(FL * value[row + 2] if row == 0 else FL * (value[row + 2] + up[-1]))
                back = value[ROWS + 1 - row]
                down.append(FL * back if row == 0 else FL * (back + down[-1]))
            down = down[::-1]
            for row in range(ROWS):
                tails = up[row] if row == ROWS - 1 else down[row] if row == 0 else up[row] + down[row]
                edges = E1 * (value[row + 1] + value[row + 3]) + E2 * (value[row] + value[row + 4])
                near[row, at] = FK * tails + (FK + E0) * value[row + 2] + edges
        return carry

    lax.fori_loop(0, BLOCKS // 2, near_group, 0)
    keep = pltpu.make_async_copy(near, near_hbm, keep_sem)
    keep.start()
    for part in range(2):
        wait_starts(1, part)

    own_copy.wait()
    for step in range(1, 16):
        owner_copy(step).wait_recv()
    keep.wait()

    for which in range(2):
        for part in range(2):
            wait_moment_sends(which, part)
            wait_start_sends(which, part)
            for step in range(1, AXIAL):
                edge_copy(which, part, step).wait_send()
        for copy in halo_copies(which):
            copy.wait_send()
    for step in range(1, 8):
        part_copy(step).wait_send()
    for step in range(1, 16):
        owner_copy(step).wait_send()
    for which in range(2):
        plane_wait(which, plane_send_sem)
        for step in range(1, AXIAL):
            axial_copy(which, step).wait_send()


def per_device(
    density,
    velocity,
    pressure,
    axial_metric,
    azim_metric,
    volume,
    radial_term,
    panel_area,
    observer_ids,
    bin_ids,
    weight_ids,
    bin_weights,
):
    sent, taken, full = both_tables()
    rows = PLANES * ROWS
    slabs = [PLANES * count for _, count in PARTS]
    hbm = pl.BlockSpec(memory_space=pltpu.HBM)
    dma = pltpu.SemaphoreType.DMA
    near, starts, parts = pl.pallas_call(
        kernel,
        out_shape=(
            jax.ShapeDtypeStruct((ROWS, SLAB, LANES), F32),
            jax.ShapeDtypeStruct((SLOTS, TILE_ROWS, LANES), F32),
            jax.ShapeDtypeStruct((16, 8, TIME_BINS), F32),
        ),
        in_specs=[hbm] * 16,
        out_specs=(hbm, hbm, hbm),
        scratch_shapes=[
            pltpu.VMEM((2, 2 * LANES, 2 * LANES), BF16),
            pltpu.VMEM((2, 2, 32, 2 * LANES), BF16),
            pltpu.VMEM((2, 2, 64, 2 * LANES), BF16),
            pltpu.VMEM((rows, LANES), F32),
            pltpu.VMEM((3, rows, LANES), F32),
            pltpu.VMEM((rows, LANES), F32),
            pltpu.VMEM((3, rows, LANES), F32),
            pltpu.VMEM((3, rows, LANES), F32),
            pltpu.VMEM((rows, LANES), F32),
            pltpu.VMEM((FIELDS, rows, LANES), F32),
            pltpu.VMEM((ROWS, LANES), F32),
            pltpu.VMEM((ENTRY_ROWS, LANES), jnp.int32),
            pltpu.VMEM((ENTRY_ROWS, LANES), jnp.int32),
            pltpu.VMEM((ENTRY_ROWS, LANES), jnp.int32),
            pltpu.VMEM((2, LANES), F32),
            pltpu.VMEM((2, ROWS, NAZ), F32),
            pltpu.VMEM((2, NA, LANES), F32),
            pltpu.VMEM((ROWS, SLAB, LANES), F32),
            pltpu.VMEM((ROWS, SLAB, LANES), F32),
            pltpu.VMEM((ROWS, PLANES, LANES), F32),
            *[pltpu.VMEM((2, ROWS * slab, 2 * LANES), BF16) for slab in slabs],
            *[pltpu.VMEM((ROWS, slab, LANES), F32) for slab in slabs],
            *[pltpu.VMEM((2, 2, 8, 4 * slab), F32) for slab in slabs],
            *[pltpu.VMEM((2, AXIAL, 8, 4 * slab), F32) for slab in slabs],
            pltpu.VMEM((2, SLOTS, TILE_ROWS, LANES), F32),
            pltpu.VMEM((2, 2, AZIM, 16, LANES), F32),
            pltpu.VMEM((2, 2, AZIM, 16, LANES), F32),
            pltpu.VMEM((SLOTS, TILE_ROWS, LANES), F32),
            pltpu.VMEM((2, 1, SLAB, LANES), F32),
            pltpu.VMEM((2, 2, SLAB, LANES), F32),
            pltpu.VMEM((ROWS, SLAB, LANES), F32),
            pltpu.VMEM((OBSERVERS, ENTRY_ROWS * LANES), BF16),
            pltpu.VMEM((2 * TIME_BINS, ENTRY_ROWS * LANES), BF16),
            pltpu.VMEM((OBSERVERS, TIME_BINS), F32),
            pltpu.VMEM((7, 64, TIME_BINS), F32),
            pltpu.VMEM((16, 8, TIME_BINS), F32),
            pltpu.VMEM((2, ROWS, LANES), F32),
            pltpu.VMEM((2, AZIM, ROWS, LANES), F32),
            pltpu.VMEM((2, ROWS, LANES), F32),
            pltpu.VMEM((2, AXIAL, ROWS, LANES), F32),
            pltpu.VMEM((BLOCKS // 2, ROWS, LANES), F32),
            dma(()),
            dma(()),
            dma((11,)),
            dma((5, BLOCKS // 2)),
            dma((2, BLOCKS // 2)),
            dma((2, 2, 3)),
            dma((2, 2, 3)),
            dma((2, 2)),
            dma((2, 2)),
            dma((2, 2)),
            dma((2, 2)),
            dma((2, 2, 2)),
            dma((2, 2, 2)),
            dma((7,)),
            dma((7,)),
            dma((15,)),
            dma((15,)),
            dma((2,)),
            dma((2,)),
            dma((2, 3)),
            dma((2, 3)),
        ],
        compiler_params=pltpu.CompilerParams(
            collective_id=0, has_side_effects=True
        ),
    )(
        jnp.asarray(sent),
        jnp.asarray(taken),
        density.reshape(rows, LANES),
        velocity.reshape(3, rows, LANES),
        pressure.reshape(rows, LANES),
        axial_metric.reshape(3, rows, LANES),
        azim_metric.reshape(3, rows, LANES),
        volume.reshape(rows, LANES),
        radial_term.reshape(FIELDS, rows, LANES),
        panel_area,
        observer_ids.reshape(ENTRY_ROWS, LANES),
        bin_ids.reshape(ENTRY_ROWS, LANES),
        weight_ids.reshape(ENTRY_ROWS, LANES),
        bin_weights.reshape(2, LANES),
        jnp.asarray(azimuth_rows()),
        jnp.asarray(full),
    )
    state, signals = pl.pallas_call(
        finish_kernel,
        out_shape=(
            jax.ShapeDtypeStruct((FIELDS, rows, LANES), F32),
            jax.ShapeDtypeStruct((4, TIME_BINS), F32),
        ),
        in_specs=[hbm] * 3,
        out_specs=(hbm, hbm),
        scratch_shapes=[
            pltpu.VMEM((ROWS, FIELDS, PLANES, LANES), F32),
            pltpu.VMEM((SLOTS, TILE_ROWS, LANES), F32),
            pltpu.VMEM((FIELDS, rows, LANES), F32),
            pltpu.VMEM((16, 8, TIME_BINS), F32),
            pltpu.VMEM((4, TIME_BINS), F32),
            dma((BLOCKS // 2, 3)),
            dma((BLOCKS // 2,)),
            dma((2,)),
        ],
    )(
        near.reshape(ROWS, FIELDS, PLANES, LANES),
        starts,
        parts,
    )
    return state.reshape(FIELDS, PLANES, ROWS, LANES), signals


def solution(mesh):
    placed = (
        P(None, "azim", "axial"),
        P(None, None, "azim", "axial"),
        P(None, "azim", "axial"),
        P(None, None, "azim", "axial"),
        P(None, None, "azim", "axial"),
        P(None, "azim", "axial"),
        P(None, None, "azim", "axial"),
        P("azim", "axial"),
        P(None, "azim", "axial"),
        P(None, "azim", "axial"),
        P(None, "azim", "axial"),
        P(),
    )
    return jax.shard_map(
        per_device,
        mesh=mesh,
        in_specs=placed,
        out_specs=(P(None, None, "azim", "axial"), P(("axial", "azim"), None)),
        check_vma=False,
    )
```

```python
import functools
import math

import jax
import jax.numpy as jnp
import ml_dtypes
import numpy as np
from jax import lax
from jax.experimental import pallas as pl
from jax.experimental.pallas import tpu as pltpu
from jax.sharding import PartitionSpec as P

F32 = jnp.float32
BF16 = jnp.bfloat16
MESH = pl.DeviceIdType.MESH

PLANES = 64
FIELDS = 5
ROWS = 8
LANES = 128
AXIAL = 4
AZIM = 32
NA = AXIAL * LANES
NAZ = AZIM * ROWS
SLAB = FIELDS * PLANES
BLOCKS = PLANES // 8
SLOTS = 2 * BLOCKS
TILE_ROWS = 8 * FIELDS
PARTS = ((0, 3), (3, 2))
PART_OF = (0, 0, 0, 1, 1)
SHARE = (((0, 16), (16, 8)), ((24, 8), (32, 8)))
STEPS = (2, 1, 3, 0)
AWAY = tuple((dz, dy) for dz in STEPS[:3] for dy in STEPS[:3]) + ((2, 0), (0, 2), (1, 0), (3, 0), (0, 1), (0, 3))
ENTRY_ROWS = 32
OBSERVERS = 512
TIME_BINS = 128
PEERS = (AZIM - 1) + 2 * (AXIAL - 1)

SECTION = 0.25
DERIV_ALPHA = 1.0 / 3.0
BETA = 0.499


def decay_root(alpha):
    return (-1.0 + math.sqrt(1.0 - 4.0 * alpha * alpha)) / (2.0 * alpha)


DL = decay_root(DERIV_ALPHA)
FL = decay_root(BETA)
C1 = (1.0 / 36.0) / DERIV_ALPHA
DS = 1.0 / math.sqrt(1.0 - 4.0 * DERIV_ALPHA**2)
DK = (7.0 / 9.0 - C1) * DS * (1.0 / DL - DL)
FC = [
    (11.0 + 10.0 * BETA) / 16.0,
    (15.0 + 34.0 * BETA) / 32.0,
    (-3.0 + 6.0 * BETA) / 16.0,
    (1.0 - 2.0 * BETA) / 32.0,
]
FS = 1.0 / math.sqrt(1.0 - 4.0 * BETA**2)
E2 = FC[3] / (2.0 * BETA)
E1 = (FC[2] / 2.0 - E2) / BETA
E0 = (FC[1] / 2.0 - E1 - BETA * E2) / BETA
FK = (FC[0] - E0 - 2.0 * BETA * E1) * FS


def split(values):
    high = values.astype(ml_dtypes.bfloat16)
    low = (values - high.astype(np.float64)).astype(ml_dtypes.bfloat16)
    return high, low


def axial_tables(root, scale, band):
    n, w = NA, LANES
    index = np.arange(n)
    green = scale * (
        np.power(root, np.abs(index[:, None] - index[None, :]))
        - np.power(root, 2 * n - index[:, None] - index[None, :])
    )
    side = np.zeros((n, n))
    for shift, value in band.items():
        side += value * np.eye(n, k=shift)
    whole = green @ side
    left = np.zeros((AXIAL, w))
    right = np.zeros((AXIAL, w))
    for k in range(AXIAL):
        cols = slice(k * w, (k + 1) * w)
        lo, hi = max(0, k * w - 3), min(n, (k + 1) * w + 3)
        m = np.arange(lo, hi)
        left[k] = np.power(root, ((k + 1) * w - m).astype(np.float64)) @ side[lo:hi, cols]
        right[k] = (
            np.power(root, (m - k * w + 1).astype(np.float64))
            - np.power(root, (2 * n - m - k * w + 1).astype(np.float64))
        ) @ side[lo:hi, cols]
    t = np.arange(w)
    full = np.stack([whole[d * w : (d + 1) * w].T for d in range(AXIAL)]).astype(np.float32)
    sent = np.zeros((AXIAL, 2, 32, 2 * w), ml_dtypes.bfloat16)
    taken = np.zeros((AXIAL, 2, 64, 2 * w), ml_dtypes.bfloat16)
    for d in range(AXIAL):
        for half in range(2):
            rows = np.zeros((16, w))
            base = half * 4
            rows[base] = left[d]
            rows[base + 1, w - 1] = 1.0
            rows[base + 2, w - 2] = 1.0
            rows[8 + base] = right[d]
            rows[8 + base + 1, 0] = 1.0
            rows[8 + base + 2, 1] = 1.0
            high, low = split(rows)
            sent[d, half] = np.concatenate(
                [np.concatenate([high, high], axis=1), np.concatenate([low, low], axis=1)], axis=0
            )
            rows = np.zeros((32, w))
            for k in range(AXIAL):
                row = k * 8 + half * 4
                i = d * w + t
                if k < d:
                    rows[row] = scale * (
                        np.power(root, (i - (k + 1) * w).astype(np.float64))
                        - np.power(root, (2 * n - i - (k + 1) * w).astype(np.float64))
                    )
                    if k == d - 1:
                        for edge in range(2):
                            col = d * w - 1 - edge
                            for near in range(2 - edge):
                                rows[row + 1 + edge, near] = (
                                    whole[d * w + near, col] - rows[row, near] * left[k, col - k * w]
                                )
                if k > d:
                    rows[row] = scale * np.power(root, (k * w - 1 - i).astype(np.float64))
                    if k == d + 1:
                        for edge in range(2):
                            col = k * w + edge
                            for near in range(2 - edge):
                                rows[row + 1 + edge, w - 1 - near] = (
                                    whole[k * w - 1 - near, col] - rows[row, w - 1 - near] * right[k, edge]
                                )
            high, low = split(rows)
            pair = np.concatenate([high, low], axis=1)
            taken[d, half] = np.concatenate([pair, pair], axis=0)
    return sent, taken, full


def both_tables():
    deriv = axial_tables(DL, DS, {1: 7.0 / 9.0, -1: -7.0 / 9.0, 2: 1.0 / 36.0, -2: -1.0 / 36.0})
    band = {0: FC[0]}
    for shift in range(1, 4):
        band[shift] = band[-shift] = FC[shift] / 2.0
    smooth = axial_tables(FL, FS, band)
    return [np.stack(pair, axis=1) for pair in zip(deriv, smooth)]


def azimuth_rows():
    gap = np.arange(NAZ)
    slope = DK * (np.power(DL, gap) - np.power(DL, NAZ - gap)) / (1.0 - DL**NAZ)
    slope[0] = 0.0
    slope[1] += C1
    slope[-1] -= C1
    line = FK * (np.power(FL, gap) + np.power(FL, NAZ - gap)) / (1.0 - FL**NAZ)
    line[0] = FK * (1.0 + 2.0 * FL**NAZ / (1.0 - FL**NAZ)) + E0
    for shift, value in ((1, E1), (2, E2)):
        line[shift] += value
        line[-shift] += value
    rows = np.arange(ROWS)
    at = (gap[None, :] - rows[:, None]) % NAZ
    return np.stack([slope[at], line[at]]).astype(np.float32)


def two_terms(value):
    high = value.astype(BF16)
    low = (value - high.astype(F32)).astype(BF16)
    return high, low


def dot_last(left, right):
    return lax.dot_general(left, right, (((1,), (1,)), ((), ())), preferred_element_type=F32)


def dot_first(left, right):
    return lax.dot_general(left, right, (((0,), (0,)), ((), ())), preferred_element_type=F32)


def near_tails(values, root):
    up, down = [None], [None]
    for row in range(ROWS - 1):
        last, back = values[row], values[ROWS - 1 - row]
        up.append(root * (last if up[-1] is None else last + up[-1]))
        down.append(root * (back if down[-1] is None else back + down[-1]))
    return list(zip(up, down[::-1]))


def start_of(starts, group, field, side):
    return jnp.concatenate(
        [starts[4 * group + 2 * half + side, pl.ds(8 * field, 8)] for half in range(2)], axis=0
    )


def finish_kernel(
    near_hbm, start_hbm, part_hbm, state_hbm, signal_hbm, near, starts, final, parts, signals, load_sem, store_sem, part_sem
):
    part_copy = pltpu.make_async_copy(part_hbm, parts, part_sem.at[0])
    signal_copy = pltpu.make_async_copy(signals, signal_hbm, part_sem.at[1])

    def loads(group):
        slots = pl.ds(4 * group, 4)
        planes = pl.ds(16 * group, 16)
        return [
            pltpu.make_async_copy(start_hbm.at[slots], starts.at[slots], load_sem.at[group, 0]),
            pltpu.make_async_copy(near_hbm.at[:, :, planes], near.at[:, :, planes], load_sem.at[group, 1]),
        ]

    def store(group):
        planes = pl.ds(128 * group, 128)
        return pltpu.make_async_copy(final.at[:, planes], state_hbm.at[:, planes], store_sem.at[group])

    for group in range(BLOCKS // 2):
        for load in loads(group):
            load.start()
    part_copy.start()

    for group in range(BLOCKS // 2):
        for load in loads(group):
            load.wait()
        planes = pl.ds(16 * group, 16)
        for field in range(FIELDS):
            up = FK * start_of(starts, group, field, 0)
            down = FK * start_of(starts, group, field, 1)
            for row in range(ROWS):
                result = near[row, field, planes] + (FL**row * up + FL ** (ROWS - 1 - row) * down)
                final[field, pl.ds(128 * group + row, 16, stride=ROWS)] = result
        store(group).start()
        if group == 0:
            part_copy.wait()
            signals[...] = jnp.sum(parts[...], axis=0)[:4]
            signal_copy.start()

    for group in range(BLOCKS // 2):
        store(group).wait()
    signal_copy.wait()


def kernel(
    sent_hbm,
    taken_hbm,
    density_hbm,
    velocity_hbm,
    pressure_hbm,
    axial_hbm,
    azim_hbm,
    volume_hbm,
    radial_hbm,
    area_hbm,
    observer_hbm,
    bin_hbm,
    weight_hbm,
    table_hbm,
    azimuth_hbm,
    full_hbm,
    near_hbm,
    start_hbm,
    owner_hbm,
    own,
    sent,
    taken,
    density,
    velocity,
    pressure,
    axial_metric,
    azim_metric,
    volume,
    radial,
    area_ref,
    observer_ref,
    bin_ref,
    weight_ref,
    table_ref,
    azimuth_ref,
    full,
    azim_flux,
    base,
    ratio,
    cells_a,
    cells_b,
    lined_a,
    lined_b,
    edge_send_a,
    edge_send_b,
    edge_recv_a,
    edge_recv_b,
    moment_send,
    moment_recv,
    start_send,
    start_recv,
    deriv_halo,
    filter_halo,
    near,
    observer_hot,
    bin_hot,
    partial,
    part_recv,
    owner_send,
    plane_send,
    plane_recv,
    axial_send,
    axial_recv,
    panel_axial,
    keep_sem,
    owner_sem,
    load_sem,
    early_sem,
    late_sem,
    edge_send_sem,
    edge_recv_sem,
    moment_send_sem,
    moment_recv_sem,
    start_send_sem,
    start_recv_sem,
    halo_send_sem,
    halo_recv_sem,
    part_send_sem,
    part_recv_sem,
    owner_send_sem,
    owner_recv_sem,
    plane_send_sem,
    plane_recv_sem,
    axial_send_sem,
    axial_recv_sem,
):
    me_a = lax.axis_index("axial")
    me_z = lax.axis_index("azim")
    core = lax.rem(me_z, 2)
    chip = me_z // 2
    twin = me_z + 1 - 2 * core
    after = lax.rem(me_z + 1, AZIM)
    before = lax.rem(me_z + AZIM - 1, AZIM)

    def chip_at(step):
        return 4 * lax.rem(chip // 4 + step[0], 4) + lax.rem(chip + step[1], 4)

    def group_at(step):
        away = jnp.where(step == 0, STEPS[0], jnp.where(step == 1, STEPS[1], jnp.where(step == 2, STEPS[2], 0)))
        return lax.rem(chip // 4 + away, 4)

    def early_loads(group):
        part = pl.ds(pl.multiple_of(group * 128, 128), 128)
        whole = slice(None)
        return [
            pltpu.make_async_copy(source.at[where], dest.at[where], early_sem.at[number, group])
            for number, (source, dest, where) in enumerate(
                (
                    (density_hbm, density, (part,)),
                    (velocity_hbm, velocity, (whole, part)),
                    (pressure_hbm, pressure, (part,)),
                    (volume_hbm, volume, (part,)),
                    (azim_hbm, azim_metric, (whole, part)),
                )
            )
        ]

    def late_loads(group):
        part = pl.ds(pl.multiple_of(group * 128, 128), 128)
        return [
            pltpu.make_async_copy(axial_hbm.at[:, part], axial_metric.at[:, part], late_sem.at[0, group]),
            pltpu.make_async_copy(radial_hbm.at[:, part], radial.at[:, part], late_sem.at[1, group]),
        ]

    loads = [
        pltpu.make_async_copy(area_hbm, area_ref, load_sem.at[0]),
        pltpu.make_async_copy(observer_hbm, observer_ref, load_sem.at[1]),
        pltpu.make_async_copy(bin_hbm, bin_ref, load_sem.at[2]),
        pltpu.make_async_copy(weight_hbm, weight_ref, load_sem.at[3]),
        pltpu.make_async_copy(table_hbm, table_ref, load_sem.at[4]),
        pltpu.make_async_copy(azimuth_hbm, azimuth_ref, load_sem.at[5]),
        pltpu.make_async_copy(full_hbm.at[me_a], full, load_sem.at[6]),
    ]
    for which in range(2):
        loads.append(pltpu.make_async_copy(sent_hbm.at[me_a, which], sent.at[which], load_sem.at[7 + 2 * which]))
        loads.append(pltpu.make_async_copy(taken_hbm.at[me_a, which], taken.at[which], load_sem.at[8 + 2 * which]))
    for step in range(BLOCKS // 2):
        for load in early_loads(group_at(step)):
            load.start()

    starts = (start_recv, start_hbm)
    cells, lined = (cells_a, cells_b), (lined_a, lined_b)
    edge_send, edge_recv = (edge_send_a, edge_send_b), (edge_recv_a, edge_recv_b)

    barrier = pltpu.get_barrier_semaphore()

    def greet_azim(step, carry):
        other = lax.rem(me_z + step, AZIM)
        pl.semaphore_signal(barrier, inc=1, device_id=(me_a, other), device_id_type=MESH)
        return carry

    lax.fori_loop(1, AZIM, greet_azim, 0)

    def greet_axial(step, carry):
        other = lax.rem(me_a + step, AXIAL)
        pl.semaphore_signal(barrier, inc=1, device_id=(other, me_z), device_id_type=MESH)
        pl.semaphore_signal(barrier, inc=1, device_id=(other, twin), device_id_type=MESH)
        return carry

    lax.fori_loop(1, AXIAL, greet_axial, 0)

    for part in range(2):
        for which in range(2):
            edge_recv[part][which, pl.ds(me_a, 1)] = jnp.zeros((1, 8, 4 * PLANES * PARTS[part][1]), F32)

    def moment_source(which, part, slot, share):
        first, rows = SHARE[part][share]
        return moment_send.at[which, slot, pl.ds(first, rows)]

    def moment_copy(which, part, slot, share):
        return pltpu.make_async_remote_copy(
            src_ref=moment_source(which, part, slot, share),
            dst_ref=moment_recv.at[which, part, me_z, pl.ds(0, SHARE[part][share][1])],
            send_sem=moment_send_sem.at[which, part],
            recv_sem=moment_recv_sem.at[which, part],
            device_id=(me_a, 2 * slot + share),
            device_id_type=MESH,
        )

    def send_moments(which, part, step):
        row = 4 * group_at(step)
        for turn in STEPS[:3]:
            for share in range(2):
                moment_copy(which, part, row + lax.rem(chip + turn, 4), share).start()

        @pl.when(step < 3)
        def _():
            for share in range(2):
                moment_copy(which, part, row + lax.rem(chip, 4), share).start()

        for share in range(2):

            @pl.when(jnp.logical_and(step == 3, core == share))
            def _():
                moment_copy(which, part, chip, 1 - share).start()
                pltpu.make_async_copy(
                    moment_source(which, part, chip, share),
                    moment_recv.at[which, part, me_z, pl.ds(0, SHARE[part][share][1])],
                    moment_recv_sem.at[which, part],
                ).start()

    def wait_moment_sends(which, part):
        for share in range(2):

            @pl.when(core == share)
            def _():
                rows = pl.ds(8 * PARTS[part][0], 8 * PARTS[part][1])
                sent_rows = moment_send.at[which, pl.ds(0, SLOTS - 1), rows]
                pltpu.make_async_copy(sent_rows, sent_rows, moment_send_sem.at[which, part]).wait()
                sent_rows = moment_source(which, part, SLOTS - 1, 1 - share)
                pltpu.make_async_copy(sent_rows, sent_rows, moment_send_sem.at[which, part]).wait()

    def reduce_moments(which, part, root):
        factor = root**ROWS
        wrap = 1.0 / (1.0 - root**NAZ)
        side = lax.rem(chip, 2)

        def place(step):
            return step + side * (AZIM - 1 - 2 * step)

        for share in range(2):
            first_row, count = SHARE[part][share]
            rows, there = pl.ds(0, count), pl.ds(first_row, count)

            @pl.when(core == share)
            def _():
                arrived = moment_recv.at[which, part, :, rows]
                pltpu.make_async_copy(arrived, arrived, moment_recv_sem.at[which, part]).wait()

                def gather(step, total):
                    return factor * total + moment_recv[which, part, place(step), rows]

                first = lax.fori_loop(0, AZIM, gather, jnp.zeros((count, LANES), F32), unroll=8) * wrap

                def follow(step, now):
                    other = place(step)
                    start_send[which, part, other, rows] = now
                    return factor * now + moment_recv[which, part, other, rows]

                lax.fori_loop(0, AZIM, follow, first, unroll=8)

                def hand_out(other):
                    pltpu.make_async_remote_copy(
                        src_ref=start_send.at[which, part, other, rows],
                        dst_ref=starts[which].at[chip, there],
                        send_sem=start_send_sem.at[which, part],
                        recv_sem=start_recv_sem.at[which, part],
                        device_id=(me_a, other),
                        device_id_type=MESH,
                    ).start()

                for step in AWAY:
                    for half in range(2):
                        hand_out(2 * chip_at(step) + half)
                hand_out(twin)
                pltpu.make_async_copy(
                    start_send.at[which, part, me_z, rows],
                    starts[which].at[chip, there],
                    start_recv_sem.at[which, part],
                ).start()

    def wait_starts(which, part):
        arrived = starts[which].at[:, pl.ds(8 * PARTS[part][0], 8 * PARTS[part][1])]
        pltpu.make_async_copy(arrived, arrived, start_recv_sem.at[which, part]).wait()

    def wait_start_sends(which, part):
        for share in range(2):

            @pl.when(core == share)
            def _():
                gone = start_send.at[which, part, pl.ds(0, AZIM - 1), pl.ds(0, SHARE[part][share][1])]
                pltpu.make_async_copy(gone, gone, start_send_sem.at[which, part]).wait()

    def moments_of(values, root):
        up = root * values[0]
        for row in range(1, ROWS):
            up = root * (up + values[row])
        down = root * values[ROWS - 1]
        for row in range(ROWS - 2, -1, -1):
            down = root * (down + values[row])
        return up, down

    def keep_moments(which, group, field, values, root):
        up, down = moments_of(values, root)
        for half in range(2):
            for side, value in ((0, up), (1, down)):
                moment_send[which, 4 * group + 2 * half + side, pl.ds(8 * field, 8)] = value[8 * half : 8 * half + 8]

    def halo_copies(which):
        copies = []
        for part in range(2):
            if which == 1:
                source, halo, depth = lined[part], filter_halo, 2
                there = pl.ds(PLANES * PARTS[part][0], PLANES * PARTS[part][1])
            else:
                source, halo, depth = azim_flux, deriv_halo, 1
                there = pl.ds(0, SLAB)
                if part == 1:
                    break
            for side, other, rows in ((0, after, pl.ds(ROWS - depth, depth)), (1, before, pl.ds(0, depth))):
                copies.append(
                    pltpu.make_async_remote_copy(
                        src_ref=source.at[rows],
                        dst_ref=halo.at[side, :, there],
                        send_sem=halo_send_sem.at[which, part, side],
                        recv_sem=halo_recv_sem.at[which, part, side],
                        device_id=(me_a, other),
                        device_id_type=MESH,
                    )
                )
        return copies

    def edge_copy(which, part, step):
        other = lax.rem(me_a + step, AXIAL)
        down = jnp.where(other < me_a, 1, 0)
        return pltpu.make_async_remote_copy(
            src_ref=edge_send[part].at[which, down],
            dst_ref=edge_recv[part].at[which, me_a],
            send_sem=edge_send_sem.at[which, part, step - 1],
            recv_sem=edge_recv_sem.at[which, part, step - 1],
            device_id=(other, me_z),
            device_id_type=MESH,
        )

    def send_edges(which, part):
        slab = PLANES * PARTS[part][1]

        def piece(step, carry):
            at = pl.multiple_of(step * 2 * slab, 2 * slab)
            total = dot_last(sent[which, 0], cells[part][which, pl.ds(at, 2 * slab)]) + dot_last(
                sent[which, 1], cells[part][which, pl.ds(4 * slab + at, 2 * slab)]
            )
            total = total[:16] + total[16:]
            edge_send[part][which, 0, :, pl.ds(at, 2 * slab)] = total[:8]
            edge_send[part][which, 1, :, pl.ds(at, 2 * slab)] = total[8:]
            return carry

        lax.fori_loop(0, 2, piece, 0, unroll=True)
        for step in STEPS[:3]:
            edge_copy(which, part, step).start()

    def own_part(which, part):
        slab = PLANES * PARTS[part][1]

        def piece(step, carry):
            at = pl.multiple_of(step * 2 * slab, 2 * slab)
            total = jnp.dot(cells[part][which, pl.ds(at, 2 * slab)], own[which], preferred_element_type=F32)
            lined[part][pl.ds(2 * step, 2)] = (total[:, :LANES] + total[:, LANES:]).reshape(2, slab, LANES)
            return carry

        lax.fori_loop(0, 4, piece, 0, unroll=True)

    def add_edges(which, part):
        slab = PLANES * PARTS[part][1]
        for step in range(1, AXIAL):
            edge_copy(which, part, step).wait_recv()

        def piece(step, carry):
            at = pl.multiple_of(lax.rem(step, 2) * 2 * slab, 2 * slab)
            received = edge_recv[part][which, :, :, pl.ds(at, 2 * slab)].reshape(32, 2 * slab)
            high, low = two_terms(received)
            total = dot_first(jnp.concatenate([high, low], axis=0), taken[which, step // 2])
            total = (total[:, :LANES] + total[:, LANES:]).reshape(2, slab, LANES)
            lined[part][pl.ds(2 * step, 2)] = lined[part][pl.ds(2 * step, 2)] + total
            return carry

        lax.fori_loop(0, 4, piece, 0, unroll=True)

    def keep_cells(which, row, field, group, value):
        part = PART_OF[field]
        first, count = PARTS[part]
        high, low = two_terms(value)
        at = pl.multiple_of((row * count + field - first) * PLANES + group * 16, 16)
        cells[part][which, pl.ds(at, 16), pl.ds(0, LANES)] = high
        cells[part][which, pl.ds(at, 16), pl.ds(LANES, LANES)] = low

    def axial_copy(which, step):
        return pltpu.make_async_remote_copy(
            src_ref=axial_send.at[which],
            dst_ref=axial_recv.at[which, me_a],
            send_sem=axial_send_sem.at[which, step - 1],
            recv_sem=axial_recv_sem.at[which, step - 1],
            device_id=(lax.rem(me_a + step, AXIAL), me_z),
            device_id_type=MESH,
        )

    def send_axial(which, value):
        axial_send[which] = value
        axial_recv[which, pl.ds(me_a, 1)] = value[None]
        for step in STEPS[:3]:
            axial_copy(which, step).start()

    def take_axial(which):
        for step in range(1, AXIAL):
            axial_copy(which, step).wait_recv()
        line = jnp.concatenate([axial_recv[which, k] for k in range(AXIAL)], axis=1)
        return jnp.dot(line, full[which], preferred_element_type=F32, precision=lax.Precision.HIGHEST)

    def send_plane(which, value):
        plane_send[which] = value
        plane_recv[which, 0] = value

        def piece(other):
            pltpu.make_async_remote_copy(
                src_ref=plane_send.at[which],
                dst_ref=plane_recv.at[which, lax.rem(me_z - other + AZIM, AZIM)],
                send_sem=plane_send_sem.at[which],
                recv_sem=plane_recv_sem.at[which],
                device_id=(me_a, other),
                device_id_type=MESH,
            ).start()

        for step in AWAY:
            for half in range(2):
                piece(2 * chip_at(step) + half)
        piece(twin)

    def plane_wait(which, sem):
        part = plane_recv.at[which, pl.ds(1, AZIM - 1)]
        pltpu.make_async_copy(part, part, sem.at[which]).wait()

    def take_plane(which):
        plane_wait(which, plane_recv_sem)
        return jnp.dot(
            azimuth_ref[which],
            plane_recv[which].reshape(NAZ, LANES),
            preferred_element_type=F32,
            precision=lax.Precision.HIGHEST,
        )

    def flux_of(metric, at, rho, vel, prs, vol, heat):
        grad = [metric[comp, at] for comp in range(3)]
        contra = vol * (grad[0] * vel[0] + grad[1] * vel[1] + grad[2] * vel[2])
        flow = rho * contra
        push = vol * prs
        return [flow] + [flow * vel[comp] + grad[comp] * push for comp in range(3)] + [heat * contra]

    def cells_at(group, row):
        at = pl.ds(group * 128 + row, 16, stride=ROWS)
        rho, prs, vol = density[at], pressure[at], volume[at]
        vel = [velocity[comp, at] for comp in range(3)]
        energy = 2.5 * prs + 0.5 * rho * (vel[0] * vel[0] + vel[1] * vel[1] + vel[2] * vel[2])
        return at, rho, vel, prs, vol, energy

    def azim_group(step, carry):
        group = group_at(step)
        for load in early_loads(group):
            load.wait()
        for load in late_loads(group):
            load.start()
        flux = [[None] * ROWS for _ in range(FIELDS)]
        for row in range(ROWS):
            at, rho, vel, prs, vol, energy = cells_at(group, row)
            parts = flux_of(azim_metric, at, rho, vel, prs, vol, energy + prs)
            for field in range(FIELDS):
                flux[field][row] = parts[field]
                azim_flux[row, pl.ds(pl.multiple_of(field * PLANES + group * 16, 16), 16)] = parts[field]
        for field in range(FIELDS):
            keep_moments(0, group, field, flux[field], DL)

        @pl.when(step == 0)
        def _():
            pl.semaphore_wait(barrier, PEERS)

        send_moments(0, 0, step)
        return carry

    lax.fori_loop(0, BLOCKS // 2, azim_group, 0)

    for load in loads:
        load.start()

    def send_rest(step, carry):
        send_moments(0, 1, step)
        return carry

    lax.fori_loop(0, BLOCKS // 2, send_rest, 0)
    send_plane(0, azim_flux[:, 0] + azim_flux[:, 2 * PLANES])
    for copy in halo_copies(0):
        copy.start()

    def axial_group(group, carry):
        for load in late_loads(group):
            load.wait()
        for row in range(ROWS):
            at, rho, vel, prs, vol, energy = cells_at(group, row)
            state = [rho, rho * vel[0], rho * vel[1], rho * vel[2], energy]
            ratio[row, pl.ds(pl.multiple_of(group * 16, 16), 16)] = SECTION / vol
            for field in range(FIELDS):
                base[row, pl.ds(pl.multiple_of(field * PLANES + group * 16, 16), 16)] = (
                    state[field] + SECTION * radial[field, at]
                )
            parts = flux_of(axial_metric, at, rho, vel, prs, vol, energy + prs)
            for field in range(FIELDS):
                keep_cells(0, row, field, group, parts[field])
            panel_axial[group, pl.ds(row, 1)] = parts[0][:1] + parts[2][:1]
        return carry

    lax.fori_loop(0, BLOCKS // 2, axial_group, 0)
    send_axial(0, panel_axial[0])
    for load in loads:
        load.wait()
    send_edges(0, 0)
    send_edges(0, 1)

    ids = observer_ref[...]
    order = (
        lax.shift_right_logical(ids, 7) * 128
        + (lax.shift_right_logical(ids, 2) & 1) * 64
        + (lax.shift_right_logical(ids, 3) & 15) * 4
        + (ids & 3)
    )
    partial[pl.ds(0, ENTRY_ROWS)] = order.astype(F32)

    def hot_row(row, carry):
        wanted = partial[pl.ds(row, 1)].astype(jnp.int32)
        rows = lax.broadcasted_iota(jnp.int32, (OBSERVERS, LANES), 0)
        at = pl.multiple_of(row * LANES, LANES)
        observer_hot[:, pl.ds(at, LANES)] = jnp.where(rows == wanted, 1.0, 0.0).astype(BF16)
        same = lax.broadcasted_iota(jnp.int32, (TIME_BINS, LANES), 0) == bin_ref[pl.ds(row, 1)]
        bin_hot[pl.ds(0, TIME_BINS), pl.ds(at, LANES)] = jnp.where(same, 1.0, 0.0).astype(BF16)
        return carry

    lax.fori_loop(0, ENTRY_ROWS, hot_row, 0)

    for which in range(2):
        high, low = two_terms(full[which, pl.ds(pl.multiple_of(me_a * LANES, LANES), LANES)])
        for top in range(2):
            own[which, pl.ds(top * LANES, LANES), pl.ds(0, LANES)] = high
            own[which, pl.ds(top * LANES, LANES), pl.ds(LANES, LANES)] = low
    own_part(0, 0)
    own_part(0, 1)
    reduce_moments(0, 0, DL)
    reduce_moments(0, 1, DL)
    change = take_axial(0) + take_plane(0)
    send_axial(1, base[:, 0] + base[:, 2 * PLANES] - ratio[:, 0] * change)
    add_edges(0, 0)
    add_edges(0, 1)

    def near_section(group, carry):
        here = pl.ds(pl.multiple_of(group * 16, 16), 16)
        for field in range(FIELDS):
            part = PART_OF[field]
            at = pl.ds(pl.multiple_of(field * PLANES + group * 16, 16), 16)
            inside = pl.ds(pl.multiple_of((field - PARTS[part][0]) * PLANES + group * 16, 16), 16)
            flux = [deriv_halo[0, 0, at]] + [azim_flux[row, at] for row in range(ROWS)] + [deriv_halo[1, 0, at]]
            tails = near_tails(flux[1:-1], DL)
            for row in range(ROWS):
                up, down = tails[row]
                spread = down if up is None else -up if down is None else down - up
                deriv = DK * spread + C1 * (flux[row + 2] - flux[row])
                base[row, at] = base[row, at] - ratio[row, here] * (lined[part][row, inside] + deriv)
        return carry

    def section(part):
        first, count = PARTS[part]

        def section_group(group, carry):
            here = pl.ds(pl.multiple_of(group * 16, 16), 16)
            for field in range(first, first + count):
                at = pl.ds(pl.multiple_of(field * PLANES + group * 16, 16), 16)
                up = DK * start_of(start_recv, group, field, 0)
                down = DK * start_of(start_recv, group, field, 1)
                for row in range(ROWS):
                    far = DL ** (ROWS - 1 - row) * down - DL**row * up
                    keep_cells(1, row, field, group, base[row, at] - ratio[row, here] * far)
            return carry

        lax.fori_loop(0, BLOCKS // 2, section_group, 0)

    def smoothed_moments(part):
        first, count = PARTS[part]

        def moment_group(step, carry):
            group = group_at(step)
            for field in range(first, first + count):
                inside = pl.ds(pl.multiple_of((field - first) * PLANES + group * 16, 16), 16)
                keep_moments(1, group, field, [lined[part][row, inside] for row in range(ROWS)], FL)
            send_moments(1, part, step)
            return carry

        lax.fori_loop(0, BLOCKS // 2, moment_group, 0)

    for copy in halo_copies(0):
        copy.wait_recv()
    lax.fori_loop(0, BLOCKS // 2, near_section, 0)
    wait_starts(0, 0)
    section(0)
    send_edges(1, 0)
    send_plane(1, take_axial(1))
    wait_starts(0, 1)
    section(1)
    send_edges(1, 1)
    own_part(1, 0)
    own_part(1, 1)
    add_edges(1, 0)
    smoothed_moments(0)
    add_edges(1, 1)
    smoothed_moments(1)
    for copy in halo_copies(1):
        copy.start()

    source = area_ref[...] * (take_plane(1) - 1.0)
    picks = weight_ref[...]
    low_half = jnp.take_along_axis(
        jnp.broadcast_to(table_ref[pl.ds(0, 1)], (ENTRY_ROWS, LANES)), picks & 127, axis=1
    )
    high_half = jnp.take_along_axis(
        jnp.broadcast_to(table_ref[pl.ds(1, 1)], (ENTRY_ROWS, LANES)), picks & 127, axis=1
    )
    weights = jnp.where(picks < LANES, low_half, high_half)
    values = weights * jnp.concatenate([source] * 4, axis=0)
    high, low = two_terms(values)
    partial[pl.ds(0, ENTRY_ROWS)] = high.astype(F32)
    partial[pl.ds(ENTRY_ROWS, ENTRY_ROWS)] = low.astype(F32)

    def bin_row(row, carry):
        at = pl.multiple_of(row * LANES, LANES)
        mask = bin_hot[pl.ds(0, TIME_BINS), pl.ds(at, LANES)]
        for term in range(2):
            value = jnp.broadcast_to(partial[pl.ds(term * ENTRY_ROWS + row, 1)], (TIME_BINS, LANES)).astype(BF16)
            bin_hot[pl.ds(term * TIME_BINS, TIME_BINS), pl.ds(at, LANES)] = mask * value
        return carry

    lax.fori_loop(0, ENTRY_ROWS, bin_row, 0)

    total = dot_last(observer_hot[...], bin_hot[...])
    partial[...] = total[:, :TIME_BINS] + total[:, TIME_BINS:]

    mine = me_a * 2 + core

    def part_copy(step):
        other = lax.rem(mine + step, 8)
        other_z = me_z - core + lax.rem(other, 2)
        return pltpu.make_async_remote_copy(
            src_ref=partial.at[pl.ds(pl.multiple_of(other * 64, 64), 64)],
            dst_ref=part_recv.at[step - 1],
            send_sem=part_send_sem.at[step - 1],
            recv_sem=part_recv_sem.at[step - 1],
            device_id=(other // 2, other_z),
            device_id_type=MESH,
        )

    for step in range(1, 8):
        part_copy(step).start()
    reduce_moments(1, 0, FL)
    reduce_moments(1, 1, FL)
    total = partial[pl.ds(pl.multiple_of(mine * 64, 64), 64)]
    for step in range(1, 8):
        part_copy(step).wait_recv()
        total = total + part_recv[step - 1]
    for owner in range(16):
        owner_send[owner, pl.ds(0, 4)] = total[4 * owner : 4 * owner + 4]
        owner_send[owner, pl.ds(4, 4)] = jnp.zeros((4, LANES), F32)

    def owner_copy(step):
        other = lax.rem(chip + step, 16)
        return pltpu.make_async_remote_copy(
            src_ref=owner_send.at[other],
            dst_ref=owner_hbm.at[step],
            send_sem=owner_send_sem.at[step - 1],
            recv_sem=owner_recv_sem.at[step - 1],
            device_id=(me_a, 2 * other + core),
            device_id_type=MESH,
        )

    for step in range(1, 16):
        owner_copy(step).start()
    own_copy = pltpu.make_async_copy(owner_send.at[chip], owner_hbm.at[0], owner_sem)
    own_copy.start()
    for copy in halo_copies(1):
        copy.wait_recv()

    def near_group(group, carry):
        for field in range(FIELDS):
            part = PART_OF[field]
            at = pl.ds(pl.multiple_of(field * PLANES + group * 16, 16), 16)
            inside = pl.ds(pl.multiple_of((field - PARTS[part][0]) * PLANES + group * 16, 16), 16)
            value = [filter_halo[0, row, at] for row in range(2)]
            value += [lined[part][row, inside] for row in range(ROWS)]
            value += [filter_halo[1, row, at] for row in range(2)]
            ends = near_tails(value[2:-2], FL)
            for row in range(ROWS):
                up, down = ends[row]
                tails = down if up is None else up if down is None else up + down
                edges = E1 * (value[row + 1] + value[row + 3]) + E2 * (value[row] + value[row + 4])
                near[row, at] = FK * tails + (FK + E0) * value[row + 2] + edges
        return carry

    lax.fori_loop(0, BLOCKS // 2, near_group, 0)
    keep = pltpu.make_async_copy(near, near_hbm, keep_sem)
    keep.start()
    for part in range(2):
        wait_starts(1, part)

    own_copy.wait()
    for step in range(1, 16):
        owner_copy(step).wait_recv()
    keep.wait()

    for which in range(2):
        for part in range(2):
            wait_moment_sends(which, part)
            wait_start_sends(which, part)
            for step in range(1, AXIAL):
                edge_copy(which, part, step).wait_send()
        for copy in halo_copies(which):
            copy.wait_send()
    for step in range(1, 8):
        part_copy(step).wait_send()
    for step in range(1, 16):
        owner_copy(step).wait_send()
    for which in range(2):
        plane_wait(which, plane_send_sem)
        for step in range(1, AXIAL):
            axial_copy(which, step).wait_send()


def per_device(
    density,
    velocity,
    pressure,
    axial_metric,
    azim_metric,
    volume,
    radial_term,
    panel_area,
    observer_ids,
    bin_ids,
    weight_ids,
    bin_weights,
):
    sent, taken, full = both_tables()
    rows = PLANES * ROWS
    slabs = [PLANES * count for _, count in PARTS]
    hbm = pl.BlockSpec(memory_space=pltpu.HBM)
    dma = pltpu.SemaphoreType.DMA
    near, starts, parts = pl.pallas_call(
        kernel,
        out_shape=(
            jax.ShapeDtypeStruct((ROWS, SLAB, LANES), F32),
            jax.ShapeDtypeStruct((SLOTS, TILE_ROWS, LANES), F32),
            jax.ShapeDtypeStruct((16, 8, TIME_BINS), F32),
        ),
        in_specs=[hbm] * 16,
        out_specs=(hbm, hbm, hbm),
        scratch_shapes=[
            pltpu.VMEM((2, 2 * LANES, 2 * LANES), BF16),
            pltpu.VMEM((2, 2, 32, 2 * LANES), BF16),
            pltpu.VMEM((2, 2, 64, 2 * LANES), BF16),
            pltpu.VMEM((rows, LANES), F32),
            pltpu.VMEM((3, rows, LANES), F32),
            pltpu.VMEM((rows, LANES), F32),
            pltpu.VMEM((3, rows, LANES), F32),
            pltpu.VMEM((3, rows, LANES), F32),
            pltpu.VMEM((rows, LANES), F32),
            pltpu.VMEM((FIELDS, rows, LANES), F32),
            pltpu.VMEM((ROWS, LANES), F32),
            pltpu.VMEM((ENTRY_ROWS, LANES), jnp.int32),
            pltpu.VMEM((ENTRY_ROWS, LANES), jnp.int32),
            pltpu.VMEM((ENTRY_ROWS, LANES), jnp.int32),
            pltpu.VMEM((2, LANES), F32),
            pltpu.VMEM((2, ROWS, NAZ), F32),
            pltpu.VMEM((2, NA, LANES), F32),
            pltpu.VMEM((ROWS, SLAB, LANES), F32),
            pltpu.VMEM((ROWS, SLAB, LANES), F32),
            pltpu.VMEM((ROWS, PLANES, LANES), F32),
            *[pltpu.VMEM((2, ROWS * slab, 2 * LANES), BF16) for slab in slabs],
            *[pltpu.VMEM((ROWS, slab, LANES), F32) for slab in slabs],
            *[pltpu.VMEM((2, 2, 8, 4 * slab), F32) for slab in slabs],
            *[pltpu.VMEM((2, AXIAL, 8, 4 * slab), F32) for slab in slabs],
            pltpu.VMEM((2, SLOTS, TILE_ROWS, LANES), F32),
            pltpu.VMEM((2, 2, AZIM, 16, LANES), F32),
            pltpu.VMEM((2, 2, AZIM, 16, LANES), F32),
            pltpu.VMEM((SLOTS, TILE_ROWS, LANES), F32),
            pltpu.VMEM((2, 1, SLAB, LANES), F32),
            pltpu.VMEM((2, 2, SLAB, LANES), F32),
            pltpu.VMEM((ROWS, SLAB, LANES), F32),
            pltpu.VMEM((OBSERVERS, ENTRY_ROWS * LANES), BF16),
            pltpu.VMEM((2 * TIME_BINS, ENTRY_ROWS * LANES), BF16),
            pltpu.VMEM((OBSERVERS, TIME_BINS), F32),
            pltpu.VMEM((7, 64, TIME_BINS), F32),
            pltpu.VMEM((16, 8, TIME_BINS), F32),
            pltpu.VMEM((2, ROWS, LANES), F32),
            pltpu.VMEM((2, AZIM, ROWS, LANES), F32),
            pltpu.VMEM((2, ROWS, LANES), F32),
            pltpu.VMEM((2, AXIAL, ROWS, LANES), F32),
            pltpu.VMEM((BLOCKS // 2, ROWS, LANES), F32),
            dma(()),
            dma(()),
            dma((11,)),
            dma((5, BLOCKS // 2)),
            dma((2, BLOCKS // 2)),
            dma((2, 2, 3)),
            dma((2, 2, 3)),
            dma((2, 2)),
            dma((2, 2)),
            dma((2, 2)),
            dma((2, 2)),
            dma((2, 2, 2)),
            dma((2, 2, 2)),
            dma((7,)),
            dma((7,)),
            dma((15,)),
            dma((15,)),
            dma((2,)),
            dma((2,)),
            dma((2, 3)),
            dma((2, 3)),
        ],
        compiler_params=pltpu.CompilerParams(
            collective_id=0, has_side_effects=True
        ),
    )(
        jnp.asarray(sent),
        jnp.asarray(taken),
        density.reshape(rows, LANES),
        velocity.reshape(3, rows, LANES),
        pressure.reshape(rows, LANES),
        axial_metric.reshape(3, rows, LANES),
        azim_metric.reshape(3, rows, LANES),
        volume.reshape(rows, LANES),
        radial_term.reshape(FIELDS, rows, LANES),
        panel_area,
        observer_ids.reshape(ENTRY_ROWS, LANES),
        bin_ids.reshape(ENTRY_ROWS, LANES),
        weight_ids.reshape(ENTRY_ROWS, LANES),
        bin_weights.reshape(2, LANES),
        jnp.asarray(azimuth_rows()),
        jnp.asarray(full),
    )
    state, signals = pl.pallas_call(
        finish_kernel,
        out_shape=(
            jax.ShapeDtypeStruct((FIELDS, rows, LANES), F32),
            jax.ShapeDtypeStruct((4, TIME_BINS), F32),
        ),
        in_specs=[hbm] * 3,
        out_specs=(hbm, hbm),
        scratch_shapes=[
            pltpu.VMEM((ROWS, FIELDS, PLANES, LANES), F32),
            pltpu.VMEM((SLOTS, TILE_ROWS, LANES), F32),
            pltpu.VMEM((FIELDS, rows, LANES), F32),
            pltpu.VMEM((16, 8, TIME_BINS), F32),
            pltpu.VMEM((4, TIME_BINS), F32),
            dma((BLOCKS // 2, 3)),
            dma((BLOCKS // 2,)),
            dma((2,)),
        ],
    )(
        near.reshape(ROWS, FIELDS, PLANES, LANES),
        starts,
        parts,
    )
    return state.reshape(FIELDS, PLANES, ROWS, LANES), signals


def solution(mesh):
    placed = (
        P(None, "azim", "axial"),
        P(None, None, "azim", "axial"),
        P(None, "azim", "axial"),
        P(None, None, "azim", "axial"),
        P(None, None, "azim", "axial"),
        P(None, "azim", "axial"),
        P(None, None, "azim", "axial"),
        P("azim", "axial"),
        P(None, "azim", "axial"),
        P(None, "azim", "axial"),
        P(None, "azim", "axial"),
        P(),
    )
    return jax.shard_map(
        per_device,
        mesh=mesh,
        in_specs=placed,
        out_specs=(P(None, None, "azim", "axial"), P(("axial", "azim"), None)),
        check_vma=False,
    )
```

```python
import functools
import math

import jax
import jax.numpy as jnp
import ml_dtypes
import numpy as np
from jax import lax
from jax.experimental import pallas as pl
from jax.experimental.pallas import tpu as pltpu
from jax.sharding import PartitionSpec as P

F32 = jnp.float32
BF16 = jnp.bfloat16
MESH = pl.DeviceIdType.MESH

PLANES = 64
FIELDS = 5
ROWS = 8
LANES = 128
AXIAL = 4
AZIM = 32
NA = AXIAL * LANES
NAZ = AZIM * ROWS
SLAB = FIELDS * PLANES
BLOCKS = PLANES // 8
SLOTS = 2 * BLOCKS
TILE_ROWS = 8 * FIELDS
PARTS = ((0, 3), (3, 2))
PART_OF = (0, 0, 0, 1, 1)
SHARE = (((0, 16), (16, 8)), ((24, 8), (32, 8)))
STEPS = (2, 1, 3, 0)
AWAY = tuple((dz, dy) for dz in STEPS[:3] for dy in STEPS[:3]) + ((2, 0), (0, 2), (1, 0), (3, 0), (0, 1), (0, 3))
ENTRY_ROWS = 32
OBSERVERS = 512
TIME_BINS = 128
PEERS = (AZIM - 1) + 2 * (AXIAL - 1)

SECTION = 0.25
DERIV_ALPHA = 1.0 / 3.0
BETA = 0.499


def decay_root(alpha):
    return (-1.0 + math.sqrt(1.0 - 4.0 * alpha * alpha)) / (2.0 * alpha)


DL = decay_root(DERIV_ALPHA)
FL = decay_root(BETA)
C1 = (1.0 / 36.0) / DERIV_ALPHA
DS = 1.0 / math.sqrt(1.0 - 4.0 * DERIV_ALPHA**2)
DK = (7.0 / 9.0 - C1) * DS * (1.0 / DL - DL)
FC = [
    (11.0 + 10.0 * BETA) / 16.0,
    (15.0 + 34.0 * BETA) / 32.0,
    (-3.0 + 6.0 * BETA) / 16.0,
    (1.0 - 2.0 * BETA) / 32.0,
]
FS = 1.0 / math.sqrt(1.0 - 4.0 * BETA**2)
E2 = FC[3] / (2.0 * BETA)
E1 = (FC[2] / 2.0 - E2) / BETA
E0 = (FC[1] / 2.0 - E1 - BETA * E2) / BETA
FK = (FC[0] - E0 - 2.0 * BETA * E1) * FS


def split(values):
    high = values.astype(ml_dtypes.bfloat16)
    low = (values - high.astype(np.float64)).astype(ml_dtypes.bfloat16)
    return high, low


def axial_tables(root, scale, band):
    n, w = NA, LANES
    index = np.arange(n)
    green = scale * (
        np.power(root, np.abs(index[:, None] - index[None, :]))
        - np.power(root, 2 * n - index[:, None] - index[None, :])
    )
    side = np.zeros((n, n))
    for shift, value in band.items():
        side += value * np.eye(n, k=shift)
    whole = green @ side
    left = np.zeros((AXIAL, w))
    right = np.zeros((AXIAL, w))
    for k in range(AXIAL):
        cols = slice(k * w, (k + 1) * w)
        lo, hi = max(0, k * w - 3), min(n, (k + 1) * w + 3)
        m = np.arange(lo, hi)
        left[k] = np.power(root, ((k + 1) * w - m).astype(np.float64)) @ side[lo:hi, cols]
        right[k] = (
            np.power(root, (m - k * w + 1).astype(np.float64))
            - np.power(root, (2 * n - m - k * w + 1).astype(np.float64))
        ) @ side[lo:hi, cols]
    t = np.arange(w)
    full = np.stack([whole[d * w : (d + 1) * w].T for d in range(AXIAL)]).astype(np.float32)
    sent = np.zeros((AXIAL, 2, 32, 2 * w), ml_dtypes.bfloat16)
    taken = np.zeros((AXIAL, 2, 64, 2 * w), ml_dtypes.bfloat16)
    for d in range(AXIAL):
        for half in range(2):
            rows = np.zeros((16, w))
            base = half * 4
            rows[base] = left[d]
            rows[base + 1, w - 1] = 1.0
            rows[base + 2, w - 2] = 1.0
            rows[8 + base] = right[d]
            rows[8 + base + 1, 0] = 1.0
            rows[8 + base + 2, 1] = 1.0
            high, low = split(rows)
            sent[d, half] = np.concatenate(
                [np.concatenate([high, high], axis=1), np.concatenate([low, low], axis=1)], axis=0
            )
            rows = np.zeros((32, w))
            for k in range(AXIAL):
                row = k * 8 + half * 4
                i = d * w + t
                if k < d:
                    rows[row] = scale * (
                        np.power(root, (i - (k + 1) * w).astype(np.float64))
                        - np.power(root, (2 * n - i - (k + 1) * w).astype(np.float64))
                    )
                    if k == d - 1:
                        for edge in range(2):
                            col = d * w - 1 - edge
                            for near in range(2 - edge):
                                rows[row + 1 + edge, near] = (
                                    whole[d * w + near, col] - rows[row, near] * left[k, col - k * w]
                                )
                if k > d:
                    rows[row] = scale * np.power(root, (k * w - 1 - i).astype(np.float64))
                    if k == d + 1:
                        for edge in range(2):
                            col = k * w + edge
                            for near in range(2 - edge):
                                rows[row + 1 + edge, w - 1 - near] = (
                                    whole[k * w - 1 - near, col] - rows[row, w - 1 - near] * right[k, edge]
                                )
            high, low = split(rows)
            pair = np.concatenate([high, low], axis=1)
            taken[d, half] = np.concatenate([pair, pair], axis=0)
    return sent, taken, full


def both_tables():
    deriv = axial_tables(DL, DS, {1: 7.0 / 9.0, -1: -7.0 / 9.0, 2: 1.0 / 36.0, -2: -1.0 / 36.0})
    band = {0: FC[0]}
    for shift in range(1, 4):
        band[shift] = band[-shift] = FC[shift] / 2.0
    smooth = axial_tables(FL, FS, band)
    return [np.stack(pair, axis=1) for pair in zip(deriv, smooth)]


def azimuth_rows():
    gap = np.arange(NAZ)
    slope = DK * (np.power(DL, gap) - np.power(DL, NAZ - gap)) / (1.0 - DL**NAZ)
    slope[0] = 0.0
    slope[1] += C1
    slope[-1] -= C1
    line = FK * (np.power(FL, gap) + np.power(FL, NAZ - gap)) / (1.0 - FL**NAZ)
    line[0] = FK * (1.0 + 2.0 * FL**NAZ / (1.0 - FL**NAZ)) + E0
    for shift, value in ((1, E1), (2, E2)):
        line[shift] += value
        line[-shift] += value
    rows = np.arange(ROWS)
    at = (gap[None, :] - rows[:, None]) % NAZ
    return np.stack([slope[at], line[at]]).astype(np.float32)


def two_terms(value):
    high = value.astype(BF16)
    low = (value - high.astype(F32)).astype(BF16)
    return high, low


def dot_last(left, right):
    return lax.dot_general(left, right, (((1,), (1,)), ((), ())), preferred_element_type=F32)


def dot_first(left, right):
    return lax.dot_general(left, right, (((0,), (0,)), ((), ())), preferred_element_type=F32)


def near_tails(values, root):
    up, down = [None], [None]
    for row in range(ROWS - 1):
        last, back = values[row], values[ROWS - 1 - row]
        up.append(root * (last if up[-1] is None else last + up[-1]))
        down.append(root * (back if down[-1] is None else back + down[-1]))
    return list(zip(up, down[::-1]))


def start_of(starts, group, field, side):
    return jnp.concatenate(
        [starts[4 * group + 2 * half + side, pl.ds(8 * field, 8)] for half in range(2)], axis=0
    )


def finish_kernel(
    near_hbm, start_hbm, part_hbm, state_hbm, signal_hbm, near, starts, final, parts, signals, load_sem, store_sem, part_sem
):
    part_copy = pltpu.make_async_copy(part_hbm, parts, part_sem.at[0])
    signal_copy = pltpu.make_async_copy(signals, signal_hbm, part_sem.at[1])

    def loads(group):
        slots = pl.ds(4 * group, 4)
        planes = pl.ds(16 * group, 16)
        return [
            pltpu.make_async_copy(start_hbm.at[slots], starts.at[slots], load_sem.at[group, 0]),
            pltpu.make_async_copy(near_hbm.at[:, :, planes], near.at[:, :, planes], load_sem.at[group, 1]),
        ]

    def store(group):
        planes = pl.ds(128 * group, 128)
        return pltpu.make_async_copy(final.at[:, planes], state_hbm.at[:, planes], store_sem.at[group])

    for group in range(BLOCKS // 2):
        for load in loads(group):
            load.start()
    part_copy.start()

    for group in range(BLOCKS // 2):
        for load in loads(group):
            load.wait()
        planes = pl.ds(16 * group, 16)
        for field in range(FIELDS):
            up = FK * start_of(starts, group, field, 0)
            down = FK * start_of(starts, group, field, 1)
            for row in range(ROWS):
                result = near[row, field, planes] + (FL**row * up + FL ** (ROWS - 1 - row) * down)
                final[field, pl.ds(128 * group + row, 16, stride=ROWS)] = result
        store(group).start()
        if group == 0:
            part_copy.wait()
            signals[...] = jnp.sum(parts[...], axis=0)[:4]
            signal_copy.start()

    for group in range(BLOCKS // 2):
        store(group).wait()
    signal_copy.wait()


def kernel(
    sent_hbm,
    taken_hbm,
    density_hbm,
    velocity_hbm,
    pressure_hbm,
    axial_hbm,
    azim_hbm,
    volume_hbm,
    radial_hbm,
    area_hbm,
    observer_hbm,
    bin_hbm,
    weight_hbm,
    table_hbm,
    azimuth_hbm,
    full_hbm,
    near_hbm,
    start_hbm,
    owner_hbm,
    own,
    sent,
    taken,
    density,
    velocity,
    pressure,
    axial_metric,
    azim_metric,
    volume,
    radial,
    area_ref,
    observer_ref,
    bin_ref,
    weight_ref,
    table_ref,
    azimuth_ref,
    full,
    azim_flux,
    base,
    ratio,
    cells_a,
    cells_b,
    lined_a,
    lined_b,
    edge_send_a,
    edge_send_b,
    edge_recv_a,
    edge_recv_b,
    moment_send,
    moment_recv,
    start_send,
    start_recv,
    deriv_halo,
    filter_halo,
    near,
    observer_hot,
    bin_hot,
    partial,
    part_recv,
    owner_send,
    plane_send,
    plane_recv,
    axial_send,
    axial_recv,
    panel_axial,
    keep_sem,
    owner_sem,
    load_sem,
    early_sem,
    late_sem,
    edge_send_sem,
    edge_recv_sem,
    moment_send_sem,
    moment_recv_sem,
    start_send_sem,
    start_recv_sem,
    halo_send_sem,
    halo_recv_sem,
    part_send_sem,
    part_recv_sem,
    owner_send_sem,
    owner_recv_sem,
    plane_send_sem,
    plane_recv_sem,
    axial_send_sem,
    axial_recv_sem,
):
    me_a = lax.axis_index("axial")
    me_z = lax.axis_index("azim")
    core = lax.rem(me_z, 2)
    chip = me_z // 2
    twin = me_z + 1 - 2 * core
    after = lax.rem(me_z + 1, AZIM)
    before = lax.rem(me_z + AZIM - 1, AZIM)

    def chip_at(step):
        return 4 * lax.rem(chip // 4 + step[0], 4) + lax.rem(chip + step[1], 4)

    def group_at(step):
        away = jnp.where(step == 0, STEPS[0], jnp.where(step == 1, STEPS[1], jnp.where(step == 2, STEPS[2], 0)))
        return lax.rem(chip // 4 + away, 4)

    barrier = pltpu.get_barrier_semaphore()

    def greet(other_a, other_z):
        pl.semaphore_signal(barrier, inc=1, device_id=(other_a, other_z), device_id_type=MESH)

    for step in AWAY:
        for half in range(2):
            greet(me_a, 2 * chip_at(step) + half)
    for step in STEPS[:3]:
        greet(lax.rem(me_a + step, AXIAL), me_z)
        greet(lax.rem(me_a + step, AXIAL), twin)
    greet(me_a, twin)

    def early_loads(group):
        part = pl.ds(pl.multiple_of(group * 128, 128), 128)
        whole = slice(None)
        return [
            pltpu.make_async_copy(source.at[where], dest.at[where], early_sem.at[number, group])
            for number, (source, dest, where) in enumerate(
                (
                    (density_hbm, density, (part,)),
                    (velocity_hbm, velocity, (whole, part)),
                    (pressure_hbm, pressure, (part,)),
                    (volume_hbm, volume, (part,)),
                    (azim_hbm, azim_metric, (whole, part)),
                )
            )
        ]

    def late_loads(group):
        part = pl.ds(pl.multiple_of(group * 128, 128), 128)
        return [
            pltpu.make_async_copy(axial_hbm.at[:, part], axial_metric.at[:, part], late_sem.at[0, group]),
            pltpu.make_async_copy(radial_hbm.at[:, part], radial.at[:, part], late_sem.at[1, group]),
        ]

    loads = [
        pltpu.make_async_copy(area_hbm, area_ref, load_sem.at[0]),
        pltpu.make_async_copy(observer_hbm, observer_ref, load_sem.at[1]),
        pltpu.make_async_copy(bin_hbm, bin_ref, load_sem.at[2]),
        pltpu.make_async_copy(weight_hbm, weight_ref, load_sem.at[3]),
        pltpu.make_async_copy(table_hbm, table_ref, load_sem.at[4]),
        pltpu.make_async_copy(azimuth_hbm, azimuth_ref, load_sem.at[5]),
        pltpu.make_async_copy(full_hbm.at[me_a], full, load_sem.at[6]),
    ]
    for which in range(2):
        loads.append(pltpu.make_async_copy(sent_hbm.at[me_a, which], sent.at[which], load_sem.at[7 + 2 * which]))
        loads.append(pltpu.make_async_copy(taken_hbm.at[me_a, which], taken.at[which], load_sem.at[8 + 2 * which]))
    for step in range(BLOCKS // 2):
        for load in early_loads(group_at(step)):
            load.start()

    starts = (start_recv, start_hbm)
    cells, lined = (cells_a, cells_b), (lined_a, lined_b)
    edge_send, edge_recv = (edge_send_a, edge_send_b), (edge_recv_a, edge_recv_b)


    for part in range(2):
        for which in range(2):
            edge_recv[part][which, pl.ds(me_a, 1)] = jnp.zeros((1, 8, 4 * PLANES * PARTS[part][1]), F32)

    def moment_source(which, part, slot, share):
        first, rows = SHARE[part][share]
        return moment_send.at[which, slot, pl.ds(first, rows)]

    def moment_copy(which, part, slot, share):
        return pltpu.make_async_remote_copy(
            src_ref=moment_source(which, part, slot, share),
            dst_ref=moment_recv.at[which, part, me_z, pl.ds(0, SHARE[part][share][1])],
            send_sem=moment_send_sem.at[which, part],
            recv_sem=moment_recv_sem.at[which, part],
            device_id=(me_a, 2 * slot + share),
            device_id_type=MESH,
        )

    def send_moments(which, part, step):
        row = 4 * group_at(step)
        for turn in STEPS[:3]:
            for share in range(2):
                moment_copy(which, part, row + lax.rem(chip + turn, 4), share).start()

        @pl.when(step < 3)
        def _():
            for share in range(2):
                moment_copy(which, part, row + lax.rem(chip, 4), share).start()

        for share in range(2):

            @pl.when(jnp.logical_and(step == 3, core == share))
            def _():
                moment_copy(which, part, chip, 1 - share).start()
                pltpu.make_async_copy(
                    moment_source(which, part, chip, share),
                    moment_recv.at[which, part, me_z, pl.ds(0, SHARE[part][share][1])],
                    moment_recv_sem.at[which, part],
                ).start()

    def wait_moment_sends(which, part):
        for share in range(2):

            @pl.when(core == share)
            def _():
                rows = pl.ds(8 * PARTS[part][0], 8 * PARTS[part][1])
                sent_rows = moment_send.at[which, pl.ds(0, SLOTS - 1), rows]
                pltpu.make_async_copy(sent_rows, sent_rows, moment_send_sem.at[which, part]).wait()
                sent_rows = moment_source(which, part, SLOTS - 1, 1 - share)
                pltpu.make_async_copy(sent_rows, sent_rows, moment_send_sem.at[which, part]).wait()

    def reduce_moments(which, part, root):
        factor = root**ROWS
        wrap = 1.0 / (1.0 - root**NAZ)
        side = lax.rem(chip, 2)

        def place(step):
            return step + side * (AZIM - 1 - 2 * step)

        for share in range(2):
            first_row, count = SHARE[part][share]
            rows, there = pl.ds(0, count), pl.ds(first_row, count)

            @pl.when(core == share)
            def _():
                arrived = moment_recv.at[which, part, :, rows]
                pltpu.make_async_copy(arrived, arrived, moment_recv_sem.at[which, part]).wait()

                def gather(step, total):
                    return factor * total + moment_recv[which, part, place(step), rows]

                first = lax.fori_loop(0, AZIM, gather, jnp.zeros((count, LANES), F32), unroll=8) * wrap

                def follow(step, now):
                    other = place(step)
                    start_send[which, part, other, rows] = now
                    return factor * now + moment_recv[which, part, other, rows]

                lax.fori_loop(0, AZIM, follow, first, unroll=8)

                def hand_out(other):
                    pltpu.make_async_remote_copy(
                        src_ref=start_send.at[which, part, other, rows],
                        dst_ref=starts[which].at[chip, there],
                        send_sem=start_send_sem.at[which, part],
                        recv_sem=start_recv_sem.at[which, part],
                        device_id=(me_a, other),
                        device_id_type=MESH,
                    ).start()

                for step in AWAY:
                    for half in range(2):
                        hand_out(2 * chip_at(step) + half)
                hand_out(twin)
                pltpu.make_async_copy(
                    start_send.at[which, part, me_z, rows],
                    starts[which].at[chip, there],
                    start_recv_sem.at[which, part],
                ).start()

    def wait_starts(which, part):
        arrived = starts[which].at[:, pl.ds(8 * PARTS[part][0], 8 * PARTS[part][1])]
        pltpu.make_async_copy(arrived, arrived, start_recv_sem.at[which, part]).wait()

    def wait_start_sends(which, part):
        for share in range(2):

            @pl.when(core == share)
            def _():
                gone = start_send.at[which, part, pl.ds(0, AZIM - 1), pl.ds(0, SHARE[part][share][1])]
                pltpu.make_async_copy(gone, gone, start_send_sem.at[which, part]).wait()

    def moments_of(values, root):
        up = root * values[0]
        for row in range(1, ROWS):
            up = root * (up + values[row])
        down = root * values[ROWS - 1]
        for row in range(ROWS - 2, -1, -1):
            down = root * (down + values[row])
        return up, down

    def keep_moments(which, group, field, values, root):
        up, down = moments_of(values, root)
        for half in range(2):
            for side, value in ((0, up), (1, down)):
                moment_send[which, 4 * group + 2 * half + side, pl.ds(8 * field, 8)] = value[8 * half : 8 * half + 8]

    def halo_copies(which):
        copies = []
        for part in range(2):
            if which == 1:
                source, halo, depth = lined[part], filter_halo, 2
                there = pl.ds(PLANES * PARTS[part][0], PLANES * PARTS[part][1])
            else:
                source, halo, depth = azim_flux, deriv_halo, 1
                there = pl.ds(0, SLAB)
                if part == 1:
                    break
            for side, other, rows in ((0, after, pl.ds(ROWS - depth, depth)), (1, before, pl.ds(0, depth))):
                copies.append(
                    pltpu.make_async_remote_copy(
                        src_ref=source.at[rows],
                        dst_ref=halo.at[side, :, there],
                        send_sem=halo_send_sem.at[which, part, side],
                        recv_sem=halo_recv_sem.at[which, part, side],
                        device_id=(me_a, other),
                        device_id_type=MESH,
                    )
                )
        return copies

    def edge_copy(which, part, step):
        other = lax.rem(me_a + step, AXIAL)
        down = jnp.where(other < me_a, 1, 0)
        return pltpu.make_async_remote_copy(
            src_ref=edge_send[part].at[which, down],
            dst_ref=edge_recv[part].at[which, me_a],
            send_sem=edge_send_sem.at[which, part, step - 1],
            recv_sem=edge_recv_sem.at[which, part, step - 1],
            device_id=(other, me_z),
            device_id_type=MESH,
        )

    def send_edges(which, part):
        slab = PLANES * PARTS[part][1]

        def piece(step, carry):
            at = pl.multiple_of(step * 2 * slab, 2 * slab)
            total = dot_last(sent[which, 0], cells[part][which, pl.ds(at, 2 * slab)]) + dot_last(
                sent[which, 1], cells[part][which, pl.ds(4 * slab + at, 2 * slab)]
            )
            total = total[:16] + total[16:]
            edge_send[part][which, 0, :, pl.ds(at, 2 * slab)] = total[:8]
            edge_send[part][which, 1, :, pl.ds(at, 2 * slab)] = total[8:]
            return carry

        lax.fori_loop(0, 2, piece, 0, unroll=True)
        for step in STEPS[:3]:
            edge_copy(which, part, step).start()

    def own_part(which, part):
        slab = PLANES * PARTS[part][1]

        def piece(step, carry):
            at = pl.multiple_of(step * 2 * slab, 2 * slab)
            total = jnp.dot(cells[part][which, pl.ds(at, 2 * slab)], own[which], preferred_element_type=F32)
            lined[part][pl.ds(2 * step, 2)] = (total[:, :LANES] + total[:, LANES:]).reshape(2, slab, LANES)
            return carry

        lax.fori_loop(0, 4, piece, 0, unroll=True)

    def add_edges(which, part):
        slab = PLANES * PARTS[part][1]
        for step in range(1, AXIAL):
            edge_copy(which, part, step).wait_recv()

        def piece(step, carry):
            at = pl.multiple_of(lax.rem(step, 2) * 2 * slab, 2 * slab)
            received = edge_recv[part][which, :, :, pl.ds(at, 2 * slab)].reshape(32, 2 * slab)
            high, low = two_terms(received)
            total = dot_first(jnp.concatenate([high, low], axis=0), taken[which, step // 2])
            total = (total[:, :LANES] + total[:, LANES:]).reshape(2, slab, LANES)
            lined[part][pl.ds(2 * step, 2)] = lined[part][pl.ds(2 * step, 2)] + total
            return carry

        lax.fori_loop(0, 4, piece, 0, unroll=True)

    def keep_cells(which, row, field, group, value):
        part = PART_OF[field]
        first, count = PARTS[part]
        high, low = two_terms(value)
        at = pl.multiple_of((row * count + field - first) * PLANES + group * 16, 16)
        cells[part][which, pl.ds(at, 16), pl.ds(0, LANES)] = high
        cells[part][which, pl.ds(at, 16), pl.ds(LANES, LANES)] = low

    def axial_copy(which, step):
        return pltpu.make_async_remote_copy(
            src_ref=axial_send.at[which],
            dst_ref=axial_recv.at[which, me_a],
            send_sem=axial_send_sem.at[which, step - 1],
            recv_sem=axial_recv_sem.at[which, step - 1],
            device_id=(lax.rem(me_a + step, AXIAL), me_z),
            device_id_type=MESH,
        )

    def send_axial(which, value):
        axial_send[which] = value
        axial_recv[which, pl.ds(me_a, 1)] = value[None]
        for step in STEPS[:3]:
            axial_copy(which, step).start()

    def take_axial(which):
        for step in range(1, AXIAL):
            axial_copy(which, step).wait_recv()
        line = jnp.concatenate([axial_recv[which, k] for k in range(AXIAL)], axis=1)
        return jnp.dot(line, full[which], preferred_element_type=F32, precision=lax.Precision.HIGHEST)

    def send_plane(which, value):
        plane_send[which] = value
        plane_recv[which, 0] = value

        def piece(other):
            pltpu.make_async_remote_copy(
                src_ref=plane_send.at[which],
                dst_ref=plane_recv.at[which, lax.rem(me_z - other + AZIM, AZIM)],
                send_sem=plane_send_sem.at[which],
                recv_sem=plane_recv_sem.at[which],
                device_id=(me_a, other),
                device_id_type=MESH,
            ).start()

        for step in AWAY:
            for half in range(2):
                piece(2 * chip_at(step) + half)
        piece(twin)

    def plane_wait(which, sem):
        part = plane_recv.at[which, pl.ds(1, AZIM - 1)]
        pltpu.make_async_copy(part, part, sem.at[which]).wait()

    def take_plane(which):
        plane_wait(which, plane_recv_sem)
        return jnp.dot(
            azimuth_ref[which],
            plane_recv[which].reshape(NAZ, LANES),
            preferred_element_type=F32,
            precision=lax.Precision.HIGHEST,
        )

    def flux_of(metric, at, rho, vel, prs, vol, heat):
        grad = [metric[comp, at] for comp in range(3)]
        contra = vol * (grad[0] * vel[0] + grad[1] * vel[1] + grad[2] * vel[2])
        flow = rho * contra
        push = vol * prs
        return [flow] + [flow * vel[comp] + grad[comp] * push for comp in range(3)] + [heat * contra]

    def cells_at(group, row):
        at = pl.ds(group * 128 + row, 16, stride=ROWS)
        rho, prs, vol = density[at], pressure[at], volume[at]
        vel = [velocity[comp, at] for comp in range(3)]
        energy = 2.5 * prs + 0.5 * rho * (vel[0] * vel[0] + vel[1] * vel[1] + vel[2] * vel[2])
        return at, rho, vel, prs, vol, energy

    def azim_group(step, carry):
        group = group_at(step)
        for load in early_loads(group):
            load.wait()
        for load in late_loads(group):
            load.start()
        flux = [[None] * ROWS for _ in range(FIELDS)]
        for row in range(ROWS):
            at, rho, vel, prs, vol, energy = cells_at(group, row)
            parts = flux_of(azim_metric, at, rho, vel, prs, vol, energy + prs)
            for field in range(FIELDS):
                flux[field][row] = parts[field]
                azim_flux[row, pl.ds(pl.multiple_of(field * PLANES + group * 16, 16), 16)] = parts[field]
        for field in range(FIELDS):
            keep_moments(0, group, field, flux[field], DL)
        return carry

    lax.fori_loop(0, BLOCKS // 2, azim_group, 0)

    for load in loads:
        load.start()

    pl.semaphore_wait(barrier, PEERS)
    for part in range(2):

        def send_part(step, carry, part=part):
            send_moments(0, part, step)
            return carry

        lax.fori_loop(0, BLOCKS // 2, send_part, 0)
    send_plane(0, azim_flux[:, 0] + azim_flux[:, 2 * PLANES])
    for copy in halo_copies(0):
        copy.start()

    def axial_group(group, carry):
        for load in late_loads(group):
            load.wait()
        for row in range(ROWS):
            at, rho, vel, prs, vol, energy = cells_at(group, row)
            state = [rho, rho * vel[0], rho * vel[1], rho * vel[2], energy]
            ratio[row, pl.ds(pl.multiple_of(group * 16, 16), 16)] = SECTION / vol
            for field in range(FIELDS):
                base[row, pl.ds(pl.multiple_of(field * PLANES + group * 16, 16), 16)] = (
                    state[field] + SECTION * radial[field, at]
                )
            parts = flux_of(axial_metric, at, rho, vel, prs, vol, energy + prs)
            for field in range(FIELDS):
                keep_cells(0, row, field, group, parts[field])
            panel_axial[group, pl.ds(row, 1)] = parts[0][:1] + parts[2][:1]
        return carry

    lax.fori_loop(0, BLOCKS // 2, axial_group, 0)
    send_axial(0, panel_axial[0])
    for load in loads:
        load.wait()
    send_edges(0, 0)
    send_edges(0, 1)

    ids = observer_ref[...]
    order = (
        lax.shift_right_logical(ids, 7) * 128
        + (lax.shift_right_logical(ids, 2) & 1) * 64
        + (lax.shift_right_logical(ids, 3) & 15) * 4
        + (ids & 3)
    )
    partial[pl.ds(0, ENTRY_ROWS)] = order.astype(F32)

    def hot_row(row, carry):
        wanted = partial[pl.ds(row, 1)].astype(jnp.int32)
        rows = lax.broadcasted_iota(jnp.int32, (OBSERVERS, LANES), 0)
        at = pl.multiple_of(row * LANES, LANES)
        observer_hot[:, pl.ds(at, LANES)] = jnp.where(rows == wanted, 1.0, 0.0).astype(BF16)
        same = lax.broadcasted_iota(jnp.int32, (TIME_BINS, LANES), 0) == bin_ref[pl.ds(row, 1)]
        bin_hot[pl.ds(0, TIME_BINS), pl.ds(at, LANES)] = jnp.where(same, 1.0, 0.0).astype(BF16)
        return carry

    lax.fori_loop(0, ENTRY_ROWS, hot_row, 0)

    for which in range(2):
        high, low = two_terms(full[which, pl.ds(pl.multiple_of(me_a * LANES, LANES), LANES)])
        for top in range(2):
            own[which, pl.ds(top * LANES, LANES), pl.ds(0, LANES)] = high
            own[which, pl.ds(top * LANES, LANES), pl.ds(LANES, LANES)] = low
    own_part(0, 0)
    own_part(0, 1)
    reduce_moments(0, 0, DL)
    reduce_moments(0, 1, DL)
    change = take_axial(0) + take_plane(0)
    send_axial(1, base[:, 0] + base[:, 2 * PLANES] - ratio[:, 0] * change)
    add_edges(0, 0)
    add_edges(0, 1)

    def near_section(group, carry):
        here = pl.ds(pl.multiple_of(group * 16, 16), 16)
        for field in range(FIELDS):
            part = PART_OF[field]
            at = pl.ds(pl.multiple_of(field * PLANES + group * 16, 16), 16)
            inside = pl.ds(pl.multiple_of((field - PARTS[part][0]) * PLANES + group * 16, 16), 16)
            flux = [deriv_halo[0, 0, at]] + [azim_flux[row, at] for row in range(ROWS)] + [deriv_halo[1, 0, at]]
            tails = near_tails(flux[1:-1], DL)
            for row in range(ROWS):
                up, down = tails[row]
                spread = down if up is None else -up if down is None else down - up
                deriv = DK * spread + C1 * (flux[row + 2] - flux[row])
                base[row, at] = base[row, at] - ratio[row, here] * (lined[part][row, inside] + deriv)
        return carry

    def section(part):
        first, count = PARTS[part]

        def section_group(group, carry):
            here = pl.ds(pl.multiple_of(group * 16, 16), 16)
            for field in range(first, first + count):
                at = pl.ds(pl.multiple_of(field * PLANES + group * 16, 16), 16)
                up = DK * start_of(start_recv, group, field, 0)
                down = DK * start_of(start_recv, group, field, 1)
                for row in range(ROWS):
                    far = DL ** (ROWS - 1 - row) * down - DL**row * up
                    keep_cells(1, row, field, group, base[row, at] - ratio[row, here] * far)
            return carry

        lax.fori_loop(0, BLOCKS // 2, section_group, 0)

    def smoothed_moments(part):
        first, count = PARTS[part]

        def moment_group(step, carry):
            group = group_at(step)
            for field in range(first, first + count):
                inside = pl.ds(pl.multiple_of((field - first) * PLANES + group * 16, 16), 16)
                keep_moments(1, group, field, [lined[part][row, inside] for row in range(ROWS)], FL)
            send_moments(1, part, step)
            return carry

        lax.fori_loop(0, BLOCKS // 2, moment_group, 0)

    for copy in halo_copies(0):
        copy.wait_recv()
    lax.fori_loop(0, BLOCKS // 2, near_section, 0)
    wait_starts(0, 0)
    section(0)
    send_edges(1, 0)
    send_plane(1, take_axial(1))
    wait_starts(0, 1)
    section(1)
    send_edges(1, 1)
    own_part(1, 0)
    own_part(1, 1)
    add_edges(1, 0)
    smoothed_moments(0)
    add_edges(1, 1)
    smoothed_moments(1)
    for copy in halo_copies(1):
        copy.start()

    source = area_ref[...] * (take_plane(1) - 1.0)
    picks = weight_ref[...]
    low_half = jnp.take_along_axis(
        jnp.broadcast_to(table_ref[pl.ds(0, 1)], (ENTRY_ROWS, LANES)), picks & 127, axis=1
    )
    high_half = jnp.take_along_axis(
        jnp.broadcast_to(table_ref[pl.ds(1, 1)], (ENTRY_ROWS, LANES)), picks & 127, axis=1
    )
    weights = jnp.where(picks < LANES, low_half, high_half)
    values = weights * jnp.concatenate([source] * 4, axis=0)
    high, low = two_terms(values)
    partial[pl.ds(0, ENTRY_ROWS)] = high.astype(F32)
    partial[pl.ds(ENTRY_ROWS, ENTRY_ROWS)] = low.astype(F32)

    def bin_row(row, carry):
        at = pl.multiple_of(row * LANES, LANES)
        mask = bin_hot[pl.ds(0, TIME_BINS), pl.ds(at, LANES)]
        for term in range(2):
            value = jnp.broadcast_to(partial[pl.ds(term * ENTRY_ROWS + row, 1)], (TIME_BINS, LANES)).astype(BF16)
            bin_hot[pl.ds(term * TIME_BINS, TIME_BINS), pl.ds(at, LANES)] = mask * value
        return carry

    lax.fori_loop(0, ENTRY_ROWS, bin_row, 0)

    total = dot_last(observer_hot[...], bin_hot[...])
    partial[...] = total[:, :TIME_BINS] + total[:, TIME_BINS:]

    mine = me_a * 2 + core

    def part_copy(step):
        other = lax.rem(mine + step, 8)
        other_z = me_z - core + lax.rem(other, 2)
        return pltpu.make_async_remote_copy(
            src_ref=partial.at[pl.ds(pl.multiple_of(other * 64, 64), 64)],
            dst_ref=part_recv.at[step - 1],
            send_sem=part_send_sem.at[step - 1],
            recv_sem=part_recv_sem.at[step - 1],
            device_id=(other // 2, other_z),
            device_id_type=MESH,
        )

    for step in range(1, 8):
        part_copy(step).start()
    reduce_moments(1, 0, FL)
    reduce_moments(1, 1, FL)
    total = partial[pl.ds(pl.multiple_of(mine * 64, 64), 64)]
    for step in range(1, 8):
        part_copy(step).wait_recv()
        total = total + part_recv[step - 1]
    for owner in range(16):
        owner_send[owner, pl.ds(0, 4)] = total[4 * owner : 4 * owner + 4]
        owner_send[owner, pl.ds(4, 4)] = jnp.zeros((4, LANES), F32)

    def owner_copy(step):
        other = lax.rem(chip + step, 16)
        return pltpu.make_async_remote_copy(
            src_ref=owner_send.at[other],
            dst_ref=owner_hbm.at[step],
            send_sem=owner_send_sem.at[step - 1],
            recv_sem=owner_recv_sem.at[step - 1],
            device_id=(me_a, 2 * other + core),
            device_id_type=MESH,
        )

    for step in range(1, 16):
        owner_copy(step).start()
    own_copy = pltpu.make_async_copy(owner_send.at[chip], owner_hbm.at[0], owner_sem)
    own_copy.start()
    for copy in halo_copies(1):
        copy.wait_recv()

    def near_group(group, carry):
        for field in range(FIELDS):
            part = PART_OF[field]
            at = pl.ds(pl.multiple_of(field * PLANES + group * 16, 16), 16)
            inside = pl.ds(pl.multiple_of((field - PARTS[part][0]) * PLANES + group * 16, 16), 16)
            value = [filter_halo[0, row, at] for row in range(2)]
            value += [lined[part][row, inside] for row in range(ROWS)]
            value += [filter_halo[1, row, at] for row in range(2)]
            ends = near_tails(value[2:-2], FL)
            for row in range(ROWS):
                up, down = ends[row]
                tails = down if up is None else up if down is None else up + down
                edges = E1 * (value[row + 1] + value[row + 3]) + E2 * (value[row] + value[row + 4])
                near[row, at] = FK * tails + (FK + E0) * value[row + 2] + edges
        return carry

    lax.fori_loop(0, BLOCKS // 2, near_group, 0)
    keep = pltpu.make_async_copy(near, near_hbm, keep_sem)
    keep.start()
    for part in range(2):
        wait_starts(1, part)

    own_copy.wait()
    for step in range(1, 16):
        owner_copy(step).wait_recv()
    keep.wait()

    for which in range(2):
        for part in range(2):
            wait_moment_sends(which, part)
            wait_start_sends(which, part)
            for step in range(1, AXIAL):
                edge_copy(which, part, step).wait_send()
        for copy in halo_copies(which):
            copy.wait_send()
    for step in range(1, 8):
        part_copy(step).wait_send()
    for step in range(1, 16):
        owner_copy(step).wait_send()
    for which in range(2):
        plane_wait(which, plane_send_sem)
        for step in range(1, AXIAL):
            axial_copy(which, step).wait_send()


def per_device(
    density,
    velocity,
    pressure,
    axial_metric,
    azim_metric,
    volume,
    radial_term,
    panel_area,
    observer_ids,
    bin_ids,
    weight_ids,
    bin_weights,
):
    sent, taken, full = both_tables()
    rows = PLANES * ROWS
    slabs = [PLANES * count for _, count in PARTS]
    hbm = pl.BlockSpec(memory_space=pltpu.HBM)
    dma = pltpu.SemaphoreType.DMA
    near, starts, parts = pl.pallas_call(
        kernel,
        out_shape=(
            jax.ShapeDtypeStruct((ROWS, SLAB, LANES), F32),
            jax.ShapeDtypeStruct((SLOTS, TILE_ROWS, LANES), F32),
            jax.ShapeDtypeStruct((16, 8, TIME_BINS), F32),
        ),
        in_specs=[hbm] * 16,
        out_specs=(hbm, hbm, hbm),
        scratch_shapes=[
            pltpu.VMEM((2, 2 * LANES, 2 * LANES), BF16),
            pltpu.VMEM((2, 2, 32, 2 * LANES), BF16),
            pltpu.VMEM((2, 2, 64, 2 * LANES), BF16),
            pltpu.VMEM((rows, LANES), F32),
            pltpu.VMEM((3, rows, LANES), F32),
            pltpu.VMEM((rows, LANES), F32),
            pltpu.VMEM((3, rows, LANES), F32),
            pltpu.VMEM((3, rows, LANES), F32),
            pltpu.VMEM((rows, LANES), F32),
            pltpu.VMEM((FIELDS, rows, LANES), F32),
            pltpu.VMEM((ROWS, LANES), F32),
            pltpu.VMEM((ENTRY_ROWS, LANES), jnp.int32),
            pltpu.VMEM((ENTRY_ROWS, LANES), jnp.int32),
            pltpu.VMEM((ENTRY_ROWS, LANES), jnp.int32),
            pltpu.VMEM((2, LANES), F32),
            pltpu.VMEM((2, ROWS, NAZ), F32),
            pltpu.VMEM((2, NA, LANES), F32),
            pltpu.VMEM((ROWS, SLAB, LANES), F32),
            pltpu.VMEM((ROWS, SLAB, LANES), F32),
            pltpu.VMEM((ROWS, PLANES, LANES), F32),
            *[pltpu.VMEM((2, ROWS * slab, 2 * LANES), BF16) for slab in slabs],
            *[pltpu.VMEM((ROWS, slab, LANES), F32) for slab in slabs],
            *[pltpu.VMEM((2, 2, 8, 4 * slab), F32) for slab in slabs],
            *[pltpu.VMEM((2, AXIAL, 8, 4 * slab), F32) for slab in slabs],
            pltpu.VMEM((2, SLOTS, TILE_ROWS, LANES), F32),
            pltpu.VMEM((2, 2, AZIM, 16, LANES), F32),
            pltpu.VMEM((2, 2, AZIM, 16, LANES), F32),
            pltpu.VMEM((SLOTS, TILE_ROWS, LANES), F32),
            pltpu.VMEM((2, 1, SLAB, LANES), F32),
            pltpu.VMEM((2, 2, SLAB, LANES), F32),
            pltpu.VMEM((ROWS, SLAB, LANES), F32),
            pltpu.VMEM((OBSERVERS, ENTRY_ROWS * LANES), BF16),
            pltpu.VMEM((2 * TIME_BINS, ENTRY_ROWS * LANES), BF16),
            pltpu.VMEM((OBSERVERS, TIME_BINS), F32),
            pltpu.VMEM((7, 64, TIME_BINS), F32),
            pltpu.VMEM((16, 8, TIME_BINS), F32),
            pltpu.VMEM((2, ROWS, LANES), F32),
            pltpu.VMEM((2, AZIM, ROWS, LANES), F32),
            pltpu.VMEM((2, ROWS, LANES), F32),
            pltpu.VMEM((2, AXIAL, ROWS, LANES), F32),
            pltpu.VMEM((BLOCKS // 2, ROWS, LANES), F32),
            dma(()),
            dma(()),
            dma((11,)),
            dma((5, BLOCKS // 2)),
            dma((2, BLOCKS // 2)),
            dma((2, 2, 3)),
            dma((2, 2, 3)),
            dma((2, 2)),
            dma((2, 2)),
            dma((2, 2)),
            dma((2, 2)),
            dma((2, 2, 2)),
            dma((2, 2, 2)),
            dma((7,)),
            dma((7,)),
            dma((15,)),
            dma((15,)),
            dma((2,)),
            dma((2,)),
            dma((2, 3)),
            dma((2, 3)),
        ],
        compiler_params=pltpu.CompilerParams(
            collective_id=0, has_side_effects=True
        ),
    )(
        jnp.asarray(sent),
        jnp.asarray(taken),
        density.reshape(rows, LANES),
        velocity.reshape(3, rows, LANES),
        pressure.reshape(rows, LANES),
        axial_metric.reshape(3, rows, LANES),
        azim_metric.reshape(3, rows, LANES),
        volume.reshape(rows, LANES),
        radial_term.reshape(FIELDS, rows, LANES),
        panel_area,
        observer_ids.reshape(ENTRY_ROWS, LANES),
        bin_ids.reshape(ENTRY_ROWS, LANES),
        weight_ids.reshape(ENTRY_ROWS, LANES),
        bin_weights.reshape(2, LANES),
        jnp.asarray(azimuth_rows()),
        jnp.asarray(full),
    )
    state, signals = pl.pallas_call(
        finish_kernel,
        out_shape=(
            jax.ShapeDtypeStruct((FIELDS, rows, LANES), F32),
            jax.ShapeDtypeStruct((4, TIME_BINS), F32),
        ),
        in_specs=[hbm] * 3,
        out_specs=(hbm, hbm),
        scratch_shapes=[
            pltpu.VMEM((ROWS, FIELDS, PLANES, LANES), F32),
            pltpu.VMEM((SLOTS, TILE_ROWS, LANES), F32),
            pltpu.VMEM((FIELDS, rows, LANES), F32),
            pltpu.VMEM((16, 8, TIME_BINS), F32),
            pltpu.VMEM((4, TIME_BINS), F32),
            dma((BLOCKS // 2, 3)),
            dma((BLOCKS // 2,)),
            dma((2,)),
        ],
    )(
        near.reshape(ROWS, FIELDS, PLANES, LANES),
        starts,
        parts,
    )
    return state.reshape(FIELDS, PLANES, ROWS, LANES), signals


def solution(mesh):
    placed = (
        P(None, "azim", "axial"),
        P(None, None, "azim", "axial"),
        P(None, "azim", "axial"),
        P(None, None, "azim", "axial"),
        P(None, None, "azim", "axial"),
        P(None, "azim", "axial"),
        P(None, None, "azim", "axial"),
        P("azim", "axial"),
        P(None, "azim", "axial"),
        P(None, "azim", "axial"),
        P(None, "azim", "axial"),
        P(),
    )
    return jax.shard_map(
        per_device,
        mesh=mesh,
        in_specs=placed,
        out_specs=(P(None, None, "azim", "axial"), P(("axial", "azim"), None)),
        check_vma=False,
    )
```

```python
import functools
import math

import jax
import jax.numpy as jnp
import ml_dtypes
import numpy as np
from jax import lax
from jax.experimental import pallas as pl
from jax.experimental.pallas import tpu as pltpu
from jax.sharding import PartitionSpec as P

F32 = jnp.float32
BF16 = jnp.bfloat16
MESH = pl.DeviceIdType.MESH

PLANES = 64
FIELDS = 5
ROWS = 8
LANES = 128
AXIAL = 4
AZIM = 32
NA = AXIAL * LANES
NAZ = AZIM * ROWS
SLAB = FIELDS * PLANES
BLOCKS = PLANES // 8
SLOTS = 2 * BLOCKS
TILE_ROWS = 8 * FIELDS
PARTS = ((0, 3), (3, 2))
PART_OF = (0, 0, 0, 1, 1)
SHARE = (((0, 16), (16, 8)), ((24, 8), (32, 8)))
STEPS = (2, 1, 3, 0)
AWAY = tuple((dz, dy) for dz in STEPS[:3] for dy in STEPS[:3]) + ((2, 0), (0, 2), (1, 0), (3, 0), (0, 1), (0, 3))
ENTRY_ROWS = 32
OBSERVERS = 512
TIME_BINS = 128
PEERS = (AZIM - 1) + 2 * (AXIAL - 1)

SECTION = 0.25
DERIV_ALPHA = 1.0 / 3.0
BETA = 0.499


def decay_root(alpha):
    return (-1.0 + math.sqrt(1.0 - 4.0 * alpha * alpha)) / (2.0 * alpha)


DL = decay_root(DERIV_ALPHA)
FL = decay_root(BETA)
C1 = (1.0 / 36.0) / DERIV_ALPHA
DS = 1.0 / math.sqrt(1.0 - 4.0 * DERIV_ALPHA**2)
DK = (7.0 / 9.0 - C1) * DS * (1.0 / DL - DL)
FC = [
    (11.0 + 10.0 * BETA) / 16.0,
    (15.0 + 34.0 * BETA) / 32.0,
    (-3.0 + 6.0 * BETA) / 16.0,
    (1.0 - 2.0 * BETA) / 32.0,
]
FS = 1.0 / math.sqrt(1.0 - 4.0 * BETA**2)
E2 = FC[3] / (2.0 * BETA)
E1 = (FC[2] / 2.0 - E2) / BETA
E0 = (FC[1] / 2.0 - E1 - BETA * E2) / BETA
FK = (FC[0] - E0 - 2.0 * BETA * E1) * FS


def split(values):
    high = values.astype(ml_dtypes.bfloat16)
    low = (values - high.astype(np.float64)).astype(ml_dtypes.bfloat16)
    return high, low


def axial_tables(root, scale, band):
    n, w = NA, LANES
    index = np.arange(n)
    green = scale * (
        np.power(root, np.abs(index[:, None] - index[None, :]))
        - np.power(root, 2 * n - index[:, None] - index[None, :])
    )
    side = np.zeros((n, n))
    for shift, value in band.items():
        side += value * np.eye(n, k=shift)
    whole = green @ side
    left = np.zeros((AXIAL, w))
    right = np.zeros((AXIAL, w))
    for k in range(AXIAL):
        cols = slice(k * w, (k + 1) * w)
        lo, hi = max(0, k * w - 3), min(n, (k + 1) * w + 3)
        m = np.arange(lo, hi)
        left[k] = np.power(root, ((k + 1) * w - m).astype(np.float64)) @ side[lo:hi, cols]
        right[k] = (
            np.power(root, (m - k * w + 1).astype(np.float64))
            - np.power(root, (2 * n - m - k * w + 1).astype(np.float64))
        ) @ side[lo:hi, cols]
    t = np.arange(w)
    full = np.stack([whole[d * w : (d + 1) * w].T for d in range(AXIAL)]).astype(np.float32)
    sent = np.zeros((AXIAL, 2, 32, 2 * w), ml_dtypes.bfloat16)
    taken = np.zeros((AXIAL, 2, 64, 2 * w), ml_dtypes.bfloat16)
    for d in range(AXIAL):
        for half in range(2):
            rows = np.zeros((16, w))
            base = half * 4
            rows[base] = left[d]
            rows[base + 1, w - 1] = 1.0
            rows[base + 2, w - 2] = 1.0
            rows[8 + base] = right[d]
            rows[8 + base + 1, 0] = 1.0
            rows[8 + base + 2, 1] = 1.0
            high, low = split(rows)
            sent[d, half] = np.concatenate(
                [np.concatenate([high, high], axis=1), np.concatenate([low, low], axis=1)], axis=0
            )
            rows = np.zeros((32, w))
            for k in range(AXIAL):
                row = k * 8 + half * 4
                i = d * w + t
                if k < d:
                    rows[row] = scale * (
                        np.power(root, (i - (k + 1) * w).astype(np.float64))
                        - np.power(root, (2 * n - i - (k + 1) * w).astype(np.float64))
                    )
                    if k == d - 1:
                        for edge in range(2):
                            col = d * w - 1 - edge
                            for near in range(2 - edge):
                                rows[row + 1 + edge, near] = (
                                    whole[d * w + near, col] - rows[row, near] * left[k, col - k * w]
                                )
                if k > d:
                    rows[row] = scale * np.power(root, (k * w - 1 - i).astype(np.float64))
                    if k == d + 1:
                        for edge in range(2):
                            col = k * w + edge
                            for near in range(2 - edge):
                                rows[row + 1 + edge, w - 1 - near] = (
                                    whole[k * w - 1 - near, col] - rows[row, w - 1 - near] * right[k, edge]
                                )
            high, low = split(rows)
            pair = np.concatenate([high, low], axis=1)
            taken[d, half] = np.concatenate([pair, pair], axis=0)
    return sent, taken, full


def both_tables():
    deriv = axial_tables(DL, DS, {1: 7.0 / 9.0, -1: -7.0 / 9.0, 2: 1.0 / 36.0, -2: -1.0 / 36.0})
    band = {0: FC[0]}
    for shift in range(1, 4):
        band[shift] = band[-shift] = FC[shift] / 2.0
    smooth = axial_tables(FL, FS, band)
    return [np.stack(pair, axis=1) for pair in zip(deriv, smooth)]


def azimuth_rows():
    gap = np.arange(NAZ)
    slope = DK * (np.power(DL, gap) - np.power(DL, NAZ - gap)) / (1.0 - DL**NAZ)
    slope[0] = 0.0
    slope[1] += C1
    slope[-1] -= C1
    line = FK * (np.power(FL, gap) + np.power(FL, NAZ - gap)) / (1.0 - FL**NAZ)
    line[0] = FK * (1.0 + 2.0 * FL**NAZ / (1.0 - FL**NAZ)) + E0
    for shift, value in ((1, E1), (2, E2)):
        line[shift] += value
        line[-shift] += value
    rows = np.arange(ROWS)
    at = (gap[None, :] - rows[:, None]) % NAZ
    return np.stack([slope[at], line[at]]).astype(np.float32)


def two_terms(value):
    high = value.astype(BF16)
    low = (value - high.astype(F32)).astype(BF16)
    return high, low


def dot_last(left, right):
    return lax.dot_general(left, right, (((1,), (1,)), ((), ())), preferred_element_type=F32)


def dot_first(left, right):
    return lax.dot_general(left, right, (((0,), (0,)), ((), ())), preferred_element_type=F32)


def near_tails(values, root):
    up, down = [None], [None]
    for row in range(ROWS - 1):
        last, back = values[row], values[ROWS - 1 - row]
        up.append(root * (last if up[-1] is None else last + up[-1]))
        down.append(root * (back if down[-1] is None else back + down[-1]))
    return list(zip(up, down[::-1]))


def start_of(starts, group, field, side):
    return jnp.concatenate(
        [starts[4 * group + 2 * half + side, pl.ds(8 * field, 8)] for half in range(2)], axis=0
    )


def finish_kernel(
    near_hbm, start_hbm, part_hbm, state_hbm, signal_hbm, near, starts, final, parts, signals, load_sem, store_sem, part_sem
):
    part_copy = pltpu.make_async_copy(part_hbm, parts, part_sem.at[0])
    signal_copy = pltpu.make_async_copy(signals, signal_hbm, part_sem.at[1])

    def loads(group):
        slots = pl.ds(4 * group, 4)
        planes = pl.ds(16 * group, 16)
        return [
            pltpu.make_async_copy(start_hbm.at[slots], starts.at[slots], load_sem.at[group, 0]),
            pltpu.make_async_copy(near_hbm.at[:, :, planes], near.at[:, :, planes], load_sem.at[group, 1]),
        ]

    def store(group):
        planes = pl.ds(128 * group, 128)
        return pltpu.make_async_copy(final.at[:, planes], state_hbm.at[:, planes], store_sem.at[group])

    for group in range(BLOCKS // 2):
        for load in loads(group):
            load.start()
    part_copy.start()

    for group in range(BLOCKS // 2):
        for load in loads(group):
            load.wait()
        planes = pl.ds(16 * group, 16)
        for field in range(FIELDS):
            up = FK * start_of(starts, group, field, 0)
            down = FK * start_of(starts, group, field, 1)
            for row in range(ROWS):
                result = near[row, field, planes] + (FL**row * up + FL ** (ROWS - 1 - row) * down)
                final[field, pl.ds(128 * group + row, 16, stride=ROWS)] = result
        store(group).start()
        if group == 0:
            part_copy.wait()
            signals[...] = jnp.sum(parts[...], axis=0)[:4]
            signal_copy.start()

    for group in range(BLOCKS // 2):
        store(group).wait()
    signal_copy.wait()


def kernel(
    sent_hbm,
    taken_hbm,
    density_hbm,
    velocity_hbm,
    pressure_hbm,
    axial_hbm,
    azim_hbm,
    volume_hbm,
    radial_hbm,
    area_hbm,
    observer_hbm,
    bin_hbm,
    weight_hbm,
    table_hbm,
    azimuth_hbm,
    full_hbm,
    near_hbm,
    start_hbm,
    owner_hbm,
    own,
    sent,
    taken,
    density,
    velocity,
    pressure,
    axial_metric,
    azim_metric,
    volume,
    radial,
    area_ref,
    observer_ref,
    bin_ref,
    weight_ref,
    table_ref,
    azimuth_ref,
    full,
    azim_flux,
    base,
    ratio,
    cells_a,
    cells_b,
    lined_a,
    lined_b,
    edge_send_a,
    edge_send_b,
    edge_recv_a,
    edge_recv_b,
    moment_send,
    moment_recv,
    start_send,
    start_recv,
    deriv_halo,
    filter_halo,
    near,
    observer_hot,
    bin_hot,
    partial,
    part_recv,
    owner_send,
    plane_send,
    plane_recv,
    axial_send,
    axial_recv,
    panel_axial,
    keep_sem,
    owner_sem,
    load_sem,
    early_sem,
    late_sem,
    edge_send_sem,
    edge_recv_sem,
    moment_send_sem,
    moment_recv_sem,
    start_send_sem,
    start_recv_sem,
    halo_send_sem,
    halo_recv_sem,
    part_send_sem,
    part_recv_sem,
    owner_send_sem,
    owner_recv_sem,
    plane_send_sem,
    plane_recv_sem,
    axial_send_sem,
    axial_recv_sem,
):
    me_a = lax.axis_index("axial")
    me_z = lax.axis_index("azim")
    core = lax.rem(me_z, 2)
    chip = me_z // 2
    twin = me_z + 1 - 2 * core
    after = lax.rem(me_z + 1, AZIM)
    before = lax.rem(me_z + AZIM - 1, AZIM)

    def chip_at(step):
        return 4 * lax.rem(chip // 4 + step[0], 4) + lax.rem(chip + step[1], 4)

    def group_at(step):
        away = jnp.where(step == 0, STEPS[0], jnp.where(step == 1, STEPS[1], jnp.where(step == 2, STEPS[2], 0)))
        return lax.rem(chip // 4 + away, 4)

    barrier = pltpu.get_barrier_semaphore()

    def greet(other_a, other_z):
        pl.semaphore_signal(barrier, inc=1, device_id=(other_a, other_z), device_id_type=MESH)

    for step in AWAY:
        for half in range(2):
            greet(me_a, 2 * chip_at(step) + half)
    for step in STEPS[:3]:
        greet(lax.rem(me_a + step, AXIAL), me_z)
        greet(lax.rem(me_a + step, AXIAL), twin)
    greet(me_a, twin)

    def early_loads(group):
        part = pl.ds(pl.multiple_of(group * 128, 128), 128)
        whole = slice(None)
        return [
            pltpu.make_async_copy(source.at[where], dest.at[where], early_sem.at[number, group])
            for number, (source, dest, where) in enumerate(
                (
                    (density_hbm, density, (part,)),
                    (velocity_hbm, velocity, (whole, part)),
                    (pressure_hbm, pressure, (part,)),
                    (volume_hbm, volume, (part,)),
                    (azim_hbm, azim_metric, (whole, part)),
                )
            )
        ]

    def late_loads(group):
        part = pl.ds(pl.multiple_of(group * 128, 128), 128)
        return [
            pltpu.make_async_copy(axial_hbm.at[:, part], axial_metric.at[:, part], late_sem.at[0, group]),
            pltpu.make_async_copy(radial_hbm.at[:, part], radial.at[:, part], late_sem.at[1, group]),
        ]

    loads = [
        pltpu.make_async_copy(area_hbm, area_ref, load_sem.at[0]),
        pltpu.make_async_copy(observer_hbm, observer_ref, load_sem.at[1]),
        pltpu.make_async_copy(bin_hbm, bin_ref, load_sem.at[2]),
        pltpu.make_async_copy(weight_hbm, weight_ref, load_sem.at[3]),
        pltpu.make_async_copy(table_hbm, table_ref, load_sem.at[4]),
        pltpu.make_async_copy(azimuth_hbm, azimuth_ref, load_sem.at[5]),
        pltpu.make_async_copy(full_hbm.at[me_a], full, load_sem.at[6]),
    ]
    for which in range(2):
        loads.append(pltpu.make_async_copy(sent_hbm.at[me_a, which], sent.at[which], load_sem.at[7 + 2 * which]))
        loads.append(pltpu.make_async_copy(taken_hbm.at[me_a, which], taken.at[which], load_sem.at[8 + 2 * which]))
    for step in range(BLOCKS // 2):
        for load in early_loads(group_at(step)):
            load.start()

    starts = (start_recv, start_hbm)
    cells, lined = (cells_a, cells_b), (lined_a, lined_b)
    edge_send, edge_recv = (edge_send_a, edge_send_b), (edge_recv_a, edge_recv_b)


    for part in range(2):
        for which in range(2):
            edge_recv[part][which, pl.ds(me_a, 1)] = jnp.zeros((1, 8, 4 * PLANES * PARTS[part][1]), F32)

    def moment_source(which, part, slot, share):
        first, rows = SHARE[part][share]
        return moment_send.at[which, slot, pl.ds(first, rows)]

    def moment_copy(which, part, slot, share):
        return pltpu.make_async_remote_copy(
            src_ref=moment_source(which, part, slot, share),
            dst_ref=moment_recv.at[which, part, me_z, pl.ds(0, SHARE[part][share][1])],
            send_sem=moment_send_sem.at[which, part],
            recv_sem=moment_recv_sem.at[which, part],
            device_id=(me_a, 2 * slot + share),
            device_id_type=MESH,
        )

    def send_moments(which, part, step):
        row = 4 * group_at(step)
        for turn in STEPS[:3]:
            for share in range(2):
                moment_copy(which, part, row + lax.rem(chip + turn, 4), share).start()

        @pl.when(step < 3)
        def _():
            for share in range(2):
                moment_copy(which, part, row + lax.rem(chip, 4), share).start()

        for share in range(2):

            @pl.when(jnp.logical_and(step == 3, core == share))
            def _():
                moment_copy(which, part, chip, 1 - share).start()
                pltpu.make_async_copy(
                    moment_source(which, part, chip, share),
                    moment_recv.at[which, part, me_z, pl.ds(0, SHARE[part][share][1])],
                    moment_recv_sem.at[which, part],
                ).start()

    def wait_moment_sends(which, part):
        for share in range(2):

            @pl.when(core == share)
            def _():
                rows = pl.ds(8 * PARTS[part][0], 8 * PARTS[part][1])
                sent_rows = moment_send.at[which, pl.ds(0, SLOTS - 1), rows]
                pltpu.make_async_copy(sent_rows, sent_rows, moment_send_sem.at[which, part]).wait()
                sent_rows = moment_source(which, part, SLOTS - 1, 1 - share)
                pltpu.make_async_copy(sent_rows, sent_rows, moment_send_sem.at[which, part]).wait()

    def reduce_moments(which, part, root):
        factor = root**ROWS
        wrap = 1.0 / (1.0 - root**NAZ)
        side = lax.rem(chip, 2)

        def place(step):
            return step + side * (AZIM - 1 - 2 * step)

        for share in range(2):
            first_row, count = SHARE[part][share]
            rows, there = pl.ds(0, count), pl.ds(first_row, count)

            @pl.when(core == share)
            def _():
                arrived = moment_recv.at[which, part, :, rows]
                pltpu.make_async_copy(arrived, arrived, moment_recv_sem.at[which, part]).wait()

                def gather(step, total):
                    return factor * total + moment_recv[which, part, place(step), rows]

                first = lax.fori_loop(0, AZIM, gather, jnp.zeros((count, LANES), F32), unroll=8) * wrap

                def follow(step, now):
                    other = place(step)
                    start_send[which, part, other, rows] = now
                    return factor * now + moment_recv[which, part, other, rows]

                lax.fori_loop(0, AZIM, follow, first, unroll=8)

                def hand_out(other):
                    pltpu.make_async_remote_copy(
                        src_ref=start_send.at[which, part, other, rows],
                        dst_ref=starts[which].at[chip, there],
                        send_sem=start_send_sem.at[which, part],
                        recv_sem=start_recv_sem.at[which, part],
                        device_id=(me_a, other),
                        device_id_type=MESH,
                    ).start()

                for step in AWAY:
                    for half in range(2):
                        hand_out(2 * chip_at(step) + half)
                hand_out(twin)
                pltpu.make_async_copy(
                    start_send.at[which, part, me_z, rows],
                    starts[which].at[chip, there],
                    start_recv_sem.at[which, part],
                ).start()

    def wait_starts(which, part):
        arrived = starts[which].at[:, pl.ds(8 * PARTS[part][0], 8 * PARTS[part][1])]
        pltpu.make_async_copy(arrived, arrived, start_recv_sem.at[which, part]).wait()

    def wait_start_sends(which, part):
        for share in range(2):

            @pl.when(core == share)
            def _():
                gone = start_send.at[which, part, pl.ds(0, AZIM - 1), pl.ds(0, SHARE[part][share][1])]
                pltpu.make_async_copy(gone, gone, start_send_sem.at[which, part]).wait()

    def moments_of(values, root):
        up = root * values[0]
        for row in range(1, ROWS):
            up = root * (up + values[row])
        down = root * values[ROWS - 1]
        for row in range(ROWS - 2, -1, -1):
            down = root * (down + values[row])
        return up, down

    def keep_moments(which, group, field, values, root):
        up, down = moments_of(values, root)
        for half in range(2):
            for side, value in ((0, up), (1, down)):
                moment_send[which, 4 * group + 2 * half + side, pl.ds(8 * field, 8)] = value[8 * half : 8 * half + 8]

    def halo_copies(which):
        copies = []
        for part in range(2):
            if which == 1:
                source, halo, depth = lined[part], filter_halo, 2
                there = pl.ds(PLANES * PARTS[part][0], PLANES * PARTS[part][1])
            else:
                source, halo, depth = azim_flux, deriv_halo, 1
                there = pl.ds(0, SLAB)
                if part == 1:
                    break
            for side, other, rows in ((0, after, pl.ds(ROWS - depth, depth)), (1, before, pl.ds(0, depth))):
                copies.append(
                    pltpu.make_async_remote_copy(
                        src_ref=source.at[rows],
                        dst_ref=halo.at[side, :, there],
                        send_sem=halo_send_sem.at[which, part, side],
                        recv_sem=halo_recv_sem.at[which, part, side],
                        device_id=(me_a, other),
                        device_id_type=MESH,
                    )
                )
        return copies

    def edge_copy(which, part, step):
        other = lax.rem(me_a + step, AXIAL)
        down = jnp.where(other < me_a, 1, 0)
        return pltpu.make_async_remote_copy(
            src_ref=edge_send[part].at[which, down],
            dst_ref=edge_recv[part].at[which, me_a],
            send_sem=edge_send_sem.at[which, part, step - 1],
            recv_sem=edge_recv_sem.at[which, part, step - 1],
            device_id=(other, me_z),
            device_id_type=MESH,
        )

    def send_edges(which, part):
        slab = PLANES * PARTS[part][1]

        def piece(step, carry):
            at = pl.multiple_of(step * 2 * slab, 2 * slab)
            total = dot_last(sent[which, 0], cells[part][which, pl.ds(at, 2 * slab)]) + dot_last(
                sent[which, 1], cells[part][which, pl.ds(4 * slab + at, 2 * slab)]
            )
            total = total[:16] + total[16:]
            edge_send[part][which, 0, :, pl.ds(at, 2 * slab)] = total[:8]
            edge_send[part][which, 1, :, pl.ds(at, 2 * slab)] = total[8:]
            return carry

        lax.fori_loop(0, 2, piece, 0, unroll=True)
        for step in STEPS[:3]:
            edge_copy(which, part, step).start()

    def own_part(which, part):
        slab = PLANES * PARTS[part][1]

        def piece(step, carry):
            at = pl.multiple_of(step * 2 * slab, 2 * slab)
            total = jnp.dot(cells[part][which, pl.ds(at, 2 * slab)], own[which], preferred_element_type=F32)
            lined[part][pl.ds(2 * step, 2)] = (total[:, :LANES] + total[:, LANES:]).reshape(2, slab, LANES)
            return carry

        lax.fori_loop(0, 4, piece, 0, unroll=True)

    def add_edges(which, part):
        slab = PLANES * PARTS[part][1]
        for step in range(1, AXIAL):
            edge_copy(which, part, step).wait_recv()

        def piece(step, carry):
            at = pl.multiple_of(lax.rem(step, 2) * 2 * slab, 2 * slab)
            received = edge_recv[part][which, :, :, pl.ds(at, 2 * slab)].reshape(32, 2 * slab)
            high, low = two_terms(received)
            total = dot_first(jnp.concatenate([high, low], axis=0), taken[which, step // 2])
            total = (total[:, :LANES] + total[:, LANES:]).reshape(2, slab, LANES)
            lined[part][pl.ds(2 * step, 2)] = lined[part][pl.ds(2 * step, 2)] + total
            return carry

        lax.fori_loop(0, 4, piece, 0, unroll=True)

    def keep_cells(which, row, field, group, value):
        part = PART_OF[field]
        first, count = PARTS[part]
        high, low = two_terms(value)
        at = pl.multiple_of((row * count + field - first) * PLANES + group * 16, 16)
        cells[part][which, pl.ds(at, 16), pl.ds(0, LANES)] = high
        cells[part][which, pl.ds(at, 16), pl.ds(LANES, LANES)] = low

    def axial_copy(which, step):
        return pltpu.make_async_remote_copy(
            src_ref=axial_send.at[which],
            dst_ref=axial_recv.at[which, me_a],
            send_sem=axial_send_sem.at[which, step - 1],
            recv_sem=axial_recv_sem.at[which, step - 1],
            device_id=(lax.rem(me_a + step, AXIAL), me_z),
            device_id_type=MESH,
        )

    def send_axial(which, value):
        axial_send[which] = value
        axial_recv[which, pl.ds(me_a, 1)] = value[None]
        for step in STEPS[:3]:
            axial_copy(which, step).start()

    def take_axial(which):
        for step in range(1, AXIAL):
            axial_copy(which, step).wait_recv()
        line = jnp.concatenate([axial_recv[which, k] for k in range(AXIAL)], axis=1)
        return jnp.dot(line, full[which], preferred_element_type=F32, precision=lax.Precision.HIGHEST)

    def send_plane(which, value):
        plane_send[which] = value
        plane_recv[which, 0] = value

        def piece(other):
            pltpu.make_async_remote_copy(
                src_ref=plane_send.at[which],
                dst_ref=plane_recv.at[which, lax.rem(me_z - other + AZIM, AZIM)],
                send_sem=plane_send_sem.at[which],
                recv_sem=plane_recv_sem.at[which],
                device_id=(me_a, other),
                device_id_type=MESH,
            ).start()

        for step in AWAY:
            for half in range(2):
                piece(2 * chip_at(step) + half)
        piece(twin)

    def plane_wait(which, sem):
        part = plane_recv.at[which, pl.ds(1, AZIM - 1)]
        pltpu.make_async_copy(part, part, sem.at[which]).wait()

    def take_plane(which):
        plane_wait(which, plane_recv_sem)
        return jnp.dot(
            azimuth_ref[which],
            plane_recv[which].reshape(NAZ, LANES),
            preferred_element_type=F32,
            precision=lax.Precision.HIGHEST,
        )

    def flux_of(metric, at, rho, vel, prs, vol, heat):
        grad = [metric[comp, at] for comp in range(3)]
        contra = vol * (grad[0] * vel[0] + grad[1] * vel[1] + grad[2] * vel[2])
        flow = rho * contra
        push = vol * prs
        return [flow] + [flow * vel[comp] + grad[comp] * push for comp in range(3)] + [heat * contra]

    def cells_at(group, row):
        at = pl.ds(group * 128 + row, 16, stride=ROWS)
        rho, prs, vol = density[at], pressure[at], volume[at]
        vel = [velocity[comp, at] for comp in range(3)]
        energy = 2.5 * prs + 0.5 * rho * (vel[0] * vel[0] + vel[1] * vel[1] + vel[2] * vel[2])
        return at, rho, vel, prs, vol, energy

    def azim_group(step, carry):
        group = group_at(step)
        for load in early_loads(group):
            load.wait()
        for load in late_loads(group):
            load.start()
        flux = [[None] * ROWS for _ in range(FIELDS)]
        for row in range(ROWS):
            at, rho, vel, prs, vol, energy = cells_at(group, row)
            parts = flux_of(azim_metric, at, rho, vel, prs, vol, energy + prs)
            for field in range(FIELDS):
                flux[field][row] = parts[field]
                azim_flux[row, pl.ds(pl.multiple_of(field * PLANES + group * 16, 16), 16)] = parts[field]
        for field in range(FIELDS):
            keep_moments(0, group, field, flux[field], DL)
        return carry

    lax.fori_loop(0, BLOCKS // 2, azim_group, 0)

    for load in loads:
        load.start()

    pl.semaphore_wait(barrier, PEERS)
    for part in range(2):

        def send_part(step, carry, part=part):
            send_moments(0, part, step)
            return carry

        lax.fori_loop(0, BLOCKS // 2, send_part, 0)
    send_plane(0, azim_flux[:, 0] + azim_flux[:, 2 * PLANES])
    for copy in halo_copies(0):
        copy.start()

    def axial_group(group, carry):
        for load in late_loads(group):
            load.wait()
        for row in range(ROWS):
            at, rho, vel, prs, vol, energy = cells_at(group, row)
            state = [rho, rho * vel[0], rho * vel[1], rho * vel[2], energy]
            ratio[row, pl.ds(pl.multiple_of(group * 16, 16), 16)] = SECTION / vol
            for field in range(FIELDS):
                base[row, pl.ds(pl.multiple_of(field * PLANES + group * 16, 16), 16)] = (
                    state[field] + SECTION * radial[field, at]
                )
            parts = flux_of(axial_metric, at, rho, vel, prs, vol, energy + prs)
            for field in range(FIELDS):
                keep_cells(0, row, field, group, parts[field])
            panel_axial[group, pl.ds(row, 1)] = parts[0][:1] + parts[2][:1]
        return carry

    lax.fori_loop(0, BLOCKS // 2, axial_group, 0)
    send_axial(0, panel_axial[0])
    for load in loads:
        load.wait()
    send_edges(0, 0)
    send_edges(0, 1)

    ids = observer_ref[...]
    order = (
        lax.shift_right_logical(ids, 7) * 128
        + (lax.shift_right_logical(ids, 2) & 1) * 64
        + (lax.shift_right_logical(ids, 3) & 15) * 4
        + (ids & 3)
    )
    partial[pl.ds(0, ENTRY_ROWS)] = order.astype(F32)

    def hot_row(row, carry):
        wanted = partial[pl.ds(row, 1)].astype(jnp.int32)
        rows = lax.broadcasted_iota(jnp.int32, (OBSERVERS, LANES), 0)
        at = pl.multiple_of(row * LANES, LANES)
        observer_hot[:, pl.ds(at, LANES)] = jnp.where(rows == wanted, 1.0, 0.0).astype(BF16)
        same = lax.broadcasted_iota(jnp.int32, (TIME_BINS, LANES), 0) == bin_ref[pl.ds(row, 1)]
        bin_hot[pl.ds(0, TIME_BINS), pl.ds(at, LANES)] = jnp.where(same, 1.0, 0.0).astype(BF16)
        return carry

    lax.fori_loop(0, ENTRY_ROWS, hot_row, 0)

    for which in range(2):
        high, low = two_terms(full[which, pl.ds(pl.multiple_of(me_a * LANES, LANES), LANES)])
        for top in range(2):
            own[which, pl.ds(top * LANES, LANES), pl.ds(0, LANES)] = high
            own[which, pl.ds(top * LANES, LANES), pl.ds(LANES, LANES)] = low
    own_part(0, 0)
    own_part(0, 1)
    reduce_moments(0, 0, DL)
    reduce_moments(0, 1, DL)
    change = take_axial(0) + take_plane(0)
    send_axial(1, base[:, 0] + base[:, 2 * PLANES] - ratio[:, 0] * change)
    add_edges(0, 0)
    add_edges(0, 1)

    def near_section(group, carry):
        here = pl.ds(pl.multiple_of(group * 16, 16), 16)
        for field in range(FIELDS):
            part = PART_OF[field]
            at = pl.ds(pl.multiple_of(field * PLANES + group * 16, 16), 16)
            inside = pl.ds(pl.multiple_of((field - PARTS[part][0]) * PLANES + group * 16, 16), 16)
            flux = [deriv_halo[0, 0, at]] + [azim_flux[row, at] for row in range(ROWS)] + [deriv_halo[1, 0, at]]
            tails = near_tails(flux[1:-1], DL)
            for row in range(ROWS):
                up, down = tails[row]
                spread = down if up is None else -up if down is None else down - up
                deriv = DK * spread + C1 * (flux[row + 2] - flux[row])
                base[row, at] = base[row, at] - ratio[row, here] * (lined[part][row, inside] + deriv)
        return carry

    def section(part):
        first, count = PARTS[part]

        def section_group(group, carry):
            here = pl.ds(pl.multiple_of(group * 16, 16), 16)
            for field in range(first, first + count):
                at = pl.ds(pl.multiple_of(field * PLANES + group * 16, 16), 16)
                up = DK * start_of(start_recv, group, field, 0)
                down = DK * start_of(start_recv, group, field, 1)
                for row in range(ROWS):
                    far = DL ** (ROWS - 1 - row) * down - DL**row * up
                    keep_cells(1, row, field, group, base[row, at] - ratio[row, here] * far)
            return carry

        lax.fori_loop(0, BLOCKS // 2, section_group, 0)

    def smoothed_moments(part):
        first, count = PARTS[part]

        def moment_group(step, carry):
            group = group_at(step)
            for field in range(first, first + count):
                inside = pl.ds(pl.multiple_of((field - first) * PLANES + group * 16, 16), 16)
                keep_moments(1, group, field, [lined[part][row, inside] for row in range(ROWS)], FL)
            send_moments(1, part, step)
            return carry

        lax.fori_loop(0, BLOCKS // 2, moment_group, 0)

    for copy in halo_copies(0):
        copy.wait_recv()
    lax.fori_loop(0, BLOCKS // 2, near_section, 0)
    wait_starts(0, 0)
    section(0)
    send_edges(1, 0)
    send_plane(1, take_axial(1))
    wait_starts(0, 1)
    section(1)
    send_edges(1, 1)
    own_part(1, 0)
    own_part(1, 1)
    add_edges(1, 0)
    smoothed_moments(0)
    add_edges(1, 1)
    smoothed_moments(1)
    for copy in halo_copies(1):
        copy.start()

    source = area_ref[...] * (take_plane(1) - 1.0)
    picks = weight_ref[...]
    low_half = jnp.take_along_axis(
        jnp.broadcast_to(table_ref[pl.ds(0, 1)], (ENTRY_ROWS, LANES)), picks & 127, axis=1
    )
    high_half = jnp.take_along_axis(
        jnp.broadcast_to(table_ref[pl.ds(1, 1)], (ENTRY_ROWS, LANES)), picks & 127, axis=1
    )
    weights = jnp.where(picks < LANES, low_half, high_half)
    values = weights * jnp.concatenate([source] * 4, axis=0)
    high, low = two_terms(values)
    partial[pl.ds(0, ENTRY_ROWS)] = high.astype(F32)
    partial[pl.ds(ENTRY_ROWS, ENTRY_ROWS)] = low.astype(F32)

    def bin_row(row, carry):
        at = pl.multiple_of(row * LANES, LANES)
        mask = bin_hot[pl.ds(0, TIME_BINS), pl.ds(at, LANES)]
        for term in range(2):
            value = jnp.broadcast_to(partial[pl.ds(term * ENTRY_ROWS + row, 1)], (TIME_BINS, LANES)).astype(BF16)
            bin_hot[pl.ds(term * TIME_BINS, TIME_BINS), pl.ds(at, LANES)] = mask * value
        return carry

    lax.fori_loop(0, ENTRY_ROWS, bin_row, 0)

    total = dot_last(observer_hot[...], bin_hot[...])
    partial[...] = total[:, :TIME_BINS] + total[:, TIME_BINS:]

    mine = me_a * 2 + core

    def part_copy(step):
        other = lax.rem(mine + step, 8)
        other_z = me_z - core + lax.rem(other, 2)
        return pltpu.make_async_remote_copy(
            src_ref=partial.at[pl.ds(pl.multiple_of(other * 64, 64), 64)],
            dst_ref=part_recv.at[step - 1],
            send_sem=part_send_sem.at[step - 1],
            recv_sem=part_recv_sem.at[step - 1],
            device_id=(other // 2, other_z),
            device_id_type=MESH,
        )

    for step in range(1, 8):
        part_copy(step).start()
    reduce_moments(1, 0, FL)
    reduce_moments(1, 1, FL)
    total = partial[pl.ds(pl.multiple_of(mine * 64, 64), 64)]
    for step in range(1, 8):
        part_copy(step).wait_recv()
        total = total + part_recv[step - 1]
    for owner in range(16):
        owner_send[owner, pl.ds(0, 4)] = total[4 * owner : 4 * owner + 4]
        owner_send[owner, pl.ds(4, 4)] = jnp.zeros((4, LANES), F32)

    def owner_copy(step):
        other = chip_at(AWAY[step - 1])
        return pltpu.make_async_remote_copy(
            src_ref=owner_send.at[other],
            dst_ref=owner_hbm.at[step],
            send_sem=owner_send_sem.at[step - 1],
            recv_sem=owner_recv_sem.at[step - 1],
            device_id=(me_a, 2 * other + core),
            device_id_type=MESH,
        )

    for step in range(1, 16):
        owner_copy(step).start()
    own_copy = pltpu.make_async_copy(owner_send.at[chip], owner_hbm.at[0], owner_sem)
    own_copy.start()
    for copy in halo_copies(1):
        copy.wait_recv()

    def near_group(group, carry):
        for field in range(FIELDS):
            part = PART_OF[field]
            at = pl.ds(pl.multiple_of(field * PLANES + group * 16, 16), 16)
            inside = pl.ds(pl.multiple_of((field - PARTS[part][0]) * PLANES + group * 16, 16), 16)
            value = [filter_halo[0, row, at] for row in range(2)]
            value += [lined[part][row, inside] for row in range(ROWS)]
            value += [filter_halo[1, row, at] for row in range(2)]
            ends = near_tails(value[2:-2], FL)
            for row in range(ROWS):
                up, down = ends[row]
                tails = down if up is None else up if down is None else up + down
                edges = E1 * (value[row + 1] + value[row + 3]) + E2 * (value[row] + value[row + 4])
                near[row, at] = FK * tails + (FK + E0) * value[row + 2] + edges
        return carry

    lax.fori_loop(0, BLOCKS // 2, near_group, 0)
    keep = pltpu.make_async_copy(near, near_hbm, keep_sem)
    keep.start()
    for part in range(2):
        wait_starts(1, part)

    own_copy.wait()
    for step in range(1, 16):
        owner_copy(step).wait_recv()
    keep.wait()

    for which in range(2):
        for part in range(2):
            wait_moment_sends(which, part)
            wait_start_sends(which, part)
            for step in range(1, AXIAL):
                edge_copy(which, part, step).wait_send()
        for copy in halo_copies(which):
            copy.wait_send()
    for step in range(1, 8):
        part_copy(step).wait_send()
    for step in range(1, 16):
        owner_copy(step).wait_send()
    for which in range(2):
        plane_wait(which, plane_send_sem)
        for step in range(1, AXIAL):
            axial_copy(which, step).wait_send()


def per_device(
    density,
    velocity,
    pressure,
    axial_metric,
    azim_metric,
    volume,
    radial_term,
    panel_area,
    observer_ids,
    bin_ids,
    weight_ids,
    bin_weights,
):
    sent, taken, full = both_tables()
    rows = PLANES * ROWS
    slabs = [PLANES * count for _, count in PARTS]
    hbm = pl.BlockSpec(memory_space=pltpu.HBM)
    dma = pltpu.SemaphoreType.DMA
    near, starts, parts = pl.pallas_call(
        kernel,
        out_shape=(
            jax.ShapeDtypeStruct((ROWS, SLAB, LANES), F32),
            jax.ShapeDtypeStruct((SLOTS, TILE_ROWS, LANES), F32),
            jax.ShapeDtypeStruct((16, 8, TIME_BINS), F32),
        ),
        in_specs=[hbm] * 16,
        out_specs=(hbm, hbm, hbm),
        scratch_shapes=[
            pltpu.VMEM((2, 2 * LANES, 2 * LANES), BF16),
            pltpu.VMEM((2, 2, 32, 2 * LANES), BF16),
            pltpu.VMEM((2, 2, 64, 2 * LANES), BF16),
            pltpu.VMEM((rows, LANES), F32),
            pltpu.VMEM((3, rows, LANES), F32),
            pltpu.VMEM((rows, LANES), F32),
            pltpu.VMEM((3, rows, LANES), F32),
            pltpu.VMEM((3, rows, LANES), F32),
            pltpu.VMEM((rows, LANES), F32),
            pltpu.VMEM((FIELDS, rows, LANES), F32),
            pltpu.VMEM((ROWS, LANES), F32),
            pltpu.VMEM((ENTRY_ROWS, LANES), jnp.int32),
            pltpu.VMEM((ENTRY_ROWS, LANES), jnp.int32),
            pltpu.VMEM((ENTRY_ROWS, LANES), jnp.int32),
            pltpu.VMEM((2, LANES), F32),
            pltpu.VMEM((2, ROWS, NAZ), F32),
            pltpu.VMEM((2, NA, LANES), F32),
            pltpu.VMEM((ROWS, SLAB, LANES), F32),
            pltpu.VMEM((ROWS, SLAB, LANES), F32),
            pltpu.VMEM((ROWS, PLANES, LANES), F32),
            *[pltpu.VMEM((2, ROWS * slab, 2 * LANES), BF16) for slab in slabs],
            *[pltpu.VMEM((ROWS, slab, LANES), F32) for slab in slabs],
            *[pltpu.VMEM((2, 2, 8, 4 * slab), F32) for slab in slabs],
            *[pltpu.VMEM((2, AXIAL, 8, 4 * slab), F32) for slab in slabs],
            pltpu.VMEM((2, SLOTS, TILE_ROWS, LANES), F32),
            pltpu.VMEM((2, 2, AZIM, 16, LANES), F32),
            pltpu.VMEM((2, 2, AZIM, 16, LANES), F32),
            pltpu.VMEM((SLOTS, TILE_ROWS, LANES), F32),
            pltpu.VMEM((2, 1, SLAB, LANES), F32),
            pltpu.VMEM((2, 2, SLAB, LANES), F32),
            pltpu.VMEM((ROWS, SLAB, LANES), F32),
            pltpu.VMEM((OBSERVERS, ENTRY_ROWS * LANES), BF16),
            pltpu.VMEM((2 * TIME_BINS, ENTRY_ROWS * LANES), BF16),
            pltpu.VMEM((OBSERVERS, TIME_BINS), F32),
            pltpu.VMEM((7, 64, TIME_BINS), F32),
            pltpu.VMEM((16, 8, TIME_BINS), F32),
            pltpu.VMEM((2, ROWS, LANES), F32),
            pltpu.VMEM((2, AZIM, ROWS, LANES), F32),
            pltpu.VMEM((2, ROWS, LANES), F32),
            pltpu.VMEM((2, AXIAL, ROWS, LANES), F32),
            pltpu.VMEM((BLOCKS // 2, ROWS, LANES), F32),
            dma(()),
            dma(()),
            dma((11,)),
            dma((5, BLOCKS // 2)),
            dma((2, BLOCKS // 2)),
            dma((2, 2, 3)),
            dma((2, 2, 3)),
            dma((2, 2)),
            dma((2, 2)),
            dma((2, 2)),
            dma((2, 2)),
            dma((2, 2, 2)),
            dma((2, 2, 2)),
            dma((7,)),
            dma((7,)),
            dma((15,)),
            dma((15,)),
            dma((2,)),
            dma((2,)),
            dma((2, 3)),
            dma((2, 3)),
        ],
        compiler_params=pltpu.CompilerParams(
            collective_id=0, has_side_effects=True
        ),
    )(
        jnp.asarray(sent),
        jnp.asarray(taken),
        density.reshape(rows, LANES),
        velocity.reshape(3, rows, LANES),
        pressure.reshape(rows, LANES),
        axial_metric.reshape(3, rows, LANES),
        azim_metric.reshape(3, rows, LANES),
        volume.reshape(rows, LANES),
        radial_term.reshape(FIELDS, rows, LANES),
        panel_area,
        observer_ids.reshape(ENTRY_ROWS, LANES),
        bin_ids.reshape(ENTRY_ROWS, LANES),
        weight_ids.reshape(ENTRY_ROWS, LANES),
        bin_weights.reshape(2, LANES),
        jnp.asarray(azimuth_rows()),
        jnp.asarray(full),
    )
    state, signals = pl.pallas_call(
        finish_kernel,
        out_shape=(
            jax.ShapeDtypeStruct((FIELDS, rows, LANES), F32),
            jax.ShapeDtypeStruct((4, TIME_BINS), F32),
        ),
        in_specs=[hbm] * 3,
        out_specs=(hbm, hbm),
        scratch_shapes=[
            pltpu.VMEM((ROWS, FIELDS, PLANES, LANES), F32),
            pltpu.VMEM((SLOTS, TILE_ROWS, LANES), F32),
            pltpu.VMEM((FIELDS, rows, LANES), F32),
            pltpu.VMEM((16, 8, TIME_BINS), F32),
            pltpu.VMEM((4, TIME_BINS), F32),
            dma((BLOCKS // 2, 3)),
            dma((BLOCKS // 2,)),
            dma((2,)),
        ],
    )(
        near.reshape(ROWS, FIELDS, PLANES, LANES),
        starts,
        parts,
    )
    return state.reshape(FIELDS, PLANES, ROWS, LANES), signals


def solution(mesh):
    placed = (
        P(None, "azim", "axial"),
        P(None, None, "azim", "axial"),
        P(None, "azim", "axial"),
        P(None, None, "azim", "axial"),
        P(None, None, "azim", "axial"),
        P(None, "azim", "axial"),
        P(None, None, "azim", "axial"),
        P("azim", "axial"),
        P(None, "azim", "axial"),
        P(None, "azim", "axial"),
        P(None, "azim", "axial"),
        P(),
    )
    return jax.shard_map(
        per_device,
        mesh=mesh,
        in_specs=placed,
        out_specs=(P(None, None, "azim", "axial"), P(("axial", "azim"), None)),
        check_vma=False,
    )
```

```python
import functools
import math

import jax
import jax.numpy as jnp
import ml_dtypes
import numpy as np
from jax import lax
from jax.experimental import pallas as pl
from jax.experimental.pallas import tpu as pltpu
from jax.sharding import PartitionSpec as P

F32 = jnp.float32
BF16 = jnp.bfloat16
MESH = pl.DeviceIdType.MESH

PLANES = 64
FIELDS = 5
ROWS = 8
LANES = 128
AXIAL = 4
AZIM = 32
NA = AXIAL * LANES
NAZ = AZIM * ROWS
SLAB = FIELDS * PLANES
BLOCKS = PLANES // 8
SLOTS = 2 * BLOCKS
TILE_ROWS = 8 * FIELDS
PARTS = ((0, 3), (3, 2))
PART_OF = (0, 0, 0, 1, 1)
SHARE = (((0, 16), (16, 8)), ((24, 8), (32, 8)))
STEPS = (2, 1, 3, 0)
AWAY = tuple((dz, dy) for dz in STEPS[:3] for dy in STEPS[:3]) + ((2, 0), (0, 2), (1, 0), (3, 0), (0, 1), (0, 3))
ENTRY_ROWS = 32
OBSERVERS = 512
TIME_BINS = 128
PEERS = (AZIM - 1) + 2 * (AXIAL - 1)

SECTION = 0.25
DERIV_ALPHA = 1.0 / 3.0
BETA = 0.499


def decay_root(alpha):
    return (-1.0 + math.sqrt(1.0 - 4.0 * alpha * alpha)) / (2.0 * alpha)


DL = decay_root(DERIV_ALPHA)
FL = decay_root(BETA)
C1 = (1.0 / 36.0) / DERIV_ALPHA
DS = 1.0 / math.sqrt(1.0 - 4.0 * DERIV_ALPHA**2)
DK = (7.0 / 9.0 - C1) * DS * (1.0 / DL - DL)
FC = [
    (11.0 + 10.0 * BETA) / 16.0,
    (15.0 + 34.0 * BETA) / 32.0,
    (-3.0 + 6.0 * BETA) / 16.0,
    (1.0 - 2.0 * BETA) / 32.0,
]
FS = 1.0 / math.sqrt(1.0 - 4.0 * BETA**2)
E2 = FC[3] / (2.0 * BETA)
E1 = (FC[2] / 2.0 - E2) / BETA
E0 = (FC[1] / 2.0 - E1 - BETA * E2) / BETA
FK = (FC[0] - E0 - 2.0 * BETA * E1) * FS


def split(values):
    high = values.astype(ml_dtypes.bfloat16)
    low = (values - high.astype(np.float64)).astype(ml_dtypes.bfloat16)
    return high, low


def axial_tables(root, scale, band):
    n, w = NA, LANES
    index = np.arange(n)
    green = scale * (
        np.power(root, np.abs(index[:, None] - index[None, :]))
        - np.power(root, 2 * n - index[:, None] - index[None, :])
    )
    side = np.zeros((n, n))
    for shift, value in band.items():
        side += value * np.eye(n, k=shift)
    whole = green @ side
    left = np.zeros((AXIAL, w))
    right = np.zeros((AXIAL, w))
    for k in range(AXIAL):
        cols = slice(k * w, (k + 1) * w)
        lo, hi = max(0, k * w - 3), min(n, (k + 1) * w + 3)
        m = np.arange(lo, hi)
        left[k] = np.power(root, ((k + 1) * w - m).astype(np.float64)) @ side[lo:hi, cols]
        right[k] = (
            np.power(root, (m - k * w + 1).astype(np.float64))
            - np.power(root, (2 * n - m - k * w + 1).astype(np.float64))
        ) @ side[lo:hi, cols]
    t = np.arange(w)
    full = np.stack([whole[d * w : (d + 1) * w].T for d in range(AXIAL)]).astype(np.float32)
    sent = np.zeros((AXIAL, 2, 32, 2 * w), ml_dtypes.bfloat16)
    taken = np.zeros((AXIAL, 2, 64, 2 * w), ml_dtypes.bfloat16)
    for d in range(AXIAL):
        for half in range(2):
            rows = np.zeros((16, w))
            base = half * 4
            rows[base] = left[d]
            rows[base + 1, w - 1] = 1.0
            rows[base + 2, w - 2] = 1.0
            rows[8 + base] = right[d]
            rows[8 + base + 1, 0] = 1.0
            rows[8 + base + 2, 1] = 1.0
            high, low = split(rows)
            sent[d, half] = np.concatenate(
                [np.concatenate([high, high], axis=1), np.concatenate([low, low], axis=1)], axis=0
            )
            rows = np.zeros((32, w))
            for k in range(AXIAL):
                row = k * 8 + half * 4
                i = d * w + t
                if k < d:
                    rows[row] = scale * (
                        np.power(root, (i - (k + 1) * w).astype(np.float64))
                        - np.power(root, (2 * n - i - (k + 1) * w).astype(np.float64))
                    )
                    if k == d - 1:
                        for edge in range(2):
                            col = d * w - 1 - edge
                            for near in range(2 - edge):
                                rows[row + 1 + edge, near] = (
                                    whole[d * w + near, col] - rows[row, near] * left[k, col - k * w]
                                )
                if k > d:
                    rows[row] = scale * np.power(root, (k * w - 1 - i).astype(np.float64))
                    if k == d + 1:
                        for edge in range(2):
                            col = k * w + edge
                            for near in range(2 - edge):
                                rows[row + 1 + edge, w - 1 - near] = (
                                    whole[k * w - 1 - near, col] - rows[row, w - 1 - near] * right[k, edge]
                                )
            high, low = split(rows)
            pair = np.concatenate([high, low], axis=1)
            taken[d, half] = np.concatenate([pair, pair], axis=0)
    return sent, taken, full


def both_tables():
    deriv = axial_tables(DL, DS, {1: 7.0 / 9.0, -1: -7.0 / 9.0, 2: 1.0 / 36.0, -2: -1.0 / 36.0})
    band = {0: FC[0]}
    for shift in range(1, 4):
        band[shift] = band[-shift] = FC[shift] / 2.0
    smooth = axial_tables(FL, FS, band)
    return [np.stack(pair, axis=1) for pair in zip(deriv, smooth)]


def azimuth_rows():
    gap = np.arange(NAZ)
    slope = DK * (np.power(DL, gap) - np.power(DL, NAZ - gap)) / (1.0 - DL**NAZ)
    slope[0] = 0.0
    slope[1] += C1
    slope[-1] -= C1
    line = FK * (np.power(FL, gap) + np.power(FL, NAZ - gap)) / (1.0 - FL**NAZ)
    line[0] = FK * (1.0 + 2.0 * FL**NAZ / (1.0 - FL**NAZ)) + E0
    for shift, value in ((1, E1), (2, E2)):
        line[shift] += value
        line[-shift] += value
    rows = np.arange(ROWS)
    at = (gap[None, :] - rows[:, None]) % NAZ
    return np.stack([slope[at], line[at]]).astype(np.float32)


def two_terms(value):
    high = value.astype(BF16)
    low = (value - high.astype(F32)).astype(BF16)
    return high, low


def dot_last(left, right):
    return lax.dot_general(left, right, (((1,), (1,)), ((), ())), preferred_element_type=F32)


def dot_first(left, right):
    return lax.dot_general(left, right, (((0,), (0,)), ((), ())), preferred_element_type=F32)


def near_tails(values, root):
    up, down = [None], [None]
    for row in range(ROWS - 1):
        last, back = values[row], values[ROWS - 1 - row]
        up.append(root * (last if up[-1] is None else last + up[-1]))
        down.append(root * (back if down[-1] is None else back + down[-1]))
    return list(zip(up, down[::-1]))


def start_of(starts, group, field, side):
    return jnp.concatenate(
        [starts[4 * group + 2 * half + side, pl.ds(8 * field, 8)] for half in range(2)], axis=0
    )


def finish_kernel(
    near_hbm, start_hbm, part_hbm, state_hbm, signal_hbm, near, starts, final, parts, signals, load_sem, store_sem, part_sem
):
    part_copy = pltpu.make_async_copy(part_hbm, parts, part_sem.at[0])
    signal_copy = pltpu.make_async_copy(signals, signal_hbm, part_sem.at[1])

    def loads(group):
        slots = pl.ds(4 * group, 4)
        planes = pl.ds(16 * group, 16)
        return [
            pltpu.make_async_copy(start_hbm.at[slots], starts.at[slots], load_sem.at[group, 0]),
            pltpu.make_async_copy(near_hbm.at[:, :, planes], near.at[:, :, planes], load_sem.at[group, 1]),
        ]

    def store(group):
        planes = pl.ds(128 * group, 128)
        return pltpu.make_async_copy(final.at[:, planes], state_hbm.at[:, planes], store_sem.at[group])

    for group in range(BLOCKS // 2):
        for load in loads(group):
            load.start()
    part_copy.start()

    for group in range(BLOCKS // 2):
        for load in loads(group):
            load.wait()
        planes = pl.ds(16 * group, 16)
        for field in range(FIELDS):
            up = FK * start_of(starts, group, field, 0)
            down = FK * start_of(starts, group, field, 1)
            for row in range(ROWS):
                result = near[row, field, planes] + (FL**row * up + FL ** (ROWS - 1 - row) * down)
                final[field, pl.ds(128 * group + row, 16, stride=ROWS)] = result
        store(group).start()
        if group == 0:
            part_copy.wait()
            signals[...] = jnp.sum(parts[...], axis=0)[:4]
            signal_copy.start()

    for group in range(BLOCKS // 2):
        store(group).wait()
    signal_copy.wait()


def kernel(
    sent_hbm,
    taken_hbm,
    density_hbm,
    velocity_hbm,
    pressure_hbm,
    axial_hbm,
    azim_hbm,
    volume_hbm,
    radial_hbm,
    area_hbm,
    observer_hbm,
    bin_hbm,
    weight_hbm,
    table_hbm,
    azimuth_hbm,
    full_hbm,
    near_hbm,
    start_hbm,
    owner_hbm,
    own,
    sent,
    taken,
    density,
    velocity,
    pressure,
    axial_metric,
    azim_metric,
    volume,
    radial,
    area_ref,
    observer_ref,
    bin_ref,
    weight_ref,
    table_ref,
    azimuth_ref,
    full,
    azim_flux,
    base,
    ratio,
    cells_a,
    cells_b,
    lined_a,
    lined_b,
    edge_send_a,
    edge_send_b,
    edge_recv_a,
    edge_recv_b,
    moment_send,
    moment_recv,
    start_send,
    start_recv,
    deriv_halo,
    filter_halo,
    near,
    observer_hot,
    bin_hot,
    partial,
    part_recv,
    owner_send,
    plane_send,
    plane_recv,
    axial_send,
    axial_recv,
    panel_axial,
    keep_sem,
    owner_sem,
    load_sem,
    early_sem,
    late_sem,
    edge_send_sem,
    edge_recv_sem,
    moment_send_sem,
    moment_recv_sem,
    start_send_sem,
    start_recv_sem,
    halo_send_sem,
    halo_recv_sem,
    part_send_sem,
    part_recv_sem,
    owner_send_sem,
    owner_recv_sem,
    plane_send_sem,
    plane_recv_sem,
    axial_send_sem,
    axial_recv_sem,
):
    me_a = lax.axis_index("axial")
    me_z = lax.axis_index("azim")
    core = lax.rem(me_z, 2)
    chip = me_z // 2
    twin = me_z + 1 - 2 * core
    after = lax.rem(me_z + 1, AZIM)
    before = lax.rem(me_z + AZIM - 1, AZIM)

    def chip_at(step):
        return 4 * lax.rem(chip // 4 + step[0], 4) + lax.rem(chip + step[1], 4)

    def group_at(step):
        away = jnp.where(step == 0, STEPS[0], jnp.where(step == 1, STEPS[1], jnp.where(step == 2, STEPS[2], 0)))
        return lax.rem(chip // 4 + away, 4)

    barrier = pltpu.get_barrier_semaphore()

    def greet(other_a, other_z):
        pl.semaphore_signal(barrier, inc=1, device_id=(other_a, other_z), device_id_type=MESH)

    for step in AWAY:
        for half in range(2):
            greet(me_a, 2 * chip_at(step) + half)
    for step in STEPS[:3]:
        greet(lax.rem(me_a + step, AXIAL), me_z)
        greet(lax.rem(me_a + step, AXIAL), twin)
    greet(me_a, twin)

    def early_loads(group):
        part = pl.ds(pl.multiple_of(group * 128, 128), 128)
        whole = slice(None)
        return [
            pltpu.make_async_copy(source.at[where], dest.at[where], early_sem.at[number, group])
            for number, (source, dest, where) in enumerate(
                (
                    (density_hbm, density, (part,)),
                    (velocity_hbm, velocity, (whole, part)),
                    (pressure_hbm, pressure, (part,)),
                    (volume_hbm, volume, (part,)),
                    (azim_hbm, azim_metric, (whole, part)),
                )
            )
        ]

    def late_loads(group):
        part = pl.ds(pl.multiple_of(group * 128, 128), 128)
        return [
            pltpu.make_async_copy(axial_hbm.at[:, part], axial_metric.at[:, part], late_sem.at[0, group]),
            pltpu.make_async_copy(radial_hbm.at[:, part], radial.at[:, part], late_sem.at[1, group]),
        ]

    loads = [
        pltpu.make_async_copy(area_hbm, area_ref, load_sem.at[0]),
        pltpu.make_async_copy(observer_hbm, observer_ref, load_sem.at[1]),
        pltpu.make_async_copy(bin_hbm, bin_ref, load_sem.at[2]),
        pltpu.make_async_copy(weight_hbm, weight_ref, load_sem.at[3]),
        pltpu.make_async_copy(table_hbm, table_ref, load_sem.at[4]),
        pltpu.make_async_copy(azimuth_hbm, azimuth_ref, load_sem.at[5]),
        pltpu.make_async_copy(full_hbm.at[me_a], full, load_sem.at[6]),
    ]
    for which in range(2):
        loads.append(pltpu.make_async_copy(sent_hbm.at[me_a, which], sent.at[which], load_sem.at[7 + 2 * which]))
        loads.append(pltpu.make_async_copy(taken_hbm.at[me_a, which], taken.at[which], load_sem.at[8 + 2 * which]))
    for step in range(BLOCKS // 2):
        for load in early_loads(group_at(step)):
            load.start()

    starts = (start_recv, start_hbm)
    cells, lined = (cells_a, cells_b), (lined_a, lined_b)
    edge_send, edge_recv = (edge_send_a, edge_send_b), (edge_recv_a, edge_recv_b)


    for part in range(2):
        for which in range(2):
            edge_recv[part][which, pl.ds(me_a, 1)] = jnp.zeros((1, 8, 4 * PLANES * PARTS[part][1]), F32)

    def moment_source(which, part, slot, share):
        first, rows = SHARE[part][share]
        return moment_send.at[which, slot, pl.ds(first, rows)]

    def moment_copy(which, part, slot, share):
        return pltpu.make_async_remote_copy(
            src_ref=moment_source(which, part, slot, share),
            dst_ref=moment_recv.at[which, part, me_z, pl.ds(0, SHARE[part][share][1])],
            send_sem=moment_send_sem.at[which, part],
            recv_sem=moment_recv_sem.at[which, part],
            device_id=(me_a, 2 * slot + share),
            device_id_type=MESH,
        )

    def send_moments(which, part, step):
        row = 4 * group_at(step)
        for turn in STEPS[:3]:
            for share in range(2):
                moment_copy(which, part, row + lax.rem(chip + turn, 4), share).start()

        @pl.when(step < 3)
        def _():
            for share in range(2):
                moment_copy(which, part, row + lax.rem(chip, 4), share).start()

        for share in range(2):

            @pl.when(jnp.logical_and(step == 3, core == share))
            def _():
                moment_copy(which, part, chip, 1 - share).start()
                pltpu.make_async_copy(
                    moment_source(which, part, chip, share),
                    moment_recv.at[which, part, me_z, pl.ds(0, SHARE[part][share][1])],
                    moment_recv_sem.at[which, part],
                ).start()

    def wait_moment_sends(which, part):
        for share in range(2):

            @pl.when(core == share)
            def _():
                rows = pl.ds(8 * PARTS[part][0], 8 * PARTS[part][1])
                sent_rows = moment_send.at[which, pl.ds(0, SLOTS - 1), rows]
                pltpu.make_async_copy(sent_rows, sent_rows, moment_send_sem.at[which, part]).wait()
                sent_rows = moment_source(which, part, SLOTS - 1, 1 - share)
                pltpu.make_async_copy(sent_rows, sent_rows, moment_send_sem.at[which, part]).wait()

    def reduce_moments(which, part, root):
        factor = root**ROWS
        wrap = 1.0 / (1.0 - root**NAZ)
        side = lax.rem(chip, 2)

        def place(step):
            return step + side * (AZIM - 1 - 2 * step)

        for share in range(2):
            first_row, count = SHARE[part][share]
            rows, there = pl.ds(0, count), pl.ds(first_row, count)

            @pl.when(core == share)
            def _():
                arrived = moment_recv.at[which, part, :, rows]
                pltpu.make_async_copy(arrived, arrived, moment_recv_sem.at[which, part]).wait()

                def follow(step, now):
                    other = place(step)
                    start_send[which, part, other, rows] = now
                    return factor * now + moment_recv[which, part, other, rows]

                first = lax.fori_loop(0, AZIM, follow, jnp.zeros((count, LANES), F32), unroll=8) * wrap
                for step in range(AZIM):
                    other = place(step)
                    start_send[which, part, other, rows] = start_send[which, part, other, rows] + factor**step * first

                def hand_out(other):
                    pltpu.make_async_remote_copy(
                        src_ref=start_send.at[which, part, other, rows],
                        dst_ref=starts[which].at[chip, there],
                        send_sem=start_send_sem.at[which, part],
                        recv_sem=start_recv_sem.at[which, part],
                        device_id=(me_a, other),
                        device_id_type=MESH,
                    ).start()

                for step in AWAY:
                    for half in range(2):
                        hand_out(2 * chip_at(step) + half)
                hand_out(twin)
                pltpu.make_async_copy(
                    start_send.at[which, part, me_z, rows],
                    starts[which].at[chip, there],
                    start_recv_sem.at[which, part],
                ).start()

    def wait_starts(which, part):
        arrived = starts[which].at[:, pl.ds(8 * PARTS[part][0], 8 * PARTS[part][1])]
        pltpu.make_async_copy(arrived, arrived, start_recv_sem.at[which, part]).wait()

    def wait_start_sends(which, part):
        for share in range(2):

            @pl.when(core == share)
            def _():
                gone = start_send.at[which, part, pl.ds(0, AZIM - 1), pl.ds(0, SHARE[part][share][1])]
                pltpu.make_async_copy(gone, gone, start_send_sem.at[which, part]).wait()

    def moments_of(values, root):
        up = root * values[0]
        for row in range(1, ROWS):
            up = root * (up + values[row])
        down = root * values[ROWS - 1]
        for row in range(ROWS - 2, -1, -1):
            down = root * (down + values[row])
        return up, down

    def keep_moments(which, group, field, values, root):
        up, down = moments_of(values, root)
        for half in range(2):
            for side, value in ((0, up), (1, down)):
                moment_send[which, 4 * group + 2 * half + side, pl.ds(8 * field, 8)] = value[8 * half : 8 * half + 8]

    def halo_copies(which):
        copies = []
        for part in range(2):
            if which == 1:
                source, halo, depth = lined[part], filter_halo, 2
                there = pl.ds(PLANES * PARTS[part][0], PLANES * PARTS[part][1])
            else:
                source, halo, depth = azim_flux, deriv_halo, 1
                there = pl.ds(0, SLAB)
                if part == 1:
                    break
            for side, other, rows in ((0, after, pl.ds(ROWS - depth, depth)), (1, before, pl.ds(0, depth))):
                copies.append(
                    pltpu.make_async_remote_copy(
                        src_ref=source.at[rows],
                        dst_ref=halo.at[side, :, there],
                        send_sem=halo_send_sem.at[which, part, side],
                        recv_sem=halo_recv_sem.at[which, part, side],
                        device_id=(me_a, other),
                        device_id_type=MESH,
                    )
                )
        return copies

    def edge_copy(which, part, step):
        other = lax.rem(me_a + step, AXIAL)
        down = jnp.where(other < me_a, 1, 0)
        return pltpu.make_async_remote_copy(
            src_ref=edge_send[part].at[which, down],
            dst_ref=edge_recv[part].at[which, me_a],
            send_sem=edge_send_sem.at[which, part, step - 1],
            recv_sem=edge_recv_sem.at[which, part, step - 1],
            device_id=(other, me_z),
            device_id_type=MESH,
        )

    def send_edges(which, part):
        slab = PLANES * PARTS[part][1]

        def piece(step, carry):
            at = pl.multiple_of(step * 2 * slab, 2 * slab)
            total = dot_last(sent[which, 0], cells[part][which, pl.ds(at, 2 * slab)]) + dot_last(
                sent[which, 1], cells[part][which, pl.ds(4 * slab + at, 2 * slab)]
            )
            total = total[:16] + total[16:]
            edge_send[part][which, 0, :, pl.ds(at, 2 * slab)] = total[:8]
            edge_send[part][which, 1, :, pl.ds(at, 2 * slab)] = total[8:]
            return carry

        lax.fori_loop(0, 2, piece, 0, unroll=True)
        for step in STEPS[:3]:
            edge_copy(which, part, step).start()

    def own_part(which, part):
        slab = PLANES * PARTS[part][1]

        def piece(step, carry):
            at = pl.multiple_of(step * 2 * slab, 2 * slab)
            total = jnp.dot(cells[part][which, pl.ds(at, 2 * slab)], own[which], preferred_element_type=F32)
            lined[part][pl.ds(2 * step, 2)] = (total[:, :LANES] + total[:, LANES:]).reshape(2, slab, LANES)
            return carry

        lax.fori_loop(0, 4, piece, 0, unroll=True)

    def add_edges(which, part):
        slab = PLANES * PARTS[part][1]
        for step in range(1, AXIAL):
            edge_copy(which, part, step).wait_recv()

        def piece(step, carry):
            at = pl.multiple_of(lax.rem(step, 2) * 2 * slab, 2 * slab)
            received = edge_recv[part][which, :, :, pl.ds(at, 2 * slab)].reshape(32, 2 * slab)
            high, low = two_terms(received)
            total = dot_first(jnp.concatenate([high, low], axis=0), taken[which, step // 2])
            total = (total[:, :LANES] + total[:, LANES:]).reshape(2, slab, LANES)
            lined[part][pl.ds(2 * step, 2)] = lined[part][pl.ds(2 * step, 2)] + total
            return carry

        lax.fori_loop(0, 4, piece, 0, unroll=True)

    def keep_cells(which, row, field, group, value):
        part = PART_OF[field]
        first, count = PARTS[part]
        high, low = two_terms(value)
        at = pl.multiple_of((row * count + field - first) * PLANES + group * 16, 16)
        cells[part][which, pl.ds(at, 16), pl.ds(0, LANES)] = high
        cells[part][which, pl.ds(at, 16), pl.ds(LANES, LANES)] = low

    def axial_copy(which, step):
        return pltpu.make_async_remote_copy(
            src_ref=axial_send.at[which],
            dst_ref=axial_recv.at[which, me_a],
            send_sem=axial_send_sem.at[which, step - 1],
            recv_sem=axial_recv_sem.at[which, step - 1],
            device_id=(lax.rem(me_a + step, AXIAL), me_z),
            device_id_type=MESH,
        )

    def send_axial(which, value):
        axial_send[which] = value
        axial_recv[which, pl.ds(me_a, 1)] = value[None]
        for step in STEPS[:3]:
            axial_copy(which, step).start()

    def take_axial(which):
        for step in range(1, AXIAL):
            axial_copy(which, step).wait_recv()
        line = jnp.concatenate([axial_recv[which, k] for k in range(AXIAL)], axis=1)
        return jnp.dot(line, full[which], preferred_element_type=F32, precision=lax.Precision.HIGHEST)

    def send_plane(which, value):
        plane_send[which] = value
        plane_recv[which, 0] = value

        def piece(other):
            pltpu.make_async_remote_copy(
                src_ref=plane_send.at[which],
                dst_ref=plane_recv.at[which, lax.rem(me_z - other + AZIM, AZIM)],
                send_sem=plane_send_sem.at[which],
                recv_sem=plane_recv_sem.at[which],
                device_id=(me_a, other),
                device_id_type=MESH,
            ).start()

        for step in AWAY:
            for half in range(2):
                piece(2 * chip_at(step) + half)
        piece(twin)

    def plane_wait(which, sem):
        part = plane_recv.at[which, pl.ds(1, AZIM - 1)]
        pltpu.make_async_copy(part, part, sem.at[which]).wait()

    def take_plane(which):
        plane_wait(which, plane_recv_sem)
        return jnp.dot(
            azimuth_ref[which],
            plane_recv[which].reshape(NAZ, LANES),
            preferred_element_type=F32,
            precision=lax.Precision.HIGHEST,
        )

    def flux_of(metric, at, rho, vel, prs, vol, heat):
        grad = [metric[comp, at] for comp in range(3)]
        contra = vol * (grad[0] * vel[0] + grad[1] * vel[1] + grad[2] * vel[2])
        flow = rho * contra
        push = vol * prs
        return [flow] + [flow * vel[comp] + grad[comp] * push for comp in range(3)] + [heat * contra]

    def cells_at(group, row):
        at = pl.ds(group * 128 + row, 16, stride=ROWS)
        rho, prs, vol = density[at], pressure[at], volume[at]
        vel = [velocity[comp, at] for comp in range(3)]
        energy = 2.5 * prs + 0.5 * rho * (vel[0] * vel[0] + vel[1] * vel[1] + vel[2] * vel[2])
        return at, rho, vel, prs, vol, energy

    def azim_group(step, carry):
        group = group_at(step)
        for load in early_loads(group):
            load.wait()
        for load in late_loads(group):
            load.start()
        flux = [[None] * ROWS for _ in range(FIELDS)]
        for row in range(ROWS):
            at, rho, vel, prs, vol, energy = cells_at(group, row)
            parts = flux_of(azim_metric, at, rho, vel, prs, vol, energy + prs)
            for field in range(FIELDS):
                flux[field][row] = parts[field]
                azim_flux[row, pl.ds(pl.multiple_of(field * PLANES + group * 16, 16), 16)] = parts[field]
        for field in range(FIELDS):
            keep_moments(0, group, field, flux[field], DL)
        return carry

    lax.fori_loop(0, BLOCKS // 2, azim_group, 0)

    for load in loads:
        load.start()

    pl.semaphore_wait(barrier, PEERS)
    for part in range(2):

        def send_part(step, carry, part=part):
            send_moments(0, part, step)
            return carry

        lax.fori_loop(0, BLOCKS // 2, send_part, 0)
    send_plane(0, azim_flux[:, 0] + azim_flux[:, 2 * PLANES])
    for copy in halo_copies(0):
        copy.start()

    def axial_group(group, carry):
        for load in late_loads(group):
            load.wait()
        for row in range(ROWS):
            at, rho, vel, prs, vol, energy = cells_at(group, row)
            state = [rho, rho * vel[0], rho * vel[1], rho * vel[2], energy]
            ratio[row, pl.ds(pl.multiple_of(group * 16, 16), 16)] = SECTION / vol
            for field in range(FIELDS):
                base[row, pl.ds(pl.multiple_of(field * PLANES + group * 16, 16), 16)] = (
                    state[field] + SECTION * radial[field, at]
                )
            parts = flux_of(axial_metric, at, rho, vel, prs, vol, energy + prs)
            for field in range(FIELDS):
                keep_cells(0, row, field, group, parts[field])
            panel_axial[group, pl.ds(row, 1)] = parts[0][:1] + parts[2][:1]
        return carry

    lax.fori_loop(0, BLOCKS // 2, axial_group, 0)
    send_axial(0, panel_axial[0])
    for load in loads:
        load.wait()
    send_edges(0, 0)
    send_edges(0, 1)

    ids = observer_ref[...]
    order = (
        lax.shift_right_logical(ids, 7) * 128
        + (lax.shift_right_logical(ids, 2) & 1) * 64
        + (lax.shift_right_logical(ids, 3) & 15) * 4
        + (ids & 3)
    )
    partial[pl.ds(0, ENTRY_ROWS)] = order.astype(F32)

    def hot_row(row, carry):
        wanted = partial[pl.ds(row, 1)].astype(jnp.int32)
        rows = lax.broadcasted_iota(jnp.int32, (OBSERVERS, LANES), 0)
        at = pl.multiple_of(row * LANES, LANES)
        observer_hot[:, pl.ds(at, LANES)] = jnp.where(rows == wanted, 1.0, 0.0).astype(BF16)
        same = lax.broadcasted_iota(jnp.int32, (TIME_BINS, LANES), 0) == bin_ref[pl.ds(row, 1)]
        bin_hot[pl.ds(0, TIME_BINS), pl.ds(at, LANES)] = jnp.where(same, 1.0, 0.0).astype(BF16)
        return carry

    lax.fori_loop(0, ENTRY_ROWS, hot_row, 0)

    for which in range(2):
        high, low = two_terms(full[which, pl.ds(pl.multiple_of(me_a * LANES, LANES), LANES)])
        for top in range(2):
            own[which, pl.ds(top * LANES, LANES), pl.ds(0, LANES)] = high
            own[which, pl.ds(top * LANES, LANES), pl.ds(LANES, LANES)] = low
    own_part(0, 0)
    own_part(0, 1)
    reduce_moments(0, 0, DL)
    reduce_moments(0, 1, DL)
    change = take_axial(0) + take_plane(0)
    send_axial(1, base[:, 0] + base[:, 2 * PLANES] - ratio[:, 0] * change)
    add_edges(0, 0)
    add_edges(0, 1)

    def near_section(group, carry):
        here = pl.ds(pl.multiple_of(group * 16, 16), 16)
        for field in range(FIELDS):
            part = PART_OF[field]
            at = pl.ds(pl.multiple_of(field * PLANES + group * 16, 16), 16)
            inside = pl.ds(pl.multiple_of((field - PARTS[part][0]) * PLANES + group * 16, 16), 16)
            flux = [deriv_halo[0, 0, at]] + [azim_flux[row, at] for row in range(ROWS)] + [deriv_halo[1, 0, at]]
            tails = near_tails(flux[1:-1], DL)
            for row in range(ROWS):
                up, down = tails[row]
                spread = down if up is None else -up if down is None else down - up
                deriv = DK * spread + C1 * (flux[row + 2] - flux[row])
                base[row, at] = base[row, at] - ratio[row, here] * (lined[part][row, inside] + deriv)
        return carry

    def section(part):
        first, count = PARTS[part]

        def section_group(group, carry):
            here = pl.ds(pl.multiple_of(group * 16, 16), 16)
            for field in range(first, first + count):
                at = pl.ds(pl.multiple_of(field * PLANES + group * 16, 16), 16)
                up = DK * start_of(start_recv, group, field, 0)
                down = DK * start_of(start_recv, group, field, 1)
                for row in range(ROWS):
                    far = DL ** (ROWS - 1 - row) * down - DL**row * up
                    keep_cells(1, row, field, group, base[row, at] - ratio[row, here] * far)
            return carry

        lax.fori_loop(0, BLOCKS // 2, section_group, 0)

    def smoothed_moments(part):
        first, count = PARTS[part]

        def moment_group(step, carry):
            group = group_at(step)
            for field in range(first, first + count):
                inside = pl.ds(pl.multiple_of((field - first) * PLANES + group * 16, 16), 16)
                keep_moments(1, group, field, [lined[part][row, inside] for row in range(ROWS)], FL)
            send_moments(1, part, step)
            return carry

        lax.fori_loop(0, BLOCKS // 2, moment_group, 0)

    for copy in halo_copies(0):
        copy.wait_recv()
    lax.fori_loop(0, BLOCKS // 2, near_section, 0)
    wait_starts(0, 0)
    section(0)
    send_edges(1, 0)
    send_plane(1, take_axial(1))
    wait_starts(0, 1)
    section(1)
    send_edges(1, 1)
    own_part(1, 0)
    own_part(1, 1)
    add_edges(1, 0)
    smoothed_moments(0)
    add_edges(1, 1)
    smoothed_moments(1)
    for copy in halo_copies(1):
        copy.start()

    source = area_ref[...] * (take_plane(1) - 1.0)
    picks = weight_ref[...]
    low_half = jnp.take_along_axis(
        jnp.broadcast_to(table_ref[pl.ds(0, 1)], (ENTRY_ROWS, LANES)), picks & 127, axis=1
    )
    high_half = jnp.take_along_axis(
        jnp.broadcast_to(table_ref[pl.ds(1, 1)], (ENTRY_ROWS, LANES)), picks & 127, axis=1
    )
    weights = jnp.where(picks < LANES, low_half, high_half)
    values = weights * jnp.concatenate([source] * 4, axis=0)
    high, low = two_terms(values)
    partial[pl.ds(0, ENTRY_ROWS)] = high.astype(F32)
    partial[pl.ds(ENTRY_ROWS, ENTRY_ROWS)] = low.astype(F32)

    def bin_row(row, carry):
        at = pl.multiple_of(row * LANES, LANES)
        mask = bin_hot[pl.ds(0, TIME_BINS), pl.ds(at, LANES)]
        for term in range(2):
            value = jnp.broadcast_to(partial[pl.ds(term * ENTRY_ROWS + row, 1)], (TIME_BINS, LANES)).astype(BF16)
            bin_hot[pl.ds(term * TIME_BINS, TIME_BINS), pl.ds(at, LANES)] = mask * value
        return carry

    lax.fori_loop(0, ENTRY_ROWS, bin_row, 0)

    total = dot_last(observer_hot[...], bin_hot[...])
    partial[...] = total[:, :TIME_BINS] + total[:, TIME_BINS:]

    mine = me_a * 2 + core

    def part_copy(step):
        other = lax.rem(mine + step, 8)
        other_z = me_z - core + lax.rem(other, 2)
        return pltpu.make_async_remote_copy(
            src_ref=partial.at[pl.ds(pl.multiple_of(other * 64, 64), 64)],
            dst_ref=part_recv.at[step - 1],
            send_sem=part_send_sem.at[step - 1],
            recv_sem=part_recv_sem.at[step - 1],
            device_id=(other // 2, other_z),
            device_id_type=MESH,
        )

    for step in range(1, 8):
        part_copy(step).start()
    reduce_moments(1, 0, FL)
    reduce_moments(1, 1, FL)
    total = partial[pl.ds(pl.multiple_of(mine * 64, 64), 64)]
    for step in range(1, 8):
        part_copy(step).wait_recv()
        total = total + part_recv[step - 1]
    for owner in range(16):
        owner_send[owner, pl.ds(0, 4)] = total[4 * owner : 4 * owner + 4]
        owner_send[owner, pl.ds(4, 4)] = jnp.zeros((4, LANES), F32)

    def owner_copy(step):
        other = chip_at(AWAY[step - 1])
        return pltpu.make_async_remote_copy(
            src_ref=owner_send.at[other],
            dst_ref=owner_hbm.at[step],
            send_sem=owner_send_sem.at[step - 1],
            recv_sem=owner_recv_sem.at[step - 1],
            device_id=(me_a, 2 * other + core),
            device_id_type=MESH,
        )

    for step in range(1, 16):
        owner_copy(step).start()
    own_copy = pltpu.make_async_copy(owner_send.at[chip], owner_hbm.at[0], owner_sem)
    own_copy.start()
    for copy in halo_copies(1):
        copy.wait_recv()

    def near_group(group, carry):
        for field in range(FIELDS):
            part = PART_OF[field]
            at = pl.ds(pl.multiple_of(field * PLANES + group * 16, 16), 16)
            inside = pl.ds(pl.multiple_of((field - PARTS[part][0]) * PLANES + group * 16, 16), 16)
            value = [filter_halo[0, row, at] for row in range(2)]
            value += [lined[part][row, inside] for row in range(ROWS)]
            value += [filter_halo[1, row, at] for row in range(2)]
            ends = near_tails(value[2:-2], FL)
            for row in range(ROWS):
                up, down = ends[row]
                tails = down if up is None else up if down is None else up + down
                edges = E1 * (value[row + 1] + value[row + 3]) + E2 * (value[row] + value[row + 4])
                near[row, at] = FK * tails + (FK + E0) * value[row + 2] + edges
        return carry

    lax.fori_loop(0, BLOCKS // 2, near_group, 0)
    keep = pltpu.make_async_copy(near, near_hbm, keep_sem)
    keep.start()
    for part in range(2):
        wait_starts(1, part)

    own_copy.wait()
    for step in range(1, 16):
        owner_copy(step).wait_recv()
    keep.wait()

    for which in range(2):
        for part in range(2):
            wait_moment_sends(which, part)
            wait_start_sends(which, part)
            for step in range(1, AXIAL):
                edge_copy(which, part, step).wait_send()
        for copy in halo_copies(which):
            copy.wait_send()
    for step in range(1, 8):
        part_copy(step).wait_send()
    for step in range(1, 16):
        owner_copy(step).wait_send()
    for which in range(2):
        plane_wait(which, plane_send_sem)
        for step in range(1, AXIAL):
            axial_copy(which, step).wait_send()


def per_device(
    density,
    velocity,
    pressure,
    axial_metric,
    azim_metric,
    volume,
    radial_term,
    panel_area,
    observer_ids,
    bin_ids,
    weight_ids,
    bin_weights,
):
    sent, taken, full = both_tables()
    rows = PLANES * ROWS
    slabs = [PLANES * count for _, count in PARTS]
    hbm = pl.BlockSpec(memory_space=pltpu.HBM)
    dma = pltpu.SemaphoreType.DMA
    near, starts, parts = pl.pallas_call(
        kernel,
        out_shape=(
            jax.ShapeDtypeStruct((ROWS, SLAB, LANES), F32),
            jax.ShapeDtypeStruct((SLOTS, TILE_ROWS, LANES), F32),
            jax.ShapeDtypeStruct((16, 8, TIME_BINS), F32),
        ),
        in_specs=[hbm] * 16,
        out_specs=(hbm, hbm, hbm),
        scratch_shapes=[
            pltpu.VMEM((2, 2 * LANES, 2 * LANES), BF16),
            pltpu.VMEM((2, 2, 32, 2 * LANES), BF16),
            pltpu.VMEM((2, 2, 64, 2 * LANES), BF16),
            pltpu.VMEM((rows, LANES), F32),
            pltpu.VMEM((3, rows, LANES), F32),
            pltpu.VMEM((rows, LANES), F32),
            pltpu.VMEM((3, rows, LANES), F32),
            pltpu.VMEM((3, rows, LANES), F32),
            pltpu.VMEM((rows, LANES), F32),
            pltpu.VMEM((FIELDS, rows, LANES), F32),
            pltpu.VMEM((ROWS, LANES), F32),
            pltpu.VMEM((ENTRY_ROWS, LANES), jnp.int32),
            pltpu.VMEM((ENTRY_ROWS, LANES), jnp.int32),
            pltpu.VMEM((ENTRY_ROWS, LANES), jnp.int32),
            pltpu.VMEM((2, LANES), F32),
            pltpu.VMEM((2, ROWS, NAZ), F32),
            pltpu.VMEM((2, NA, LANES), F32),
            pltpu.VMEM((ROWS, SLAB, LANES), F32),
            pltpu.VMEM((ROWS, SLAB, LANES), F32),
            pltpu.VMEM((ROWS, PLANES, LANES), F32),
            *[pltpu.VMEM((2, ROWS * slab, 2 * LANES), BF16) for slab in slabs],
            *[pltpu.VMEM((ROWS, slab, LANES), F32) for slab in slabs],
            *[pltpu.VMEM((2, 2, 8, 4 * slab), F32) for slab in slabs],
            *[pltpu.VMEM((2, AXIAL, 8, 4 * slab), F32) for slab in slabs],
            pltpu.VMEM((2, SLOTS, TILE_ROWS, LANES), F32),
            pltpu.VMEM((2, 2, AZIM, 16, LANES), F32),
            pltpu.VMEM((2, 2, AZIM, 16, LANES), F32),
            pltpu.VMEM((SLOTS, TILE_ROWS, LANES), F32),
            pltpu.VMEM((2, 1, SLAB, LANES), F32),
            pltpu.VMEM((2, 2, SLAB, LANES), F32),
            pltpu.VMEM((ROWS, SLAB, LANES), F32),
            pltpu.VMEM((OBSERVERS, ENTRY_ROWS * LANES), BF16),
            pltpu.VMEM((2 * TIME_BINS, ENTRY_ROWS * LANES), BF16),
            pltpu.VMEM((OBSERVERS, TIME_BINS), F32),
            pltpu.VMEM((7, 64, TIME_BINS), F32),
            pltpu.VMEM((16, 8, TIME_BINS), F32),
            pltpu.VMEM((2, ROWS, LANES), F32),
            pltpu.VMEM((2, AZIM, ROWS, LANES), F32),
            pltpu.VMEM((2, ROWS, LANES), F32),
            pltpu.VMEM((2, AXIAL, ROWS, LANES), F32),
            pltpu.VMEM((BLOCKS // 2, ROWS, LANES), F32),
            dma(()),
            dma(()),
            dma((11,)),
            dma((5, BLOCKS // 2)),
            dma((2, BLOCKS // 2)),
            dma((2, 2, 3)),
            dma((2, 2, 3)),
            dma((2, 2)),
            dma((2, 2)),
            dma((2, 2)),
            dma((2, 2)),
            dma((2, 2, 2)),
            dma((2, 2, 2)),
            dma((7,)),
            dma((7,)),
            dma((15,)),
            dma((15,)),
            dma((2,)),
            dma((2,)),
            dma((2, 3)),
            dma((2, 3)),
        ],
        compiler_params=pltpu.CompilerParams(
            collective_id=0, has_side_effects=True
        ),
    )(
        jnp.asarray(sent),
        jnp.asarray(taken),
        density.reshape(rows, LANES),
        velocity.reshape(3, rows, LANES),
        pressure.reshape(rows, LANES),
        axial_metric.reshape(3, rows, LANES),
        azim_metric.reshape(3, rows, LANES),
        volume.reshape(rows, LANES),
        radial_term.reshape(FIELDS, rows, LANES),
        panel_area,
        observer_ids.reshape(ENTRY_ROWS, LANES),
        bin_ids.reshape(ENTRY_ROWS, LANES),
        weight_ids.reshape(ENTRY_ROWS, LANES),
        bin_weights.reshape(2, LANES),
        jnp.asarray(azimuth_rows()),
        jnp.asarray(full),
    )
    state, signals = pl.pallas_call(
        finish_kernel,
        out_shape=(
            jax.ShapeDtypeStruct((FIELDS, rows, LANES), F32),
            jax.ShapeDtypeStruct((4, TIME_BINS), F32),
        ),
        in_specs=[hbm] * 3,
        out_specs=(hbm, hbm),
        scratch_shapes=[
            pltpu.VMEM((ROWS, FIELDS, PLANES, LANES), F32),
            pltpu.VMEM((SLOTS, TILE_ROWS, LANES), F32),
            pltpu.VMEM((FIELDS, rows, LANES), F32),
            pltpu.VMEM((16, 8, TIME_BINS), F32),
            pltpu.VMEM((4, TIME_BINS), F32),
            dma((BLOCKS // 2, 3)),
            dma((BLOCKS // 2,)),
            dma((2,)),
        ],
    )(
        near.reshape(ROWS, FIELDS, PLANES, LANES),
        starts,
        parts,
    )
    return state.reshape(FIELDS, PLANES, ROWS, LANES), signals


def solution(mesh):
    placed = (
        P(None, "azim", "axial"),
        P(None, None, "azim", "axial"),
        P(None, "azim", "axial"),
        P(None, None, "azim", "axial"),
        P(None, None, "azim", "axial"),
        P(None, "azim", "axial"),
        P(None, None, "azim", "axial"),
        P("azim", "axial"),
        P(None, "azim", "axial"),
        P(None, "azim", "axial"),
        P(None, "azim", "axial"),
        P(),
    )
    return jax.shard_map(
        per_device,
        mesh=mesh,
        in_specs=placed,
        out_specs=(P(None, None, "azim", "axial"), P(("axial", "azim"), None)),
        check_vma=False,
    )
```
